32 devices in a mesh: dp: 8 (over y, x, core), rep: 4 (over z).
Axes of the slice: x: 2, y: 2, z: 4, core: 2. Of those that a mesh axis runs over, the one named last changes fastest.
Arguments:
- tokens: int32 [8, 1024], P('dp', 'rep'), may hold values from 0 to 31999
- segments: int32 [8, 1024], P('dp'), may hold values from 0 to 3, never falling along the last dimension, each value on 1 to 800 neighbouring positions
- completion: int32 [8, 256], P('dp'), may hold values from 0 to 1023, as said below
- targets: int32 [8, 256], P('dp'), may hold values from 0 to 31999
- owners: int32 [32], replicated, may hold values from 0 to 7, as said below
- step_count: int32 [1], replicated, may hold values from 2 to 20
- tile_weight: float32 [192, 192, 768], P(('dp', 'rep')), may hold values from -0.21875 to 0.21875
- tile_first: float32 [192, 192, 768], P(('dp', 'rep')), may hold values from -9.536743e-06 to 9.536743e-06
- tile_second: float32 [192, 192, 768], P(('dp', 'rep')), may hold values from 3.6748382e-13 to 1.4699353e-12
- table_weight: float32 [32000, 768], P(('dp', 'rep')), may hold values from -5 to 5
- table_first: float32 [32000, 768], P(('dp', 'rep')), may hold values from -9.536743e-06 to 9.536743e-06
- table_second: float32 [32000, 768], P(('dp', 'rep')), may hold values from 3.6748382e-13 to 1.4699353e-12
- head_weight: float32 [32000, 768], P(('dp', 'rep')), may hold values from -0.625 to 0.625
- head_first: float32 [32000, 768], P(('dp', 'rep')), may hold values from -9.536743e-06 to 9.536743e-06
- head_second: float32 [32000, 768], P(('dp', 'rep')), may hold values from 3.6748382e-13 to 1.4699353e-12
- gain_weight: float32 [5, 768], replicated, may hold values from 0.5 to 1.5
- gain_first: float32 [5, 768], replicated, may hold values from -3.8146973e-05 to 3.8146973e-05
- gain_second: float32 [5, 768], replicated, may hold values from 5.879741e-12 to 2.3518965e-11
Outputs:
- loss: float32 [], replicated
- clip_norm: float32 [], replicated
- new_tile_weight: float32 [192, 192, 768], P(('dp', 'rep'))
- new_tile_copy: bfloat16 [192, 192, 768], P(('dp', 'rep'))
- new_tile_first: float32 [192, 192, 768], P(('dp', 'rep'))
- new_tile_second: float32 [192, 192, 768], P(('dp', 'rep'))
- new_table_weight: float32 [32000, 768], P(('dp', 'rep'))
- new_table_copy: bfloat16 [32000, 768], P(('dp', 'rep'))
- new_table_first: float32 [32000, 768], P(('dp', 'rep'))
- new_table_second: float32 [32000, 768], P(('dp', 'rep'))
- new_head_weight: float32 [32000, 768], P(('dp', 'rep'))
- new_head_copy: bfloat16 [32000, 768], P(('dp', 'rep'))
- new_head_first: float32 [32000, 768], P(('dp', 'rep'))
- new_head_second: float32 [32000, 768], P(('dp', 'rep'))
- new_gain_weight: float32 [5, 768], replicated
- new_gain_first: float32 [5, 768], replicated
- new_gain_second: float32 [5, 768], replicated
The draws below stay inside these ranges and needn't reach their ends.
Inputs may be any that keep to these rules, and one draw needn't show every extreme that they name: `completion`: in every sequence the 256 positions are distinct and ascending; of each aligned block of 256 positions at most 96 are listed, and in every sequence some block holds exactly 96. `owners`: at most 6 matrices share an owner, and some owner holds exactly 6.
All inputs are finite; a program needn't handle non-finite values.
Results may differ from the reference program's by a relative error of at most 0.012.
The reference program's roundings to bfloat16 on the way count: a program that leaves them out, or rounds other values in their place, can miss the bound.
Values may be sent and summed in bfloat16 or wider, within the bound.
A program may use at most 640 MiB of HBM per device.

```python
import math
import jax
import jax.numpy as jnp
import numpy as np
from jax import lax

D = 768
HEADS = 12
HD = 64
FF = 3072
VOCAB = 32000
LAYERS = 2
SEQ_LEN = 1024
COMP = 256
SEQS = 8
TPL = 16
NTILE = 32
CAP = 6
NPARAM = 68030208
N_DP = 8
N_REP = 4


def draw_completion(key, part):
    block = SEQ_LEN // N_REP
    capacity = 3 * COMP // (2 * N_REP)

    def one_sequence(sequence_key):
        first, second, third = jax.random.split(sequence_key, 3)
        heavy = jax.random.randint(first, (), 0, N_REP)
        offsets = jax.vmap(lambda inner: jax.random.permutation(inner, block))(jax.random.split(second, N_REP))
        order = (heavy + jnp.arange(N_REP)) % N_REP
        starts = order[:, None] * block + jnp.take(offsets, order, axis=0)[:, :capacity]
        others = jax.random.permutation(third, starts[1:].reshape(-1))[:COMP - capacity]
        return jnp.sort(jnp.concatenate([starts[0], others])).astype(jnp.int32)
    return jax.vmap(one_sequence)(jax.random.split(key, SEQS))


def draw_owners(key, part):
    first, second, third = jax.random.split(key, 3)
    heavy = jax.random.randint(first, (), 0, N_DP)
    others = (heavy + 1 + jnp.arange((N_DP - 1) * CAP) // CAP) % N_DP
    chosen = jax.random.permutation(third, others)[:NTILE - CAP]
    ranked = jnp.concatenate([jnp.full((CAP,), heavy, jnp.int32), chosen.astype(jnp.int32)])
    places = jax.random.permutation(second, NTILE)
    return jnp.zeros((NTILE,), jnp.int32).at[places].set(ranked)


def place_ends(array, own_key, least, high):
    extent = array.shape
    spot = [jax.random.randint(jax.random.fold_in(own_key, axis), (), 0, extent[axis]) for axis in range(len(extent))]
    array = array.at[tuple(spot)].set(least)
    longest = extent.index(max(extent))
    spot[longest] = (spot[longest] + 1) % extent[longest]
    return array.at[tuple(spot)].set(high)


def block_levels(key, dims, shards, least, largest):
    level = 1.0
    for axis_at, shards_of in shards:
        heights = jax.random.uniform(jax.random.fold_in(jax.random.fold_in(key, 6), axis_at), (shards_of,), jnp.float32, least / len(shards), largest / len(shards))
        level = level * jnp.repeat(jnp.exp(heights), dims[axis_at] // shards_of).reshape((-1,) + (1,) * (len(dims) - 1 - axis_at))
    return level


def cumulative_ranks(amount, slope):
    portions = [(1 << 20) // math.isqrt(rank ** slope) + 1 for rank in range(1, amount + 1)]
    spread = 1 + sum(portions) // (1 << 30)
    return np.cumsum(np.array([max(1, weight // spread) for weight in portions]))


def ranked_ids(stream_key, shape, amount, slope):
    table = cumulative_ranks(amount, slope)
    lot = jax.random.randint(jax.random.fold_in(stream_key, 1), shape, 0, int(table[amount - 1]))
    standing = jnp.searchsorted(jnp.asarray(table, jnp.int32), lot, side="right")
    return jax.random.permutation(jax.random.fold_in(stream_key, 2), amount)[standing].astype(jnp.int32)


def length_profile(count, total, bound, skew):
    portions = [(1 << 20) // math.isqrt(rank ** skew) + 1 for rank in range(2, count + 1)]
    rest, holding = total - bound - (count - 1), [1] * (count - 1)
    while rest > 0:
        movable = [i for i in range(count - 1) if holding[i] < bound]
        mass, left = sum([portions[i] for i in movable]), rest
        for i in movable:
            addition = min(bound - holding[i], max(1, left * portions[i] // mass), rest)
            holding[i] = holding[i] + addition
            rest = rest - addition
    return np.array([bound] + holding)


def uneven_parts(rng, count, total, bound, slope):
    if count == 2:
        one = jax.random.randint(rng, (), max(1, total - bound), min(bound, total - 1) + 1)
        return jnp.stack([one, total - one])
    lengths = jnp.asarray(length_profile(count, total, bound, slope), jnp.int32)
    pairs = (count - 1) // 2
    giver, sink = lengths[1:1 + 2 * pairs:2], lengths[2:2 + 2 * pairs:2]
    slack = jnp.minimum(giver - 1, bound - sink)
    shifted = jax.random.randint(jax.random.fold_in(rng, 1), (pairs,), 0, 1 << 20) % (slack + 1)
    lengths = lengths.at[1:1 + 2 * pairs:2].set(giver - shifted).at[2:2 + 2 * pairs:2].set(sink + shifted)
    return lengths[jax.random.permutation(jax.random.fold_in(rng, 2), count)]


def centred(stream_key, dims, scale, limit, cuts=(), held_as=jnp.bfloat16):
    result = jax.random.normal(stream_key, dims, jnp.float32) * scale
    if len(cuts) > 0:
        result = block_levels(stream_key, dims, cuts, -0.22, 0.18) * result
    return jnp.clip(result, min=-limit, max=limit).astype(held_as)


def setup_inputs(seed: int = 0) -> dict:
    seeds = jax.random.split(jax.random.key(seed), 19)
    tokens = place_ends(ranked_ids(seeds[0], (SEQS, SEQ_LEN), VOCAB, 2), jax.random.fold_in(seeds[0], 3), 0, VOCAB - 1).astype(jnp.int32)
    segments = jax.vmap(lambda own: jnp.searchsorted(jnp.cumsum(uneven_parts(own, 4, SEQ_LEN, SEQ_LEN * 25 // 32, 0)), jnp.arange(SEQ_LEN), side="right"))(jax.random.split(seeds[1], SEQS)).reshape((SEQS, SEQ_LEN)).astype(jnp.int32)
    completion = draw_completion(jax.random.fold_in(seeds[18], 71), 0)
    targets = place_ends(ranked_ids(seeds[3], (SEQS, COMP), VOCAB, 2), jax.random.fold_in(seeds[3], 3), 0, VOCAB - 1).astype(jnp.int32)
    owners = draw_owners(jax.random.fold_in(seeds[18], 71), 0)
    step_count = jax.random.randint(seeds[5], (1,), 2, 21).astype(jnp.int32)
    tile_weight = centred(seeds[6], (N_DP * N_REP * CAP, D // N_REP, D), D ** -0.5, 0.21875, ((0, 32),), jnp.float32)
    tile_first = centred(seeds[7], (N_DP * N_REP * CAP, D // N_REP, D), (0.005 * NPARAM ** -0.5), 9.5367431640625e-06, ((0, 32),), jnp.float32)
    tile_second = jnp.clip(jnp.exp(math.log(1.4699352846037073e-12) - 1.3862944 * jax.random.uniform(seeds[8], (N_DP * N_REP * CAP, D // N_REP, D), jnp.float32) ** block_levels(seeds[8], (N_DP * N_REP * CAP, D // N_REP, D), ((0, 32),), -0.2, 0.2)), 3.674838211509268e-13, 1.4699352846037073e-12)
    table_weight = centred(seeds[9], (VOCAB, D), 1.0, 5.0, ((0, 32),), jnp.float32)
    table_first = centred(seeds[10], (VOCAB, D), (0.005 * NPARAM ** -0.5), 9.5367431640625e-06, ((0, 32),), jnp.float32)
    table_second = jnp.clip(jnp.exp(math.log(1.4699352846037073e-12) - 1.3862944 * jax.random.uniform(seeds[11], (VOCAB, D), jnp.float32) ** block_levels(seeds[11], (VOCAB, D), ((0, 32),), -0.2, 0.2)), 3.674838211509268e-13, 1.4699352846037073e-12)
    head_weight = centred(seeds[12], (VOCAB, D), (3.0 * D ** -0.5), 0.625, ((0, 32),), jnp.float32)
    head_first = centred(seeds[13], (VOCAB, D), (0.005 * NPARAM ** -0.5), 9.5367431640625e-06, ((0, 32),), jnp.float32)
    head_second = jnp.clip(jnp.exp(math.log(1.4699352846037073e-12) - 1.3862944 * jax.random.uniform(seeds[14], (VOCAB, D), jnp.float32) ** block_levels(seeds[14], (VOCAB, D), ((0, 32),), -0.2, 0.2)), 3.674838211509268e-13, 1.4699352846037073e-12)
    gain_weight = jnp.clip(1.0 + 0.1 * jax.random.normal(seeds[15], (2 * LAYERS + 1, D), jnp.float32), 0.5, 1.5)
    gain_first = centred(seeds[16], (2 * LAYERS + 1, D), (0.02 * NPARAM ** -0.5), 3.814697265625e-05, (), jnp.float32)
    gain_second = jnp.clip(jnp.exp(jax.random.uniform(seeds[17], (2 * LAYERS + 1, D), jnp.float32, math.log(5.879741138414829e-12), math.log(2.3518964553659316e-11))), 5.879741138414829e-12, 2.3518964553659316e-11)
    return {"tokens": tokens, "segments": segments, "completion": completion, "targets": targets, "owners": owners, "step_count": step_count, "tile_weight": tile_weight, "tile_first": tile_first, "tile_second": tile_second, "table_weight": table_weight, "table_first": table_first, "table_second": table_second, "head_weight": head_weight, "head_first": head_first, "head_second": head_second, "gain_weight": gain_weight, "gain_first": gain_first, "gain_second": gain_second}


HIGHEST_ACCURACY = lax.Precision.HIGHEST
EPS_NORM = 1e-05
EPS_ADAM = 1e-08
CLIP_NORM = 0.005
BETA_FIRST = 0.5
BETA_SECOND = 0.5
DECAY = 0.1
RATE_TILE = 0.02
RATE_HEAD = 0.05
RATE_TABLE = 0.5
RATE_GAIN = 0.3
MASKED = -1e+30

@jax.custom_vjp
def low(v):
    return lax.optimization_barrier(v.astype(jnp.bfloat16)).astype(jnp.float32)

@jax.custom_vjp
def lowered_backward(v):
    return v

def low_keep(v):
    return (low(v), None)

def low_pass(kept, grad):
    return (grad,)

def back_keep(v):
    return (v, None)

def back_low(kept, grad):
    return (low(grad),)
low.defvjp(low_keep, low_pass)
lowered_backward.defvjp(back_keep, back_low)

def root_norm(training_state, gain):
    return training_state * lax.rsqrt(lax.optimization_barrier(jnp.mean(training_state * training_state, axis=-1, keepdims=True)) + EPS_NORM) * gain

def rope_tables(places, width):
    half = width // 2
    freqs = jnp.power(10000.0, -2.0 * jnp.arange(half).astype(jnp.float32) / width)
    angle = places[:, None] * freqs[None, :]
    return (jnp.cos(angle), jnp.sin(angle))

def rotate(field, cosine, sine):
    half = field.shape[-1] // 2
    first, second = (field[..., :half], field[..., half:])
    cosine, sine = (cosine[:, None, :], sine[:, None, :])
    return jnp.concatenate([first * cosine - second * sine, second * cosine + first * sine], axis=-1)

def tile_slots(owners):
    order = jnp.arange(owners.shape[0], dtype=jnp.int32)
    same = (owners[:, None] == owners[None, :]) & (order[None, :] < order[:, None])
    return lax.optimization_barrier(jnp.sum(same.astype(jnp.int32), axis=1))

def from_owners(stored, owners, slots, dp_size, rep_size, slots_cap):
    width = stored.shape[-1]
    grid = stored.reshape(dp_size, rep_size, slots_cap, -1, width).transpose(0, 2, 1, 3, 4)
    grid = grid.reshape(dp_size * slots_cap, -1, width)
    return jnp.take(grid, owners * slots_cap + slots, axis=0)

def to_owners(tiles, owners, slots, dp_size, rep_size, slots_cap):
    width = tiles.shape[-1]
    grid = jnp.zeros((dp_size * slots_cap,) + tiles.shape[1:], tiles.dtype).at[owners * slots_cap + slots].set(tiles)
    grid = grid.reshape(dp_size, slots_cap, rep_size, -1, width).transpose(0, 2, 1, 3, 4)
    return grid.reshape(dp_size * rep_size * slots_cap, -1, width)

def layer_weights(tiles):
    units = FF // D
    input_projection_weight = tiles[0:3].transpose(1, 0, 2).reshape(D, 3 * D)
    output_projection_weight = tiles[3]
    gate_projection_weight = tiles[4:4 + 2 * units].transpose(1, 0, 2).reshape(D, 2 * FF)
    down_projection_weight = tiles[4 + 2 * units:4 + 3 * units].reshape(FF, D)
    return (input_projection_weight, output_projection_weight, gate_projection_weight, down_projection_weight)

def attend(query, keys, value, segment):
    raw = lowered_backward(jnp.einsum('qhd,khd->hqk', query, keys, precision=HIGHEST_ACCURACY))
    scores = raw * HD ** (-0.5)
    place = jnp.arange(query.shape[0])
    allowed = (place[None, :] <= place[:, None]) & (segment[None, :] == segment[:, None])
    scores = jnp.where(allowed[None], scores, MASKED)
    top = lax.optimization_barrier(jnp.max(scores, axis=-1, keepdims=True))
    exponent = jnp.exp(scores - top)
    prob = low(exponent / lax.optimization_barrier(jnp.sum(exponent, axis=-1, keepdims=True)))
    return jnp.einsum('hqk,khd->qhd', prob, value, precision=HIGHEST_ACCURACY)

def layer(training_state, tiles, gains, index, cosine, sine, segments):
    input_projection_weight, output_projection_weight, gate_projection_weight, down_projection_weight = layer_weights(low(tiles))
    batch, length = (training_state.shape[0], training_state.shape[1])
    normalized_input = low(root_norm(training_state, gains[2 * index]))
    mixed_heads_output = lowered_backward(jnp.einsum('chf,fr->chr', normalized_input, input_projection_weight, precision=HIGHEST_ACCURACY))
    parts = mixed_heads_output.reshape(batch, length, 3, HEADS, HD)
    query = low(rotate(parts[:, :, 0], cosine, sine))
    keys = low(rotate(parts[:, :, 1], cosine, sine))
    value = low(parts[:, :, 2])
    attention_heads = lax.map(lambda item: jax.checkpoint(attend)(*item), (query, keys, value, segments))
    attention_heads = lowered_backward(low(attention_heads.reshape(batch, length, D)))
    middle_activation = training_state + lowered_backward(jnp.einsum('chf,fr->chr', attention_heads, output_projection_weight, precision=HIGHEST_ACCURACY))
    normalized_input = low(root_norm(middle_activation, gains[2 * index + 1]))
    gate_upward_product = lowered_backward(jnp.einsum('chf,fr->chr', normalized_input, gate_projection_weight, precision=HIGHEST_ACCURACY))
    hidden_state = low(jax.nn.silu(gate_upward_product[..., :FF]) * gate_upward_product[..., FF:])
    return middle_activation + lowered_backward(jnp.einsum('yxt,th->yxh', hidden_state, down_projection_weight, precision=HIGHEST_ACCURACY))

def forward(tiles, table, head, gains, tokens, segments, completion, targets):
    length = tokens.shape[1]
    cosine, sine = rope_tables(jnp.arange(length).astype(jnp.float32), HD)
    training_state = lowered_backward(jnp.take(low(table), tokens, axis=0))
    for index in range(LAYERS):
        training_state = layer(training_state, tiles[index * TPL:(index + 1) * TPL], gains, index, cosine, sine, segments)
    final = low(root_norm(training_state, gains[2 * LAYERS]))
    picked = jnp.take_along_axis(final, completion[:, :, None], axis=1)
    head_low = low(head)

    def row_loss(rows, wanted):
        logits = lowered_backward(jnp.dot(rows, head_low.T, precision=HIGHEST_ACCURACY))
        top = lax.optimization_barrier(jnp.max(logits, axis=-1, keepdims=True))
        log_total = jnp.log(lax.optimization_barrier(jnp.sum(jnp.exp(logits - top), axis=-1))) + top[:, 0]
        chosen = jnp.take_along_axis(logits, wanted[:, None], axis=1)[:, 0]
        return jnp.sum(log_total - chosen)
    losses = lax.map(lambda item: jax.checkpoint(row_loss)(*item), (picked, targets))
    return jnp.sum(losses) / (picked.shape[0] * picked.shape[1])

def adam(weight, first, second, grad, factor, rate, decay, steps):
    grad = grad * factor
    first = BETA_FIRST * first + (1.0 - BETA_FIRST) * grad
    second = BETA_SECOND * second + (1.0 - BETA_SECOND) * grad * grad
    first_hat = first / (1.0 - jnp.power(BETA_FIRST, steps))
    second_hat = second / (1.0 - jnp.power(BETA_SECOND, steps))
    weight = weight - rate * (first_hat / (jnp.sqrt(second_hat) + EPS_ADAM) + decay * weight)
    return (weight, first, second)

def reference(tokens, segments, completion, targets, owners, step_count, tile_weight, tile_first, tile_second, table_weight, table_first, table_second, head_weight, head_first, head_second, gain_weight, gain_first, gain_second):
    slots = tile_slots(owners)
    tiles = from_owners(tile_weight, owners, slots, N_DP, N_REP, CAP)

    def loss_of(tile_set, table, head, gains):
        return forward(tile_set, table, head, gains, tokens, segments, completion, targets)
    loss, pullback = jax.vjp(loss_of, tiles, table_weight, head_weight, gain_weight)
    tile_grad, table_grad, head_grad, gain_grad = pullback(jnp.ones_like(loss))
    square = jnp.sum(tile_grad * tile_grad) + jnp.sum(table_grad * table_grad)
    square = square + jnp.sum(head_grad * head_grad) + jnp.sum(gain_grad * gain_grad)
    norm = jnp.sqrt(square)
    factor = jnp.minimum(1.0, CLIP_NORM / norm)
    steps = step_count[0].astype(jnp.float32)
    new_tiles, new_first, new_second = adam(tiles, from_owners(tile_first, owners, slots, N_DP, N_REP, CAP), from_owners(tile_second, owners, slots, N_DP, N_REP, CAP), tile_grad, factor, RATE_TILE, DECAY, steps)
    tile_out = to_owners(new_tiles, owners, slots, N_DP, N_REP, CAP)
    first_out = to_owners(new_first, owners, slots, N_DP, N_REP, CAP)
    second_out = to_owners(new_second, owners, slots, N_DP, N_REP, CAP)
    table_new, table_first_new, table_second_new = adam(table_weight, table_first, table_second, table_grad, factor, RATE_TABLE, DECAY, steps)
    head_new, head_first_new, head_second_new = adam(head_weight, head_first, head_second, head_grad, factor, RATE_HEAD, DECAY, steps)
    gain_new, gain_first_new, gain_second_new = adam(gain_weight, gain_first, gain_second, gain_grad, factor, RATE_GAIN, 0.0, steps)
    return (loss, norm, tile_out, tile_out.astype(jnp.bfloat16), first_out, second_out, table_new, table_new.astype(jnp.bfloat16), table_first_new, table_second_new, head_new, head_new.astype(jnp.bfloat16), head_first_new, head_second_new, gain_new, gain_first_new, gain_second_new)
```

```python
import jax
import jax.numpy as jnp
from jax import lax
from jax.sharding import Mesh, PartitionSpec as P

D = 768
HEADS = 12
HD = 64
FF = 3072
LAYERS = 2


EPS_NORM = 1e-05
EPS_ADAM = 1e-08
CLIP_NORM = 0.005
BETA_FIRST = 0.5
BETA_SECOND = 0.5
DECAY = 0.1
RATE_TILE = 0.02
RATE_HEAD = 0.05
RATE_TABLE = 0.5
RATE_GAIN = 0.3
MASKED = -1e30


def root_norm(training_state, gain):
    return (
        training_state
        * lax.rsqrt(jnp.mean(training_state * training_state, axis=-1, keepdims=True) + EPS_NORM)
        * gain
    )


def norm_back(training_state, gain, grad):
    scale = lax.rsqrt(jnp.mean(training_state * training_state, axis=-1, keepdims=True) + EPS_NORM)
    scaled = grad * gain
    state_grad = scale * scaled - training_state * scale**3 * jnp.mean(
        scaled * training_state, axis=-1, keepdims=True
    )
    gain_grad = jnp.sum(
        (grad * training_state * scale).reshape(-1, training_state.shape[-1]), axis=0
    )
    return (state_grad, gain_grad)


def rope_tables(places, width):
    half = width // 2
    freqs = jnp.power(10000.0, -2.0 * jnp.arange(half).astype(jnp.float32) / width)
    angle = places[:, None] * freqs[None, :]
    return (jnp.cos(angle), jnp.sin(angle))


def rotate(field, cosine, sine):
    half = field.shape[-1] // 2
    first, second = (field[..., :half], field[..., half:])
    cosine, sine = (cosine[:, None, :], sine[:, None, :])
    return jnp.concatenate(
        [first * cosine - second * sine, second * cosine + first * sine], axis=-1
    )


def rotate_back(field, cosine, sine):
    half = field.shape[-1] // 2
    first, second = (field[..., :half], field[..., half:])
    cosine, sine = (cosine[:, None, :], sine[:, None, :])
    return jnp.concatenate(
        [first * cosine + second * sine, second * cosine - first * sine], axis=-1
    )


def tile_slots(owners):
    order = jnp.arange(owners.shape[0], dtype=jnp.int32)
    same = (owners[:, None] == owners[None, :]) & (order[None, :] < order[:, None])
    return jnp.sum(same.astype(jnp.int32), axis=1)


def adam(weight, first, second, grad, factor, rate, decay, steps):
    grad = grad * factor
    first = BETA_FIRST * first + (1.0 - BETA_FIRST) * grad
    second = BETA_SECOND * second + (1.0 - BETA_SECOND) * grad * grad
    first_hat = first / (1.0 - jnp.power(BETA_FIRST, steps))
    second_hat = second / (1.0 - jnp.power(BETA_SECOND, steps))
    weight = weight - rate * (first_hat / (jnp.sqrt(second_hat) + EPS_ADAM) + decay * weight)
    return (weight, first, second)


ALL = ("a", "b", "rep")
DP = ("a", "b")
UNITS = FF // D
TILES_PER = 4 + 3 * UNITS


def mm(x, w):
    return jnp.einsum("ld,de->le", x, w, preferred_element_type=jnp.float32)


def mm_t(x, w):
    return jnp.einsum("le,de->ld", x, w, preferred_element_type=jnp.float32)


def mm_g(x, y):
    return jnp.einsum("ld,le->de", x, y, preferred_element_type=jnp.float32)


def heads(x):
    return x.reshape(x.shape[0], HEADS, HD)


def layer_forward(state, tiles, gain_pair, cosine, sine, allowed):
    rows = state.shape[0]
    normed = root_norm(state, gain_pair[0]).astype(jnp.bfloat16)
    query, keys, value = [mm(normed, tiles[i]) for i in range(3)]
    query = rotate(heads(query), cosine, sine).astype(jnp.bfloat16)
    keys = rotate(heads(keys), cosine, sine).astype(jnp.bfloat16).reshape(rows, D)
    both = jnp.concatenate([keys, value.astype(jnp.bfloat16)], axis=1)
    both = lax.all_gather(both, "b", axis=0, tiled=True)
    keys_all, value_all = heads(both[:, :D]), heads(both[:, D:])
    scores = jnp.einsum("qhd,khd->hqk", query, keys_all, preferred_element_type=jnp.float32) * HD ** (
        -0.5
    )
    scores = jnp.where(allowed, scores, MASKED)
    top = jnp.max(scores, axis=-1, keepdims=True)
    exponent = jnp.exp(scores - top)
    total = jnp.sum(exponent, axis=-1, keepdims=True)
    prob = (exponent / total).astype(jnp.bfloat16)
    log_total = top + jnp.log(total)
    attended = jnp.einsum("hqk,khd->qhd", prob, value_all, preferred_element_type=jnp.float32)
    attended = attended.reshape(rows, D).astype(jnp.bfloat16)
    middle = state + mm(attended, tiles[3])
    normed_feed = root_norm(middle, gain_pair[1]).astype(jnp.bfloat16)
    gates = [mm(normed_feed, tiles[4 + i]) for i in range(UNITS)]
    ups = [mm(normed_feed, tiles[4 + UNITS + i]) for i in range(UNITS)]
    hidden = [(jax.nn.silu(g) * u).astype(jnp.bfloat16) for g, u in zip(gates, ups)]
    output = middle + sum(mm(h, tiles[4 + 2 * UNITS + i]) for i, h in enumerate(hidden))
    return output, (
        state,
        middle,
        normed,
        normed_feed,
        query,
        keys_all,
        value_all,
        log_total,
        attended,
        gates,
        ups,
        hidden,
    )


def layer_backward(grad, kept, tiles, gain_pair, cosine, sine, allowed):
    (
        state,
        middle,
        normed,
        normed_feed,
        query,
        keys_all,
        value_all,
        log_total,
        attended,
        gates,
        ups,
        hidden,
    ) = kept
    rows = state.shape[0]
    branch = grad.astype(jnp.bfloat16)
    down_grads, gate_grads, up_grads = [], [], []
    feed_back = 0.0
    for i in range(UNITS):
        down_grads.append(mm_g(hidden[i], branch))
        hidden_grad = mm_t(branch, tiles[4 + 2 * UNITS + i])
        sigma = jax.nn.sigmoid(gates[i])
        gate_back = (hidden_grad * ups[i] * sigma * (1.0 + gates[i] * (1.0 - sigma))).astype(
            jnp.bfloat16
        )
        up_back = (hidden_grad * gates[i] * sigma).astype(jnp.bfloat16)
        gate_grads.append(mm_g(normed_feed, gate_back))
        up_grads.append(mm_g(normed_feed, up_back))
        feed_back = (
            feed_back + mm_t(gate_back, tiles[4 + i]) + mm_t(up_back, tiles[4 + UNITS + i])
        )
    back, feed_gain = norm_back(middle, gain_pair[1], feed_back)
    middle_grad = grad + back
    branch = middle_grad.astype(jnp.bfloat16)
    out_grad = mm_g(attended, branch)
    heads_grad = heads(mm_t(branch, tiles[3]).astype(jnp.bfloat16))
    scores = jnp.einsum("qhd,khd->hqk", query, keys_all, preferred_element_type=jnp.float32) * HD ** (
        -0.5
    )
    prob = jnp.exp(jnp.where(allowed, scores, MASKED) - log_total)
    value_part = jnp.einsum(
        "hqk,qhd->khd", prob.astype(jnp.bfloat16), heads_grad, preferred_element_type=jnp.float32
    )
    prob_grad = jnp.einsum("qhd,khd->hqk", heads_grad, value_all, preferred_element_type=jnp.float32)
    score_grad = (
        prob * (prob_grad - jnp.sum(prob * prob_grad, axis=-1, keepdims=True)) * HD ** (-0.5)
    ).astype(jnp.bfloat16)
    query_grad = jnp.einsum("hqk,khd->qhd", score_grad, keys_all, preferred_element_type=jnp.float32)
    keys_part = jnp.einsum("hqk,qhd->khd", score_grad, query, preferred_element_type=jnp.float32)
    length = keys_part.shape[0]
    both = jnp.concatenate([keys_part.reshape(length, D), value_part.reshape(length, D)], axis=1)
    both = lax.psum_scatter(both.astype(jnp.bfloat16), "b", scatter_dimension=0, tiled=True)
    keys_grad, value_grad = both[:, :D].astype(jnp.float32), both[:, D:]
    parts = [
        rotate_back(query_grad, cosine, sine).reshape(rows, D).astype(jnp.bfloat16),
        rotate_back(heads(keys_grad), cosine, sine).reshape(rows, D).astype(jnp.bfloat16),
        value_grad,
    ]
    input_grads = [mm_g(normed, p) for p in parts]
    back, attend_gain = norm_back(
        state, gain_pair[0], sum(mm_t(p, tiles[i]) for i, p in enumerate(parts))
    )
    tiles_grad = jnp.stack(
        [
            t.astype(jnp.bfloat16)
            for t in input_grads + [out_grad] + gate_grads + up_grads + down_grads
        ]
    )
    return middle_grad + back, tiles_grad, [attend_gain, feed_gain]


def shards(
    tokens,
    segments,
    completion,
    targets,
    owners,
    step_count,
    tile_weight,
    tile_first,
    tile_second,
    table_weight,
    table_first,
    table_second,
    head_weight,
    head_first,
    head_second,
    gain_weight,
    gain_first,
    gain_second,
):
    a_size, b_size, rep_size = [lax.axis_size(n) for n in ALL]
    a_index, b_index, rep_index = [lax.axis_index(n) for n in ALL]
    dp_size = a_size * b_size
    devices = dp_size * rep_size
    dp_index = a_index * b_size + b_index
    device = dp_index * rep_size + rep_index
    rows = tokens.shape[1]
    length = segments.shape[1]
    comp = completion.shape[1]
    slots_cap, tile_rows = tile_weight.shape[:2]
    tile_count = owners.shape[0]
    home_tiles = tile_count // dp_size
    vocab_rows = table_weight.shape[0]
    vocab_start = device * vocab_rows
    sequence = a_index * rep_size + rep_index

    own_part = jnp.concatenate(
        [
            tokens[0],
            lax.dynamic_slice_in_dim(segments[0], rep_index * rows, rows),
            lax.dynamic_slice_in_dim(completion[0], rep_index * (comp // rep_size), comp // rep_size),
            lax.dynamic_slice_in_dim(targets[0], rep_index * (comp // rep_size), comp // rep_size),
        ]
    )
    packed = lax.all_gather(own_part, ALL, axis=0, tiled=False).reshape(dp_size, rep_size, -1)
    tokens_all = packed[:, :, :rows].reshape(dp_size, length)
    segments_all = packed[:, :, rows : 2 * rows].reshape(dp_size, length)
    edge = 2 * rows + comp // rep_size
    completion_all = packed[:, :, 2 * rows : edge].reshape(dp_size, comp)
    targets_all = packed[:, :, edge:].reshape(dp_size, comp)

    slots = tile_slots(owners)
    mine = owners == dp_index
    tile_low = tile_weight.astype(jnp.bfloat16)
    placed = jnp.where(mine[:, None, None], jnp.take(tile_low, jnp.where(mine, slots, 0), axis=0), 0)
    home = lax.psum_scatter(placed, DP, scatter_dimension=0, tiled=True)
    spread = lax.all_gather(home, ALL, axis=0, tiled=True)
    spread = spread.reshape(dp_size, rep_size, home_tiles, tile_rows, D)
    tiles = spread.transpose(0, 2, 1, 3, 4).reshape(tile_count, D, D)

    order = tokens_all.reshape(a_size, rep_size, b_size, rows).transpose(0, 2, 1, 3).reshape(-1)
    place = order - vocab_start
    vocab_iota = jnp.arange(vocab_rows)
    token_hot = (place[:, None] == vocab_iota[None, :]).astype(jnp.bfloat16)
    picked = jnp.dot(
        token_hot, table_weight.astype(jnp.bfloat16), preferred_element_type=jnp.float32
    ).astype(jnp.bfloat16)
    state = lax.psum_scatter(picked, ALL, scatter_dimension=0, tiled=True).astype(jnp.float32)

    first_place = b_index * rows
    places = first_place + jnp.arange(rows)
    cosine, sine = rope_tables(places.astype(jnp.float32), HD)
    own_segments = lax.dynamic_index_in_dim(segments_all, sequence, 0, False)
    query_segments = lax.dynamic_slice_in_dim(own_segments, first_place, rows)
    allowed = (jnp.arange(length)[None, :] <= places[:, None]) & (
        query_segments[:, None] == own_segments[None, :]
    )
    allowed = allowed[None]
    kept_list = []
    for index in range(LAYERS):
        state, kept = layer_forward(
            state,
            tiles[index * TILES_PER : (index + 1) * TILES_PER],
            gain_weight[2 * index : 2 * index + 2],
            cosine,
            sine,
            allowed,
        )
        kept_list.append(kept)
    final_gain = gain_weight[2 * LAYERS]
    final = root_norm(state, final_gain).astype(jnp.bfloat16)

    capacity = 3 * comp // (2 * rep_size)
    block = completion_all // rows
    inside = block[:, None, :] == jnp.arange(b_size)[None, :, None]
    rank = jnp.cumsum(inside.astype(jnp.int32), axis=2) - 1
    slot_pick = inside[..., None] & (rank[..., None] == jnp.arange(capacity))
    filled = jnp.any(slot_pick, axis=2)
    wanted = jnp.where(
        filled, jnp.sum(jnp.where(slot_pick, targets_all[:, None, :, None], 0), axis=2), -1
    )
    spots = jnp.where(
        filled, jnp.sum(jnp.where(slot_pick, (completion_all % rows)[:, None, :, None], 0), axis=2), -1
    )
    all_wanted = (
        wanted.reshape(a_size, rep_size, b_size, capacity).transpose(0, 2, 1, 3).reshape(-1)
    )
    own_spots = lax.dynamic_index_in_dim(
        lax.dynamic_index_in_dim(spots, sequence, 0, False), b_index, 0, False
    )
    select = (own_spots[:, None] == jnp.arange(rows)[None, :]).astype(jnp.bfloat16)
    chosen = jnp.dot(select, final, preferred_element_type=jnp.float32).astype(jnp.bfloat16)
    all_rows = lax.all_gather(chosen, ALL, axis=0, tiled=True)
    head_low = head_weight.astype(jnp.bfloat16)
    logits = jnp.einsum("rd,vd->rv", all_rows, head_low, preferred_element_type=jnp.float32)
    hot = vocab_iota[None, :] == (all_wanted - vocab_start)[:, None]
    local_top = jnp.max(logits, axis=-1)
    local_total = jnp.sum(jnp.exp(logits - local_top[:, None]), axis=-1)
    local_hit = jnp.sum(jnp.where(hot, logits, 0.0), axis=-1)
    stats = lax.all_gather(
        jnp.stack([local_top, local_total, local_hit]), ALL, axis=0, tiled=False
    )
    top = jnp.max(stats[:, 0], axis=0)
    total = jnp.sum(stats[:, 1] * jnp.exp(stats[:, 0] - top[None]), axis=0)
    log_total = top + jnp.log(total)
    valid = all_wanted >= 0
    scored = dp_size * comp
    loss = jnp.sum(jnp.where(valid, log_total - jnp.sum(stats[:, 2], axis=0), 0.0)) / scored
    logit_grad = jnp.where(
        valid[:, None],
        (jnp.exp(logits - log_total[:, None]) - jnp.where(hot, 1.0, 0.0)) / scored,
        0.0,
    ).astype(jnp.bfloat16)
    rows_grad = jnp.dot(logit_grad, head_low, preferred_element_type=jnp.float32)
    own_rows = lax.psum_scatter(
        rows_grad.astype(jnp.bfloat16), ALL, scatter_dimension=0, tiled=True
    )
    head_grad = jnp.einsum("rv,rd->vd", logit_grad, all_rows, preferred_element_type=jnp.float32)
    final_grad = jnp.einsum("ct,cd->td", select, own_rows, preferred_element_type=jnp.float32)
    state_grad, final_gain_grad = norm_back(state, final_gain, final_grad)
    tile_parts = [None] * LAYERS
    gain_parts = [None] * LAYERS
    for index in reversed(range(LAYERS)):
        state_grad, tile_parts[index], gain_parts[index] = layer_backward(
            state_grad,
            kept_list[index],
            tiles[index * TILES_PER : (index + 1) * TILES_PER],
            gain_weight[2 * index : 2 * index + 2],
            cosine,
            sine,
            allowed,
        )
    piece_grads = lax.all_gather(state_grad.astype(jnp.bfloat16), ALL, axis=0, tiled=True)
    table_grad = jnp.einsum(
        "tv,td->vd", token_hot, piece_grads, preferred_element_type=jnp.float32
    )
    tile_grads = jnp.concatenate(tile_parts, axis=0).reshape(
        dp_size, home_tiles, rep_size, tile_rows, D
    )
    home_grad = lax.psum_scatter(
        tile_grads.transpose(0, 2, 1, 3, 4).reshape(-1, tile_rows, D),
        ALL,
        scatter_dimension=0,
        tiled=True,
    )
    plane_grad = lax.all_gather(home_grad, DP, axis=0, tiled=True)
    own_count = jnp.sum(mine.astype(jnp.int32))
    slot_ids = jnp.arange(slots_cap)
    tile_of_slot = jnp.sum(
        jnp.where(
            mine[None, :] & (slots[None, :] == slot_ids[:, None]), jnp.arange(tile_count)[None, :], 0
        ),
        axis=1,
    )
    slot_valid = (slot_ids < own_count)[:, None, None]
    own_grad = jnp.where(
        slot_valid, jnp.take(plane_grad, tile_of_slot, axis=0).astype(jnp.float32), 0.0
    )
    gain_grads = jnp.stack([g for pair in gain_parts for g in pair] + [final_gain_grad])
    square = (
        jnp.sum(own_grad * own_grad)
        + jnp.sum(table_grad * table_grad)
        + jnp.sum(head_grad * head_grad)
    )
    square, gain_grads = lax.psum((square, gain_grads), ALL)
    norm = jnp.sqrt(square + jnp.sum(gain_grads * gain_grads))
    factor = jnp.minimum(1.0, CLIP_NORM / norm)
    steps = step_count[0].astype(jnp.float32)
    tile_new, tile_first_new, tile_second_new = adam(
        tile_weight, tile_first, tile_second, own_grad, factor, RATE_TILE, DECAY, steps
    )
    tile_new = jnp.where(slot_valid, tile_new, 0.0)
    tile_first_new = jnp.where(slot_valid, tile_first_new, 0.0)
    tile_second_new = jnp.where(slot_valid, tile_second_new, 0.0)
    table_new, table_first_new, table_second_new = adam(
        table_weight, table_first, table_second, table_grad, factor, RATE_TABLE, DECAY, steps
    )
    head_new, head_first_new, head_second_new = adam(
        head_weight, head_first, head_second, head_grad, factor, RATE_HEAD, DECAY, steps
    )
    gain_new, gain_first_new, gain_second_new = adam(
        gain_weight, gain_first, gain_second, gain_grads, factor, RATE_GAIN, 0.0, steps
    )
    return (
        loss,
        norm,
        tile_new,
        tile_new.astype(jnp.bfloat16),
        tile_first_new,
        tile_second_new,
        table_new,
        table_new.astype(jnp.bfloat16),
        table_first_new,
        table_second_new,
        head_new,
        head_new.astype(jnp.bfloat16),
        head_first_new,
        head_second_new,
        gain_new,
        gain_first_new,
        gain_second_new,
    )


def solution(mesh):
    dp_size, rep_size = mesh.shape["dp"], mesh.shape["rep"]
    split = Mesh(mesh.devices.reshape(dp_size // rep_size, rep_size, rep_size), ALL)
    return jax.shard_map(
        shards,
        mesh=split,
        in_specs=(
            P(("a", "b"), "rep"),
            P(("a", "b"), None),
            P(("a", "b"), None),
            P(("a", "b"), None),
            P(),
            P(),
            P(("a", "b", "rep"), None, None),
            P(("a", "b", "rep"), None, None),
            P(("a", "b", "rep"), None, None),
            P(("a", "b", "rep"), None),
            P(("a", "b", "rep"), None),
            P(("a", "b", "rep"), None),
            P(("a", "b", "rep"), None),
            P(("a", "b", "rep"), None),
            P(("a", "b", "rep"), None),
            P(),
            P(),
            P(),
        ),
        out_specs=(
            P(),
            P(),
            P(("a", "b", "rep"), None, None),
            P(("a", "b", "rep"), None, None),
            P(("a", "b", "rep"), None, None),
            P(("a", "b", "rep"), None, None),
            P(("a", "b", "rep"), None),
            P(("a", "b", "rep"), None),
            P(("a", "b", "rep"), None),
            P(("a", "b", "rep"), None),
            P(("a", "b", "rep"), None),
            P(("a", "b", "rep"), None),
            P(("a", "b", "rep"), None),
            P(("a", "b", "rep"), None),
            P(),
            P(),
            P(),
        ),
        check_vma=False,
    )
```

```python
import functools

import jax
import jax.numpy as jnp
from jax import lax
from jax.experimental import pallas as pl
from jax.experimental.pallas import tpu as pltpu
from jax.sharding import Mesh, PartitionSpec as P

D = 768
HEADS = 12
HD = 64
FF = 3072
LAYERS = 2


EPS_NORM = 1e-05
EPS_ADAM = 1e-08
CLIP_NORM = 0.005
BETA_FIRST = 0.5
BETA_SECOND = 0.5
DECAY = 0.1
RATE_TILE = 0.02
RATE_HEAD = 0.05
RATE_TABLE = 0.5
RATE_GAIN = 0.3
MASKED = -1e30


def root_norm(training_state, gain):
    return (
        training_state
        * lax.rsqrt(jnp.mean(training_state * training_state, axis=-1, keepdims=True) + EPS_NORM)
        * gain
    )


def norm_back(training_state, gain, grad):
    scale = lax.rsqrt(jnp.mean(training_state * training_state, axis=-1, keepdims=True) + EPS_NORM)
    scaled = grad * gain
    state_grad = scale * scaled - training_state * scale**3 * jnp.mean(
        scaled * training_state, axis=-1, keepdims=True
    )
    gain_grad = jnp.sum(
        (grad * training_state * scale).reshape(-1, training_state.shape[-1]), axis=0
    )
    return (state_grad, gain_grad)


def rope_tables(places, width):
    half = width // 2
    freqs = jnp.power(10000.0, -2.0 * jnp.arange(half).astype(jnp.float32) / width)
    angle = places[:, None] * freqs[None, :]
    return (jnp.cos(angle), jnp.sin(angle))


def rotate(field, cosine, sine):
    half = field.shape[-1] // 2
    first, second = (field[..., :half], field[..., half:])
    cosine, sine = (cosine[:, None, :], sine[:, None, :])
    return jnp.concatenate(
        [first * cosine - second * sine, second * cosine + first * sine], axis=-1
    )


def rotate_back(field, cosine, sine):
    half = field.shape[-1] // 2
    first, second = (field[..., :half], field[..., half:])
    cosine, sine = (cosine[:, None, :], sine[:, None, :])
    return jnp.concatenate(
        [first * cosine + second * sine, second * cosine - first * sine], axis=-1
    )


def tile_slots(owners):
    order = jnp.arange(owners.shape[0], dtype=jnp.int32)
    same = (owners[:, None] == owners[None, :]) & (order[None, :] < order[:, None])
    return jnp.sum(same.astype(jnp.int32), axis=1)


def adam(weight, first, second, grad, factor, rate, decay, steps):
    grad = grad * factor
    first = BETA_FIRST * first + (1.0 - BETA_FIRST) * grad
    second = BETA_SECOND * second + (1.0 - BETA_SECOND) * grad * grad
    first_hat = first / (1.0 - jnp.power(BETA_FIRST, steps))
    second_hat = second / (1.0 - jnp.power(BETA_SECOND, steps))
    weight = weight - rate * (first_hat / (jnp.sqrt(second_hat) + EPS_ADAM) + decay * weight)
    return (weight, first, second)


ALL = ("y", "x", "c", "z")
DP = ("y", "x", "c")
PART = ("x", "c")
UNITS = FF // D
TILES_PER = 4 + 3 * UNITS


MESH = pl.DeviceIdType.MESH


def half_rows(rows):
    return (rows // 2 + 15) // 16 * 16


def remote(src, dst, ssem, rsem, **to):
    return pltpu.make_async_remote_copy(
        src_ref=src, dst_ref=dst, send_sem=ssem, recv_sem=rsem, device_id=to, device_id_type=MESH
    )


def greet(zn, y, x, c, z):
    barrier = pltpu.get_barrier_semaphore()
    for to in ({"x": 1 - x}, {"y": 1 - y}, {"c": 1 - c}):
        pl.semaphore_signal(barrier, inc=1, device_id=to, device_id_type=MESH)
    if zn > 1:

        @pl.when(z < zn - 1)
        def _():
            pl.semaphore_signal(barrier, inc=1, device_id={"z": z + 1}, device_id_type=MESH)

        @pl.when(z > 0)
        def _():
            pl.semaphore_signal(barrier, inc=1, device_id={"z": z - 1}, device_id_type=MESH)

        @pl.when((z > 0) & (z < zn - 1))
        def _():
            pl.semaphore_wait(barrier, 5)

        @pl.when((z == 0) | (z == zn - 1))
        def _():
            pl.semaphore_wait(barrier, 4)
    else:
        pl.semaphore_wait(barrier, 3)


def gather_kernel(zn, x_ref, o_ref, hold, ssem, rsem, lsem):
    y, x, c, z = [lax.axis_index(n) for n in ALL]
    me = z if zn > 1 else 0
    rows = x_ref.shape[0]
    h0 = half_rows(rows)
    lo, hi = pl.ds(0, h0), pl.ds(h0, rows - h0)
    X, Y, DX, DY, CO, CX, CY, C0, C1, ZU, ZD = range(11)
    nx, ny, nc = {"x": 1 - x}, {"y": 1 - y}, {"c": 1 - c}

    def slot(yy, xx, zz):
        return ((yy * 2 + xx) * 2 + c) * zn + zz

    def copy(kind, k, src, dst, to):
        return remote(src, dst, ssem.at[kind, k], rsem.at[kind, k], **to)

    def block(s):
        return o_ref.at[s]

    greet(zn, y, x, c, z)
    local = pltpu.make_async_copy(x_ref, hold, lsem)
    local.start()
    local.wait()
    local = pltpu.make_async_copy(hold, o_ref.at[slot(y, x, me)], lsem)
    local.start()

    def spread(zb, src):
        dst = block(slot(y, x, zb))
        copy(X, zb, src, dst, nx).start()
        copy(Y, zb, src, dst, ny).start()
        copy(CO, zb, src, dst, nc).start()

    def up(s):
        zb = z - (s - 1)
        b = block(slot(y, x, zb))
        return copy(ZU, s, x_ref if s == 1 else b, b, {"z": z + 1})

    def down(s):
        zb = z + (s - 1)
        b = block(slot(y, x, zb))
        return copy(ZD, s, x_ref if s == 1 else b, b, {"z": z - 1})

    for s in range(1, zn):

        @pl.when((z < zn - 1) & (z - (s - 1) >= 0))
        def _():
            up(s).start()

        @pl.when((z > 0) & (z + (s - 1) < zn))
        def _():
            down(s).start()

        if s == 1:
            spread(me, x_ref)

        @pl.when(z - s >= 0)
        def _():
            copy(ZU, s, x_ref, x_ref, nx).wait_recv()
            spread(z - s, block(slot(y, x, z - s)))

        @pl.when(z + s < zn)
        def _():
            copy(ZD, s, x_ref, x_ref, nx).wait_recv()
            spread(z + s, block(slot(y, x, z + s)))

    if zn == 1:
        spread(0, x_ref)
    order = [lax.rem(z + j, zn) if zn > 1 else 0 for j in range(zn)]
    for zb in order:
        sx, sy = slot(y, 1 - x, zb), slot(1 - y, x, zb)
        copy(X, zb, x_ref, x_ref, nx).wait_recv()
        copy(DX, zb, o_ref.at[sx, lo], o_ref.at[sx, lo], ny).start()
        copy(CX, zb, block(sx), block(sx), nc).start()
        copy(Y, zb, x_ref, x_ref, nx).wait_recv()
        copy(DY, zb, o_ref.at[sy, hi], o_ref.at[sy, hi], nx).start()
        copy(CY, zb, block(sy), block(sy), nc).start()
    for zb in order:
        sd = slot(1 - y, 1 - x, zb)
        copy(DX, zb, x_ref.at[lo], x_ref.at[lo], nx).wait_recv()
        copy(C0, zb, o_ref.at[sd, lo], o_ref.at[sd, lo], nc).start()
        copy(DY, zb, x_ref.at[hi], x_ref.at[hi], nx).wait_recv()
        copy(C1, zb, o_ref.at[sd, hi], o_ref.at[sd, hi], nc).start()
    for zb in range(zn):
        for kind, part in ((CO, x_ref), (CX, x_ref), (CY, x_ref), (C0, x_ref.at[lo]), (C1, x_ref.at[hi])):
            copy(kind, zb, part, part, nx).wait_recv()
        for kind, part in (
            (X, x_ref), (Y, x_ref), (CO, x_ref), (CX, x_ref), (CY, x_ref),
            (DX, x_ref.at[lo]), (DY, x_ref.at[hi]), (C0, x_ref.at[lo]), (C1, x_ref.at[hi]),
        ):
            copy(kind, zb, part, part, nx).wait_send()
    for s in range(1, zn):

        @pl.when((z < zn - 1) & (z - (s - 1) >= 0))
        def _():
            up(s).wait_send()

        @pl.when((z > 0) & (z + (s - 1) < zn))
        def _():
            down(s).wait_send()

    local.wait()


def all_gather(x, zn, ident, name):
    sems = pltpu.SemaphoreType.DMA((11, zn))
    return pl.pallas_call(
        functools.partial(gather_kernel, zn),
        out_shape=jax.ShapeDtypeStruct((8 * zn,) + x.shape, x.dtype),
        in_specs=[pl.BlockSpec(memory_space=pl.ANY)],
        out_specs=pl.BlockSpec(memory_space=pl.ANY),
        scratch_shapes=[pltpu.VMEM(x.shape, x.dtype), sems, sems, pltpu.SemaphoreType.DMA],
        compiler_params=pltpu.CompilerParams(collective_id=ident, has_side_effects=True),
        name=name,
    )(x)


def reduce_kernel(zn, p_ref, o_ref, acc, crecv, dxr, dyr, xr, yr, zur, zdr, ssem, rsem, lsem):
    y, x, c, z = [lax.axis_index(n) for n in ALL]
    me = z if zn > 1 else 0
    rows, cols = p_ref.shape[1:]
    h0 = half_rows(rows)
    h1 = rows - h0
    X, Y, DX, DY, C0, ZU, ZD = 0, 1, 2, 3, 4, 8, 9
    nx, ny, nc = {"x": 1 - x}, {"y": 1 - y}, {"c": 1 - c}
    kinds = [(y, x), (y, 1 - x), (1 - y, x), (1 - y, 1 - x)]
    step = 32 if rows % 32 == 0 else 16

    def slot(k, cc, zz):
        yy, xx = kinds[k]
        return ((yy * 2 + xx) * 2 + cc) * zn + zz

    def copy(kind, k, src, dst, to):
        return remote(src, dst, ssem.at[kind, k], rsem.at[kind, k], **to)

    def load(k, zb):
        return pltpu.make_async_copy(p_ref.at[slot(k, c, zb)], acc.at[k * zn + zb], lsem.at[k * zn + zb])

    def across(k, zb):
        return copy(C0 + k, zb, p_ref.at[slot(k, 1 - c, zb)], crecv.at[k * zn + zb], nc)

    def add(dst, start, count, terms):
        size = step if count % step == 0 else 16

        @pl.loop(0, count // size)
        def _(i):
            at = pl.ds(pl.multiple_of(start + i * size, 16), size)
            total = None
            for ref, base in terms:
                part = ref[pl.ds(pl.multiple_of(start - base + i * size, 16), size), :].astype(jnp.float32)
                total = part if total is None else total + part
            dst[at, :] = total.astype(dst.dtype)

    greet(zn, y, x, c, z)
    zorder = [lax.rem(z + j, zn) if zn > 1 else 0 for j in range(zn)]
    for k in (3, 1, 2, 0):
        for zb in range(zn):
            across(k, zb).start()
            load(k, zb).start()

    def ready(k, zb):
        load(k, zb).wait()
        across(k, zb).wait_recv()

    for zb in range(zn):
        ready(3, zb)
        b = 3 * zn + zb
        add(acc.at[b], 0, rows, [(acc.at[b], 0), (crecv.at[b], 0)])
        copy(DX, zb, acc.at[b, pl.ds(0, h0)], dxr.at[zb], nx).start()
        copy(DY, zb, acc.at[b, pl.ds(h0, h1)], dyr.at[zb], ny).start()
    for zb in range(zn):
        ready(1, zb)
        b = zn + zb
        add(acc.at[b], 0, h0, [(acc.at[b], 0), (crecv.at[b], 0)])
        copy(DY, zb, dyr.at[zb], dyr.at[zb], ny).wait_recv()
        add(acc.at[b], h0, h1, [(acc.at[b], 0), (crecv.at[b], 0), (dyr.at[zb], h0)])
        copy(X, zb, acc.at[b], xr.at[zb], nx).start()
        ready(2, zb)
        b = 2 * zn + zb
        add(acc.at[b], h0, h1, [(acc.at[b], 0), (crecv.at[b], 0)])
        copy(DX, zb, dxr.at[zb], dxr.at[zb], nx).wait_recv()
        add(acc.at[b], 0, h0, [(acc.at[b], 0), (crecv.at[b], 0), (dxr.at[zb], 0)])
        copy(Y, zb, acc.at[b], yr.at[zb], ny).start()

    def column(zb):
        return [(acc.at[zb], 0), (crecv.at[zb], 0), (xr.at[zb], 0), (yr.at[zb], 0)]

    for zb in range(zn):
        ready(0, zb)
        copy(X, zb, acc.at[zb], xr.at[zb], nx).wait_recv()
        copy(Y, zb, acc.at[zb], yr.at[zb], ny).wait_recv()
        if zn == 1:
            add(o_ref, 0, rows, column(0))
            continue

        def upward(zb=zb):
            return copy(ZU, zb, acc.at[zb], zur.at[zb], {"z": z + 1})

        def downward(zb=zb):
            return copy(ZD, zb, acc.at[zb], zdr.at[zb], {"z": z - 1})

        @pl.when(z == zb)
        def _():
            add(acc.at[zb], 0, rows, column(zb))

        @pl.when((z < zb) & (z == 0))
        def _():
            add(acc.at[zb], 0, rows, column(zb))
            upward().start()

        @pl.when((z < zb) & (z > 0))
        def _():
            upward().wait_recv()
            add(acc.at[zb], 0, rows, column(zb) + [(zur.at[zb], 0)])
            upward().start()

        @pl.when((z > zb) & (z == zn - 1))
        def _():
            add(acc.at[zb], 0, rows, column(zb))
            downward().start()

        @pl.when((z > zb) & (z < zn - 1))
        def _():
            downward().wait_recv()
            add(acc.at[zb], 0, rows, column(zb) + [(zdr.at[zb], 0)])
            downward().start()

    if zn > 1:

        @pl.when(z == 0)
        def _():
            copy(ZD, me, acc.at[me], zdr.at[me], {"z": z + 1}).wait_recv()
            add(o_ref, 0, rows, [(acc.at[me], 0), (zdr.at[me], 0)])

        @pl.when(z == zn - 1)
        def _():
            copy(ZU, me, acc.at[me], zur.at[me], {"z": z - 1}).wait_recv()
            add(o_ref, 0, rows, [(acc.at[me], 0), (zur.at[me], 0)])

        @pl.when((z > 0) & (z < zn - 1))
        def _():
            copy(ZD, me, acc.at[me], zdr.at[me], {"z": z + 1}).wait_recv()
            copy(ZU, me, acc.at[me], zur.at[me], {"z": z + 1}).wait_recv()
            add(o_ref, 0, rows, [(acc.at[me], 0), (zdr.at[me], 0), (zur.at[me], 0)])

    for zb in range(zn):
        for k in range(4):
            across(k, zb).wait_send()
        copy(DX, zb, dxr.at[zb], dxr.at[zb], nx).wait_send()
        copy(DY, zb, dyr.at[zb], dyr.at[zb], ny).wait_send()
        copy(X, zb, xr.at[zb], xr.at[zb], nx).wait_send()
        copy(Y, zb, yr.at[zb], yr.at[zb], ny).wait_send()
        if zn > 1:

            @pl.when(z < zb)
            def _():
                copy(ZU, zb, zur.at[zb], zur.at[zb], {"z": z + 1}).wait_send()

            @pl.when(z > zb)
            def _():
                copy(ZD, zb, zdr.at[zb], zdr.at[zb], {"z": z - 1}).wait_send()


def reduce_scatter(p, zn, ident, name, out_dtype=None):
    count, rows, cols = p.shape
    h0 = half_rows(rows)
    sems = pltpu.SemaphoreType.DMA((10, zn))
    vm = lambda n, r: pltpu.VMEM((n, r, cols), p.dtype)
    return pl.pallas_call(
        functools.partial(reduce_kernel, zn),
        out_shape=jax.ShapeDtypeStruct((rows, cols), out_dtype or p.dtype),
        in_specs=[pl.BlockSpec(memory_space=pl.ANY)],
        out_specs=pl.BlockSpec(memory_space=pltpu.VMEM),
        scratch_shapes=[
            vm(4 * zn, rows), vm(4 * zn, rows), vm(zn, h0), vm(zn, rows - h0),
            vm(zn, rows), vm(zn, rows), vm(zn, rows), vm(zn, rows),
            sems, sems, pltpu.SemaphoreType.DMA((4 * zn,)),
        ],
        compiler_params=pltpu.CompilerParams(
            collective_id=ident, has_side_effects=True, vmem_limit_bytes=56 << 20
        ),
        name=name,
    )(p)


def greet_pair(x, c):
    barrier = pltpu.get_barrier_semaphore()
    for to in ({"x": 1 - x}, {"c": 1 - c}):
        pl.semaphore_signal(barrier, inc=1, device_id=to, device_id_type=MESH)
    pl.semaphore_wait(barrier, 2)


def keys_gather_kernel(x_ref, o_ref, hold, ssem, rsem, lsem):
    x, c = lax.axis_index("x"), lax.axis_index("c")
    me, far = x * 2 + c, (1 - x) * 2 + c
    nx, nc = {"x": 1 - x}, {"c": 1 - c}
    load = pltpu.make_async_copy(x_ref, hold, lsem.at[0])
    load.start()
    greet_pair(x, c)
    out = remote(x_ref, o_ref.at[me], ssem.at[0], rsem.at[0], **nx)
    out.start()
    near = remote(x_ref, o_ref.at[me], ssem.at[1], rsem.at[1], **nc)
    near.start()
    load.wait()
    keep = pltpu.make_async_copy(hold, o_ref.at[me], lsem.at[1])
    keep.start()
    out.wait_recv()
    on = remote(o_ref.at[far], o_ref.at[far], ssem.at[2], rsem.at[2], **nc)
    on.start()
    near.wait_recv()
    on.wait_recv()
    keep.wait()
    out.wait_send()
    near.wait_send()
    on.wait_send()


def keys_gather(v, ident):
    sems = pltpu.SemaphoreType.DMA((3,))
    return pl.pallas_call(
        keys_gather_kernel,
        out_shape=jax.ShapeDtypeStruct((4,) + v.shape, v.dtype),
        in_specs=[pl.BlockSpec(memory_space=pl.ANY)],
        out_specs=pl.BlockSpec(memory_space=pl.ANY),
        scratch_shapes=[pltpu.VMEM(v.shape, v.dtype), sems, sems, pltpu.SemaphoreType.DMA((2,))],
        compiler_params=pltpu.CompilerParams(collective_id=ident, has_side_effects=True),
        name="keys_gather",
    )(v)


def keys_reduce_kernel(p_ref, o_ref, acc, crecv, xr, ssem, rsem, lsem):
    x, c = lax.axis_index("x"), lax.axis_index("c")
    nx, nc = {"x": 1 - x}, {"c": 1 - c}
    rows = p_ref.shape[1]
    places = [(1 - x) * 2, x * 2]
    loads = [pltpu.make_async_copy(p_ref.at[places[i] + c], acc.at[i], lsem.at[i]) for i in range(2)]
    for load in loads:
        load.start()
    greet_pair(x, c)
    across = [
        remote(p_ref.at[places[i] + 1 - c], crecv.at[i], ssem.at[i], rsem.at[i], **nc) for i in range(2)
    ]
    for copy in across:
        copy.start()

    def add(dst, terms):
        @pl.loop(0, rows // 16)
        def _(i):
            at = pl.ds(pl.multiple_of(i * 16, 16), 16)
            total = terms[0][at, :].astype(jnp.float32)
            for term in terms[1:]:
                total = total + term[at, :].astype(jnp.float32)
            dst[at, :] = total.astype(dst.dtype)

    loads[0].wait()
    across[0].wait_recv()
    add(acc.at[0], [acc.at[0], crecv.at[0]])
    out = remote(acc.at[0], xr, ssem.at[2], rsem.at[2], **nx)
    out.start()
    loads[1].wait()
    across[1].wait_recv()
    out.wait_recv()
    add(o_ref, [acc.at[1], crecv.at[1], xr])
    for copy in across + [out]:
        copy.wait_send()


def keys_reduce(p, ident):
    block = p.shape[1:]
    sems = pltpu.SemaphoreType.DMA((3,))
    return pl.pallas_call(
        keys_reduce_kernel,
        out_shape=jax.ShapeDtypeStruct(block, p.dtype),
        in_specs=[pl.BlockSpec(memory_space=pl.ANY)],
        out_specs=pl.BlockSpec(memory_space=pltpu.VMEM),
        scratch_shapes=[
            pltpu.VMEM((2,) + block, p.dtype), pltpu.VMEM((2,) + block, p.dtype),
            pltpu.VMEM(block, p.dtype), sems, sems, pltpu.SemaphoreType.DMA((2,)),
        ],
        compiler_params=pltpu.CompilerParams(
            collective_id=ident, has_side_effects=True, vmem_limit_bytes=32 << 20
        ),
        name="keys_reduce",
    )(p)


def fits(axes):
    return [lax.axis_size(n) for n in ALL] == [2, 2, 2, 4]


def gather_all(v, ident, name):
    if fits(ALL):
        return all_gather(v, 4, ident, name)
    return lax.all_gather(v, ALL, axis=0)


def gather_plane(v, ident, name):
    if fits(ALL):
        return all_gather(v, 1, ident, name)
    return lax.all_gather(v, DP, axis=0)


def scatter_all(p, ident, name):
    if fits(ALL):
        return reduce_scatter(p, 4, ident, name)
    return lax.psum_scatter(p, ALL, scatter_dimension=0)


def scatter_plane(p, ident, name):
    if fits(ALL):
        return reduce_scatter(p, 1, ident, name)
    return lax.psum_scatter(p, DP, scatter_dimension=0)


def keys_all_gather(v):
    if fits(ALL):
        return keys_gather(v, 11).reshape(-1, v.shape[1])
    return lax.all_gather(v, PART, axis=0, tiled=True)


def keys_sum_scatter(p):
    if fits(ALL):
        return keys_reduce(p.reshape(4, -1, p.shape[1]), 12)
    return lax.psum_scatter(p, PART, scatter_dimension=0, tiled=True)


def mm(x, w):
    return jnp.einsum("ld,de->le", x, w, preferred_element_type=jnp.float32)


def mm_t(x, w):
    return jnp.einsum("le,de->ld", x, w, preferred_element_type=jnp.float32)


def mm_g(x, y):
    return jnp.einsum("ld,le->de", x, y, preferred_element_type=jnp.float32)


def heads(x):
    return x.reshape(x.shape[0], HEADS, HD)


def layer_forward(state, tiles, gain_pair, cosine, sine, allowed):
    rows = state.shape[0]
    normed = root_norm(state, gain_pair[0]).astype(jnp.bfloat16)
    query, keys, value = [mm(normed, tiles[i]) for i in range(3)]
    query = rotate(heads(query), cosine, sine).astype(jnp.bfloat16)
    keys = rotate(heads(keys), cosine, sine).astype(jnp.bfloat16).reshape(rows, D)
    both = jnp.concatenate([keys, value.astype(jnp.bfloat16)], axis=1)
    both = keys_all_gather(both)
    keys_all, value_all = heads(both[:, :D]), heads(both[:, D:])
    scores = jnp.einsum("qhd,khd->hqk", query, keys_all, preferred_element_type=jnp.float32) * HD ** (
        -0.5
    )
    scores = jnp.where(allowed, scores, MASKED)
    top = jnp.max(scores, axis=-1, keepdims=True)
    exponent = jnp.exp(scores - top)
    total = jnp.sum(exponent, axis=-1, keepdims=True)
    prob = (exponent / total).astype(jnp.bfloat16)
    log_total = top + jnp.log(total)
    attended = jnp.einsum("hqk,khd->qhd", prob, value_all, preferred_element_type=jnp.float32)
    attended = attended.reshape(rows, D).astype(jnp.bfloat16)
    middle = state + mm(attended, tiles[3])
    normed_feed = root_norm(middle, gain_pair[1]).astype(jnp.bfloat16)
    gates = [mm(normed_feed, tiles[4 + i]) for i in range(UNITS)]
    ups = [mm(normed_feed, tiles[4 + UNITS + i]) for i in range(UNITS)]
    hidden = [(jax.nn.silu(g) * u).astype(jnp.bfloat16) for g, u in zip(gates, ups)]
    output = middle + sum(mm(h, tiles[4 + 2 * UNITS + i]) for i, h in enumerate(hidden))
    return output, (
        state,
        middle,
        normed,
        normed_feed,
        query,
        keys_all,
        value_all,
        log_total,
        attended,
        gates,
        ups,
        hidden,
    )


def layer_backward(grad, kept, tiles, gain_pair, cosine, sine, allowed):
    (
        state,
        middle,
        normed,
        normed_feed,
        query,
        keys_all,
        value_all,
        log_total,
        attended,
        gates,
        ups,
        hidden,
    ) = kept
    rows = state.shape[0]
    branch = grad.astype(jnp.bfloat16)
    down_grads, gate_grads, up_grads = [], [], []
    feed_back = 0.0
    for i in range(UNITS):
        down_grads.append(mm_g(hidden[i], branch))
        hidden_grad = mm_t(branch, tiles[4 + 2 * UNITS + i])
        sigma = jax.nn.sigmoid(gates[i])
        gate_back = (hidden_grad * ups[i] * sigma * (1.0 + gates[i] * (1.0 - sigma))).astype(
            jnp.bfloat16
        )
        up_back = (hidden_grad * gates[i] * sigma).astype(jnp.bfloat16)
        gate_grads.append(mm_g(normed_feed, gate_back))
        up_grads.append(mm_g(normed_feed, up_back))
        feed_back = (
            feed_back + mm_t(gate_back, tiles[4 + i]) + mm_t(up_back, tiles[4 + UNITS + i])
        )
    back, feed_gain = norm_back(middle, gain_pair[1], feed_back)
    middle_grad = grad + back
    branch = middle_grad.astype(jnp.bfloat16)
    out_grad = mm_g(attended, branch)
    heads_grad = heads(mm_t(branch, tiles[3]).astype(jnp.bfloat16))
    scores = jnp.einsum("qhd,khd->hqk", query, keys_all, preferred_element_type=jnp.float32) * HD ** (
        -0.5
    )
    prob = jnp.exp(jnp.where(allowed, scores, MASKED) - log_total)
    value_part = jnp.einsum(
        "hqk,qhd->khd", prob.astype(jnp.bfloat16), heads_grad, preferred_element_type=jnp.float32
    )
    prob_grad = jnp.einsum("qhd,khd->hqk", heads_grad, value_all, preferred_element_type=jnp.float32)
    score_grad = (
        prob * (prob_grad - jnp.sum(prob * prob_grad, axis=-1, keepdims=True)) * HD ** (-0.5)
    ).astype(jnp.bfloat16)
    query_grad = jnp.einsum("hqk,khd->qhd", score_grad, keys_all, preferred_element_type=jnp.float32)
    keys_part = jnp.einsum("hqk,qhd->khd", score_grad, query, preferred_element_type=jnp.float32)
    length = keys_part.shape[0]
    both = jnp.concatenate([keys_part.reshape(length, D), value_part.reshape(length, D)], axis=1)
    both = keys_sum_scatter(both.astype(jnp.bfloat16))
    keys_grad, value_grad = both[:, :D].astype(jnp.float32), both[:, D:]
    parts = [
        rotate_back(query_grad, cosine, sine).reshape(rows, D).astype(jnp.bfloat16),
        rotate_back(heads(keys_grad), cosine, sine).reshape(rows, D).astype(jnp.bfloat16),
        value_grad,
    ]
    input_grads = [mm_g(normed, p) for p in parts]
    back, attend_gain = norm_back(
        state, gain_pair[0], sum(mm_t(p, tiles[i]) for i, p in enumerate(parts))
    )
    tiles_grad = jnp.stack(
        [
            t.astype(jnp.bfloat16)
            for t in input_grads + [out_grad] + gate_grads + up_grads + down_grads
        ]
    )
    return middle_grad + back, tiles_grad, [attend_gain, feed_gain]


def padded(v):
    count = -(-v.shape[0] // 4096) * 4096
    return jnp.pad(v, (0, count - v.shape[0])).reshape(-1, 128)


def shards(
    tokens,
    segments,
    completion,
    targets,
    owners,
    step_count,
    tile_weight,
    tile_first,
    tile_second,
    table_weight,
    table_first,
    table_second,
    head_weight,
    head_first,
    head_second,
    gain_weight,
    gain_first,
    gain_second,
):
    a_size, b_size, rep_size = lax.axis_size("y"), lax.axis_size(PART), lax.axis_size("z")
    a_index, b_index, rep_index = lax.axis_index("y"), lax.axis_index(PART), lax.axis_index("z")
    dp_size = a_size * b_size
    devices = dp_size * rep_size
    dp_index = a_index * b_size + b_index
    device = dp_index * rep_size + rep_index
    rows = tokens.shape[1]
    length = segments.shape[1]
    comp = completion.shape[1]
    slots_cap, tile_rows = tile_weight.shape[:2]
    tile_count = owners.shape[0]
    home_tiles = tile_count // dp_size
    vocab_rows = table_weight.shape[0]
    vocab_start = device * vocab_rows
    sequence = a_index * rep_size + rep_index

    own_part = jnp.concatenate(
        [
            tokens[0],
            lax.dynamic_slice_in_dim(segments[0], rep_index * rows, rows),
            lax.dynamic_slice_in_dim(completion[0], rep_index * (comp // rep_size), comp // rep_size),
            lax.dynamic_slice_in_dim(targets[0], rep_index * (comp // rep_size), comp // rep_size),
        ]
    )
    packed = gather_all(padded(own_part), 0, "ids_gather").reshape(devices, -1)
    packed = packed[:, : own_part.shape[0]].reshape(dp_size, rep_size, -1)
    tokens_all = packed[:, :, :rows].reshape(dp_size, length)
    segments_all = packed[:, :, rows : 2 * rows].reshape(dp_size, length)
    edge = 2 * rows + comp // rep_size
    completion_all = packed[:, :, 2 * rows : edge].reshape(dp_size, comp)
    targets_all = packed[:, :, edge:].reshape(dp_size, comp)

    slots = tile_slots(owners)
    mine = owners == dp_index
    tile_low = tile_weight.astype(jnp.bfloat16)
    per = TILES_PER // dp_size
    home_ids = (
        jnp.arange(LAYERS)[None, :, None] * TILES_PER
        + jnp.arange(dp_size)[:, None, None] * per
        + jnp.arange(per)[None, None, :]
    ).reshape(-1)
    home_mine = jnp.take(mine, home_ids)
    home_slots = jnp.where(home_mine, jnp.take(slots, home_ids), 0)
    placed = jnp.where(home_mine[:, None, None], jnp.take(tile_low, home_slots, axis=0), 0)
    home = scatter_plane(placed.reshape(dp_size, -1, D), 7, "home_scatter")
    spread = gather_all(home, 1, "weights_gather")
    spread = spread.reshape(dp_size, rep_size, LAYERS, per, tile_rows, D)
    tiles = spread.transpose(2, 0, 3, 1, 4, 5).reshape(tile_count, D, D)

    order = tokens_all.reshape(a_size, rep_size, b_size, rows).transpose(0, 2, 1, 3).reshape(-1)
    place = order - vocab_start
    vocab_iota = jnp.arange(vocab_rows)
    token_hot = (place[:, None] == vocab_iota[None, :]).astype(jnp.bfloat16)
    picked = jnp.dot(
        token_hot, table_weight.astype(jnp.bfloat16), preferred_element_type=jnp.float32
    ).astype(jnp.bfloat16)
    state = scatter_all(picked.reshape(devices, rows, D), 8, "rows_scatter").astype(jnp.float32)

    first_place = b_index * rows
    places = first_place + jnp.arange(rows)
    cosine, sine = rope_tables(places.astype(jnp.float32), HD)
    own_segments = lax.dynamic_index_in_dim(segments_all, sequence, 0, False)
    query_segments = lax.dynamic_slice_in_dim(own_segments, first_place, rows)
    allowed = (jnp.arange(length)[None, :] <= places[:, None]) & (
        query_segments[:, None] == own_segments[None, :]
    )
    allowed = allowed[None]
    kept_list = []
    for index in range(LAYERS):
        state, kept = layer_forward(
            state,
            tiles[index * TILES_PER : (index + 1) * TILES_PER],
            gain_weight[2 * index : 2 * index + 2],
            cosine,
            sine,
            allowed,
        )
        kept_list.append(kept)
    final_gain = gain_weight[2 * LAYERS]
    final = root_norm(state, final_gain).astype(jnp.bfloat16)

    capacity = 3 * comp // (2 * rep_size)
    block = completion_all // rows
    inside = block[:, None, :] == jnp.arange(b_size)[None, :, None]
    rank = jnp.cumsum(inside.astype(jnp.int32), axis=2) - 1
    slot_pick = inside[..., None] & (rank[..., None] == jnp.arange(capacity))
    filled = jnp.any(slot_pick, axis=2)
    wanted = jnp.where(
        filled, jnp.sum(jnp.where(slot_pick, targets_all[:, None, :, None], 0), axis=2), -1
    )
    spots = jnp.where(
        filled, jnp.sum(jnp.where(slot_pick, (completion_all % rows)[:, None, :, None], 0), axis=2), -1
    )
    all_wanted = (
        wanted.reshape(a_size, rep_size, b_size, capacity).transpose(0, 2, 1, 3).reshape(-1)
    )
    own_spots = lax.dynamic_index_in_dim(
        lax.dynamic_index_in_dim(spots, sequence, 0, False), b_index, 0, False
    )
    select = (own_spots[:, None] == jnp.arange(rows)[None, :]).astype(jnp.bfloat16)
    chosen = jnp.dot(select, final, preferred_element_type=jnp.float32).astype(jnp.bfloat16)
    all_rows = gather_all(chosen, 3, "chosen_gather").reshape(-1, D)
    head_low = head_weight.astype(jnp.bfloat16)
    logits = jnp.einsum("rd,vd->rv", all_rows, head_low, preferred_element_type=jnp.float32)
    hot = vocab_iota[None, :] == (all_wanted - vocab_start)[:, None]
    local_top = jnp.max(logits, axis=-1)
    local_total = jnp.sum(jnp.exp(logits - local_top[:, None]), axis=-1)
    local_hit = jnp.sum(jnp.where(hot, logits, 0.0), axis=-1)
    own_stats = jnp.concatenate([local_top, local_total, local_hit])
    stats = gather_all(padded(own_stats), 4, "stats_gather").reshape(devices, -1)
    stats = stats[:, : own_stats.shape[0]].reshape(devices, 3, -1)
    top = jnp.max(stats[:, 0], axis=0)
    total = jnp.sum(stats[:, 1] * jnp.exp(stats[:, 0] - top[None]), axis=0)
    log_total = top + jnp.log(total)
    valid = all_wanted >= 0
    scored = dp_size * comp
    loss = jnp.sum(jnp.where(valid, log_total - jnp.sum(stats[:, 2], axis=0), 0.0)) / scored
    logit_grad = jnp.where(
        valid[:, None],
        (jnp.exp(logits - log_total[:, None]) - jnp.where(hot, 1.0, 0.0)) / scored,
        0.0,
    ).astype(jnp.bfloat16)
    rows_grad = jnp.dot(logit_grad, head_low, preferred_element_type=jnp.float32)
    own_rows = scatter_all(
        rows_grad.astype(jnp.bfloat16).reshape(devices, -1, D), 9, "back_scatter"
    )
    head_grad = jnp.einsum("rv,rd->vd", logit_grad, all_rows, preferred_element_type=jnp.float32)
    final_grad = jnp.einsum("ct,cd->td", select, own_rows, preferred_element_type=jnp.float32)
    state_grad, final_gain_grad = norm_back(state, final_gain, final_grad)
    tile_parts = [None] * LAYERS
    gain_parts = [None] * LAYERS
    for index in reversed(range(LAYERS)):
        state_grad, tile_parts[index], gain_parts[index] = layer_backward(
            state_grad,
            kept_list[index],
            tiles[index * TILES_PER : (index + 1) * TILES_PER],
            gain_weight[2 * index : 2 * index + 2],
            cosine,
            sine,
            allowed,
        )
    piece_grads = gather_all(state_grad.astype(jnp.bfloat16), 2, "entry_gather").reshape(-1, D)
    table_grad = jnp.einsum(
        "tv,td->vd", token_hot, piece_grads, preferred_element_type=jnp.float32
    )
    home_grads = []
    for index in range(LAYERS):
        part = tile_parts[index].reshape(dp_size, per, rep_size, tile_rows, D)
        part = part.transpose(0, 2, 1, 3, 4).reshape(devices, -1, D)
        home_grads.append(scatter_all(part, 10, "grads_scatter"))
    plane_grad = gather_plane(jnp.concatenate(home_grads), 6, "owners_gather")
    plane_grad = plane_grad.reshape(dp_size, LAYERS, per, tile_rows, D)
    plane_grad = plane_grad.transpose(1, 0, 2, 3, 4).reshape(tile_count, tile_rows, D)
    own_count = jnp.sum(mine.astype(jnp.int32))
    slot_ids = jnp.arange(slots_cap)
    tile_of_slot = jnp.sum(
        jnp.where(
            mine[None, :] & (slots[None, :] == slot_ids[:, None]), jnp.arange(tile_count)[None, :], 0
        ),
        axis=1,
    )
    slot_valid = (slot_ids < own_count)[:, None, None]
    own_grad = jnp.where(
        slot_valid, jnp.take(plane_grad, tile_of_slot, axis=0).astype(jnp.float32), 0.0
    )
    gain_grads = jnp.stack([g for pair in gain_parts for g in pair] + [final_gain_grad])
    square = (
        jnp.sum(own_grad * own_grad)
        + jnp.sum(table_grad * table_grad)
        + jnp.sum(head_grad * head_grad)
    )
    sums = gather_all(
        padded(jnp.concatenate([square[None], gain_grads.reshape(-1)])), 5, "sums_gather"
    )
    sums = jnp.sum(sums.reshape(devices, -1), axis=0)
    square, gain_grads = sums[0], sums[1 : 1 + gain_grads.size].reshape(gain_grads.shape)
    norm = jnp.sqrt(square + jnp.sum(gain_grads * gain_grads))
    factor = jnp.minimum(1.0, CLIP_NORM / norm)
    steps = step_count[0].astype(jnp.float32)
    tile_new, tile_first_new, tile_second_new = adam(
        tile_weight, tile_first, tile_second, own_grad, factor, RATE_TILE, DECAY, steps
    )
    tile_new = jnp.where(slot_valid, tile_new, 0.0)
    tile_first_new = jnp.where(slot_valid, tile_first_new, 0.0)
    tile_second_new = jnp.where(slot_valid, tile_second_new, 0.0)
    table_new, table_first_new, table_second_new = adam(
        table_weight, table_first, table_second, table_grad, factor, RATE_TABLE, DECAY, steps
    )
    head_new, head_first_new, head_second_new = adam(
        head_weight, head_first, head_second, head_grad, factor, RATE_HEAD, DECAY, steps
    )
    gain_new, gain_first_new, gain_second_new = adam(
        gain_weight, gain_first, gain_second, gain_grads, factor, RATE_GAIN, 0.0, steps
    )
    return (
        loss,
        norm,
        tile_new,
        tile_new.astype(jnp.bfloat16),
        tile_first_new,
        tile_second_new,
        table_new,
        table_new.astype(jnp.bfloat16),
        table_first_new,
        table_second_new,
        head_new,
        head_new.astype(jnp.bfloat16),
        head_first_new,
        head_second_new,
        gain_new,
        gain_first_new,
        gain_second_new,
    )


def solution(mesh):
    dp_size, rep_size = mesh.shape["dp"], mesh.shape["rep"]
    split = Mesh(mesh.devices.reshape(dp_size // rep_size, rep_size // 2, 2, rep_size), ALL)
    return jax.shard_map(
        shards,
        mesh=split,
        in_specs=(
            P(DP, "z"),
            P(DP, None),
            P(DP, None),
            P(DP, None),
            P(),
            P(),
            P(ALL, None, None),
            P(ALL, None, None),
            P(ALL, None, None),
            P(ALL, None),
            P(ALL, None),
            P(ALL, None),
            P(ALL, None),
            P(ALL, None),
            P(ALL, None),
            P(),
            P(),
            P(),
        ),
        out_specs=(
            P(),
            P(),
            P(ALL, None, None),
            P(ALL, None, None),
            P(ALL, None, None),
            P(ALL, None, None),
            P(ALL, None),
            P(ALL, None),
            P(ALL, None),
            P(ALL, None),
            P(ALL, None),
            P(ALL, None),
            P(ALL, None),
            P(ALL, None),
            P(),
            P(),
            P(),
        ),
        check_vma=False,
    )
```

```python
import functools

import jax
import jax.numpy as jnp
from jax import lax
from jax.experimental import pallas as pl
from jax.experimental.pallas import tpu as pltpu
from jax.sharding import Mesh, PartitionSpec as P

D = 768
HEADS = 12
HD = 64
FF = 3072
LAYERS = 2


EPS_NORM = 1e-05
EPS_ADAM = 1e-08
CLIP_NORM = 0.005
BETA_FIRST = 0.5
BETA_SECOND = 0.5
DECAY = 0.1
RATE_TILE = 0.02
RATE_HEAD = 0.05
RATE_TABLE = 0.5
RATE_GAIN = 0.3
MASKED = -1e30


def root_norm(training_state, gain):
    return (
        training_state
        * lax.rsqrt(jnp.mean(training_state * training_state, axis=-1, keepdims=True) + EPS_NORM)
        * gain
    )


def norm_back(training_state, gain, grad):
    scale = lax.rsqrt(jnp.mean(training_state * training_state, axis=-1, keepdims=True) + EPS_NORM)
    scaled = grad * gain
    state_grad = scale * scaled - training_state * scale**3 * jnp.mean(
        scaled * training_state, axis=-1, keepdims=True
    )
    gain_grad = jnp.sum(
        (grad * training_state * scale).reshape(-1, training_state.shape[-1]), axis=0
    )
    return (state_grad, gain_grad)


def rope_tables(places):
    freqs = jnp.power(10000.0, -2.0 * jnp.arange(HD // 2).astype(jnp.float32) / HD)
    angle = places[:, None] * freqs[None, :]
    cosine, sine = jnp.cos(angle), jnp.sin(angle)
    return jnp.concatenate([cosine] * 4, axis=1), jnp.concatenate([-sine, sine] * 2, axis=1)


def tile_slots(owners):
    order = jnp.arange(owners.shape[0], dtype=jnp.int32)
    same = (owners[:, None] == owners[None, :]) & (order[None, :] < order[:, None])
    return jnp.sum(same.astype(jnp.int32), axis=1)


def adam(weight, first, second, grad, factor, rate, decay, steps):
    grad = grad * factor
    first = BETA_FIRST * first + (1.0 - BETA_FIRST) * grad
    second = BETA_SECOND * second + (1.0 - BETA_SECOND) * grad * grad
    first_hat = first / (1.0 - jnp.power(BETA_FIRST, steps))
    second_hat = second / (1.0 - jnp.power(BETA_SECOND, steps))
    weight = weight - rate * (first_hat / (jnp.sqrt(second_hat) + EPS_ADAM) + decay * weight)
    return (weight, first, second)


ALL = ("y", "x", "c", "z")
DP = ("y", "x", "c")
PART = ("x", "c")
UNITS = FF // D
TILES_PER = 4 + 3 * UNITS


MESH = pl.DeviceIdType.MESH


def half_rows(rows):
    return (rows // 2 + 15) // 16 * 16


def remote(src, dst, ssem, rsem, **to):
    return pltpu.make_async_remote_copy(
        src_ref=src, dst_ref=dst, send_sem=ssem, recv_sem=rsem, device_id=to, device_id_type=MESH
    )


def greet(zn, y, x, c, z):
    barrier = pltpu.get_barrier_semaphore()
    for to in ({"x": 1 - x}, {"y": 1 - y}, {"c": 1 - c}):
        pl.semaphore_signal(barrier, inc=1, device_id=to, device_id_type=MESH)
    if zn > 1:

        @pl.when(z < zn - 1)
        def _():
            pl.semaphore_signal(barrier, inc=1, device_id={"z": z + 1}, device_id_type=MESH)

        @pl.when(z > 0)
        def _():
            pl.semaphore_signal(barrier, inc=1, device_id={"z": z - 1}, device_id_type=MESH)

        @pl.when((z > 0) & (z < zn - 1))
        def _():
            pl.semaphore_wait(barrier, 5)

        @pl.when((z == 0) | (z == zn - 1))
        def _():
            pl.semaphore_wait(barrier, 4)
    else:
        pl.semaphore_wait(barrier, 3)


def gather_kernel(zn, x_ref, o_ref, hold, ssem, rsem, lsem):
    y, x, c, z = [lax.axis_index(n) for n in ALL]
    me = z if zn > 1 else 0
    rows = x_ref.shape[0]
    h0 = half_rows(rows)
    lo, hi = pl.ds(0, h0), pl.ds(h0, rows - h0)
    X, Y, DX, DY, CO, CX, CY, C0, C1, ZU, ZD = range(11)
    nx, ny, nc = {"x": 1 - x}, {"y": 1 - y}, {"c": 1 - c}

    def slot(yy, xx, zz):
        return ((yy * 2 + xx) * 2 + c) * zn + zz

    def copy(kind, k, src, dst, to):
        return remote(src, dst, ssem.at[kind, k], rsem.at[kind, k], **to)

    def block(s):
        return o_ref.at[s]

    greet(zn, y, x, c, z)
    local = pltpu.make_async_copy(x_ref, hold, lsem)
    local.start()
    local.wait()
    local = pltpu.make_async_copy(hold, o_ref.at[slot(y, x, me)], lsem)
    local.start()

    def spread(zb, src):
        dst = block(slot(y, x, zb))
        copy(X, zb, src, dst, nx).start()
        copy(Y, zb, src, dst, ny).start()
        copy(CO, zb, src, dst, nc).start()

    def up(s):
        zb = z - (s - 1)
        b = block(slot(y, x, zb))
        return copy(ZU, s, x_ref if s == 1 else b, b, {"z": z + 1})

    def down(s):
        zb = z + (s - 1)
        b = block(slot(y, x, zb))
        return copy(ZD, s, x_ref if s == 1 else b, b, {"z": z - 1})

    for s in range(1, zn):

        @pl.when((z < zn - 1) & (z - (s - 1) >= 0))
        def _():
            up(s).start()

        @pl.when((z > 0) & (z + (s - 1) < zn))
        def _():
            down(s).start()

        if s == 1:
            spread(me, x_ref)

        @pl.when(z - s >= 0)
        def _():
            copy(ZU, s, x_ref, x_ref, nx).wait_recv()
            spread(z - s, block(slot(y, x, z - s)))

        @pl.when(z + s < zn)
        def _():
            copy(ZD, s, x_ref, x_ref, nx).wait_recv()
            spread(z + s, block(slot(y, x, z + s)))

    if zn == 1:
        spread(0, x_ref)
    order = [lax.rem(z + j, zn) if zn > 1 else 0 for j in range(zn)]
    for zb in order:
        sx, sy = slot(y, 1 - x, zb), slot(1 - y, x, zb)
        copy(X, zb, x_ref, x_ref, nx).wait_recv()
        copy(DX, zb, o_ref.at[sx, lo], o_ref.at[sx, lo], ny).start()
        copy(CX, zb, block(sx), block(sx), nc).start()
        copy(Y, zb, x_ref, x_ref, nx).wait_recv()
        copy(DY, zb, o_ref.at[sy, hi], o_ref.at[sy, hi], nx).start()
        copy(CY, zb, block(sy), block(sy), nc).start()
    for zb in order:
        sd = slot(1 - y, 1 - x, zb)
        copy(DX, zb, x_ref.at[lo], x_ref.at[lo], nx).wait_recv()
        copy(C0, zb, o_ref.at[sd, lo], o_ref.at[sd, lo], nc).start()
        copy(DY, zb, x_ref.at[hi], x_ref.at[hi], nx).wait_recv()
        copy(C1, zb, o_ref.at[sd, hi], o_ref.at[sd, hi], nc).start()
    for zb in range(zn):
        for kind, part in ((CO, x_ref), (CX, x_ref), (CY, x_ref), (C0, x_ref.at[lo]), (C1, x_ref.at[hi])):
            copy(kind, zb, part, part, nx).wait_recv()
        for kind, part in (
            (X, x_ref), (Y, x_ref), (CO, x_ref), (CX, x_ref), (CY, x_ref),
            (DX, x_ref.at[lo]), (DY, x_ref.at[hi]), (C0, x_ref.at[lo]), (C1, x_ref.at[hi]),
        ):
            copy(kind, zb, part, part, nx).wait_send()
    for s in range(1, zn):

        @pl.when((z < zn - 1) & (z - (s - 1) >= 0))
        def _():
            up(s).wait_send()

        @pl.when((z > 0) & (z + (s - 1) < zn))
        def _():
            down(s).wait_send()

    local.wait()


def all_gather(x, zn, ident, name):
    sems = pltpu.SemaphoreType.DMA((11, zn))
    return pl.pallas_call(
        functools.partial(gather_kernel, zn),
        out_shape=jax.ShapeDtypeStruct((8 * zn,) + x.shape, x.dtype),
        in_specs=[pl.BlockSpec(memory_space=pl.ANY)],
        out_specs=pl.BlockSpec(memory_space=pl.ANY),
        scratch_shapes=[pltpu.VMEM(x.shape, x.dtype), sems, sems, pltpu.SemaphoreType.DMA],
        compiler_params=pltpu.CompilerParams(collective_id=ident, has_side_effects=True),
        name=name,
    )(x)


def reduce_kernel(zn, p_ref, o_ref, acc, crecv, dxr, dyr, xr, yr, zur, zdr, ssem, rsem, lsem):
    y, x, c, z = [lax.axis_index(n) for n in ALL]
    me = z if zn > 1 else 0
    rows, cols = p_ref.shape[1:]
    h0 = half_rows(rows)
    h1 = rows - h0
    X, Y, DX, DY, C0, ZU, ZD = 0, 1, 2, 3, 4, 8, 9
    nx, ny, nc = {"x": 1 - x}, {"y": 1 - y}, {"c": 1 - c}
    kinds = [(y, x), (y, 1 - x), (1 - y, x), (1 - y, 1 - x)]
    step = 32 if rows % 32 == 0 else 16

    def slot(k, cc, zz):
        yy, xx = kinds[k]
        return ((yy * 2 + xx) * 2 + cc) * zn + zz

    def copy(kind, k, src, dst, to):
        return remote(src, dst, ssem.at[kind, k], rsem.at[kind, k], **to)

    def load(k, zb):
        return pltpu.make_async_copy(p_ref.at[slot(k, c, zb)], acc.at[k * zn + zb], lsem.at[k * zn + zb])

    def across(k, zb):
        return copy(C0 + k, zb, p_ref.at[slot(k, 1 - c, zb)], crecv.at[k * zn + zb], nc)

    def add(dst, start, count, terms):
        size = step if count % step == 0 else 16

        @pl.loop(0, count // size)
        def _(i):
            at = pl.ds(pl.multiple_of(start + i * size, 16), size)
            total = None
            for ref, base in terms:
                part = ref[pl.ds(pl.multiple_of(start - base + i * size, 16), size), :].astype(jnp.float32)
                total = part if total is None else total + part
            dst[at, :] = total.astype(dst.dtype)

    greet(zn, y, x, c, z)
    zorder = [lax.rem(z + j, zn) if zn > 1 else 0 for j in range(zn)]
    for k in (3, 1, 2, 0):
        for zb in range(zn):
            across(k, zb).start()
            load(k, zb).start()

    def ready(k, zb):
        load(k, zb).wait()
        across(k, zb).wait_recv()

    for zb in range(zn):
        ready(3, zb)
        b = 3 * zn + zb
        add(acc.at[b], 0, rows, [(acc.at[b], 0), (crecv.at[b], 0)])
        copy(DX, zb, acc.at[b, pl.ds(0, h0)], dxr.at[zb], nx).start()
        copy(DY, zb, acc.at[b, pl.ds(h0, h1)], dyr.at[zb], ny).start()
    for zb in range(zn):
        ready(1, zb)
        b = zn + zb
        add(acc.at[b], 0, h0, [(acc.at[b], 0), (crecv.at[b], 0)])
        copy(DY, zb, dyr.at[zb], dyr.at[zb], ny).wait_recv()
        add(acc.at[b], h0, h1, [(acc.at[b], 0), (crecv.at[b], 0), (dyr.at[zb], h0)])
        copy(X, zb, acc.at[b], xr.at[zb], nx).start()
        ready(2, zb)
        b = 2 * zn + zb
        add(acc.at[b], h0, h1, [(acc.at[b], 0), (crecv.at[b], 0)])
        copy(DX, zb, dxr.at[zb], dxr.at[zb], nx).wait_recv()
        add(acc.at[b], 0, h0, [(acc.at[b], 0), (crecv.at[b], 0), (dxr.at[zb], 0)])
        copy(Y, zb, acc.at[b], yr.at[zb], ny).start()

    def column(zb):
        return [(acc.at[zb], 0), (crecv.at[zb], 0), (xr.at[zb], 0), (yr.at[zb], 0)]

    for zb in range(zn):
        ready(0, zb)
        copy(X, zb, acc.at[zb], xr.at[zb], nx).wait_recv()
        copy(Y, zb, acc.at[zb], yr.at[zb], ny).wait_recv()
        if zn == 1:
            add(o_ref, 0, rows, column(0))
            continue

        def upward(zb=zb):
            return copy(ZU, zb, acc.at[zb], zur.at[zb], {"z": z + 1})

        def downward(zb=zb):
            return copy(ZD, zb, acc.at[zb], zdr.at[zb], {"z": z - 1})

        @pl.when(z == zb)
        def _():
            add(acc.at[zb], 0, rows, column(zb))

        @pl.when((z < zb) & (z == 0))
        def _():
            add(acc.at[zb], 0, rows, column(zb))
            upward().start()

        @pl.when((z < zb) & (z > 0))
        def _():
            upward().wait_recv()
            add(acc.at[zb], 0, rows, column(zb) + [(zur.at[zb], 0)])
            upward().start()

        @pl.when((z > zb) & (z == zn - 1))
        def _():
            add(acc.at[zb], 0, rows, column(zb))
            downward().start()

        @pl.when((z > zb) & (z < zn - 1))
        def _():
            downward().wait_recv()
            add(acc.at[zb], 0, rows, column(zb) + [(zdr.at[zb], 0)])
            downward().start()

    if zn > 1:

        @pl.when(z == 0)
        def _():
            copy(ZD, me, acc.at[me], zdr.at[me], {"z": z + 1}).wait_recv()
            add(o_ref, 0, rows, [(acc.at[me], 0), (zdr.at[me], 0)])

        @pl.when(z == zn - 1)
        def _():
            copy(ZU, me, acc.at[me], zur.at[me], {"z": z - 1}).wait_recv()
            add(o_ref, 0, rows, [(acc.at[me], 0), (zur.at[me], 0)])

        @pl.when((z > 0) & (z < zn - 1))
        def _():
            copy(ZD, me, acc.at[me], zdr.at[me], {"z": z + 1}).wait_recv()
            copy(ZU, me, acc.at[me], zur.at[me], {"z": z + 1}).wait_recv()
            add(o_ref, 0, rows, [(acc.at[me], 0), (zdr.at[me], 0), (zur.at[me], 0)])

    for zb in range(zn):
        for k in range(4):
            across(k, zb).wait_send()
        copy(DX, zb, dxr.at[zb], dxr.at[zb], nx).wait_send()
        copy(DY, zb, dyr.at[zb], dyr.at[zb], ny).wait_send()
        copy(X, zb, xr.at[zb], xr.at[zb], nx).wait_send()
        copy(Y, zb, yr.at[zb], yr.at[zb], ny).wait_send()
        if zn > 1:

            @pl.when(z < zb)
            def _():
                copy(ZU, zb, zur.at[zb], zur.at[zb], {"z": z + 1}).wait_send()

            @pl.when(z > zb)
            def _():
                copy(ZD, zb, zdr.at[zb], zdr.at[zb], {"z": z - 1}).wait_send()


def reduce_scatter(p, zn, ident, name, out_dtype=None):
    count, rows, cols = p.shape
    h0 = half_rows(rows)
    sems = pltpu.SemaphoreType.DMA((10, zn))
    vm = lambda n, r: pltpu.VMEM((n, r, cols), p.dtype)
    return pl.pallas_call(
        functools.partial(reduce_kernel, zn),
        out_shape=jax.ShapeDtypeStruct((rows, cols), out_dtype or p.dtype),
        in_specs=[pl.BlockSpec(memory_space=pl.ANY)],
        out_specs=pl.BlockSpec(memory_space=pltpu.VMEM),
        scratch_shapes=[
            vm(4 * zn, rows), vm(4 * zn, rows), vm(zn, h0), vm(zn, rows - h0),
            vm(zn, rows), vm(zn, rows), vm(zn, rows), vm(zn, rows),
            sems, sems, pltpu.SemaphoreType.DMA((4 * zn,)),
        ],
        compiler_params=pltpu.CompilerParams(
            collective_id=ident, has_side_effects=True, vmem_limit_bytes=56 << 20
        ),
        name=name,
    )(p)


def greet_pair(x, c):
    barrier = pltpu.get_barrier_semaphore()
    for to in ({"x": 1 - x}, {"c": 1 - c}):
        pl.semaphore_signal(barrier, inc=1, device_id=to, device_id_type=MESH)
    pl.semaphore_wait(barrier, 2)


def keys_gather_kernel(x_ref, o_ref, hold, ssem, rsem, lsem):
    x, c = lax.axis_index("x"), lax.axis_index("c")
    me, far = x * 2 + c, (1 - x) * 2 + c
    nx, nc = {"x": 1 - x}, {"c": 1 - c}
    load = pltpu.make_async_copy(x_ref, hold, lsem.at[0])
    load.start()
    greet_pair(x, c)
    out = remote(x_ref, o_ref.at[me], ssem.at[0], rsem.at[0], **nx)
    out.start()
    near = remote(x_ref, o_ref.at[me], ssem.at[1], rsem.at[1], **nc)
    near.start()
    load.wait()
    keep = pltpu.make_async_copy(hold, o_ref.at[me], lsem.at[1])
    keep.start()
    out.wait_recv()
    on = remote(o_ref.at[far], o_ref.at[far], ssem.at[2], rsem.at[2], **nc)
    on.start()
    near.wait_recv()
    on.wait_recv()
    keep.wait()
    out.wait_send()
    near.wait_send()
    on.wait_send()


def keys_gather(v, ident):
    sems = pltpu.SemaphoreType.DMA((3,))
    return pl.pallas_call(
        keys_gather_kernel,
        out_shape=jax.ShapeDtypeStruct((4,) + v.shape, v.dtype),
        in_specs=[pl.BlockSpec(memory_space=pl.ANY)],
        out_specs=pl.BlockSpec(memory_space=pl.ANY),
        scratch_shapes=[pltpu.VMEM(v.shape, v.dtype), sems, sems, pltpu.SemaphoreType.DMA((2,))],
        compiler_params=pltpu.CompilerParams(collective_id=ident, has_side_effects=True),
        name="keys_gather",
    )(v)


def keys_reduce_kernel(p_ref, o_ref, acc, crecv, xr, ssem, rsem, lsem):
    x, c = lax.axis_index("x"), lax.axis_index("c")
    nx, nc = {"x": 1 - x}, {"c": 1 - c}
    rows = p_ref.shape[1]
    places = [(1 - x) * 2, x * 2]
    loads = [pltpu.make_async_copy(p_ref.at[places[i] + c], acc.at[i], lsem.at[i]) for i in range(2)]
    for load in loads:
        load.start()
    greet_pair(x, c)
    across = [
        remote(p_ref.at[places[i] + 1 - c], crecv.at[i], ssem.at[i], rsem.at[i], **nc) for i in range(2)
    ]
    for copy in across:
        copy.start()

    def add(dst, terms):
        @pl.loop(0, rows // 16)
        def _(i):
            at = pl.ds(pl.multiple_of(i * 16, 16), 16)
            total = terms[0][at, :].astype(jnp.float32)
            for term in terms[1:]:
                total = total + term[at, :].astype(jnp.float32)
            dst[at, :] = total.astype(dst.dtype)

    loads[0].wait()
    across[0].wait_recv()
    add(acc.at[0], [acc.at[0], crecv.at[0]])
    out = remote(acc.at[0], xr, ssem.at[2], rsem.at[2], **nx)
    out.start()
    loads[1].wait()
    across[1].wait_recv()
    out.wait_recv()
    add(o_ref, [acc.at[1], crecv.at[1], xr])
    for copy in across + [out]:
        copy.wait_send()


def keys_reduce(p, ident):
    block = p.shape[1:]
    sems = pltpu.SemaphoreType.DMA((3,))
    return pl.pallas_call(
        keys_reduce_kernel,
        out_shape=jax.ShapeDtypeStruct(block, p.dtype),
        in_specs=[pl.BlockSpec(memory_space=pl.ANY)],
        out_specs=pl.BlockSpec(memory_space=pltpu.VMEM),
        scratch_shapes=[
            pltpu.VMEM((2,) + block, p.dtype), pltpu.VMEM((2,) + block, p.dtype),
            pltpu.VMEM(block, p.dtype), sems, sems, pltpu.SemaphoreType.DMA((2,)),
        ],
        compiler_params=pltpu.CompilerParams(
            collective_id=ident, has_side_effects=True, vmem_limit_bytes=32 << 20
        ),
        name="keys_reduce",
    )(p)


def fits(axes):
    return [lax.axis_size(n) for n in ALL] == [2, 2, 2, 4]


def gather_all(v, ident, name):
    if fits(ALL):
        return all_gather(v, 4, ident, name)
    return lax.all_gather(v, ALL, axis=0)


def gather_plane(v, ident, name):
    if fits(ALL):
        return all_gather(v, 1, ident, name)
    return lax.all_gather(v, DP, axis=0)


def scatter_all(p, ident, name):
    if fits(ALL):
        return reduce_scatter(p, 4, ident, name)
    return lax.psum_scatter(p, ALL, scatter_dimension=0)


def scatter_plane(p, ident, name):
    if fits(ALL):
        return reduce_scatter(p, 1, ident, name)
    return lax.psum_scatter(p, DP, scatter_dimension=0)


def keys_all_gather(v):
    if fits(ALL):
        return keys_gather(v, 11).reshape(-1, v.shape[1])
    return lax.all_gather(v, PART, axis=0, tiled=True)


def keys_sum_scatter(p):
    if fits(ALL):
        return keys_reduce(p.reshape(4, -1, p.shape[1]), 12)
    return lax.psum_scatter(p, PART, scatter_dimension=0, tiled=True)


def tile_spec(layer, per, deep, tile_rows, index):
    def place(t):
        j = index(t)
        return (j // per, 0, layer * per + j % per, 0, 0)

    return pl.BlockSpec((None, deep, None, tile_rows, D), place)


def whole(shape):
    return pl.BlockSpec(shape, lambda t: (0,) * len(shape))


def dot_nn(a, b):
    return lax.dot_general(a, b, (((1,), (0,)), ((), ())), preferred_element_type=jnp.float32)


def dot_nt(a, b):
    return lax.dot_general(a, b, (((1,), (1,)), ((), ())), preferred_element_type=jnp.float32)


def dot_tn(a, b):
    return lax.dot_general(a, b, (((0,), (0,)), ((), ())), preferred_element_type=jnp.float32)


def turned(u, cos, sin):
    lane = lax.broadcasted_iota(jnp.int32, (u.shape[0], 128), 1)
    low = (lane % HD) < HD // 2
    parts = []
    for i in range(D // 128):
        v = u[:, i * 128 : (i + 1) * 128]
        other = jnp.where(low, pltpu.roll(v, 128 - HD // 2, 1), pltpu.roll(v, HD // 2, 1))
        parts.append(v * cos + other * sin)
    return jnp.concatenate(parts, axis=1)


def project_kernel(x_ref, g_ref, cos_ref, sin_ref, w_ref, q_ref, kv_ref, a_ref):
    t = pl.program_id(0)

    @pl.when(t == 0)
    def _():
        a_ref[...] = root_norm(x_ref[...], g_ref[...]).astype(jnp.bfloat16)

    m = dot_nn(a_ref[...], w_ref[...].reshape(D, D))

    @pl.when(t == 0)
    def _():
        q_ref[...] = turned(m, cos_ref[...], sin_ref[...]).astype(jnp.bfloat16)

    @pl.when(t == 1)
    def _():
        kv_ref[...] = turned(m, cos_ref[...], sin_ref[...]).astype(jnp.bfloat16)

    @pl.when(t == 2)
    def _():
        kv_ref[...] = m.astype(jnp.bfloat16)


def project(x, gain, cos, sin, weights, layer, per):
    rows = x.shape[0]
    deep, tile_rows = weights.shape[1], weights.shape[3]
    return pl.pallas_call(
        project_kernel,
        grid=(3,),
        out_shape=(
            jax.ShapeDtypeStruct((rows, D), jnp.bfloat16),
            jax.ShapeDtypeStruct((2, rows, D), jnp.bfloat16),
        ),
        in_specs=[
            whole((rows, D)), whole((1, D)), whole((rows, 128)), whole((rows, 128)),
            tile_spec(layer, per, deep, tile_rows, lambda t: t),
        ],
        out_specs=(
            whole((rows, D)),
            pl.BlockSpec((None, rows, D), lambda t: (jnp.maximum(t - 1, 0), 0, 0)),
        ),
        scratch_shapes=[pltpu.VMEM((rows, D), jnp.bfloat16)],
        compiler_params=pltpu.CompilerParams(vmem_limit_bytes=40 << 20),
        name="project",
    )(x, gain, cos, sin, weights)


def mask_bias(bias_ref, kseg_ref, qseg_ref, qpos_ref):
    kpos = lax.broadcasted_iota(jnp.int32, bias_ref.shape, 0)
    allowed = (kpos <= qpos_ref[...]) & (kseg_ref[...] == qseg_ref[...])
    bias_ref[...] = jnp.where(allowed, 0.0, MASKED)


def head_lanes(shape, head):
    return (lax.broadcasted_iota(jnp.int32, shape, 1) // HD) == head


def attend_kernel(q_ref, k_ref, v_ref, kseg_ref, qseg_ref, qpos_ref, o_ref, lse_ref, bias_ref):
    @pl.when(pl.program_id(0) == 0)
    def _():
        mask_bias(bias_ref, kseg_ref, qseg_ref, qpos_ref)

    length = bias_ref.shape[0]
    q = q_ref[...]
    k, v = k_ref[...].reshape(length, 128), v_ref[...].reshape(length, 128)
    outs = []
    for head in range(2):
        mine = head_lanes(q.shape, head)
        s = dot_nt(k, jnp.where(mine, q, jnp.zeros_like(q))) * HD ** (-0.5) + bias_ref[...]
        top = jnp.max(s, axis=0, keepdims=True)
        e = jnp.exp(s - top)
        total = jnp.sum(e, axis=0, keepdims=True)
        p = (e * (1.0 / total)).astype(jnp.bfloat16)
        outs.append(dot_tn(p, v))
        lse_ref[head : head + 1, :] = top + jnp.log(total)
    o_ref[...] = jnp.where(head_lanes(outs[0].shape, 0), outs[0], outs[1]).astype(jnp.bfloat16)


def attend_specs(rows, parts):
    length = parts * rows
    pair = pl.BlockSpec((rows, 128), lambda t: (0, t))
    return pair, [
        pair,
        pl.BlockSpec((parts, None, rows, 128), lambda t: (0, 0, 0, t)),
        pl.BlockSpec((parts, None, rows, 128), lambda t: (0, 1, 0, t)),
        whole((length, 1)), whole((1, rows)), whole((1, rows)),
    ]


def attend(q, kv, kseg, qseg, qpos):
    rows, parts = q.shape[0], kv.shape[0]
    pair, specs = attend_specs(rows, parts)
    return pl.pallas_call(
        attend_kernel,
        grid=(HEADS // 2,),
        out_shape=(
            jax.ShapeDtypeStruct((rows, D), jnp.bfloat16),
            jax.ShapeDtypeStruct((HEADS // 2, 8, rows), jnp.float32),
        ),
        in_specs=specs,
        out_specs=(pair, pl.BlockSpec((None, 8, rows), lambda t: (t, 0, 0))),
        scratch_shapes=[pltpu.VMEM((parts * rows, rows), jnp.float32)],
        compiler_params=pltpu.CompilerParams(vmem_limit_bytes=40 << 20),
        name="attend",
    )(q, kv, kv, kseg, qseg, qpos)


def feed_kernel(x_ref, o_ref, g_ref, wo_ref, wg_ref, wu_ref, wd_ref, mid_ref, out_ref, b_ref):
    t = pl.program_id(0)

    @pl.when(t == 0)
    def _():
        mid = x_ref[...] + dot_nn(o_ref[...], wo_ref[...].reshape(D, D))
        mid_ref[...] = mid
        out_ref[...] = mid
        b_ref[...] = root_norm(mid, g_ref[...]).astype(jnp.bfloat16)

    @pl.when(t > 0)
    def _():
        gate = dot_nn(b_ref[...], wg_ref[...].reshape(D, D))
        up = dot_nn(b_ref[...], wu_ref[...].reshape(D, D))
        h = (gate * jax.nn.sigmoid(gate) * up).astype(jnp.bfloat16)
        out_ref[...] += dot_nn(h, wd_ref[...].reshape(D, D))


def feed(x, o, gain, weights, layer, per):
    rows = x.shape[0]
    deep, tile_rows = weights.shape[1], weights.shape[3]
    spec = functools.partial(tile_spec, layer, per, deep, tile_rows)
    unit = lambda t: jnp.maximum(t - 1, 0)
    state = jax.ShapeDtypeStruct((rows, D), jnp.float32)
    return pl.pallas_call(
        feed_kernel,
        grid=(1 + UNITS,),
        out_shape=(state, state),
        in_specs=[
            whole((rows, D)), whole((rows, D)), whole((1, D)),
            spec(lambda t: 3 + 0 * t), spec(lambda t: 4 + unit(t)),
            spec(lambda t: 4 + UNITS + unit(t)), spec(lambda t: 4 + 2 * UNITS + unit(t)),
        ],
        out_specs=(whole((rows, D)), whole((rows, D))),
        scratch_shapes=[pltpu.VMEM((rows, D), jnp.bfloat16)],
        compiler_params=pltpu.CompilerParams(vmem_limit_bytes=48 << 20),
        name="feed",
    )(x, o, gain, weights, weights, weights, weights)


def feed_back_kernel(
    dy_ref, mid_ref, g_ref, o_ref, wo_ref, wg_ref, wu_ref, wd_ref,
    grad_ref, dx_ref, do_ref, dgain_ref,
    b_ref, e_ref, dg_ref, du_ref, db_ref,
):
    t = pl.program_id(0)
    last = pl.num_programs(0) - 1
    deep, tile_rows = grad_ref.shape[0], grad_ref.shape[1]

    def emit(g):
        grad_ref[...] = g.astype(jnp.bfloat16).reshape(deep, tile_rows, D)

    @pl.when(t == 0)
    def _():
        b_ref[...] = root_norm(mid_ref[...], g_ref[...]).astype(jnp.bfloat16)
        e_ref[...] = dy_ref[...].astype(jnp.bfloat16)
        db_ref[...] = jnp.zeros_like(db_ref)

    @pl.when((t % 3 == 0) & (t < last))
    def _():
        gate = dot_nn(b_ref[...], wg_ref[...].reshape(D, D))
        up = dot_nn(b_ref[...], wu_ref[...].reshape(D, D))
        sigma = jax.nn.sigmoid(gate)
        h = (gate * sigma * up).astype(jnp.bfloat16)
        emit(dot_tn(h, e_ref[...]))
        dh = dot_nt(e_ref[...], wd_ref[...].reshape(D, D))
        dg_ref[...] = (dh * up * sigma * (1.0 + gate * (1.0 - sigma))).astype(jnp.bfloat16)
        du_ref[...] = (dh * gate * sigma).astype(jnp.bfloat16)

    @pl.when(t % 3 == 1)
    def _():
        emit(dot_tn(b_ref[...], dg_ref[...]))
        db_ref[...] += dot_nt(dg_ref[...], wg_ref[...].reshape(D, D))

    @pl.when(t % 3 == 2)
    def _():
        emit(dot_tn(b_ref[...], du_ref[...]))
        db_ref[...] += dot_nt(du_ref[...], wu_ref[...].reshape(D, D))

    @pl.when(t == last)
    def _():
        back, gain_back = norm_back(mid_ref[...], g_ref[...], db_ref[...])
        dx = dy_ref[...] + back
        dx_ref[...] = dx
        dgain_ref[...] = jnp.broadcast_to(gain_back[None, :], dgain_ref.shape)
        e1 = dx.astype(jnp.bfloat16)
        emit(dot_tn(o_ref[...], e1))
        do_ref[...] = dot_nt(e1, wo_ref[...].reshape(D, D)).astype(jnp.bfloat16)


def feed_back(dy, mid, gain, o, weights, layer, per):
    rows = dy.shape[0]
    dp, deep, tile_rows = weights.shape[0], weights.shape[1], weights.shape[3]
    spec = functools.partial(tile_spec, layer, per, deep, tile_rows)
    unit = lambda t: jnp.minimum(t // 3, UNITS - 1)

    def grad_tile(t):
        kind = t % 3
        base = jnp.where(kind == 0, 4 + 2 * UNITS, jnp.where(kind == 1, 4, 4 + UNITS))
        return jnp.where(t == 3 * UNITS, 3, base + unit(t))

    return pl.pallas_call(
        feed_back_kernel,
        grid=(3 * UNITS + 1,),
        out_shape=(
            jax.ShapeDtypeStruct((dp, deep, per, tile_rows, D), jnp.bfloat16),
            jax.ShapeDtypeStruct((rows, D), jnp.float32),
            jax.ShapeDtypeStruct((rows, D), jnp.bfloat16),
            jax.ShapeDtypeStruct((8, D), jnp.float32),
        ),
        in_specs=[
            whole((rows, D)), whole((rows, D)), whole((1, D)), whole((rows, D)),
            spec(lambda t: 3 + 0 * t), spec(lambda t: 4 + unit(t)),
            spec(lambda t: 4 + UNITS + unit(t)), spec(lambda t: 4 + 2 * UNITS + unit(t)),
        ],
        out_specs=(
            tile_spec(0, per, deep, tile_rows, grad_tile),
            whole((rows, D)), whole((rows, D)), whole((8, D)),
        ),
        scratch_shapes=[
            pltpu.VMEM((rows, D), jnp.bfloat16), pltpu.VMEM((rows, D), jnp.bfloat16),
            pltpu.VMEM((rows, D), jnp.bfloat16), pltpu.VMEM((rows, D), jnp.bfloat16),
            pltpu.VMEM((rows, D), jnp.float32),
        ],
        compiler_params=pltpu.CompilerParams(vmem_limit_bytes=48 << 20),
        name="feed_back",
    )(dy, mid, gain, o, weights, weights, weights, weights)


def attend_back_kernel(
    q_ref, k_ref, v_ref, kseg_ref, qseg_ref, qpos_ref, do_ref, lse_ref, dq_ref, dkv_ref, bias_ref
):
    @pl.when(pl.program_id(0) == 0)
    def _():
        mask_bias(bias_ref, kseg_ref, qseg_ref, qpos_ref)

    length = bias_ref.shape[0]
    parts, rows = dkv_ref.shape[0], q_ref.shape[0]
    q, do = q_ref[...], do_ref[...]
    k, v = k_ref[...].reshape(length, 128), v_ref[...].reshape(length, 128)
    dqs, dk, dv = [], None, None
    for head in range(2):
        mine = head_lanes(q.shape, head)
        qm = jnp.where(mine, q, jnp.zeros_like(q))
        dom = jnp.where(mine, do, jnp.zeros_like(do))
        s = dot_nt(k, qm) * HD ** (-0.5) + bias_ref[...]
        p = jnp.exp(s - lse_ref[head : head + 1, :])
        dp = dot_nt(v, dom)
        delta = jnp.sum(p * dp, axis=0, keepdims=True)
        ds = (p * (dp - delta) * HD ** (-0.5)).astype(jnp.bfloat16)
        dv_part = dot_nn(p.astype(jnp.bfloat16), dom)
        dk_part = dot_nn(ds, qm)
        dv = dv_part if dv is None else dv + dv_part
        dk = dk_part if dk is None else dk + dk_part
        dqs.append(dot_tn(ds, k))
    dq_ref[...] = jnp.where(head_lanes(dqs[0].shape, 0), dqs[0], dqs[1])
    dkv_ref[:, 0] = dk.astype(jnp.bfloat16).reshape(parts, rows, 128)
    dkv_ref[:, 1] = dv.astype(jnp.bfloat16).reshape(parts, rows, 128)


def attend_back(q, kv, kseg, qseg, qpos, do, lse):
    rows, parts = q.shape[0], kv.shape[0]
    pair, specs = attend_specs(rows, parts)
    return pl.pallas_call(
        attend_back_kernel,
        grid=(HEADS // 2,),
        out_shape=(
            jax.ShapeDtypeStruct((rows, D), jnp.float32),
            jax.ShapeDtypeStruct((parts, 2, rows, D), jnp.bfloat16),
        ),
        in_specs=specs + [pair, pl.BlockSpec((None, 8, rows), lambda t: (t, 0, 0))],
        out_specs=(pair, pl.BlockSpec((parts, 2, rows, 128), lambda t: (0, 0, 0, t))),
        scratch_shapes=[pltpu.VMEM((parts * rows, rows), jnp.float32)],
        compiler_params=pltpu.CompilerParams(vmem_limit_bytes=48 << 20),
        name="attend_back",
    )(q, kv, kv, kseg, qseg, qpos, do, lse)


def project_back_kernel(
    dx_ref, x_ref, g_ref, cos_ref, sin_ref, dq_ref, dkv_ref, w_ref, held_ref,
    grad_ref, out_ref, dgain_ref, a_ref, dm_ref, da_ref,
):
    t = pl.program_id(0)
    deep, tile_rows = grad_ref.shape[0], grad_ref.shape[1]

    @pl.when(t == 0)
    def _():
        a_ref[...] = root_norm(x_ref[...], g_ref[...]).astype(jnp.bfloat16)
        da_ref[...] = jnp.zeros_like(da_ref)
        dm_ref[...] = turned(dq_ref[...], cos_ref[...], -sin_ref[...]).astype(jnp.bfloat16)

    @pl.when(t == 1)
    def _():
        dk = dkv_ref[0].astype(jnp.float32)
        dm_ref[...] = turned(dk, cos_ref[...], -sin_ref[...]).astype(jnp.bfloat16)

    @pl.when(t == 2)
    def _():
        dm_ref[...] = dkv_ref[1]

    grad = dot_tn(a_ref[...], dm_ref[...])
    grad_ref[...] = grad.astype(jnp.bfloat16).reshape(deep, tile_rows, D)
    da_ref[...] += dot_nt(dm_ref[...], w_ref[...].reshape(D, D))

    @pl.when(t == 2)
    def _():
        back, gain_back = norm_back(x_ref[...], g_ref[...], da_ref[...])
        out_ref[...] = dx_ref[...] + back
        dgain_ref[...] = jnp.broadcast_to(gain_back[None, :], dgain_ref.shape)


def project_back(dx, x, gain, cos, sin, dq, dkv, weights, grads, layer, per):
    rows = x.shape[0]
    deep, tile_rows = weights.shape[1], weights.shape[3]
    return pl.pallas_call(
        project_back_kernel,
        grid=(3,),
        out_shape=(
            jax.ShapeDtypeStruct(grads.shape, grads.dtype),
            jax.ShapeDtypeStruct((rows, D), jnp.float32),
            jax.ShapeDtypeStruct((8, D), jnp.float32),
        ),
        in_specs=[
            whole((rows, D)), whole((rows, D)), whole((1, D)), whole((rows, 128)),
            whole((rows, 128)), whole((rows, D)), whole((2, rows, D)),
            tile_spec(layer, per, deep, tile_rows, lambda t: t),
            pl.BlockSpec(memory_space=pl.ANY),
        ],
        out_specs=(
            tile_spec(0, per, deep, tile_rows, lambda t: t), whole((rows, D)), whole((8, D)),
        ),
        scratch_shapes=[
            pltpu.VMEM((rows, D), jnp.bfloat16), pltpu.VMEM((rows, D), jnp.bfloat16),
            pltpu.VMEM((rows, D), jnp.float32),
        ],
        input_output_aliases={8: 0},
        compiler_params=pltpu.CompilerParams(vmem_limit_bytes=40 << 20),
        name="project_back",
    )(dx, x, gain, cos, sin, dq, dkv, weights, grads)


def layer_forward(state, weights, layer, per, gains, cos, sin, marks):
    rows = state.shape[0]
    q, kv = project(state, gains[2 * layer : 2 * layer + 1], cos, sin, weights, layer, per)
    kv = keys_all_gather(kv.reshape(2 * rows, D)).reshape(-1, 2, rows, D)
    o, lse = attend(q, kv, *marks)
    mid, out = feed(state, o, gains[2 * layer + 1 : 2 * layer + 2], weights, layer, per)
    return out, (state, mid, q, kv, lse, o)


def layer_backward(grad, kept, weights, layer, per, gains, cos, sin, marks):
    state, mid, q, kv, lse, o = kept
    rows = state.shape[0]
    grads, dx, do, feed_gain = feed_back(
        grad, mid, gains[2 * layer + 1 : 2 * layer + 2], o, weights, layer, per
    )
    dq, dkv = attend_back(q, kv, *marks, do, lse)
    dkv = keys_sum_scatter(dkv.reshape(-1, D)).reshape(2, rows, D)
    grads, dx, input_gain = project_back(
        dx, state, gains[2 * layer : 2 * layer + 1], cos, sin, dq, dkv, weights, grads, layer, per
    )
    return dx, grads, [input_gain[0], feed_gain[0]]


def padded(v):
    count = -(-v.shape[0] // 4096) * 4096
    return jnp.pad(v, (0, count - v.shape[0])).reshape(-1, 128)


def shards(
    tokens,
    segments,
    completion,
    targets,
    owners,
    step_count,
    tile_weight,
    tile_first,
    tile_second,
    table_weight,
    table_first,
    table_second,
    head_weight,
    head_first,
    head_second,
    gain_weight,
    gain_first,
    gain_second,
):
    a_size, b_size, rep_size = lax.axis_size("y"), lax.axis_size(PART), lax.axis_size("z")
    a_index, b_index, rep_index = lax.axis_index("y"), lax.axis_index(PART), lax.axis_index("z")
    dp_size = a_size * b_size
    devices = dp_size * rep_size
    dp_index = a_index * b_size + b_index
    device = dp_index * rep_size + rep_index
    rows = tokens.shape[1]
    length = segments.shape[1]
    comp = completion.shape[1]
    slots_cap, tile_rows = tile_weight.shape[:2]
    tile_count = owners.shape[0]
    home_tiles = tile_count // dp_size
    vocab_rows = table_weight.shape[0]
    vocab_start = device * vocab_rows
    sequence = a_index * rep_size + rep_index

    own_part = jnp.concatenate(
        [
            tokens[0],
            lax.dynamic_slice_in_dim(segments[0], rep_index * rows, rows),
            lax.dynamic_slice_in_dim(completion[0], rep_index * (comp // rep_size), comp // rep_size),
            lax.dynamic_slice_in_dim(targets[0], rep_index * (comp // rep_size), comp // rep_size),
        ]
    )
    packed = gather_all(padded(own_part), 0, "ids_gather").reshape(devices, -1)
    packed = packed[:, : own_part.shape[0]].reshape(dp_size, rep_size, -1)
    tokens_all = packed[:, :, :rows].reshape(dp_size, length)
    segments_all = packed[:, :, rows : 2 * rows].reshape(dp_size, length)
    edge = 2 * rows + comp // rep_size
    completion_all = packed[:, :, 2 * rows : edge].reshape(dp_size, comp)
    targets_all = packed[:, :, edge:].reshape(dp_size, comp)

    slots = tile_slots(owners)
    mine = owners == dp_index
    tile_low = tile_weight.astype(jnp.bfloat16)
    per = TILES_PER // dp_size
    home_ids = (
        jnp.arange(LAYERS)[None, :, None] * TILES_PER
        + jnp.arange(dp_size)[:, None, None] * per
        + jnp.arange(per)[None, None, :]
    ).reshape(-1)
    home_mine = jnp.take(mine, home_ids)
    home_slots = jnp.where(home_mine, jnp.take(slots, home_ids), 0)
    placed = jnp.where(home_mine[:, None, None], jnp.take(tile_low, home_slots, axis=0), 0)
    home = scatter_plane(placed.reshape(dp_size, -1, D), 7, "home_scatter")
    spread = gather_all(home, 1, "weights_gather")
    weights = spread.reshape(dp_size, rep_size, LAYERS * per, tile_rows, D)

    order = tokens_all.reshape(a_size, rep_size, b_size, rows).transpose(0, 2, 1, 3).reshape(-1)
    place = order - vocab_start
    vocab_iota = jnp.arange(vocab_rows)
    token_hot = (place[:, None] == vocab_iota[None, :]).astype(jnp.bfloat16)
    picked = jnp.dot(
        token_hot, table_weight.astype(jnp.bfloat16), preferred_element_type=jnp.float32
    ).astype(jnp.bfloat16)
    state = scatter_all(picked.reshape(devices, rows, D), 8, "rows_scatter").astype(jnp.float32)

    first_place = b_index * rows
    places = first_place + jnp.arange(rows)
    cosine, sine = rope_tables(places.astype(jnp.float32))
    own_segments = lax.dynamic_index_in_dim(segments_all, sequence, 0, False)
    query_segments = lax.dynamic_slice_in_dim(own_segments, first_place, rows)
    marks = (own_segments[:, None], query_segments[None, :], places[None, :])
    kept_list = []
    for index in range(LAYERS):
        state, kept = layer_forward(
            state, weights, index, per, gain_weight, cosine, sine, marks
        )
        kept_list.append(kept)
    final_gain = gain_weight[2 * LAYERS]
    final = root_norm(state, final_gain).astype(jnp.bfloat16)

    capacity = 3 * comp // (2 * rep_size)
    block = completion_all // rows
    inside = block[:, None, :] == jnp.arange(b_size)[None, :, None]
    rank = jnp.cumsum(inside.astype(jnp.int32), axis=2) - 1
    slot_pick = inside[..., None] & (rank[..., None] == jnp.arange(capacity))
    filled = jnp.any(slot_pick, axis=2)
    wanted = jnp.where(
        filled, jnp.sum(jnp.where(slot_pick, targets_all[:, None, :, None], 0), axis=2), -1
    )
    spots = jnp.where(
        filled, jnp.sum(jnp.where(slot_pick, (completion_all % rows)[:, None, :, None], 0), axis=2), -1
    )
    all_wanted = (
        wanted.reshape(a_size, rep_size, b_size, capacity).transpose(0, 2, 1, 3).reshape(-1)
    )
    own_spots = lax.dynamic_index_in_dim(
        lax.dynamic_index_in_dim(spots, sequence, 0, False), b_index, 0, False
    )
    select = (own_spots[:, None] == jnp.arange(rows)[None, :]).astype(jnp.bfloat16)
    chosen = jnp.dot(select, final, preferred_element_type=jnp.float32).astype(jnp.bfloat16)
    all_rows = gather_all(chosen, 3, "chosen_gather").reshape(-1, D)
    head_low = head_weight.astype(jnp.bfloat16)
    logits = jnp.einsum("rd,vd->rv", all_rows, head_low, preferred_element_type=jnp.float32)
    hot = vocab_iota[None, :] == (all_wanted - vocab_start)[:, None]
    local_top = jnp.max(logits, axis=-1)
    local_total = jnp.sum(jnp.exp(logits - local_top[:, None]), axis=-1)
    local_hit = jnp.sum(jnp.where(hot, logits, 0.0), axis=-1)
    own_stats = jnp.concatenate([local_top, local_total, local_hit])
    stats = gather_all(padded(own_stats), 4, "stats_gather").reshape(devices, -1)
    stats = stats[:, : own_stats.shape[0]].reshape(devices, 3, -1)
    top = jnp.max(stats[:, 0], axis=0)
    total = jnp.sum(stats[:, 1] * jnp.exp(stats[:, 0] - top[None]), axis=0)
    log_total = top + jnp.log(total)
    valid = all_wanted >= 0
    scored = dp_size * comp
    loss = jnp.sum(jnp.where(valid, log_total - jnp.sum(stats[:, 2], axis=0), 0.0)) / scored
    logit_grad = jnp.where(
        valid[:, None],
        (jnp.exp(logits - log_total[:, None]) - jnp.where(hot, 1.0, 0.0)) / scored,
        0.0,
    ).astype(jnp.bfloat16)
    rows_grad = jnp.dot(logit_grad, head_low, preferred_element_type=jnp.float32)
    own_rows = scatter_all(
        rows_grad.astype(jnp.bfloat16).reshape(devices, -1, D), 9, "back_scatter"
    )
    head_grad = jnp.einsum("rv,rd->vd", logit_grad, all_rows, preferred_element_type=jnp.float32)
    final_grad = jnp.einsum("ct,cd->td", select, own_rows, preferred_element_type=jnp.float32)
    state_grad, final_gain_grad = norm_back(state, final_gain, final_grad)
    tile_parts = [None] * LAYERS
    gain_parts = [None] * LAYERS
    for index in reversed(range(LAYERS)):
        state_grad, tile_parts[index], gain_parts[index] = layer_backward(
            state_grad, kept_list[index], weights, index, per, gain_weight, cosine, sine, marks
        )
    piece_grads = gather_all(state_grad.astype(jnp.bfloat16), 2, "entry_gather").reshape(-1, D)
    table_grad = jnp.einsum(
        "tv,td->vd", token_hot, piece_grads, preferred_element_type=jnp.float32
    )
    home_grads = []
    for index in range(LAYERS):
        part = tile_parts[index].reshape(devices, -1, D)
        home_grads.append(scatter_all(part, 10, "grads_scatter"))
    plane_grad = gather_plane(jnp.concatenate(home_grads), 6, "owners_gather")
    plane_grad = plane_grad.reshape(dp_size, LAYERS, per, tile_rows, D)
    plane_grad = plane_grad.transpose(1, 0, 2, 3, 4).reshape(tile_count, tile_rows, D)
    own_count = jnp.sum(mine.astype(jnp.int32))
    slot_ids = jnp.arange(slots_cap)
    tile_of_slot = jnp.sum(
        jnp.where(
            mine[None, :] & (slots[None, :] == slot_ids[:, None]), jnp.arange(tile_count)[None, :], 0
        ),
        axis=1,
    )
    slot_valid = (slot_ids < own_count)[:, None, None]
    own_grad = jnp.where(
        slot_valid, jnp.take(plane_grad, tile_of_slot, axis=0).astype(jnp.float32), 0.0
    )
    gain_grads = jnp.stack([g for pair in gain_parts for g in pair] + [final_gain_grad])
    square = (
        jnp.sum(own_grad * own_grad)
        + jnp.sum(table_grad * table_grad)
        + jnp.sum(head_grad * head_grad)
    )
    sums = gather_all(
        padded(jnp.concatenate([square[None], gain_grads.reshape(-1)])), 5, "sums_gather"
    )
    sums = jnp.sum(sums.reshape(devices, -1), axis=0)
    square, gain_grads = sums[0], sums[1 : 1 + gain_grads.size].reshape(gain_grads.shape)
    norm = jnp.sqrt(square + jnp.sum(gain_grads * gain_grads))
    factor = jnp.minimum(1.0, CLIP_NORM / norm)
    steps = step_count[0].astype(jnp.float32)
    tile_new, tile_first_new, tile_second_new = adam(
        tile_weight, tile_first, tile_second, own_grad, factor, RATE_TILE, DECAY, steps
    )
    tile_new = jnp.where(slot_valid, tile_new, 0.0)
    tile_first_new = jnp.where(slot_valid, tile_first_new, 0.0)
    tile_second_new = jnp.where(slot_valid, tile_second_new, 0.0)
    table_new, table_first_new, table_second_new = adam(
        table_weight, table_first, table_second, table_grad, factor, RATE_TABLE, DECAY, steps
    )
    head_new, head_first_new, head_second_new = adam(
        head_weight, head_first, head_second, head_grad, factor, RATE_HEAD, DECAY, steps
    )
    gain_new, gain_first_new, gain_second_new = adam(
        gain_weight, gain_first, gain_second, gain_grads, factor, RATE_GAIN, 0.0, steps
    )
    return (
        loss,
        norm,
        tile_new,
        tile_new.astype(jnp.bfloat16),
        tile_first_new,
        tile_second_new,
        table_new,
        table_new.astype(jnp.bfloat16),
        table_first_new,
        table_second_new,
        head_new,
        head_new.astype(jnp.bfloat16),
        head_first_new,
        head_second_new,
        gain_new,
        gain_first_new,
        gain_second_new,
    )


def solution(mesh):
    dp_size, rep_size = mesh.shape["dp"], mesh.shape["rep"]
    split = Mesh(mesh.devices.reshape(dp_size // rep_size, rep_size // 2, 2, rep_size), ALL)
    return jax.shard_map(
        shards,
        mesh=split,
        in_specs=(
            P(DP, "z"),
            P(DP, None),
            P(DP, None),
            P(DP, None),
            P(),
            P(),
            P(ALL, None, None),
            P(ALL, None, None),
            P(ALL, None, None),
            P(ALL, None),
            P(ALL, None),
            P(ALL, None),
            P(ALL, None),
            P(ALL, None),
            P(ALL, None),
            P(),
            P(),
            P(),
        ),
        out_specs=(
            P(),
            P(),
            P(ALL, None, None),
            P(ALL, None, None),
            P(ALL, None, None),
            P(ALL, None, None),
            P(ALL, None),
            P(ALL, None),
            P(ALL, None),
            P(ALL, None),
            P(ALL, None),
            P(ALL, None),
            P(ALL, None),
            P(ALL, None),
            P(),
            P(),
            P(),
        ),
        check_vma=False,
    )
```

```python
import functools

import jax
import jax.numpy as jnp
from jax import lax
from jax.experimental import pallas as pl
from jax.experimental.pallas import tpu as pltpu
from jax.sharding import Mesh, PartitionSpec as P

D = 768
HEADS = 12
HD = 64
FF = 3072
LAYERS = 2


EPS_NORM = 1e-05
EPS_ADAM = 1e-08
CLIP_NORM = 0.005
BETA_FIRST = 0.5
BETA_SECOND = 0.5
DECAY = 0.1
RATE_TILE = 0.02
RATE_HEAD = 0.05
RATE_TABLE = 0.5
RATE_GAIN = 0.3
MASKED = -1e30


def root_norm(training_state, gain):
    return (
        training_state
        * lax.rsqrt(jnp.mean(training_state * training_state, axis=-1, keepdims=True) + EPS_NORM)
        * gain
    )


def norm_back(training_state, gain, grad):
    scale = lax.rsqrt(jnp.mean(training_state * training_state, axis=-1, keepdims=True) + EPS_NORM)
    scaled = grad * gain
    state_grad = scale * scaled - training_state * scale**3 * jnp.mean(
        scaled * training_state, axis=-1, keepdims=True
    )
    gain_grad = jnp.sum(
        (grad * training_state * scale).reshape(-1, training_state.shape[-1]), axis=0
    )
    return (state_grad, gain_grad)


def rope_tables(places):
    freqs = jnp.power(10000.0, -2.0 * jnp.arange(HD // 2).astype(jnp.float32) / HD)
    angle = places[:, None] * freqs[None, :]
    cosine, sine = jnp.cos(angle), jnp.sin(angle)
    return jnp.concatenate([cosine] * 4, axis=1), jnp.concatenate([-sine, sine] * 2, axis=1)


def tile_slots(owners):
    order = jnp.arange(owners.shape[0], dtype=jnp.int32)
    same = (owners[:, None] == owners[None, :]) & (order[None, :] < order[:, None])
    return jnp.sum(same.astype(jnp.int32), axis=1)


def adam(weight, first, second, grad, factor, rate, decay, steps):
    grad = grad * factor
    first = BETA_FIRST * first + (1.0 - BETA_FIRST) * grad
    second = BETA_SECOND * second + (1.0 - BETA_SECOND) * grad * grad
    first_hat = first / (1.0 - jnp.power(BETA_FIRST, steps))
    second_hat = second / (1.0 - jnp.power(BETA_SECOND, steps))
    weight = weight - rate * (first_hat / (jnp.sqrt(second_hat) + EPS_ADAM) + decay * weight)
    return (weight, first, second)


ALL = ("y", "x", "c", "z")
DP = ("y", "x", "c")
PART = ("x", "c")
UNITS = FF // D
TILES_PER = 4 + 3 * UNITS


MESH = pl.DeviceIdType.MESH


def half_rows(rows, dtype):
    unit = 16 if jnp.dtype(dtype).itemsize == 2 else 8
    return (rows // 2 + unit - 1) // unit * unit


def remote(src, dst, ssem, rsem, **to):
    return pltpu.make_async_remote_copy(
        src_ref=src, dst_ref=dst, send_sem=ssem, recv_sem=rsem, device_id=to, device_id_type=MESH
    )


def greet(zn, y, x, c, z):
    barrier = pltpu.get_barrier_semaphore()
    for to in ({"x": 1 - x}, {"y": 1 - y}, {"c": 1 - c}):
        pl.semaphore_signal(barrier, inc=1, device_id=to, device_id_type=MESH)
    if zn > 1:

        @pl.when(z < zn - 1)
        def _():
            pl.semaphore_signal(barrier, inc=1, device_id={"z": z + 1}, device_id_type=MESH)

        @pl.when(z > 0)
        def _():
            pl.semaphore_signal(barrier, inc=1, device_id={"z": z - 1}, device_id_type=MESH)

        @pl.when((z > 0) & (z < zn - 1))
        def _():
            pl.semaphore_wait(barrier, 5)

        @pl.when((z == 0) | (z == zn - 1))
        def _():
            pl.semaphore_wait(barrier, 4)
    else:
        pl.semaphore_wait(barrier, 3)


def gather_steps(zn, x_ref, o_ref, hold, ssem, rsem, lsem):
    y, x, c, z = [lax.axis_index(n) for n in ALL]
    me = z if zn > 1 else 0
    rows = x_ref.shape[0]
    h0 = half_rows(rows, x_ref.dtype)
    lo, hi = pl.ds(0, h0), pl.ds(h0, rows - h0)
    X, Y, DX, DY, CO, CX, CY, C0, C1, ZU, ZD = range(11)
    nx, ny, nc = {"x": 1 - x}, {"y": 1 - y}, {"c": 1 - c}

    def slot(yy, xx, zz):
        return ((yy * 2 + xx) * 2 + c) * zn + zz

    def copy(kind, k, src, dst, to):
        return remote(src, dst, ssem.at[kind, k], rsem.at[kind, k], **to)

    def block(s):
        return o_ref.at[s]

    local = pltpu.make_async_copy(x_ref, hold, lsem.at[0])
    local.start()
    keep = pltpu.make_async_copy(hold, o_ref.at[slot(y, x, me)], lsem.at[1])

    def spread(zb, src):
        dst = block(slot(y, x, zb))
        copy(X, zb, src, dst, nx).start()
        copy(Y, zb, src, dst, ny).start()
        copy(CO, zb, src, dst, nc).start()

    def up(s):
        zb = z - (s - 1)
        b = block(slot(y, x, zb))
        return copy(ZU, s, x_ref if s == 1 else b, b, {"z": z + 1})

    def down(s):
        zb = z + (s - 1)
        b = block(slot(y, x, zb))
        return copy(ZD, s, x_ref if s == 1 else b, b, {"z": z - 1})

    for s in range(1, zn):

        @pl.when((z < zn - 1) & (z - (s - 1) >= 0))
        def _():
            up(s).start()

        @pl.when((z > 0) & (z + (s - 1) < zn))
        def _():
            down(s).start()

        if s == 1:
            spread(me, x_ref)
            local.wait()
            keep.start()
        yield

        @pl.when(z - s >= 0)
        def _():
            copy(ZU, s, x_ref, x_ref, nx).wait_recv()
            spread(z - s, block(slot(y, x, z - s)))

        @pl.when(z + s < zn)
        def _():
            copy(ZD, s, x_ref, x_ref, nx).wait_recv()
            spread(z + s, block(slot(y, x, z + s)))

    if zn == 1:
        spread(0, x_ref)
        local.wait()
        keep.start()
    order = [lax.rem(z + j, zn) if zn > 1 else 0 for j in range(zn)]
    for zb in order:
        yield
        sx, sy = slot(y, 1 - x, zb), slot(1 - y, x, zb)
        copy(X, zb, x_ref, x_ref, nx).wait_recv()
        copy(DX, zb, o_ref.at[sx, lo], o_ref.at[sx, lo], ny).start()
        copy(CX, zb, block(sx), block(sx), nc).start()
        copy(Y, zb, x_ref, x_ref, nx).wait_recv()
        copy(DY, zb, o_ref.at[sy, hi], o_ref.at[sy, hi], nx).start()
        copy(CY, zb, block(sy), block(sy), nc).start()
    for zb in order:
        yield
        sd = slot(1 - y, 1 - x, zb)
        copy(DX, zb, x_ref.at[lo], x_ref.at[lo], nx).wait_recv()
        copy(C0, zb, o_ref.at[sd, lo], o_ref.at[sd, lo], nc).start()
        copy(DY, zb, x_ref.at[hi], x_ref.at[hi], nx).wait_recv()
        copy(C1, zb, o_ref.at[sd, hi], o_ref.at[sd, hi], nc).start()
    yield
    for zb in range(zn):
        for kind, part in ((CO, x_ref), (CX, x_ref), (CY, x_ref), (C0, x_ref.at[lo]), (C1, x_ref.at[hi])):
            copy(kind, zb, part, part, nx).wait_recv()
        for kind, part in (
            (X, x_ref), (Y, x_ref), (CO, x_ref), (CX, x_ref), (CY, x_ref),
            (DX, x_ref.at[lo]), (DY, x_ref.at[hi]), (C0, x_ref.at[lo]), (C1, x_ref.at[hi]),
        ):
            copy(kind, zb, part, part, nx).wait_send()
    for s in range(1, zn):

        @pl.when((z < zn - 1) & (z - (s - 1) >= 0))
        def _():
            up(s).wait_send()

        @pl.when((z > 0) & (z + (s - 1) < zn))
        def _():
            down(s).wait_send()

    keep.wait()


def run_steps(*parts):
    parts = list(parts)
    while parts:
        for part in list(parts):
            if next(part, part) is part:
                parts.remove(part)


def gather_kernel(zn, *refs):
    greet(zn, *[lax.axis_index(n) for n in ALL])
    run_steps(gather_steps(zn, *refs))


def gather_scratch(zn, shape, dtype):
    sems = pltpu.SemaphoreType.DMA((11, zn))
    return [pltpu.VMEM(shape, dtype), sems, sems, pltpu.SemaphoreType.DMA((2,))]


def all_gather(x, zn, ident, name):
    return pl.pallas_call(
        functools.partial(gather_kernel, zn),
        out_shape=jax.ShapeDtypeStruct((8 * zn,) + x.shape, x.dtype),
        in_specs=[pl.BlockSpec(memory_space=pl.ANY)],
        out_specs=pl.BlockSpec(memory_space=pl.ANY),
        scratch_shapes=gather_scratch(zn, x.shape, x.dtype),
        compiler_params=pltpu.CompilerParams(collective_id=ident, has_side_effects=True),
        name=name,
    )(x)


def reduce_steps(zn, p_ref, o_ref, acc, crecv, dxr, dyr, xr, yr, zur, zdr, ssem, rsem, lsem):
    y, x, c, z = [lax.axis_index(n) for n in ALL]
    me = z if zn > 1 else 0
    rows, cols = p_ref.shape[1:]
    h0 = half_rows(rows, p_ref.dtype)
    h1 = rows - h0
    X, Y, DX, DY, C0, ZU, ZD = 0, 1, 2, 3, 4, 8, 9
    nx, ny, nc = {"x": 1 - x}, {"y": 1 - y}, {"c": 1 - c}
    kinds = [(y, x), (y, 1 - x), (1 - y, x), (1 - y, 1 - x)]
    step = 32 if rows % 32 == 0 else 16

    def slot(k, cc, zz):
        yy, xx = kinds[k]
        return ((yy * 2 + xx) * 2 + cc) * zn + zz

    def copy(kind, k, src, dst, to):
        return remote(src, dst, ssem.at[kind, k], rsem.at[kind, k], **to)

    def load(k, zb):
        return pltpu.make_async_copy(p_ref.at[slot(k, c, zb)], acc.at[k * zn + zb], lsem.at[k * zn + zb])

    def across(k, zb):
        return copy(C0 + k, zb, p_ref.at[slot(k, 1 - c, zb)], crecv.at[k * zn + zb], nc)

    def add(dst, start, count, terms):
        size = step if count % step == 0 else 16

        @pl.loop(0, count // size)
        def _(i):
            at = pl.ds(pl.multiple_of(start + i * size, 16), size)
            total = None
            for ref, base in terms:
                part = ref[pl.ds(pl.multiple_of(start - base + i * size, 16), size), :].astype(jnp.float32)
                total = part if total is None else total + part
            dst[at, :] = total.astype(dst.dtype)

    zorder = [lax.rem(z + j, zn) if zn > 1 else 0 for j in range(zn)]
    for k in (3, 1, 2, 0):
        for zb in range(zn):
            across(k, zb).start()
            load(k, zb).start()

    def ready(k, zb):
        load(k, zb).wait()
        across(k, zb).wait_recv()

    for zb in range(zn):
        yield
        ready(3, zb)
        b = 3 * zn + zb
        add(acc.at[b], 0, rows, [(acc.at[b], 0), (crecv.at[b], 0)])
        copy(DX, zb, acc.at[b, pl.ds(0, h0)], dxr.at[zb], nx).start()
        copy(DY, zb, acc.at[b, pl.ds(h0, h1)], dyr.at[zb], ny).start()
    for zb in range(zn):
        yield
        ready(1, zb)
        b = zn + zb
        add(acc.at[b], 0, h0, [(acc.at[b], 0), (crecv.at[b], 0)])
        copy(DY, zb, dyr.at[zb], dyr.at[zb], ny).wait_recv()
        add(acc.at[b], h0, h1, [(acc.at[b], 0), (crecv.at[b], 0), (dyr.at[zb], h0)])
        copy(X, zb, acc.at[b], xr.at[zb], nx).start()
        yield
        ready(2, zb)
        b = 2 * zn + zb
        add(acc.at[b], h0, h1, [(acc.at[b], 0), (crecv.at[b], 0)])
        copy(DX, zb, dxr.at[zb], dxr.at[zb], nx).wait_recv()
        add(acc.at[b], 0, h0, [(acc.at[b], 0), (crecv.at[b], 0), (dxr.at[zb], 0)])
        copy(Y, zb, acc.at[b], yr.at[zb], ny).start()

    def column(zb):
        return [(acc.at[zb], 0), (crecv.at[zb], 0), (xr.at[zb], 0), (yr.at[zb], 0)]

    for zb in range(zn):
        yield
        ready(0, zb)
        copy(X, zb, acc.at[zb], xr.at[zb], nx).wait_recv()
        copy(Y, zb, acc.at[zb], yr.at[zb], ny).wait_recv()
        if zn == 1:
            add(o_ref, 0, rows, column(0))
            continue

        def upward(zb=zb):
            return copy(ZU, zb, acc.at[zb], zur.at[zb], {"z": z + 1})

        def downward(zb=zb):
            return copy(ZD, zb, acc.at[zb], zdr.at[zb], {"z": z - 1})

        @pl.when(z == zb)
        def _():
            add(acc.at[zb], 0, rows, column(zb))

        @pl.when((z < zb) & (z == 0))
        def _():
            add(acc.at[zb], 0, rows, column(zb))
            upward().start()

        @pl.when((z < zb) & (z > 0))
        def _():
            upward().wait_recv()
            add(acc.at[zb], 0, rows, column(zb) + [(zur.at[zb], 0)])
            upward().start()

        @pl.when((z > zb) & (z == zn - 1))
        def _():
            add(acc.at[zb], 0, rows, column(zb))
            downward().start()

        @pl.when((z > zb) & (z < zn - 1))
        def _():
            downward().wait_recv()
            add(acc.at[zb], 0, rows, column(zb) + [(zdr.at[zb], 0)])
            downward().start()

    yield
    if zn > 1:

        @pl.when(z == 0)
        def _():
            copy(ZD, me, acc.at[me], zdr.at[me], {"z": z + 1}).wait_recv()
            add(o_ref, 0, rows, [(acc.at[me], 0), (zdr.at[me], 0)])

        @pl.when(z == zn - 1)
        def _():
            copy(ZU, me, acc.at[me], zur.at[me], {"z": z - 1}).wait_recv()
            add(o_ref, 0, rows, [(acc.at[me], 0), (zur.at[me], 0)])

        @pl.when((z > 0) & (z < zn - 1))
        def _():
            copy(ZD, me, acc.at[me], zdr.at[me], {"z": z + 1}).wait_recv()
            copy(ZU, me, acc.at[me], zur.at[me], {"z": z + 1}).wait_recv()
            add(o_ref, 0, rows, [(acc.at[me], 0), (zdr.at[me], 0), (zur.at[me], 0)])

    for zb in range(zn):
        for k in range(4):
            across(k, zb).wait_send()
        copy(DX, zb, dxr.at[zb], dxr.at[zb], nx).wait_send()
        copy(DY, zb, dyr.at[zb], dyr.at[zb], ny).wait_send()
        copy(X, zb, xr.at[zb], xr.at[zb], nx).wait_send()
        copy(Y, zb, yr.at[zb], yr.at[zb], ny).wait_send()
        if zn > 1:

            @pl.when(z < zb)
            def _():
                copy(ZU, zb, zur.at[zb], zur.at[zb], {"z": z + 1}).wait_send()

            @pl.when(z > zb)
            def _():
                copy(ZD, zb, zdr.at[zb], zdr.at[zb], {"z": z - 1}).wait_send()


def reduce_kernel(zn, *refs):
    greet(zn, *[lax.axis_index(n) for n in ALL])
    run_steps(reduce_steps(zn, *refs))


def reduce_scratch(zn, rows, cols, dtype):
    h0 = half_rows(rows, dtype)
    sems = pltpu.SemaphoreType.DMA((10, zn))
    counts = [(4 * zn, rows), (4 * zn, rows), (zn, h0), (zn, rows - h0)] + [(zn, rows)] * 4
    blocks = [pltpu.VMEM((n, r, cols), dtype) for n, r in counts]
    return blocks + [sems, sems, pltpu.SemaphoreType.DMA((4 * zn,))]


def reduce_scatter(p, zn, ident, name, out_dtype=None):
    count, rows, cols = p.shape
    return pl.pallas_call(
        functools.partial(reduce_kernel, zn),
        out_shape=jax.ShapeDtypeStruct((rows, cols), out_dtype or p.dtype),
        in_specs=[pl.BlockSpec(memory_space=pl.ANY)],
        out_specs=pl.BlockSpec(memory_space=pltpu.VMEM),
        scratch_shapes=reduce_scratch(zn, rows, cols, p.dtype),
        compiler_params=pltpu.CompilerParams(
            collective_id=ident, has_side_effects=True, vmem_limit_bytes=56 << 20
        ),
        name=name,
    )(p)


def both_kernel(zr, zg, p_ref, x_ref, r_ref, o_ref, *scratch):
    greet(max(zr, zg), *[lax.axis_index(n) for n in ALL])
    count = len(reduce_scratch(1, 32, 128, jnp.float32))
    run_steps(
        reduce_steps(zr, p_ref, r_ref, *scratch[:count]),
        gather_steps(zg, x_ref, o_ref, *scratch[count:]),
    )


def scatter_and_gather(p, zr, x, zg, ident, name):
    count, rows, cols = p.shape
    return pl.pallas_call(
        functools.partial(both_kernel, zr, zg),
        out_shape=(
            jax.ShapeDtypeStruct((rows, cols), p.dtype),
            jax.ShapeDtypeStruct((8 * zg,) + x.shape, x.dtype),
        ),
        in_specs=[pl.BlockSpec(memory_space=pl.ANY)] * 2,
        out_specs=(pl.BlockSpec(memory_space=pltpu.VMEM), pl.BlockSpec(memory_space=pl.ANY)),
        scratch_shapes=reduce_scratch(zr, rows, cols, p.dtype) + gather_scratch(zg, x.shape, x.dtype),
        compiler_params=pltpu.CompilerParams(
            collective_id=ident, has_side_effects=True, vmem_limit_bytes=56 << 20
        ),
        name=name,
    )(p, x)


def greet_pair(x, c):
    barrier = pltpu.get_barrier_semaphore()
    for to in ({"x": 1 - x}, {"c": 1 - c}):
        pl.semaphore_signal(barrier, inc=1, device_id=to, device_id_type=MESH)
    pl.semaphore_wait(barrier, 2)


def keys_gather_kernel(x_ref, o_ref, hold, ssem, rsem, lsem):
    x, c = lax.axis_index("x"), lax.axis_index("c")
    me, far = x * 2 + c, (1 - x) * 2 + c
    nx, nc = {"x": 1 - x}, {"c": 1 - c}
    load = pltpu.make_async_copy(x_ref, hold, lsem.at[0])
    load.start()
    greet_pair(x, c)
    out = remote(x_ref, o_ref.at[me], ssem.at[0], rsem.at[0], **nx)
    out.start()
    near = remote(x_ref, o_ref.at[me], ssem.at[1], rsem.at[1], **nc)
    near.start()
    load.wait()
    keep = pltpu.make_async_copy(hold, o_ref.at[me], lsem.at[1])
    keep.start()
    out.wait_recv()
    on = remote(o_ref.at[far], o_ref.at[far], ssem.at[2], rsem.at[2], **nc)
    on.start()
    near.wait_recv()
    on.wait_recv()
    keep.wait()
    out.wait_send()
    near.wait_send()
    on.wait_send()


def keys_gather(v, ident):
    sems = pltpu.SemaphoreType.DMA((3,))
    return pl.pallas_call(
        keys_gather_kernel,
        out_shape=jax.ShapeDtypeStruct((4,) + v.shape, v.dtype),
        in_specs=[pl.BlockSpec(memory_space=pl.ANY)],
        out_specs=pl.BlockSpec(memory_space=pl.ANY),
        scratch_shapes=[pltpu.VMEM(v.shape, v.dtype), sems, sems, pltpu.SemaphoreType.DMA((2,))],
        compiler_params=pltpu.CompilerParams(collective_id=ident, has_side_effects=True),
        name="keys_gather",
    )(v)


def keys_reduce_kernel(p_ref, o_ref, acc, crecv, xr, ssem, rsem, lsem):
    x, c = lax.axis_index("x"), lax.axis_index("c")
    nx, nc = {"x": 1 - x}, {"c": 1 - c}
    rows = p_ref.shape[1]
    places = [(1 - x) * 2, x * 2]
    loads = [pltpu.make_async_copy(p_ref.at[places[i] + c], acc.at[i], lsem.at[i]) for i in range(2)]
    for load in loads:
        load.start()
    greet_pair(x, c)
    across = [
        remote(p_ref.at[places[i] + 1 - c], crecv.at[i], ssem.at[i], rsem.at[i], **nc) for i in range(2)
    ]
    for copy in across:
        copy.start()

    def add(dst, terms):
        @pl.loop(0, rows // 16)
        def _(i):
            at = pl.ds(pl.multiple_of(i * 16, 16), 16)
            total = terms[0][at, :].astype(jnp.float32)
            for term in terms[1:]:
                total = total + term[at, :].astype(jnp.float32)
            dst[at, :] = total.astype(dst.dtype)

    loads[0].wait()
    across[0].wait_recv()
    add(acc.at[0], [acc.at[0], crecv.at[0]])
    out = remote(acc.at[0], xr, ssem.at[2], rsem.at[2], **nx)
    out.start()
    loads[1].wait()
    across[1].wait_recv()
    out.wait_recv()
    add(o_ref, [acc.at[1], crecv.at[1], xr])
    for copy in across + [out]:
        copy.wait_send()


def keys_reduce(p, ident):
    block = p.shape[1:]
    sems = pltpu.SemaphoreType.DMA((3,))
    return pl.pallas_call(
        keys_reduce_kernel,
        out_shape=jax.ShapeDtypeStruct(block, p.dtype),
        in_specs=[pl.BlockSpec(memory_space=pl.ANY)],
        out_specs=pl.BlockSpec(memory_space=pltpu.VMEM),
        scratch_shapes=[
            pltpu.VMEM((2,) + block, p.dtype), pltpu.VMEM((2,) + block, p.dtype),
            pltpu.VMEM(block, p.dtype), sems, sems, pltpu.SemaphoreType.DMA((2,)),
        ],
        compiler_params=pltpu.CompilerParams(
            collective_id=ident, has_side_effects=True, vmem_limit_bytes=32 << 20
        ),
        name="keys_reduce",
    )(p)


def fits():
    return [lax.axis_size(n) for n in ALL] == [2, 2, 2, 4]


def gather_all(v, ident, name):
    if fits():
        return all_gather(v, 4, ident, name)
    return lax.all_gather(v, ALL, axis=0)


def gather_plane(v, ident, name):
    if fits():
        return all_gather(v, 1, ident, name)
    return lax.all_gather(v, DP, axis=0)


def scatter_all(p, ident, name):
    if fits():
        return reduce_scatter(p, 4, ident, name)
    return lax.psum_scatter(p, ALL, scatter_dimension=0)


def scatter_plane(p, ident, name):
    if fits():
        return reduce_scatter(p, 1, ident, name)
    return lax.psum_scatter(p, DP, scatter_dimension=0)


def keys_all_gather(v):
    if fits():
        return keys_gather(v, 11).reshape(-1, v.shape[1])
    return lax.all_gather(v, PART, axis=0, tiled=True)


def keys_sum_scatter(p):
    if fits():
        return keys_reduce(p.reshape(4, -1, p.shape[1]), 12)
    return lax.psum_scatter(p, PART, scatter_dimension=0, tiled=True)


def tile_spec(dp, deep, tile_rows, index, local=None):
    def place(t):
        j = index(t)
        return (j % dp, 0, j // dp if local is None else local, 0, 0)

    return pl.BlockSpec((None, deep, None, tile_rows, D), place)


def weight_specs(weights, *groups):
    arrays, specs = [], []
    for first, offset in groups:
        array, local = weights[first // weights[0][0].shape[0]]
        dp, deep, _, tile_rows, _ = array.shape
        arrays.append(array)
        specs.append(
            tile_spec(dp, deep, tile_rows, lambda t, f=first, o=offset: f + o(t), local)
        )
    return arrays, specs


def whole(shape):
    return pl.BlockSpec(shape, lambda t: (0,) * len(shape))


def dot_nn(a, b):
    return lax.dot_general(a, b, (((1,), (0,)), ((), ())), preferred_element_type=jnp.float32)


def dot_nt(a, b):
    return lax.dot_general(a, b, (((1,), (1,)), ((), ())), preferred_element_type=jnp.float32)


def dot_tn(a, b):
    return lax.dot_general(a, b, (((0,), (0,)), ((), ())), preferred_element_type=jnp.float32)


def turned(u, cos, sin):
    lane = lax.broadcasted_iota(jnp.int32, (u.shape[0], 128), 1)
    low = (lane % HD) < HD // 2
    parts = []
    for i in range(D // 128):
        v = u[:, i * 128 : (i + 1) * 128]
        other = jnp.where(low, pltpu.roll(v, 128 - HD // 2, 1), pltpu.roll(v, HD // 2, 1))
        parts.append(v * cos + other * sin)
    return jnp.concatenate(parts, axis=1)


def project_kernel(x_ref, g_ref, cos_ref, sin_ref, w_ref, q_ref, kv_ref, a_ref):
    t = pl.program_id(0)

    @pl.when(t == 0)
    def _():
        a_ref[...] = root_norm(x_ref[...], g_ref[...]).astype(jnp.bfloat16)

    m = dot_nn(a_ref[...], w_ref[...].reshape(D, D))

    @pl.when(t == 0)
    def _():
        q_ref[...] = turned(m, cos_ref[...], sin_ref[...]).astype(jnp.bfloat16)

    @pl.when(t == 1)
    def _():
        kv_ref[...] = turned(m, cos_ref[...], sin_ref[...]).astype(jnp.bfloat16)

    @pl.when(t == 2)
    def _():
        kv_ref[...] = m.astype(jnp.bfloat16)


def project(x, gain, cos, sin, weights):
    rows = x.shape[0]
    arrays, specs = weight_specs(weights, (0, lambda t: t))
    return pl.pallas_call(
        project_kernel,
        grid=(3,),
        out_shape=(
            jax.ShapeDtypeStruct((rows, D), jnp.bfloat16),
            jax.ShapeDtypeStruct((2, rows, D), jnp.bfloat16),
        ),
        in_specs=[
            whole((rows, D)), whole((1, D)), whole((rows, 128)), whole((rows, 128)), *specs,
        ],
        out_specs=(
            whole((rows, D)),
            pl.BlockSpec((None, rows, D), lambda t: (jnp.maximum(t - 1, 0), 0, 0)),
        ),
        scratch_shapes=[pltpu.VMEM((rows, D), jnp.bfloat16)],
        compiler_params=pltpu.CompilerParams(vmem_limit_bytes=40 << 20),
        name="project",
    )(x, gain, cos, sin, *arrays)


def mask_bias(bias_ref, kseg_ref, qseg_ref, qpos_ref):
    kpos = lax.broadcasted_iota(jnp.int32, bias_ref.shape, 0)
    allowed = (kpos <= qpos_ref[...]) & (kseg_ref[...] == qseg_ref[...])
    bias_ref[...] = jnp.where(allowed, 0.0, MASKED)


def head_lanes(shape, head):
    return (lax.broadcasted_iota(jnp.int32, shape, 1) // HD) == head


def attend_kernel(q_ref, k_ref, v_ref, kseg_ref, qseg_ref, qpos_ref, o_ref, lse_ref, bias_ref):
    @pl.when(pl.program_id(0) == 0)
    def _():
        mask_bias(bias_ref, kseg_ref, qseg_ref, qpos_ref)

    length = bias_ref.shape[0]
    q = q_ref[...]
    k, v = k_ref[...].reshape(length, 128), v_ref[...].reshape(length, 128)
    outs = []
    for head in range(2):
        mine = head_lanes(q.shape, head)
        s = dot_nt(k, jnp.where(mine, q, jnp.zeros_like(q))) * HD ** (-0.5) + bias_ref[...]
        top = jnp.max(s, axis=0, keepdims=True)
        e = jnp.exp(s - top)
        total = jnp.sum(e, axis=0, keepdims=True)
        p = (e * (1.0 / total)).astype(jnp.bfloat16)
        outs.append(dot_tn(p, v))
        lse_ref[head : head + 1, :] = top + jnp.log(total)
    o_ref[...] = jnp.where(head_lanes(outs[0].shape, 0), outs[0], outs[1]).astype(jnp.bfloat16)


def attend_specs(rows, parts):
    length = parts * rows
    pair = pl.BlockSpec((rows, 128), lambda t: (0, t))
    return pair, [
        pair,
        pl.BlockSpec((parts, None, rows, 128), lambda t: (0, 0, 0, t)),
        pl.BlockSpec((parts, None, rows, 128), lambda t: (0, 1, 0, t)),
        whole((length, 1)), whole((1, rows)), whole((1, rows)),
    ]


def attend(q, kv, kseg, qseg, qpos):
    rows, parts = q.shape[0], kv.shape[0]
    pair, specs = attend_specs(rows, parts)
    return pl.pallas_call(
        attend_kernel,
        grid=(HEADS // 2,),
        out_shape=(
            jax.ShapeDtypeStruct((rows, D), jnp.bfloat16),
            jax.ShapeDtypeStruct((HEADS // 2, 8, rows), jnp.float32),
        ),
        in_specs=specs,
        out_specs=(pair, pl.BlockSpec((None, 8, rows), lambda t: (t, 0, 0))),
        scratch_shapes=[pltpu.VMEM((parts * rows, rows), jnp.float32)],
        compiler_params=pltpu.CompilerParams(vmem_limit_bytes=40 << 20),
        name="attend",
    )(q, kv, kv, kseg, qseg, qpos)


def feed_kernel(x_ref, o_ref, g_ref, wo_ref, wg_ref, wu_ref, wd_ref, mid_ref, out_ref, b_ref):
    t = pl.program_id(0)

    @pl.when(t == 0)
    def _():
        mid = x_ref[...] + dot_nn(o_ref[...], wo_ref[...].reshape(D, D))
        mid_ref[...] = mid
        out_ref[...] = mid
        b_ref[...] = root_norm(mid, g_ref[...]).astype(jnp.bfloat16)

    @pl.when(t > 0)
    def _():
        gate = dot_nn(b_ref[...], wg_ref[...].reshape(D, D))
        up = dot_nn(b_ref[...], wu_ref[...].reshape(D, D))
        h = (gate * jax.nn.sigmoid(gate) * up).astype(jnp.bfloat16)
        out_ref[...] += dot_nn(h, wd_ref[...].reshape(D, D))


def feed(x, o, gain, weights):
    rows = x.shape[0]
    unit = lambda t: jnp.maximum(t - 1, 0)
    arrays, specs = weight_specs(
        weights, (3, lambda t: 0 * t), (4, unit), (4 + UNITS, unit), (4 + 2 * UNITS, unit)
    )
    state = jax.ShapeDtypeStruct((rows, D), jnp.float32)
    return pl.pallas_call(
        feed_kernel,
        grid=(1 + UNITS,),
        out_shape=(state, state),
        in_specs=[
            whole((rows, D)), whole((rows, D)), whole((1, D)), *specs,
        ],
        out_specs=(whole((rows, D)), whole((rows, D))),
        scratch_shapes=[pltpu.VMEM((rows, D), jnp.bfloat16)],
        compiler_params=pltpu.CompilerParams(vmem_limit_bytes=48 << 20),
        name="feed",
    )(x, o, gain, *arrays)


def feed_back_kernel(
    dy_ref, mid_ref, g_ref, o_ref, wo_ref, wg_ref, wu_ref, wd_ref,
    grad_ref, dx_ref, do_ref, dgain_ref,
    b_ref, e_ref, dg_ref, du_ref, db_ref,
):
    t = pl.program_id(0)
    last = pl.num_programs(0) - 1
    deep, tile_rows = grad_ref.shape[0], grad_ref.shape[1]

    def emit(g):
        grad_ref[...] = g.astype(jnp.bfloat16).reshape(deep, tile_rows, D)

    @pl.when(t == 0)
    def _():
        b_ref[...] = root_norm(mid_ref[...], g_ref[...]).astype(jnp.bfloat16)
        e_ref[...] = dy_ref[...].astype(jnp.bfloat16)
        db_ref[...] = jnp.zeros_like(db_ref)

    @pl.when((t % 3 == 0) & (t < last))
    def _():
        gate = dot_nn(b_ref[...], wg_ref[...].reshape(D, D))
        up = dot_nn(b_ref[...], wu_ref[...].reshape(D, D))
        sigma = jax.nn.sigmoid(gate)
        h = (gate * sigma * up).astype(jnp.bfloat16)
        emit(dot_tn(h, e_ref[...]))
        dh = dot_nt(e_ref[...], wd_ref[...].reshape(D, D))
        dg_ref[...] = (dh * up * sigma * (1.0 + gate * (1.0 - sigma))).astype(jnp.bfloat16)
        du_ref[...] = (dh * gate * sigma).astype(jnp.bfloat16)

    @pl.when(t % 3 == 1)
    def _():
        emit(dot_tn(b_ref[...], dg_ref[...]))
        db_ref[...] += dot_nt(dg_ref[...], wg_ref[...].reshape(D, D))

    @pl.when(t % 3 == 2)
    def _():
        emit(dot_tn(b_ref[...], du_ref[...]))
        db_ref[...] += dot_nt(du_ref[...], wu_ref[...].reshape(D, D))

    @pl.when(t == last)
    def _():
        back, gain_back = norm_back(mid_ref[...], g_ref[...], db_ref[...])
        dx = dy_ref[...] + back
        dx_ref[...] = dx
        dgain_ref[...] = jnp.broadcast_to(gain_back[None, :], dgain_ref.shape)
        e1 = dx.astype(jnp.bfloat16)
        emit(dot_tn(o_ref[...], e1))
        do_ref[...] = dot_nt(e1, wo_ref[...].reshape(D, D)).astype(jnp.bfloat16)


def feed_back(dy, mid, gain, o, weights):
    rows = dy.shape[0]
    dp, deep, _, tile_rows, _ = weights[0][0].shape
    unit = lambda t: jnp.minimum(t // 3, UNITS - 1)
    arrays, specs = weight_specs(
        weights, (3, lambda t: 0 * t), (4, unit), (4 + UNITS, unit), (4 + 2 * UNITS, unit)
    )

    def grad_tile(t):
        kind = t % 3
        base = jnp.where(kind == 0, 4 + 2 * UNITS, jnp.where(kind == 1, 4, 4 + UNITS))
        return jnp.where(t == 3 * UNITS, 3, base + unit(t))

    return pl.pallas_call(
        feed_back_kernel,
        grid=(3 * UNITS + 1,),
        out_shape=(
            jax.ShapeDtypeStruct((dp, deep, len(weights), tile_rows, D), jnp.bfloat16),
            jax.ShapeDtypeStruct((rows, D), jnp.float32),
            jax.ShapeDtypeStruct((rows, D), jnp.bfloat16),
            jax.ShapeDtypeStruct((8, D), jnp.float32),
        ),
        in_specs=[
            whole((rows, D)), whole((rows, D)), whole((1, D)), whole((rows, D)), *specs,
        ],
        out_specs=(
            tile_spec(dp, deep, tile_rows, grad_tile),
            whole((rows, D)), whole((rows, D)), whole((8, D)),
        ),
        scratch_shapes=[
            pltpu.VMEM((rows, D), jnp.bfloat16), pltpu.VMEM((rows, D), jnp.bfloat16),
            pltpu.VMEM((rows, D), jnp.bfloat16), pltpu.VMEM((rows, D), jnp.bfloat16),
            pltpu.VMEM((rows, D), jnp.float32),
        ],
        compiler_params=pltpu.CompilerParams(vmem_limit_bytes=48 << 20),
        name="feed_back",
    )(dy, mid, gain, o, *arrays)


def attend_back_kernel(
    q_ref, k_ref, v_ref, kseg_ref, qseg_ref, qpos_ref, do_ref, lse_ref, dq_ref, dkv_ref, bias_ref
):
    @pl.when(pl.program_id(0) == 0)
    def _():
        mask_bias(bias_ref, kseg_ref, qseg_ref, qpos_ref)

    length = bias_ref.shape[0]
    parts, rows = dkv_ref.shape[0], q_ref.shape[0]
    q, do = q_ref[...], do_ref[...]
    k, v = k_ref[...].reshape(length, 128), v_ref[...].reshape(length, 128)
    dqs, dk, dv = [], None, None
    for head in range(2):
        mine = head_lanes(q.shape, head)
        qm = jnp.where(mine, q, jnp.zeros_like(q))
        dom = jnp.where(mine, do, jnp.zeros_like(do))
        s = dot_nt(k, qm) * HD ** (-0.5) + bias_ref[...]
        p = jnp.exp(s - lse_ref[head : head + 1, :])
        dp = dot_nt(v, dom)
        delta = jnp.sum(p * dp, axis=0, keepdims=True)
        ds = (p * (dp - delta) * HD ** (-0.5)).astype(jnp.bfloat16)
        dv_part = dot_nn(p.astype(jnp.bfloat16), dom)
        dk_part = dot_nn(ds, qm)
        dv = dv_part if dv is None else dv + dv_part
        dk = dk_part if dk is None else dk + dk_part
        dqs.append(dot_tn(ds, k))
    dq_ref[...] = jnp.where(head_lanes(dqs[0].shape, 0), dqs[0], dqs[1])
    dkv_ref[:, 0] = dk.astype(jnp.bfloat16).reshape(parts, rows, 128)
    dkv_ref[:, 1] = dv.astype(jnp.bfloat16).reshape(parts, rows, 128)


def attend_back(q, kv, kseg, qseg, qpos, do, lse):
    rows, parts = q.shape[0], kv.shape[0]
    pair, specs = attend_specs(rows, parts)
    return pl.pallas_call(
        attend_back_kernel,
        grid=(HEADS // 2,),
        out_shape=(
            jax.ShapeDtypeStruct((rows, D), jnp.float32),
            jax.ShapeDtypeStruct((parts, 2, rows, D), jnp.bfloat16),
        ),
        in_specs=specs + [pair, pl.BlockSpec((None, 8, rows), lambda t: (t, 0, 0))],
        out_specs=(pair, pl.BlockSpec((parts, 2, rows, 128), lambda t: (0, 0, 0, t))),
        scratch_shapes=[pltpu.VMEM((parts * rows, rows), jnp.float32)],
        compiler_params=pltpu.CompilerParams(vmem_limit_bytes=48 << 20),
        name="attend_back",
    )(q, kv, kv, kseg, qseg, qpos, do, lse)


def project_back_kernel(
    dx_ref, x_ref, g_ref, cos_ref, sin_ref, dq_ref, dkv_ref, w_ref, held_ref,
    grad_ref, out_ref, dgain_ref, a_ref, dm_ref, da_ref,
):
    t = pl.program_id(0)
    deep, tile_rows = grad_ref.shape[0], grad_ref.shape[1]

    @pl.when(t == 0)
    def _():
        a_ref[...] = root_norm(x_ref[...], g_ref[...]).astype(jnp.bfloat16)
        da_ref[...] = jnp.zeros_like(da_ref)
        dm_ref[...] = turned(dq_ref[...], cos_ref[...], -sin_ref[...]).astype(jnp.bfloat16)

    @pl.when(t == 1)
    def _():
        dk = dkv_ref[0].astype(jnp.float32)
        dm_ref[...] = turned(dk, cos_ref[...], -sin_ref[...]).astype(jnp.bfloat16)

    @pl.when(t == 2)
    def _():
        dm_ref[...] = dkv_ref[1]

    grad = dot_tn(a_ref[...], dm_ref[...])
    grad_ref[...] = grad.astype(jnp.bfloat16).reshape(deep, tile_rows, D)
    da_ref[...] += dot_nt(dm_ref[...], w_ref[...].reshape(D, D))

    @pl.when(t == 2)
    def _():
        back, gain_back = norm_back(x_ref[...], g_ref[...], da_ref[...])
        out_ref[...] = dx_ref[...] + back
        dgain_ref[...] = jnp.broadcast_to(gain_back[None, :], dgain_ref.shape)


def project_back(dx, x, gain, cos, sin, dq, dkv, weights, grads):
    rows = x.shape[0]
    dp, deep, _, tile_rows, _ = weights[0][0].shape
    arrays, specs = weight_specs(weights, (0, lambda t: t))
    return pl.pallas_call(
        project_back_kernel,
        grid=(3,),
        out_shape=(
            jax.ShapeDtypeStruct(grads.shape, grads.dtype),
            jax.ShapeDtypeStruct((rows, D), jnp.float32),
            jax.ShapeDtypeStruct((8, D), jnp.float32),
        ),
        in_specs=[
            whole((rows, D)), whole((rows, D)), whole((1, D)), whole((rows, 128)),
            whole((rows, 128)), whole((rows, D)), whole((2, rows, D)),
            *specs,
            pl.BlockSpec(memory_space=pl.ANY),
        ],
        out_specs=(
            tile_spec(dp, deep, tile_rows, lambda t: t), whole((rows, D)), whole((8, D)),
        ),
        scratch_shapes=[
            pltpu.VMEM((rows, D), jnp.bfloat16), pltpu.VMEM((rows, D), jnp.bfloat16),
            pltpu.VMEM((rows, D), jnp.float32),
        ],
        input_output_aliases={8: 0},
        compiler_params=pltpu.CompilerParams(vmem_limit_bytes=40 << 20),
        name="project_back",
    )(dx, x, gain, cos, sin, dq, dkv, *arrays, grads)


def layer_forward(state, weights, layer, gains, cos, sin, marks):
    rows = state.shape[0]
    q, kv = project(state, gains[2 * layer : 2 * layer + 1], cos, sin, weights)
    kv = keys_all_gather(kv.reshape(2 * rows, D)).reshape(-1, 2, rows, D)
    o, lse = attend(q, kv, *marks)
    mid, out = feed(state, o, gains[2 * layer + 1 : 2 * layer + 2], weights)
    return out, (state, mid, q, kv, lse, o)


def layer_backward(grad, kept, weights, layer, gains, cos, sin, marks):
    state, mid, q, kv, lse, o = kept
    rows = state.shape[0]
    grads, dx, do, feed_gain = feed_back(
        grad, mid, gains[2 * layer + 1 : 2 * layer + 2], o, weights
    )
    dq, dkv = attend_back(q, kv, *marks, do, lse)
    dkv = keys_sum_scatter(dkv.reshape(-1, D)).reshape(2, rows, D)
    grads, dx, input_gain = project_back(
        dx, state, gains[2 * layer : 2 * layer + 1], cos, sin, dq, dkv, weights, grads
    )
    return dx, grads, [input_gain[0], feed_gain[0]]


def padded(v):
    count = -(-v.shape[0] // 2048) * 2048
    return jnp.pad(v, (0, count - v.shape[0])).reshape(-1, 128)


def place_kernel(slot_ref, mine_ref, w_ref, o_ref):
    g = pl.program_id(0)
    count = o_ref.shape[0]
    for i in range(count):
        t = g * count + i
        o_ref[i] = jnp.where(mine_ref[t] > 0, w_ref[slot_ref[t]], 0.0).astype(jnp.bfloat16)


def place_tiles(tile_weight, slots, mine, dp_size):
    count = slots.shape[0] // dp_size
    cap, rows, cols = tile_weight.shape
    return pl.pallas_call(
        place_kernel,
        grid_spec=pltpu.PrefetchScalarGridSpec(
            num_scalar_prefetch=2,
            grid=(dp_size,),
            in_specs=[pl.BlockSpec((cap, rows, cols), lambda g, *_: (0, 0, 0))],
            out_specs=pl.BlockSpec((count, rows, cols), lambda g, *_: (g, 0, 0)),
        ),
        out_shape=jax.ShapeDtypeStruct((dp_size * count, rows, cols), jnp.bfloat16),
        compiler_params=pltpu.CompilerParams(vmem_limit_bytes=24 << 20),
        name="place_tiles",
    )(slots, mine, tile_weight)


def shards(
    tokens,
    segments,
    completion,
    targets,
    owners,
    step_count,
    tile_weight,
    tile_first,
    tile_second,
    table_weight,
    table_first,
    table_second,
    head_weight,
    head_first,
    head_second,
    gain_weight,
    gain_first,
    gain_second,
):
    a_size, b_size, rep_size = lax.axis_size("y"), lax.axis_size(PART), lax.axis_size("z")
    a_index, b_index, rep_index = lax.axis_index("y"), lax.axis_index(PART), lax.axis_index("z")
    dp_size = a_size * b_size
    devices = dp_size * rep_size
    dp_index = a_index * b_size + b_index
    device = dp_index * rep_size + rep_index
    rows = tokens.shape[1]
    length = segments.shape[1]
    comp = completion.shape[1]
    slots_cap, tile_rows = tile_weight.shape[:2]
    tile_count = owners.shape[0]
    home_tiles = tile_count // dp_size
    vocab_rows = table_weight.shape[0]
    vocab_start = device * vocab_rows
    sequence = a_index * rep_size + rep_index

    own_part = jnp.concatenate(
        [
            tokens[0],
            lax.dynamic_slice_in_dim(segments[0], rep_index * rows, rows),
            lax.dynamic_slice_in_dim(completion[0], rep_index * (comp // rep_size), comp // rep_size),
            lax.dynamic_slice_in_dim(targets[0], rep_index * (comp // rep_size), comp // rep_size),
        ]
    )
    slots = tile_slots(owners)
    mine = owners == dp_index
    per = TILES_PER // dp_size
    home_ids = (
        jnp.arange(LAYERS)[None, :, None] * TILES_PER
        + jnp.arange(per)[None, None, :] * dp_size
        + jnp.arange(dp_size)[:, None, None]
    ).reshape(-1)
    home_mine = jnp.take(mine, home_ids)
    home_slots = jnp.where(home_mine, jnp.take(slots, home_ids), 0)
    placed = place_tiles(tile_weight, home_slots, home_mine.astype(jnp.int32), dp_size)
    placed = placed.reshape(dp_size, -1, D)
    if fits():
        home, packed = scatter_and_gather(placed, 1, padded(own_part), 4, 0, "home_and_ids")
    else:
        home = lax.psum_scatter(placed, DP, scatter_dimension=0)
        packed = lax.all_gather(padded(own_part), ALL, axis=0)
    packed = packed.reshape(devices, -1)[:, : own_part.shape[0]]
    packed = packed.reshape(dp_size, rep_size, -1)
    tokens_all = packed[:, :, :rows].reshape(dp_size, length)
    segments_all = packed[:, :, rows : 2 * rows].reshape(dp_size, length)
    edge = 2 * rows + comp // rep_size
    completion_all = packed[:, :, 2 * rows : edge].reshape(dp_size, comp)
    targets_all = packed[:, :, edge:].reshape(dp_size, comp)

    home = home.reshape(LAYERS, per, tile_rows, D)
    spread = lax.all_gather(home[0], ALL, axis=0)
    spread = spread.reshape(dp_size, rep_size, per, tile_rows, D)
    weights = [[(spread, i) for i in range(per)]]
    later = [[lax.all_gather(home[index, i], ALL, axis=0) for i in range(1, per)] for index in range(1, LAYERS)]

    order = tokens_all.reshape(a_size, rep_size, b_size, rows).transpose(0, 2, 1, 3).reshape(-1)
    place = order - vocab_start
    vocab_iota = jnp.arange(vocab_rows)
    token_hot = (place[:, None] == vocab_iota[None, :]).astype(jnp.bfloat16)
    picked = jnp.dot(
        token_hot, table_weight.astype(jnp.bfloat16), preferred_element_type=jnp.float32
    ).astype(jnp.bfloat16)
    state = scatter_all(picked.reshape(devices, rows, D), 8, "rows_scatter").astype(jnp.float32)

    for index in range(1, LAYERS):
        first, state = lax.optimization_barrier((home[index, 0], state))
        first = gather_all(first, 1, "weights_gather")
        weights.append(
            [
                (array.reshape(dp_size, rep_size, 1, tile_rows, D), 0)
                for array in [first] + later[index - 1]
            ]
        )
    first_place = b_index * rows
    places = first_place + jnp.arange(rows)
    cosine, sine = rope_tables(places.astype(jnp.float32))
    own_segments = lax.dynamic_index_in_dim(segments_all, sequence, 0, False)
    query_segments = lax.dynamic_slice_in_dim(own_segments, first_place, rows)
    marks = (own_segments[:, None], query_segments[None, :], places[None, :])
    kept_list = []
    for index in range(LAYERS):
        state, kept = layer_forward(
            state, weights[index], index, gain_weight, cosine, sine, marks
        )
        kept_list.append(kept)
    final_gain = gain_weight[2 * LAYERS]
    final = root_norm(state, final_gain).astype(jnp.bfloat16)

    capacity = 3 * comp // (2 * rep_size)
    block = completion_all // rows
    inside = block[:, None, :] == jnp.arange(b_size)[None, :, None]
    rank = jnp.cumsum(inside.astype(jnp.int32), axis=2) - 1
    slot_pick = inside[..., None] & (rank[..., None] == jnp.arange(capacity))
    filled = jnp.any(slot_pick, axis=2)
    wanted = jnp.where(
        filled, jnp.sum(jnp.where(slot_pick, targets_all[:, None, :, None], 0), axis=2), -1
    )
    spots = jnp.where(
        filled, jnp.sum(jnp.where(slot_pick, (completion_all % rows)[:, None, :, None], 0), axis=2), -1
    )
    all_wanted = (
        wanted.reshape(a_size, rep_size, b_size, capacity).transpose(0, 2, 1, 3).reshape(-1)
    )
    own_spots = lax.dynamic_index_in_dim(
        lax.dynamic_index_in_dim(spots, sequence, 0, False), b_index, 0, False
    )
    select = (own_spots[:, None] == jnp.arange(rows)[None, :]).astype(jnp.bfloat16)
    chosen = jnp.dot(select, final, preferred_element_type=jnp.float32).astype(jnp.bfloat16)
    all_rows = gather_all(chosen, 3, "chosen_gather").reshape(-1, D)
    head_low = head_weight.astype(jnp.bfloat16)
    logits = jnp.einsum("rd,vd->rv", all_rows, head_low, preferred_element_type=jnp.float32)
    hot = vocab_iota[None, :] == (all_wanted - vocab_start)[:, None]
    local_top = jnp.max(logits, axis=-1)
    local_total = jnp.sum(jnp.exp(logits - local_top[:, None]), axis=-1)
    local_hit = jnp.sum(jnp.where(hot, logits, 0.0), axis=-1)
    own_stats = jnp.concatenate(
        [v.reshape(-1, 128) for v in (local_top, local_total, local_hit)]
    )
    stats = gather_all(own_stats, 4, "stats_gather")
    tops, totals, hits = jnp.split(stats, 3, axis=1)
    top = jnp.max(tops, axis=0)
    total = jnp.sum(totals * jnp.exp(tops - top[None]), axis=0)
    log_total = (top + jnp.log(total)).reshape(-1)
    target_hit = jnp.sum(hits, axis=0).reshape(-1)
    valid = all_wanted >= 0
    scored = dp_size * comp
    loss = jnp.sum(jnp.where(valid, log_total - target_hit, 0.0)) / scored
    logit_grad = jnp.where(
        valid[:, None],
        (jnp.exp(logits - log_total[:, None]) - jnp.where(hot, 1.0, 0.0)) / scored,
        0.0,
    ).astype(jnp.bfloat16)
    rows_grad = jnp.dot(logit_grad, head_low, preferred_element_type=jnp.float32)
    own_rows = scatter_all(
        rows_grad.astype(jnp.bfloat16).reshape(devices, -1, D), 9, "back_scatter"
    )
    head_grad = jnp.einsum("rv,rd->vd", logit_grad, all_rows, preferred_element_type=jnp.float32)
    final_grad = jnp.einsum("ct,cd->td", select, own_rows, preferred_element_type=jnp.float32)
    state_grad, final_gain_grad = norm_back(state, final_gain, final_grad)
    tile_parts = [None] * LAYERS
    gain_parts = [None] * LAYERS
    for index in reversed(range(LAYERS)):
        state_grad, tile_parts[index], gain_parts[index] = layer_backward(
            state_grad, kept_list[index], weights[index], index, gain_weight, cosine, sine, marks
        )
    entry = state_grad.astype(jnp.bfloat16)
    parts = [part.reshape(devices, -1, D) for part in tile_parts]
    home_grads = [None] + [
        lax.psum_scatter(part, ALL, scatter_dimension=0) for part in parts[1:]
    ]
    if fits():
        home_grads[0], piece_grads = scatter_and_gather(parts[0], 4, entry, 4, 2, "grads_and_entry")
    else:
        home_grads[0] = lax.psum_scatter(parts[0], ALL, scatter_dimension=0)
        piece_grads = lax.all_gather(entry, ALL, axis=0)
    table_grad = jnp.einsum(
        "tv,td->vd", token_hot, piece_grads.reshape(-1, D), preferred_element_type=jnp.float32
    )
    plane_grad = gather_plane(jnp.concatenate(home_grads), 6, "owners_gather")
    plane_grad = plane_grad.reshape(tile_count, tile_rows, D)
    own_count = jnp.sum(mine.astype(jnp.int32))
    slot_ids = jnp.arange(slots_cap)
    picks = mine[home_ids][None, :] & (slots[home_ids][None, :] == slot_ids[:, None])
    tile_of_slot = jnp.sum(jnp.where(picks, jnp.arange(tile_count)[None, :], 0), axis=1)
    slot_valid = (slot_ids < own_count)[:, None, None]
    own_grad = jnp.where(
        slot_valid, jnp.take(plane_grad, tile_of_slot, axis=0).astype(jnp.float32), 0.0
    )
    gain_grads = jnp.stack([g for pair in gain_parts for g in pair] + [final_gain_grad])
    square = (
        jnp.sum(own_grad * own_grad)
        + jnp.sum(table_grad * table_grad)
        + jnp.sum(head_grad * head_grad)
    )
    sums = gather_all(
        padded(jnp.concatenate([square[None], gain_grads.reshape(-1)])), 5, "sums_gather"
    )
    sums = jnp.sum(sums.reshape(devices, -1), axis=0)
    square, gain_grads = sums[0], sums[1 : 1 + gain_grads.size].reshape(gain_grads.shape)
    norm = jnp.sqrt(square + jnp.sum(gain_grads * gain_grads))
    factor = jnp.minimum(1.0, CLIP_NORM / norm)
    steps = step_count[0].astype(jnp.float32)
    tile_new, tile_first_new, tile_second_new = adam(
        tile_weight, tile_first, tile_second, own_grad, factor, RATE_TILE, DECAY, steps
    )
    tile_new = jnp.where(slot_valid, tile_new, 0.0)
    tile_first_new = jnp.where(slot_valid, tile_first_new, 0.0)
    tile_second_new = jnp.where(slot_valid, tile_second_new, 0.0)
    table_new, table_first_new, table_second_new = adam(
        table_weight, table_first, table_second, table_grad, factor, RATE_TABLE, DECAY, steps
    )
    head_new, head_first_new, head_second_new = adam(
        head_weight, head_first, head_second, head_grad, factor, RATE_HEAD, DECAY, steps
    )
    gain_new, gain_first_new, gain_second_new = adam(
        gain_weight, gain_first, gain_second, gain_grads, factor, RATE_GAIN, 0.0, steps
    )
    return (
        loss,
        norm,
        tile_new,
        tile_new.astype(jnp.bfloat16),
        tile_first_new,
        tile_second_new,
        table_new,
        table_new.astype(jnp.bfloat16),
        table_first_new,
        table_second_new,
        head_new,
        head_new.astype(jnp.bfloat16),
        head_first_new,
        head_second_new,
        gain_new,
        gain_first_new,
        gain_second_new,
    )


def solution(mesh):
    dp_size, rep_size = mesh.shape["dp"], mesh.shape["rep"]
    split = Mesh(mesh.devices.reshape(dp_size // rep_size, rep_size // 2, 2, rep_size), ALL)
    return jax.shard_map(
        shards,
        mesh=split,
        in_specs=(
            P(DP, "z"),
            P(DP, None),
            P(DP, None),
            P(DP, None),
            P(),
            P(),
            P(ALL, None, None),
            P(ALL, None, None),
            P(ALL, None, None),
            P(ALL, None),
            P(ALL, None),
            P(ALL, None),
            P(ALL, None),
            P(ALL, None),
            P(ALL, None),
            P(),
            P(),
            P(),
        ),
        out_specs=(
            P(),
            P(),
            P(ALL, None, None),
            P(ALL, None, None),
            P(ALL, None, None),
            P(ALL, None, None),
            P(ALL, None),
            P(ALL, None),
            P(ALL, None),
            P(ALL, None),
            P(ALL, None),
            P(ALL, None),
            P(ALL, None),
            P(ALL, None),
            P(),
            P(),
            P(),
        ),
        check_vma=False,
    )
```

```python
import functools

import jax
import jax.numpy as jnp
from jax import lax
from jax.experimental import pallas as pl
from jax.experimental.pallas import tpu as pltpu
from jax.sharding import Mesh, PartitionSpec as P

D = 768
HEADS = 12
HD = 64
FF = 3072
LAYERS = 2


EPS_NORM = 1e-05
EPS_ADAM = 1e-08
CLIP_NORM = 0.005
BETA_FIRST = 0.5
BETA_SECOND = 0.5
DECAY = 0.1
RATE_TILE = 0.02
RATE_HEAD = 0.05
RATE_TABLE = 0.5
RATE_GAIN = 0.3
MASKED = -1e30


def root_norm(training_state, gain):
    return (
        training_state
        * lax.rsqrt(jnp.mean(training_state * training_state, axis=-1, keepdims=True) + EPS_NORM)
        * gain
    )


def norm_back(training_state, gain, grad):
    scale = lax.rsqrt(jnp.mean(training_state * training_state, axis=-1, keepdims=True) + EPS_NORM)
    scaled = grad * gain
    state_grad = scale * scaled - training_state * scale**3 * jnp.mean(
        scaled * training_state, axis=-1, keepdims=True
    )
    gain_grad = jnp.sum(
        (grad * training_state * scale).reshape(-1, training_state.shape[-1]), axis=0
    )
    return (state_grad, gain_grad)


def rope_tables(places):
    freqs = jnp.power(10000.0, -2.0 * jnp.arange(HD // 2).astype(jnp.float32) / HD)
    angle = places[:, None] * freqs[None, :]
    cosine, sine = jnp.cos(angle), jnp.sin(angle)
    return jnp.concatenate([cosine] * 4, axis=1), jnp.concatenate([-sine, sine] * 2, axis=1)


def tile_slots(owners):
    order = jnp.arange(owners.shape[0], dtype=jnp.int32)
    same = (owners[:, None] == owners[None, :]) & (order[None, :] < order[:, None])
    return jnp.sum(same.astype(jnp.int32), axis=1)


def adam(weight, first, second, grad, factor, rate, decay, steps):
    grad = grad * factor
    first = BETA_FIRST * first + (1.0 - BETA_FIRST) * grad
    second = BETA_SECOND * second + (1.0 - BETA_SECOND) * grad * grad
    first_hat = first / (1.0 - jnp.power(BETA_FIRST, steps))
    second_hat = second / (1.0 - jnp.power(BETA_SECOND, steps))
    weight = weight - rate * (first_hat / (jnp.sqrt(second_hat) + EPS_ADAM) + decay * weight)
    return (weight, first, second)


ALL = ("y", "x", "c", "z")
DP = ("y", "x", "c")
PART = ("x", "c")
UNITS = FF // D
TILES_PER = 4 + 3 * UNITS


MESH = pl.DeviceIdType.MESH


def half_rows(rows, dtype):
    unit = 16 if jnp.dtype(dtype).itemsize == 2 else 8
    return (rows // 2 + unit - 1) // unit * unit


def remote(src, dst, ssem, rsem, **to):
    return pltpu.make_async_remote_copy(
        src_ref=src, dst_ref=dst, send_sem=ssem, recv_sem=rsem, device_id=to, device_id_type=MESH
    )


def greet(zn, y, x, c, z):
    barrier = pltpu.get_barrier_semaphore()
    for to in ({"x": 1 - x}, {"y": 1 - y}, {"c": 1 - c}):
        pl.semaphore_signal(barrier, inc=1, device_id=to, device_id_type=MESH)
    if zn > 1:

        @pl.when(z < zn - 1)
        def _():
            pl.semaphore_signal(barrier, inc=1, device_id={"z": z + 1}, device_id_type=MESH)

        @pl.when(z > 0)
        def _():
            pl.semaphore_signal(barrier, inc=1, device_id={"z": z - 1}, device_id_type=MESH)

        @pl.when((z > 0) & (z < zn - 1))
        def _():
            pl.semaphore_wait(barrier, 5)

        @pl.when((z == 0) | (z == zn - 1))
        def _():
            pl.semaphore_wait(barrier, 4)
    else:
        pl.semaphore_wait(barrier, 3)


def gather_steps(zn, x_ref, o_ref, hold, ssem, rsem, lsem):
    y, x, c, z = [lax.axis_index(n) for n in ALL]
    me = z if zn > 1 else 0
    rows = x_ref.shape[0]
    h0 = half_rows(rows, x_ref.dtype)
    lo, hi = pl.ds(0, h0), pl.ds(h0, rows - h0)
    X, Y, DX, DY, CO, CX, CY, C0, C1, ZU, ZD = range(11)
    nx, ny, nc = {"x": 1 - x}, {"y": 1 - y}, {"c": 1 - c}

    def slot(yy, xx, zz):
        return ((yy * 2 + xx) * 2 + c) * zn + zz

    def copy(kind, k, src, dst, to):
        return remote(src, dst, ssem.at[kind, k], rsem.at[kind, k], **to)

    def block(s):
        return o_ref.at[s]

    local = pltpu.make_async_copy(x_ref, hold, lsem.at[0])
    local.start()
    keep = pltpu.make_async_copy(hold, o_ref.at[slot(y, x, me)], lsem.at[1])

    def spread(zb, src):
        dst = block(slot(y, x, zb))
        copy(X, zb, src, dst, nx).start()
        copy(Y, zb, src, dst, ny).start()
        copy(CO, zb, src, dst, nc).start()

    def up(s):
        zb = z - (s - 1)
        b = block(slot(y, x, zb))
        return copy(ZU, s, x_ref if s == 1 else b, b, {"z": z + 1})

    def down(s):
        zb = z + (s - 1)
        b = block(slot(y, x, zb))
        return copy(ZD, s, x_ref if s == 1 else b, b, {"z": z - 1})

    for s in range(1, zn):

        @pl.when((z < zn - 1) & (z - (s - 1) >= 0))
        def _():
            up(s).start()

        @pl.when((z > 0) & (z + (s - 1) < zn))
        def _():
            down(s).start()

        if s == 1:
            spread(me, x_ref)
            local.wait()
            keep.start()
        yield

        @pl.when(z - s >= 0)
        def _():
            copy(ZU, s, x_ref, x_ref, nx).wait_recv()
            spread(z - s, block(slot(y, x, z - s)))

        @pl.when(z + s < zn)
        def _():
            copy(ZD, s, x_ref, x_ref, nx).wait_recv()
            spread(z + s, block(slot(y, x, z + s)))

    if zn == 1:
        spread(0, x_ref)
        local.wait()
        keep.start()
    order = [lax.rem(z + j, zn) if zn > 1 else 0 for j in range(zn)]
    for zb in order:
        yield
        sx, sy = slot(y, 1 - x, zb), slot(1 - y, x, zb)
        copy(X, zb, x_ref, x_ref, nx).wait_recv()
        copy(DX, zb, o_ref.at[sx, lo], o_ref.at[sx, lo], ny).start()
        copy(CX, zb, block(sx), block(sx), nc).start()
        copy(Y, zb, x_ref, x_ref, nx).wait_recv()
        copy(DY, zb, o_ref.at[sy, hi], o_ref.at[sy, hi], nx).start()
        copy(CY, zb, block(sy), block(sy), nc).start()
    for zb in order:
        yield
        sd = slot(1 - y, 1 - x, zb)
        copy(DX, zb, x_ref.at[lo], x_ref.at[lo], nx).wait_recv()
        copy(C0, zb, o_ref.at[sd, lo], o_ref.at[sd, lo], nc).start()
        copy(DY, zb, x_ref.at[hi], x_ref.at[hi], nx).wait_recv()
        copy(C1, zb, o_ref.at[sd, hi], o_ref.at[sd, hi], nc).start()
    yield
    for zb in range(zn):
        for kind, part in ((CO, x_ref), (CX, x_ref), (CY, x_ref), (C0, x_ref.at[lo]), (C1, x_ref.at[hi])):
            copy(kind, zb, part, part, nx).wait_recv()
        for kind, part in (
            (X, x_ref), (Y, x_ref), (CO, x_ref), (CX, x_ref), (CY, x_ref),
            (DX, x_ref.at[lo]), (DY, x_ref.at[hi]), (C0, x_ref.at[lo]), (C1, x_ref.at[hi]),
        ):
            copy(kind, zb, part, part, nx).wait_send()
    for s in range(1, zn):

        @pl.when((z < zn - 1) & (z - (s - 1) >= 0))
        def _():
            up(s).wait_send()

        @pl.when((z > 0) & (z + (s - 1) < zn))
        def _():
            down(s).wait_send()

    keep.wait()


def run_steps(*parts):
    parts = list(parts)
    while parts:
        for part in list(parts):
            if next(part, part) is part:
                parts.remove(part)


def gather_kernel(zn, *refs):
    greet(zn, *[lax.axis_index(n) for n in ALL])
    run_steps(gather_steps(zn, *refs))


def gather_scratch(zn, shape, dtype):
    sems = pltpu.SemaphoreType.DMA((11, zn))
    return [pltpu.VMEM(shape, dtype), sems, sems, pltpu.SemaphoreType.DMA((2,))]


def all_gather(x, zn, ident, name):
    return pl.pallas_call(
        functools.partial(gather_kernel, zn),
        out_shape=jax.ShapeDtypeStruct((8 * zn,) + x.shape, x.dtype),
        in_specs=[pl.BlockSpec(memory_space=pl.ANY)],
        out_specs=pl.BlockSpec(memory_space=pl.ANY),
        scratch_shapes=gather_scratch(zn, x.shape, x.dtype),
        compiler_params=pltpu.CompilerParams(collective_id=ident, has_side_effects=True),
        name=name,
    )(x)


def reduce_steps(zn, p_refs, o_ref, acc, crecv, dxr, dyr, xr, yr, zur, zdr, ssem, rsem, lsem):
    y, x, c, z = [lax.axis_index(n) for n in ALL]
    me = z if zn > 1 else 0
    rows, each = acc.shape[1], p_refs[0].shape[1]
    h0 = half_rows(rows, acc.dtype)
    h1 = rows - h0
    X, Y, DX, DY, ZU, ZD = range(6)
    nx, ny, nc = {"x": 1 - x}, {"y": 1 - y}, {"c": 1 - c}
    kinds = [(y, x), (y, 1 - x), (1 - y, x), (1 - y, 1 - x)]
    step = 32 if rows % 32 == 0 else 16

    def slot(k, cc, zz):
        yy, xx = kinds[k]
        return ((yy * 2 + xx) * 2 + cc) * zn + zz

    def copy(kind, k, src, dst, to):
        return remote(src, dst, ssem.at[kind, k], rsem.at[kind, k], **to)

    def load(k, zb):
        b = k * zn + zb
        return [
            pltpu.make_async_copy(
                p.at[slot(k, c, zb)], acc.at[b, pl.ds(i * each, each)], lsem.at[b, i]
            )
            for i, p in enumerate(p_refs)
        ]

    def across(k, zb):
        b = k * zn + zb
        return [
            copy(10 + 4 * i + k, zb, p.at[slot(k, 1 - c, zb)], crecv.at[b, pl.ds(i * each, each)], nc)
            for i, p in enumerate(p_refs)
        ]

    def add(dst, start, count, terms):
        size = step if count % step == 0 else 16

        @pl.loop(0, count // size)
        def _(i):
            at = pl.ds(pl.multiple_of(start + i * size, 16), size)
            total = None
            for ref, base in terms:
                part = ref[pl.ds(pl.multiple_of(start - base + i * size, 16), size), :].astype(jnp.float32)
                total = part if total is None else total + part
            dst[at, :] = total.astype(dst.dtype)

    zorder = [lax.rem(z + j, zn) if zn > 1 else 0 for j in range(zn)]
    for k in (3, 1, 2, 0):
        for zb in range(zn):
            for over, near in zip(across(k, zb), load(k, zb)):
                over.start()
                near.start()

    def ready(k, zb):
        for over, near in zip(across(k, zb), load(k, zb)):
            near.wait()
            over.wait_recv()

    for zb in range(zn):
        yield
        ready(3, zb)
        b = 3 * zn + zb
        add(acc.at[b], 0, rows, [(acc.at[b], 0), (crecv.at[b], 0)])
        copy(DX, zb, acc.at[b, pl.ds(0, h0)], dxr.at[zb], nx).start()
        copy(DY, zb, acc.at[b, pl.ds(h0, h1)], dyr.at[zb], ny).start()
    for zb in range(zn):
        yield
        ready(1, zb)
        b = zn + zb
        add(acc.at[b], 0, h0, [(acc.at[b], 0), (crecv.at[b], 0)])
        copy(DY, zb, dyr.at[zb], dyr.at[zb], ny).wait_recv()
        add(acc.at[b], h0, h1, [(acc.at[b], 0), (crecv.at[b], 0), (dyr.at[zb], h0)])
        copy(X, zb, acc.at[b], xr.at[zb], nx).start()
        yield
        ready(2, zb)
        b = 2 * zn + zb
        add(acc.at[b], h0, h1, [(acc.at[b], 0), (crecv.at[b], 0)])
        copy(DX, zb, dxr.at[zb], dxr.at[zb], nx).wait_recv()
        add(acc.at[b], 0, h0, [(acc.at[b], 0), (crecv.at[b], 0), (dxr.at[zb], 0)])
        copy(Y, zb, acc.at[b], yr.at[zb], ny).start()

    def column(zb):
        return [(acc.at[zb], 0), (crecv.at[zb], 0), (xr.at[zb], 0), (yr.at[zb], 0)]

    for zb in range(zn):
        yield
        ready(0, zb)
        copy(X, zb, acc.at[zb], xr.at[zb], nx).wait_recv()
        copy(Y, zb, acc.at[zb], yr.at[zb], ny).wait_recv()
        if zn == 1:
            add(o_ref, 0, rows, column(0))
            continue

        def upward(zb=zb):
            return copy(ZU, zb, acc.at[zb], zur.at[zb], {"z": z + 1})

        def downward(zb=zb):
            return copy(ZD, zb, acc.at[zb], zdr.at[zb], {"z": z - 1})

        @pl.when(z == zb)
        def _():
            add(acc.at[zb], 0, rows, column(zb))

        @pl.when((z < zb) & (z == 0))
        def _():
            add(acc.at[zb], 0, rows, column(zb))
            upward().start()

        @pl.when((z < zb) & (z > 0))
        def _():
            upward().wait_recv()
            add(acc.at[zb], 0, rows, column(zb) + [(zur.at[zb], 0)])
            upward().start()

        @pl.when((z > zb) & (z == zn - 1))
        def _():
            add(acc.at[zb], 0, rows, column(zb))
            downward().start()

        @pl.when((z > zb) & (z < zn - 1))
        def _():
            downward().wait_recv()
            add(acc.at[zb], 0, rows, column(zb) + [(zdr.at[zb], 0)])
            downward().start()

    yield
    if zn > 1:

        @pl.when(z == 0)
        def _():
            copy(ZD, me, acc.at[me], zdr.at[me], {"z": z + 1}).wait_recv()
            add(o_ref, 0, rows, [(acc.at[me], 0), (zdr.at[me], 0)])

        @pl.when(z == zn - 1)
        def _():
            copy(ZU, me, acc.at[me], zur.at[me], {"z": z - 1}).wait_recv()
            add(o_ref, 0, rows, [(acc.at[me], 0), (zur.at[me], 0)])

        @pl.when((z > 0) & (z < zn - 1))
        def _():
            copy(ZD, me, acc.at[me], zdr.at[me], {"z": z + 1}).wait_recv()
            copy(ZU, me, acc.at[me], zur.at[me], {"z": z + 1}).wait_recv()
            add(o_ref, 0, rows, [(acc.at[me], 0), (zdr.at[me], 0), (zur.at[me], 0)])

    for zb in range(zn):
        for k in range(4):
            for over in across(k, zb):
                over.wait_send()
        copy(DX, zb, dxr.at[zb], dxr.at[zb], nx).wait_send()
        copy(DY, zb, dyr.at[zb], dyr.at[zb], ny).wait_send()
        copy(X, zb, xr.at[zb], xr.at[zb], nx).wait_send()
        copy(Y, zb, yr.at[zb], yr.at[zb], ny).wait_send()
        if zn > 1:

            @pl.when(z < zb)
            def _():
                copy(ZU, zb, zur.at[zb], zur.at[zb], {"z": z + 1}).wait_send()

            @pl.when(z > zb)
            def _():
                copy(ZD, zb, zdr.at[zb], zdr.at[zb], {"z": z - 1}).wait_send()


def reduce_kernel(zn, p_ref, *refs):
    greet(zn, *[lax.axis_index(n) for n in ALL])
    run_steps(reduce_steps(zn, [p_ref], *refs))


def reduce_scratch(zn, rows, cols, dtype, inputs=1):
    h0 = half_rows(rows, dtype)
    sems = pltpu.SemaphoreType.DMA((10 + 4 * inputs, zn))
    counts = [(4 * zn, rows), (4 * zn, rows), (zn, h0), (zn, rows - h0)] + [(zn, rows)] * 4
    blocks = [pltpu.VMEM((n, r, cols), dtype) for n, r in counts]
    return blocks + [sems, sems, pltpu.SemaphoreType.DMA((4 * zn, inputs))]


def reduce_scatter(p, zn, ident, name, out_dtype=None):
    count, rows, cols = p.shape
    return pl.pallas_call(
        functools.partial(reduce_kernel, zn),
        out_shape=jax.ShapeDtypeStruct((rows, cols), out_dtype or p.dtype),
        in_specs=[pl.BlockSpec(memory_space=pl.ANY)],
        out_specs=pl.BlockSpec(memory_space=pltpu.VMEM),
        scratch_shapes=reduce_scratch(zn, rows, cols, p.dtype),
        compiler_params=pltpu.CompilerParams(
            collective_id=ident, has_side_effects=True, vmem_limit_bytes=56 << 20
        ),
        name=name,
    )(p)


def both_kernel(inputs, zr, zg, *refs):
    p_refs, (x_ref, r_ref, o_ref), scratch = refs[:inputs], refs[inputs : inputs + 3], refs[inputs + 3 :]
    greet(max(zr, zg), *[lax.axis_index(n) for n in ALL])
    count = len(reduce_scratch(1, 32, 128, jnp.float32))
    run_steps(
        reduce_steps(zr, p_refs, r_ref, *scratch[:count]),
        gather_steps(zg, x_ref, o_ref, *scratch[count:]),
    )


def scatter_and_gather(parts, zr, x, zg, ident, name):
    inputs = len(parts)
    count, each, cols = parts[0].shape
    rows, dtype = inputs * each, parts[0].dtype
    return pl.pallas_call(
        functools.partial(both_kernel, inputs, zr, zg),
        out_shape=(
            jax.ShapeDtypeStruct((rows, cols), dtype),
            jax.ShapeDtypeStruct((8 * zg,) + x.shape, x.dtype),
        ),
        in_specs=[pl.BlockSpec(memory_space=pl.ANY)] * (inputs + 1),
        out_specs=(pl.BlockSpec(memory_space=pltpu.VMEM), pl.BlockSpec(memory_space=pl.ANY)),
        scratch_shapes=reduce_scratch(zr, rows, cols, dtype, inputs)
        + gather_scratch(zg, x.shape, x.dtype),
        compiler_params=pltpu.CompilerParams(
            collective_id=ident, has_side_effects=True, vmem_limit_bytes=56 << 20
        ),
        name=name,
    )(*parts, x)


def greet_pair(x, c):
    barrier = pltpu.get_barrier_semaphore()
    for to in ({"x": 1 - x}, {"c": 1 - c}):
        pl.semaphore_signal(barrier, inc=1, device_id=to, device_id_type=MESH)
    pl.semaphore_wait(barrier, 2)


def keys_gather_kernel(x_ref, o_ref, hold, ssem, rsem, lsem):
    x, c = lax.axis_index("x"), lax.axis_index("c")
    me, far = x * 2 + c, (1 - x) * 2 + c
    nx, nc = {"x": 1 - x}, {"c": 1 - c}
    load = pltpu.make_async_copy(x_ref, hold, lsem.at[0])
    load.start()
    greet_pair(x, c)
    out = remote(x_ref, o_ref.at[me], ssem.at[0], rsem.at[0], **nx)
    out.start()
    near = remote(x_ref, o_ref.at[me], ssem.at[1], rsem.at[1], **nc)
    near.start()
    load.wait()
    keep = pltpu.make_async_copy(hold, o_ref.at[me], lsem.at[1])
    keep.start()
    out.wait_recv()
    on = remote(o_ref.at[far], o_ref.at[far], ssem.at[2], rsem.at[2], **nc)
    on.start()
    near.wait_recv()
    on.wait_recv()
    keep.wait()
    out.wait_send()
    near.wait_send()
    on.wait_send()


def keys_gather(v, ident):
    sems = pltpu.SemaphoreType.DMA((3,))
    return pl.pallas_call(
        keys_gather_kernel,
        out_shape=jax.ShapeDtypeStruct((4,) + v.shape, v.dtype),
        in_specs=[pl.BlockSpec(memory_space=pl.ANY)],
        out_specs=pl.BlockSpec(memory_space=pl.ANY),
        scratch_shapes=[pltpu.VMEM(v.shape, v.dtype), sems, sems, pltpu.SemaphoreType.DMA((2,))],
        compiler_params=pltpu.CompilerParams(collective_id=ident, has_side_effects=True),
        name="keys_gather",
    )(v)


def keys_reduce_kernel(p_ref, o_ref, acc, crecv, xr, ssem, rsem, lsem):
    x, c = lax.axis_index("x"), lax.axis_index("c")
    nx, nc = {"x": 1 - x}, {"c": 1 - c}
    rows = p_ref.shape[1]
    places = [(1 - x) * 2, x * 2]
    loads = [pltpu.make_async_copy(p_ref.at[places[i] + c], acc.at[i], lsem.at[i]) for i in range(2)]
    for load in loads:
        load.start()
    greet_pair(x, c)
    across = [
        remote(p_ref.at[places[i] + 1 - c], crecv.at[i], ssem.at[i], rsem.at[i], **nc) for i in range(2)
    ]
    for copy in across:
        copy.start()

    def add(dst, terms):
        @pl.loop(0, rows // 16)
        def _(i):
            at = pl.ds(pl.multiple_of(i * 16, 16), 16)
            total = terms[0][at, :].astype(jnp.float32)
            for term in terms[1:]:
                total = total + term[at, :].astype(jnp.float32)
            dst[at, :] = total.astype(dst.dtype)

    loads[0].wait()
    across[0].wait_recv()
    add(acc.at[0], [acc.at[0], crecv.at[0]])
    out = remote(acc.at[0], xr, ssem.at[2], rsem.at[2], **nx)
    out.start()
    loads[1].wait()
    across[1].wait_recv()
    out.wait_recv()
    add(o_ref, [acc.at[1], crecv.at[1], xr])
    for copy in across + [out]:
        copy.wait_send()


def keys_reduce(p, ident):
    block = p.shape[1:]
    sems = pltpu.SemaphoreType.DMA((3,))
    return pl.pallas_call(
        keys_reduce_kernel,
        out_shape=jax.ShapeDtypeStruct(block, p.dtype),
        in_specs=[pl.BlockSpec(memory_space=pl.ANY)],
        out_specs=pl.BlockSpec(memory_space=pltpu.VMEM),
        scratch_shapes=[
            pltpu.VMEM((2,) + block, p.dtype), pltpu.VMEM((2,) + block, p.dtype),
            pltpu.VMEM(block, p.dtype), sems, sems, pltpu.SemaphoreType.DMA((2,)),
        ],
        compiler_params=pltpu.CompilerParams(
            collective_id=ident, has_side_effects=True, vmem_limit_bytes=32 << 20
        ),
        name="keys_reduce",
    )(p)


def fits():
    return [lax.axis_size(n) for n in ALL] == [2, 2, 2, 4]


def gather_all(v, ident, name):
    if fits():
        return all_gather(v, 4, ident, name)
    return lax.all_gather(v, ALL, axis=0)


def gather_plane(v, ident, name):
    if fits():
        return all_gather(v, 1, ident, name)
    return lax.all_gather(v, DP, axis=0)


def scatter_all(p, ident, name):
    if fits():
        return reduce_scatter(p, 4, ident, name)
    return lax.psum_scatter(p, ALL, scatter_dimension=0)


def scatter_plane(p, ident, name):
    if fits():
        return reduce_scatter(p, 1, ident, name)
    return lax.psum_scatter(p, DP, scatter_dimension=0)


def keys_all_gather(v):
    if fits():
        return keys_gather(v, 11).reshape(-1, v.shape[1])
    return lax.all_gather(v, PART, axis=0, tiled=True)


def keys_sum_scatter(p):
    if fits():
        return keys_reduce(p.reshape(4, -1, p.shape[1]), 12)
    return lax.psum_scatter(p, PART, scatter_dimension=0, tiled=True)


def tile_spec(dp, deep, tile_rows, index, local=None):
    def place(t):
        j = index(t)
        return (j % dp, 0, j // dp if local is None else local, 0, 0)

    return pl.BlockSpec((None, deep, None, tile_rows, D), place)


def weight_specs(weights, *groups):
    arrays, specs = [], []
    for first, offset in groups:
        array, local = weights[first // weights[0][0].shape[0]]
        dp, deep, _, tile_rows, _ = array.shape
        arrays.append(array)
        specs.append(
            tile_spec(dp, deep, tile_rows, lambda t, f=first, o=offset: f + o(t), local)
        )
    return arrays, specs


def whole(shape):
    return pl.BlockSpec(shape, lambda t: (0,) * len(shape))


def dot_nn(a, b):
    return lax.dot_general(a, b, (((1,), (0,)), ((), ())), preferred_element_type=jnp.float32)


def dot_nt(a, b):
    return lax.dot_general(a, b, (((1,), (1,)), ((), ())), preferred_element_type=jnp.float32)


def dot_tn(a, b):
    return lax.dot_general(a, b, (((0,), (0,)), ((), ())), preferred_element_type=jnp.float32)


def turned(u, cos, sin):
    lane = lax.broadcasted_iota(jnp.int32, (u.shape[0], 128), 1)
    low = (lane % HD) < HD // 2
    parts = []
    for i in range(D // 128):
        v = u[:, i * 128 : (i + 1) * 128]
        other = jnp.where(low, pltpu.roll(v, 128 - HD // 2, 1), pltpu.roll(v, HD // 2, 1))
        parts.append(v * cos + other * sin)
    return jnp.concatenate(parts, axis=1)


def project_kernel(x_ref, g_ref, cos_ref, sin_ref, w_ref, q_ref, kv_ref, a_ref):
    t = pl.program_id(0)

    @pl.when(t == 0)
    def _():
        a_ref[...] = root_norm(x_ref[...], g_ref[...]).astype(jnp.bfloat16)

    m = dot_nn(a_ref[...], w_ref[...].reshape(D, D))

    @pl.when(t == 0)
    def _():
        q_ref[...] = turned(m, cos_ref[...], sin_ref[...]).astype(jnp.bfloat16)

    @pl.when(t == 1)
    def _():
        kv_ref[...] = turned(m, cos_ref[...], sin_ref[...]).astype(jnp.bfloat16)

    @pl.when(t == 2)
    def _():
        kv_ref[...] = m.astype(jnp.bfloat16)


def project(x, gain, cos, sin, weights):
    rows = x.shape[0]
    arrays, specs = weight_specs(weights, (0, lambda t: t))
    return pl.pallas_call(
        project_kernel,
        grid=(3,),
        out_shape=(
            jax.ShapeDtypeStruct((rows, D), jnp.bfloat16),
            jax.ShapeDtypeStruct((2, rows, D), jnp.bfloat16),
        ),
        in_specs=[
            whole((rows, D)), whole((1, D)), whole((rows, 128)), whole((rows, 128)), *specs,
        ],
        out_specs=(
            whole((rows, D)),
            pl.BlockSpec((None, rows, D), lambda t: (jnp.maximum(t - 1, 0), 0, 0)),
        ),
        scratch_shapes=[pltpu.VMEM((rows, D), jnp.bfloat16)],
        compiler_params=pltpu.CompilerParams(vmem_limit_bytes=40 << 20),
        name="project",
    )(x, gain, cos, sin, *arrays)


def mask_bias(bias_ref, kseg_ref, qseg_ref, qpos_ref):
    kpos = lax.broadcasted_iota(jnp.int32, bias_ref.shape, 0)
    allowed = (kpos <= qpos_ref[...]) & (kseg_ref[...] == qseg_ref[...])
    bias_ref[...] = jnp.where(allowed, 0.0, MASKED)


def head_lanes(shape, head):
    return (lax.broadcasted_iota(jnp.int32, shape, 1) // HD) == head


def attend_kernel(q_ref, k_ref, v_ref, kseg_ref, qseg_ref, qpos_ref, o_ref, lse_ref, bias_ref):
    @pl.when(pl.program_id(0) == 0)
    def _():
        mask_bias(bias_ref, kseg_ref, qseg_ref, qpos_ref)

    length = bias_ref.shape[0]
    q = q_ref[...] * HD ** (-0.5)
    k, v = k_ref[...].reshape(length, 128), v_ref[...].reshape(length, 128)
    outs = []
    for head in range(2):
        mine = head_lanes(q.shape, head)
        s = dot_nt(k, jnp.where(mine, q, jnp.zeros_like(q))) + bias_ref[...]
        top = jnp.max(s, axis=0, keepdims=True)
        e = jnp.exp(s - top)
        total = jnp.sum(e, axis=0, keepdims=True)
        p = (e * (1.0 / total)).astype(jnp.bfloat16)
        outs.append(dot_tn(p, v))
        lse_ref[head : head + 1, :] = top + jnp.log(total)
    o_ref[...] = jnp.where(head_lanes(outs[0].shape, 0), outs[0], outs[1]).astype(jnp.bfloat16)


def attend_specs(rows, parts):
    length = parts * rows
    pair = pl.BlockSpec((rows, 128), lambda t: (0, t))
    return pair, [
        pair,
        pl.BlockSpec((parts, None, rows, 128), lambda t: (0, 0, 0, t)),
        pl.BlockSpec((parts, None, rows, 128), lambda t: (0, 1, 0, t)),
        whole((length, 1)), whole((1, rows)), whole((1, rows)),
    ]


def attend(q, kv, kseg, qseg, qpos):
    rows, parts = q.shape[0], kv.shape[0]
    pair, specs = attend_specs(rows, parts)
    return pl.pallas_call(
        attend_kernel,
        grid=(HEADS // 2,),
        out_shape=(
            jax.ShapeDtypeStruct((rows, D), jnp.bfloat16),
            jax.ShapeDtypeStruct((HEADS // 2, 8, rows), jnp.float32),
        ),
        in_specs=specs,
        out_specs=(pair, pl.BlockSpec((None, 8, rows), lambda t: (t, 0, 0))),
        scratch_shapes=[pltpu.VMEM((parts * rows, rows), jnp.float32)],
        compiler_params=pltpu.CompilerParams(vmem_limit_bytes=40 << 20),
        name="attend",
    )(q, kv, kv, kseg, qseg, qpos)


def feed_kernel(x_ref, o_ref, g_ref, wo_ref, wg_ref, wu_ref, wd_ref, mid_ref, out_ref, b_ref):
    t = pl.program_id(0)

    @pl.when(t == 0)
    def _():
        mid = x_ref[...] + dot_nn(o_ref[...], wo_ref[...].reshape(D, D))
        mid_ref[...] = mid
        out_ref[...] = mid
        b_ref[...] = root_norm(mid, g_ref[...]).astype(jnp.bfloat16)

    @pl.when(t > 0)
    def _():
        gate = dot_nn(b_ref[...], wg_ref[...].reshape(D, D))
        up = dot_nn(b_ref[...], wu_ref[...].reshape(D, D))
        h = (gate * jax.nn.sigmoid(gate) * up).astype(jnp.bfloat16)
        out_ref[...] += dot_nn(h, wd_ref[...].reshape(D, D))


def feed(x, o, gain, weights):
    rows = x.shape[0]
    unit = lambda t: jnp.maximum(t - 1, 0)
    arrays, specs = weight_specs(
        weights, (3, lambda t: 0 * t), (4, unit), (4 + UNITS, unit), (4 + 2 * UNITS, unit)
    )
    state = jax.ShapeDtypeStruct((rows, D), jnp.float32)
    return pl.pallas_call(
        feed_kernel,
        grid=(1 + UNITS,),
        out_shape=(state, state),
        in_specs=[
            whole((rows, D)), whole((rows, D)), whole((1, D)), *specs,
        ],
        out_specs=(whole((rows, D)), whole((rows, D))),
        scratch_shapes=[pltpu.VMEM((rows, D), jnp.bfloat16)],
        compiler_params=pltpu.CompilerParams(vmem_limit_bytes=48 << 20),
        name="feed",
    )(x, o, gain, *arrays)


def feed_back_kernel(
    groups, dy_ref, mid_ref, g_ref, o_ref, wo_ref, wg_ref, wu_ref, wd_ref, dx_ref, do_ref, dgain_ref,
    *refs,
):
    grad_refs, (b_ref, bt_ref, e_ref, dg_ref, du_ref, db_ref) = refs[:-6], refs[-6:]
    t = pl.program_id(0)
    last = pl.num_programs(0) - 1

    def emit(kind, g):
        ref = grad_refs[groups[kind]]
        ref[...] = g.astype(jnp.bfloat16).reshape(ref.shape)

    @pl.when(t == 0)
    def _():
        b = root_norm(mid_ref[...], g_ref[...])
        b_ref[...] = b.astype(jnp.bfloat16)
        bt_ref[...] = b.T.astype(jnp.bfloat16)
        e_ref[...] = dy_ref[...].astype(jnp.bfloat16)
        db_ref[...] = jnp.zeros_like(db_ref)

    @pl.when((t % 3 == 0) & (t < last))
    def _():
        gate = dot_nn(b_ref[...], wg_ref[...].reshape(D, D))
        up = dot_nn(b_ref[...], wu_ref[...].reshape(D, D))
        sigma = jax.nn.sigmoid(gate)
        h = (gate * sigma * up).astype(jnp.bfloat16)
        emit(0, dot_tn(h, e_ref[...]))
        dh = dot_nt(e_ref[...], wd_ref[...].reshape(D, D))
        dg_ref[...] = (dh * up * sigma * (1.0 + gate * (1.0 - sigma))).astype(jnp.bfloat16)
        du_ref[...] = (dh * gate * sigma).astype(jnp.bfloat16)

    @pl.when(t % 3 == 1)
    def _():
        emit(1, dot_nn(bt_ref[...], dg_ref[...]))
        db_ref[...] += dot_nt(dg_ref[...], wg_ref[...].reshape(D, D))

    @pl.when(t % 3 == 2)
    def _():
        emit(2, dot_nn(bt_ref[...], du_ref[...]))
        db_ref[...] += dot_nt(du_ref[...], wu_ref[...].reshape(D, D))

    @pl.when(t == last)
    def _():
        back, gain_back = norm_back(mid_ref[...], g_ref[...], db_ref[...])
        dx = dy_ref[...] + back
        dx_ref[...] = dx
        dgain_ref[...] = jnp.broadcast_to(gain_back[None, :], dgain_ref.shape)
        e1 = dx.astype(jnp.bfloat16)
        emit(3, dot_tn(o_ref[...], e1))
        do_ref[...] = dot_nt(e1, wo_ref[...].reshape(D, D)).astype(jnp.bfloat16)


def feed_back(dy, mid, gain, o, weights):
    rows = dy.shape[0]
    dp, deep, _, tile_rows, _ = weights[0][0].shape
    unit = lambda t: jnp.minimum(t // 3, UNITS - 1)
    arrays, specs = weight_specs(
        weights, (3, lambda t: 0 * t), (4, unit), (4 + UNITS, unit), (4 + 2 * UNITS, unit)
    )
    firsts = [4 + 2 * UNITS, 4, 4 + UNITS, 3]
    groups = [first // dp for first in firsts]

    def grad_tile(group, t):
        kinds = [k for k in range(3) if groups[k] == group]
        s, k = unit(t), t % 3
        tile = firsts[kinds[0]] + jnp.where(k < kinds[0], jnp.maximum(s - 1, 0), s)
        for kind in kinds[1:]:
            tile = jnp.where(k >= kind, firsts[kind] + s, tile)
        final = 3 if groups[3] == group else firsts[kinds[-1]] + UNITS - 1
        return jnp.where(t == 3 * UNITS, final, tile)

    return pl.pallas_call(
        functools.partial(feed_back_kernel, groups),
        grid=(3 * UNITS + 1,),
        out_shape=(
            jax.ShapeDtypeStruct((rows, D), jnp.float32),
            jax.ShapeDtypeStruct((rows, D), jnp.bfloat16),
            jax.ShapeDtypeStruct((8, D), jnp.float32),
        )
        + (jax.ShapeDtypeStruct((dp, deep, 1, tile_rows, D), jnp.bfloat16),) * len(weights),
        in_specs=[
            whole((rows, D)), whole((rows, D)), whole((1, D)), whole((rows, D)), *specs,
        ],
        out_specs=(whole((rows, D)), whole((rows, D)), whole((8, D)))
        + tuple(
            tile_spec(dp, deep, tile_rows, functools.partial(grad_tile, group), 0)
            for group in range(len(weights))
        ),
        scratch_shapes=[
            pltpu.VMEM((rows, D), jnp.bfloat16), pltpu.VMEM((D, rows), jnp.bfloat16),
            pltpu.VMEM((rows, D), jnp.bfloat16), pltpu.VMEM((rows, D), jnp.bfloat16),
            pltpu.VMEM((rows, D), jnp.bfloat16), pltpu.VMEM((rows, D), jnp.float32),
        ],
        compiler_params=pltpu.CompilerParams(vmem_limit_bytes=48 << 20),
        name="feed_back",
    )(dy, mid, gain, o, *arrays)


def attend_back_kernel(
    q_ref, k_ref, v_ref, kseg_ref, qseg_ref, qpos_ref, do_ref, lse_ref, dq_ref, dkv_ref, bias_ref
):
    @pl.when(pl.program_id(0) == 0)
    def _():
        mask_bias(bias_ref, kseg_ref, qseg_ref, qpos_ref)

    length = bias_ref.shape[0]
    parts, rows = dkv_ref.shape[0], q_ref.shape[0]
    q, do = q_ref[...] * HD ** (-0.5), do_ref[...]
    k, v = k_ref[...].reshape(length, 128), v_ref[...].reshape(length, 128)
    dqs, dk, dv = [], None, None
    for head in range(2):
        mine = head_lanes(q.shape, head)
        qm = jnp.where(mine, q, jnp.zeros_like(q))
        dom = jnp.where(mine, do, jnp.zeros_like(do))
        s = dot_nt(k, qm) + bias_ref[...]
        p = jnp.exp(s - lse_ref[head : head + 1, :])
        dp = dot_nt(v, dom)
        delta = jnp.sum(p * dp, axis=0, keepdims=True)
        ds = (p * (dp - delta)).astype(jnp.bfloat16)
        dv_part = dot_nn(p.astype(jnp.bfloat16), dom)
        dk_part = dot_nn(ds, qm)
        dv = dv_part if dv is None else dv + dv_part
        dk = dk_part if dk is None else dk + dk_part
        dqs.append(dot_tn(ds, k))
    dq_ref[...] = jnp.where(head_lanes(dqs[0].shape, 0), dqs[0], dqs[1]) * HD ** (-0.5)
    dkv_ref[:, 0] = dk.astype(jnp.bfloat16).reshape(parts, rows, 128)
    dkv_ref[:, 1] = dv.astype(jnp.bfloat16).reshape(parts, rows, 128)


def attend_back(q, kv, kseg, qseg, qpos, do, lse):
    rows, parts = q.shape[0], kv.shape[0]
    pair, specs = attend_specs(rows, parts)
    return pl.pallas_call(
        attend_back_kernel,
        grid=(HEADS // 2,),
        out_shape=(
            jax.ShapeDtypeStruct((rows, D), jnp.float32),
            jax.ShapeDtypeStruct((parts, 2, rows, D), jnp.bfloat16),
        ),
        in_specs=specs + [pair, pl.BlockSpec((None, 8, rows), lambda t: (t, 0, 0))],
        out_specs=(pair, pl.BlockSpec((parts, 2, rows, 128), lambda t: (0, 0, 0, t))),
        scratch_shapes=[pltpu.VMEM((parts * rows, rows), jnp.float32)],
        compiler_params=pltpu.CompilerParams(vmem_limit_bytes=48 << 20),
        name="attend_back",
    )(q, kv, kv, kseg, qseg, qpos, do, lse)


def project_back_kernel(
    dx_ref, x_ref, g_ref, cos_ref, sin_ref, dq_ref, dkv_ref, w_ref, held_ref,
    grad_ref, out_ref, dgain_ref, a_ref, dm_ref, da_ref,
):
    t = pl.program_id(0)
    deep, tile_rows = grad_ref.shape[0], grad_ref.shape[1]

    @pl.when(t == 0)
    def _():
        a_ref[...] = root_norm(x_ref[...], g_ref[...]).astype(jnp.bfloat16)
        da_ref[...] = jnp.zeros_like(da_ref)
        dm_ref[...] = turned(dq_ref[...], cos_ref[...], -sin_ref[...]).astype(jnp.bfloat16)

    @pl.when(t == 1)
    def _():
        dk = dkv_ref[0].astype(jnp.float32)
        dm_ref[...] = turned(dk, cos_ref[...], -sin_ref[...]).astype(jnp.bfloat16)

    @pl.when(t == 2)
    def _():
        dm_ref[...] = dkv_ref[1]

    grad = dot_tn(a_ref[...], dm_ref[...])
    grad_ref[...] = grad.astype(jnp.bfloat16).reshape(deep, tile_rows, D)
    da_ref[...] += dot_nt(dm_ref[...], w_ref[...].reshape(D, D))

    @pl.when(t == 2)
    def _():
        back, gain_back = norm_back(x_ref[...], g_ref[...], da_ref[...])
        out_ref[...] = dx_ref[...] + back
        dgain_ref[...] = jnp.broadcast_to(gain_back[None, :], dgain_ref.shape)


def project_back(dx, x, gain, cos, sin, dq, dkv, weights, grads):
    rows = x.shape[0]
    dp, deep, _, tile_rows, _ = weights[0][0].shape
    arrays, specs = weight_specs(weights, (0, lambda t: t))
    return pl.pallas_call(
        project_back_kernel,
        grid=(3,),
        out_shape=(
            jax.ShapeDtypeStruct(grads.shape, grads.dtype),
            jax.ShapeDtypeStruct((rows, D), jnp.float32),
            jax.ShapeDtypeStruct((8, D), jnp.float32),
        ),
        in_specs=[
            whole((rows, D)), whole((rows, D)), whole((1, D)), whole((rows, 128)),
            whole((rows, 128)), whole((rows, D)), whole((2, rows, D)),
            *specs,
            pl.BlockSpec(memory_space=pl.ANY),
        ],
        out_specs=(
            tile_spec(dp, deep, tile_rows, lambda t: t, 0), whole((rows, D)), whole((8, D)),
        ),
        scratch_shapes=[
            pltpu.VMEM((rows, D), jnp.bfloat16), pltpu.VMEM((rows, D), jnp.bfloat16),
            pltpu.VMEM((rows, D), jnp.float32),
        ],
        input_output_aliases={8: 0},
        compiler_params=pltpu.CompilerParams(vmem_limit_bytes=40 << 20),
        name="project_back",
    )(dx, x, gain, cos, sin, dq, dkv, *arrays, grads)


def layer_forward(state, weights, layer, gains, cos, sin, marks):
    rows = state.shape[0]
    q, kv = project(state, gains[2 * layer : 2 * layer + 1], cos, sin, weights)
    kv = keys_all_gather(kv.reshape(2 * rows, D)).reshape(-1, 2, rows, D)
    o, lse = attend(q, kv, *marks)
    mid, out = feed(state, o, gains[2 * layer + 1 : 2 * layer + 2], weights)
    return out, (state, mid, q, kv, lse, o)


def layer_backward(grad, kept, weights, layer, gains, cos, sin, marks):
    state, mid, q, kv, lse, o = kept
    rows = state.shape[0]
    dx, do, feed_gain, *grads = feed_back(
        grad, mid, gains[2 * layer + 1 : 2 * layer + 2], o, weights
    )
    dq, dkv = attend_back(q, kv, *marks, do, lse)
    dkv = keys_sum_scatter(dkv.reshape(-1, D)).reshape(2, rows, D)
    grads[0], dx, input_gain = project_back(
        dx, state, gains[2 * layer : 2 * layer + 1], cos, sin, dq, dkv, weights, grads[0]
    )
    return dx, grads, [input_gain[0], feed_gain[0]]


def padded(v):
    count = -(-v.shape[0] // 2048) * 2048
    return jnp.pad(v, (0, count - v.shape[0])).reshape(-1, 128)


def place_kernel(slot_ref, mine_ref, w_ref, o_ref):
    g = pl.program_id(0)
    count = o_ref.shape[0]
    for i in range(count):
        t = g * count + i
        o_ref[i] = jnp.where(mine_ref[t] > 0, w_ref[slot_ref[t]], 0.0).astype(jnp.bfloat16)


def place_tiles(tile_weight, slots, mine, dp_size):
    count = slots.shape[0] // dp_size
    cap, rows, cols = tile_weight.shape
    return pl.pallas_call(
        place_kernel,
        grid_spec=pltpu.PrefetchScalarGridSpec(
            num_scalar_prefetch=2,
            grid=(dp_size,),
            in_specs=[pl.BlockSpec((cap, rows, cols), lambda g, *_: (0, 0, 0))],
            out_specs=pl.BlockSpec((count, rows, cols), lambda g, *_: (g, 0, 0)),
        ),
        out_shape=jax.ShapeDtypeStruct((dp_size * count, rows, cols), jnp.bfloat16),
        compiler_params=pltpu.CompilerParams(vmem_limit_bytes=24 << 20),
        name="place_tiles",
    )(slots, mine, tile_weight)


def shards(
    tokens,
    segments,
    completion,
    targets,
    owners,
    step_count,
    tile_weight,
    tile_first,
    tile_second,
    table_weight,
    table_first,
    table_second,
    head_weight,
    head_first,
    head_second,
    gain_weight,
    gain_first,
    gain_second,
):
    a_size, b_size, rep_size = lax.axis_size("y"), lax.axis_size(PART), lax.axis_size("z")
    a_index, b_index, rep_index = lax.axis_index("y"), lax.axis_index(PART), lax.axis_index("z")
    dp_size = a_size * b_size
    devices = dp_size * rep_size
    dp_index = a_index * b_size + b_index
    device = dp_index * rep_size + rep_index
    rows = tokens.shape[1]
    length = segments.shape[1]
    comp = completion.shape[1]
    slots_cap, tile_rows = tile_weight.shape[:2]
    tile_count = owners.shape[0]
    home_tiles = tile_count // dp_size
    vocab_rows = table_weight.shape[0]
    vocab_start = device * vocab_rows
    sequence = a_index * rep_size + rep_index

    own_part = jnp.concatenate(
        [
            tokens[0],
            lax.dynamic_slice_in_dim(segments[0], rep_index * rows, rows),
            lax.dynamic_slice_in_dim(completion[0], rep_index * (comp // rep_size), comp // rep_size),
            lax.dynamic_slice_in_dim(targets[0], rep_index * (comp // rep_size), comp // rep_size),
        ]
    )
    slots = tile_slots(owners)
    mine = owners == dp_index
    per = TILES_PER // dp_size
    home_ids = (
        jnp.arange(LAYERS)[None, :, None] * TILES_PER
        + jnp.arange(per)[None, None, :] * dp_size
        + jnp.arange(dp_size)[:, None, None]
    ).reshape(-1)
    home_mine = jnp.take(mine, home_ids)
    home_slots = jnp.where(home_mine, jnp.take(slots, home_ids), 0)
    placed = place_tiles(tile_weight, home_slots, home_mine.astype(jnp.int32), dp_size)
    placed = placed.reshape(dp_size, -1, D)
    if fits():
        home, packed = scatter_and_gather([placed], 1, padded(own_part), 4, 0, "home_and_ids")
    else:
        home = lax.psum_scatter(placed, DP, scatter_dimension=0)
        packed = lax.all_gather(padded(own_part), ALL, axis=0)
    packed = packed.reshape(devices, -1)[:, : own_part.shape[0]]
    packed = packed.reshape(dp_size, rep_size, -1)
    tokens_all = packed[:, :, :rows].reshape(dp_size, length)
    segments_all = packed[:, :, rows : 2 * rows].reshape(dp_size, length)
    edge = 2 * rows + comp // rep_size
    completion_all = packed[:, :, 2 * rows : edge].reshape(dp_size, comp)
    targets_all = packed[:, :, edge:].reshape(dp_size, comp)

    home = home.reshape(LAYERS, per, tile_rows, D)
    spread = lax.all_gather(home[0], ALL, axis=0)
    spread = spread.reshape(dp_size, rep_size, per, tile_rows, D)
    weights = [[(spread, i) for i in range(per)]]
    later = [[lax.all_gather(home[index, i], ALL, axis=0) for i in range(1, per)] for index in range(1, LAYERS)]

    order = tokens_all.reshape(a_size, rep_size, b_size, rows).transpose(0, 2, 1, 3).reshape(-1)
    place = order - vocab_start
    vocab_iota = jnp.arange(vocab_rows)
    token_hot = (place[:, None] == vocab_iota[None, :]).astype(jnp.bfloat16)
    picked = jnp.dot(
        token_hot, table_weight.astype(jnp.bfloat16), preferred_element_type=jnp.float32
    ).astype(jnp.bfloat16)
    state = scatter_all(picked.reshape(devices, rows, D), 8, "rows_scatter").astype(jnp.float32)

    for index in range(1, LAYERS):
        first, state = lax.optimization_barrier((home[index, 0], state))
        first = gather_all(first, 1, "weights_gather")
        weights.append(
            [
                (array.reshape(dp_size, rep_size, 1, tile_rows, D), 0)
                for array in [first] + later[index - 1]
            ]
        )
    first_place = b_index * rows
    places = first_place + jnp.arange(rows)
    cosine, sine = rope_tables(places.astype(jnp.float32))
    own_segments = lax.dynamic_index_in_dim(segments_all, sequence, 0, False)
    query_segments = lax.dynamic_slice_in_dim(own_segments, first_place, rows)
    marks = (own_segments[:, None], query_segments[None, :], places[None, :])
    kept_list = []
    for index in range(LAYERS):
        state, kept = layer_forward(
            state, weights[index], index, gain_weight, cosine, sine, marks
        )
        kept_list.append(kept)
    final_gain = gain_weight[2 * LAYERS]
    final = root_norm(state, final_gain).astype(jnp.bfloat16)

    capacity = 3 * comp // (2 * rep_size)
    block = completion_all // rows
    inside = block[:, None, :] == jnp.arange(b_size)[None, :, None]
    before = jnp.sum((block[:, None, :] < jnp.arange(b_size)[None, :, None]).astype(jnp.int32), axis=2)
    rank = jnp.arange(comp)[None, None, :] - before[:, :, None]
    slot_pick = inside[..., None] & (rank[..., None] == jnp.arange(capacity))
    filled = jnp.any(slot_pick, axis=2)
    wanted = jnp.where(
        filled, jnp.sum(jnp.where(slot_pick, targets_all[:, None, :, None], 0), axis=2), -1
    )
    spots = jnp.where(
        filled, jnp.sum(jnp.where(slot_pick, (completion_all % rows)[:, None, :, None], 0), axis=2), -1
    )
    all_wanted = (
        wanted.reshape(a_size, rep_size, b_size, capacity).transpose(0, 2, 1, 3).reshape(-1)
    )
    own_spots = lax.dynamic_index_in_dim(
        lax.dynamic_index_in_dim(spots, sequence, 0, False), b_index, 0, False
    )
    select = (own_spots[:, None] == jnp.arange(rows)[None, :]).astype(jnp.bfloat16)
    chosen = jnp.dot(select, final, preferred_element_type=jnp.float32).astype(jnp.bfloat16)
    all_rows = gather_all(chosen, 3, "chosen_gather").reshape(-1, D)
    head_low = head_weight.astype(jnp.bfloat16)
    logits = jnp.einsum("rd,vd->rv", all_rows, head_low, preferred_element_type=jnp.float32)
    hot = vocab_iota[None, :] == (all_wanted - vocab_start)[:, None]
    local_top = jnp.max(logits, axis=-1)
    local_total = jnp.sum(jnp.exp(logits - local_top[:, None]), axis=-1)
    local_hit = jnp.sum(jnp.where(hot, logits, 0.0), axis=-1)
    own_stats = jnp.concatenate(
        [v.reshape(-1, 128) for v in (local_top, local_total, local_hit)]
    )
    stats = gather_all(own_stats, 4, "stats_gather")
    tops, totals, hits = jnp.split(stats, 3, axis=1)
    top = jnp.max(tops, axis=0)
    total = jnp.sum(totals * jnp.exp(tops - top[None]), axis=0)
    log_total = (top + jnp.log(total)).reshape(-1)
    target_hit = jnp.sum(hits, axis=0).reshape(-1)
    valid = all_wanted >= 0
    scored = dp_size * comp
    loss = jnp.sum(jnp.where(valid, log_total - target_hit, 0.0)) / scored
    logit_grad = jnp.where(
        valid[:, None],
        (jnp.exp(logits - log_total[:, None]) - jnp.where(hot, 1.0, 0.0)) / scored,
        0.0,
    ).astype(jnp.bfloat16)
    logit_grad = lax.optimization_barrier(logit_grad)
    rows_grad = jnp.dot(logit_grad, head_low, preferred_element_type=jnp.float32)
    own_rows = scatter_all(
        rows_grad.astype(jnp.bfloat16).reshape(devices, -1, D), 9, "back_scatter"
    )
    head_grad = jnp.einsum("rv,rd->vd", logit_grad, all_rows, preferred_element_type=jnp.float32)
    final_grad = jnp.einsum("ct,cd->td", select, own_rows, preferred_element_type=jnp.float32)
    state_grad, final_gain_grad = norm_back(state, final_gain, final_grad)
    tile_parts = [None] * LAYERS
    gain_parts = [None] * LAYERS
    for index in reversed(range(LAYERS)):
        state_grad, tile_parts[index], gain_parts[index] = layer_backward(
            state_grad, kept_list[index], weights[index], index, gain_weight, cosine, sine, marks
        )
    entry = state_grad.astype(jnp.bfloat16)
    flat = [[part.reshape(devices, -1, D) for part in layer] for layer in tile_parts]
    if fits():
        tail = [lax.psum_scatter(flat[-1][-1], ALL, scatter_dimension=0)]
        firsts = [part for layer in flat for part in layer][:-1]
        body, piece_grads = scatter_and_gather(firsts, 4, entry, 4, 2, "grads_and_entry")
        home_grads = [body] + tail
    else:
        home_grads = [
            lax.psum_scatter(part, ALL, scatter_dimension=0) for layer in flat for part in layer
        ]
        piece_grads = lax.all_gather(entry, ALL, axis=0)
    table_grad = jnp.einsum(
        "tv,td->vd", token_hot, piece_grads.reshape(-1, D), preferred_element_type=jnp.float32
    )
    plane_grad = gather_plane(jnp.concatenate(home_grads), 6, "owners_gather")
    plane_grad = plane_grad.reshape(tile_count, tile_rows, D)
    own_count = jnp.sum(mine.astype(jnp.int32))
    slot_ids = jnp.arange(slots_cap)
    picks = mine[home_ids][None, :] & (slots[home_ids][None, :] == slot_ids[:, None])
    tile_of_slot = jnp.sum(jnp.where(picks, jnp.arange(tile_count)[None, :], 0), axis=1)
    slot_valid = (slot_ids < own_count)[:, None, None]
    own_grad = jnp.where(
        slot_valid, jnp.take(plane_grad, tile_of_slot, axis=0).astype(jnp.float32), 0.0
    )
    gain_grads = jnp.stack([g for pair in gain_parts for g in pair] + [final_gain_grad])
    square = (
        jnp.sum(own_grad * own_grad)
        + jnp.sum(table_grad * table_grad)
        + jnp.sum(head_grad * head_grad)
    )
    sums = gather_all(
        padded(jnp.concatenate([square[None], gain_grads.reshape(-1)])), 5, "sums_gather"
    )
    sums = jnp.sum(sums.reshape(devices, -1), axis=0)
    square, gain_grads = sums[0], sums[1 : 1 + gain_grads.size].reshape(gain_grads.shape)
    norm = jnp.sqrt(square + jnp.sum(gain_grads * gain_grads))
    factor = jnp.minimum(1.0, CLIP_NORM / norm)
    steps = step_count[0].astype(jnp.float32)
    tile_new, tile_first_new, tile_second_new = adam(
        tile_weight, tile_first, tile_second, own_grad, factor, RATE_TILE, DECAY, steps
    )
    tile_new = jnp.where(slot_valid, tile_new, 0.0)
    tile_first_new = jnp.where(slot_valid, tile_first_new, 0.0)
    tile_second_new = jnp.where(slot_valid, tile_second_new, 0.0)
    table_new, table_first_new, table_second_new = adam(
        table_weight, table_first, table_second, table_grad, factor, RATE_TABLE, DECAY, steps
    )
    head_new, head_first_new, head_second_new = adam(
        head_weight, head_first, head_second, head_grad, factor, RATE_HEAD, DECAY, steps
    )
    gain_new, gain_first_new, gain_second_new = adam(
        gain_weight, gain_first, gain_second, gain_grads, factor, RATE_GAIN, 0.0, steps
    )
    return (
        loss,
        norm,
        tile_new,
        tile_new.astype(jnp.bfloat16),
        tile_first_new,
        tile_second_new,
        table_new,
        table_new.astype(jnp.bfloat16),
        table_first_new,
        table_second_new,
        head_new,
        head_new.astype(jnp.bfloat16),
        head_first_new,
        head_second_new,
        gain_new,
        gain_first_new,
        gain_second_new,
    )


def solution(mesh):
    dp_size, rep_size = mesh.shape["dp"], mesh.shape["rep"]
    split = Mesh(mesh.devices.reshape(dp_size // rep_size, rep_size // 2, 2, rep_size), ALL)
    return jax.shard_map(
        shards,
        mesh=split,
        in_specs=(
            P(DP, "z"),
            P(DP, None),
            P(DP, None),
            P(DP, None),
            P(),
            P(),
            P(ALL, None, None),
            P(ALL, None, None),
            P(ALL, None, None),
            P(ALL, None),
            P(ALL, None),
            P(ALL, None),
            P(ALL, None),
            P(ALL, None),
            P(ALL, None),
            P(),
            P(),
            P(),
        ),
        out_specs=(
            P(),
            P(),
            P(ALL, None, None),
            P(ALL, None, None),
            P(ALL, None, None),
            P(ALL, None, None),
            P(ALL, None),
            P(ALL, None),
            P(ALL, None),
            P(ALL, None),
            P(ALL, None),
            P(ALL, None),
            P(ALL, None),
            P(ALL, None),
            P(),
            P(),
            P(),
        ),
        check_vma=False,
    )
```

```python
import functools

import jax
import jax.numpy as jnp
from jax import lax
from jax.experimental import pallas as pl
from jax.experimental.pallas import tpu as pltpu
from jax.sharding import Mesh, PartitionSpec as P

D = 768
HEADS = 12
HD = 64
FF = 3072
LAYERS = 2


EPS_NORM = 1e-05
EPS_ADAM = 1e-08
CLIP_NORM = 0.005
BETA_FIRST = 0.5
BETA_SECOND = 0.5
DECAY = 0.1
RATE_TILE = 0.02
RATE_HEAD = 0.05
RATE_TABLE = 0.5
RATE_GAIN = 0.3
MASKED = -1e30


def root_norm(training_state, gain):
    return (
        training_state
        * lax.rsqrt(jnp.mean(training_state * training_state, axis=-1, keepdims=True) + EPS_NORM)
        * gain
    )


def norm_back(training_state, gain, grad):
    scale = lax.rsqrt(jnp.mean(training_state * training_state, axis=-1, keepdims=True) + EPS_NORM)
    scaled = grad * gain
    state_grad = scale * scaled - training_state * scale**3 * jnp.mean(
        scaled * training_state, axis=-1, keepdims=True
    )
    gain_grad = jnp.sum(
        (grad * training_state * scale).reshape(-1, training_state.shape[-1]), axis=0
    )
    return (state_grad, gain_grad)


def rope_tables(places):
    freqs = jnp.power(10000.0, -2.0 * jnp.arange(HD // 2).astype(jnp.float32) / HD)
    angle = places[:, None] * freqs[None, :]
    cosine, sine = jnp.cos(angle), jnp.sin(angle)
    return jnp.concatenate([cosine] * 4, axis=1), jnp.concatenate([-sine, sine] * 2, axis=1)


def tile_slots(owners):
    order = jnp.arange(owners.shape[0], dtype=jnp.int32)
    same = (owners[:, None] == owners[None, :]) & (order[None, :] < order[:, None])
    return jnp.sum(same.astype(jnp.int32), axis=1)


def adam(weight, first, second, grad, factor, rate, decay, steps):
    grad = grad * factor
    first = BETA_FIRST * first + (1.0 - BETA_FIRST) * grad
    second = BETA_SECOND * second + (1.0 - BETA_SECOND) * grad * grad
    first_hat = first / (1.0 - jnp.power(BETA_FIRST, steps))
    second_hat = second / (1.0 - jnp.power(BETA_SECOND, steps))
    weight = weight - rate * (first_hat / (jnp.sqrt(second_hat) + EPS_ADAM) + decay * weight)
    return (weight, first, second)


ALL = ("y", "x", "c", "z")
DP = ("y", "x", "c")
PART = ("x", "c")
UNITS = FF // D
TILES_PER = 4 + 3 * UNITS


MESH = pl.DeviceIdType.MESH
LAG = 8
VMEM = 60 << 20


def half_rows(rows, dtype):
    unit = 16 if jnp.dtype(dtype).itemsize == 2 else 8
    return (rows // 2 + unit - 1) // unit * unit


def remote(src, dst, ssem, rsem, **to):
    return pltpu.make_async_remote_copy(
        src_ref=src, dst_ref=dst, send_sem=ssem, recv_sem=rsem, device_id=to, device_id_type=MESH
    )


def greet(zn, y, x, c, z):
    barrier = pltpu.get_barrier_semaphore()
    for to in ({"x": 1 - x}, {"y": 1 - y}, {"c": 1 - c}):
        pl.semaphore_signal(barrier, inc=1, device_id=to, device_id_type=MESH)
    if zn > 1:

        @pl.when(z < zn - 1)
        def _():
            pl.semaphore_signal(barrier, inc=1, device_id={"z": z + 1}, device_id_type=MESH)

        @pl.when(z > 0)
        def _():
            pl.semaphore_signal(barrier, inc=1, device_id={"z": z - 1}, device_id_type=MESH)

        @pl.when((z > 0) & (z < zn - 1))
        def _():
            pl.semaphore_wait(barrier, 5)

        @pl.when((z == 0) | (z == zn - 1))
        def _():
            pl.semaphore_wait(barrier, 4)
    else:
        pl.semaphore_wait(barrier, 3)


def gather_steps(zn, x_ref, o_ref, hold, ssem, rsem, lsem):
    y, x, c, z = [lax.axis_index(n) for n in ALL]
    me = z if zn > 1 else 0
    rows = x_ref.shape[0]
    h0 = half_rows(rows, x_ref.dtype)
    lo, hi = pl.ds(0, h0), pl.ds(h0, rows - h0)
    X, Y, DX, DY, CO, CX, CY, C0, C1, ZU, ZD = range(11)
    nx, ny, nc = {"x": 1 - x}, {"y": 1 - y}, {"c": 1 - c}

    def slot(yy, xx, zz):
        return ((yy * 2 + xx) * 2 + c) * zn + zz

    def copy(kind, k, src, dst, to):
        return remote(src, dst, ssem.at[kind, k], rsem.at[kind, k], **to)

    def block(s):
        return o_ref.at[s]

    local = pltpu.make_async_copy(x_ref, hold, lsem.at[0])
    local.start()
    keep = pltpu.make_async_copy(hold, o_ref.at[slot(y, x, me)], lsem.at[1])

    def spread(zb, src):
        dst = block(slot(y, x, zb))
        copy(X, zb, src, dst, nx).start()
        copy(Y, zb, src, dst, ny).start()
        copy(CO, zb, src, dst, nc).start()

    def up(s):
        zb = z - (s - 1)
        b = block(slot(y, x, zb))
        return copy(ZU, s, x_ref if s == 1 else b, b, {"z": z + 1})

    def down(s):
        zb = z + (s - 1)
        b = block(slot(y, x, zb))
        return copy(ZD, s, x_ref if s == 1 else b, b, {"z": z - 1})

    for s in range(1, zn):

        @pl.when((z < zn - 1) & (z - (s - 1) >= 0))
        def _():
            up(s).start()

        @pl.when((z > 0) & (z + (s - 1) < zn))
        def _():
            down(s).start()

        if s == 1:
            spread(me, x_ref)
            local.wait()
            keep.start()
        yield

        @pl.when(z - s >= 0)
        def _():
            copy(ZU, s, x_ref, x_ref, nx).wait_recv()
            spread(z - s, block(slot(y, x, z - s)))

        @pl.when(z + s < zn)
        def _():
            copy(ZD, s, x_ref, x_ref, nx).wait_recv()
            spread(z + s, block(slot(y, x, z + s)))

    if zn == 1:
        spread(0, x_ref)
        local.wait()
        keep.start()
    order = [lax.rem(z + j, zn) if zn > 1 else 0 for j in range(zn)]
    for zb in order:
        yield
        sx, sy = slot(y, 1 - x, zb), slot(1 - y, x, zb)
        copy(X, zb, x_ref, x_ref, nx).wait_recv()
        copy(DX, zb, o_ref.at[sx, lo], o_ref.at[sx, lo], ny).start()
        copy(CX, zb, block(sx), block(sx), nc).start()
        copy(Y, zb, x_ref, x_ref, nx).wait_recv()
        copy(DY, zb, o_ref.at[sy, hi], o_ref.at[sy, hi], nx).start()
        copy(CY, zb, block(sy), block(sy), nc).start()
    for zb in order:
        yield
        sd = slot(1 - y, 1 - x, zb)
        copy(DX, zb, x_ref.at[lo], x_ref.at[lo], nx).wait_recv()
        copy(C0, zb, o_ref.at[sd, lo], o_ref.at[sd, lo], nc).start()
        copy(DY, zb, x_ref.at[hi], x_ref.at[hi], nx).wait_recv()
        copy(C1, zb, o_ref.at[sd, hi], o_ref.at[sd, hi], nc).start()
    yield
    for zb in range(zn):
        for kind, part in ((CO, x_ref), (CX, x_ref), (CY, x_ref), (C0, x_ref.at[lo]), (C1, x_ref.at[hi])):
            copy(kind, zb, part, part, nx).wait_recv()
        for kind, part in (
            (X, x_ref), (Y, x_ref), (CO, x_ref), (CX, x_ref), (CY, x_ref),
            (DX, x_ref.at[lo]), (DY, x_ref.at[hi]), (C0, x_ref.at[lo]), (C1, x_ref.at[hi]),
        ):
            copy(kind, zb, part, part, nx).wait_send()
    for s in range(1, zn):

        @pl.when((z < zn - 1) & (z - (s - 1) >= 0))
        def _():
            up(s).wait_send()

        @pl.when((z > 0) & (z + (s - 1) < zn))
        def _():
            down(s).wait_send()

    keep.wait()


def run_steps(*parts):
    parts, turn = list(parts), 0
    while parts:
        for part in list(parts):
            if turn >= part[0] and next(part[1], part) is part:
                parts.remove(part)
        turn += 1


def gather_kernel(zn, *refs):
    greet(zn, *[lax.axis_index(n) for n in ALL])
    run_steps((0, gather_steps(zn, *refs)))


def gather_scratch(zn, shape, dtype):
    sems = pltpu.SemaphoreType.DMA((11, zn))
    return [pltpu.VMEM(shape, dtype), sems, sems, pltpu.SemaphoreType.DMA((2,))]


def all_gather(x, zn, ident, name):
    return pl.pallas_call(
        functools.partial(gather_kernel, zn),
        out_shape=jax.ShapeDtypeStruct((8 * zn,) + x.shape, x.dtype),
        in_specs=[pl.BlockSpec(memory_space=pl.ANY)],
        out_specs=pl.BlockSpec(memory_space=pl.ANY),
        scratch_shapes=gather_scratch(zn, x.shape, x.dtype),
        compiler_params=pltpu.CompilerParams(
            collective_id=ident, has_side_effects=True, vmem_limit_bytes=VMEM
        ),
        name=name,
    )(x)


def reduce_steps(zn, p_ref, at, o_ref, to, acc, crecv, dxr, dyr, xr, yr, zur, zdr, ssem, rsem, lsem):
    y, x, c, z = [lax.axis_index(n) for n in ALL]
    me = z if zn > 1 else 0
    rows = acc.shape[1]
    h0 = half_rows(rows, acc.dtype)
    h1 = rows - h0
    X, Y, DX, DY, ZU, ZD, C0 = range(7)
    nx, ny, nc = {"x": 1 - x}, {"y": 1 - y}, {"c": 1 - c}
    kinds = [(y, x), (y, 1 - x), (1 - y, x), (1 - y, 1 - x)]
    step = 32 if rows % 32 == 0 else 16
    zorder = sorted(range(zn), key=lambda zb: (abs(2 * zb - zn + 1), zb), reverse=True)
    out_rows = o_ref.at[pl.ds(to, rows)]

    def slot(k, cc, zz):
        yy, xx = kinds[k]
        return ((yy * 2 + xx) * 2 + cc) * zn + zz

    def copy(kind, k, src, dst, to):
        return remote(src, dst, ssem.at[kind, k], rsem.at[kind, k], **to)

    def load(k, zb):
        b = k * zn + zb
        return pltpu.make_async_copy(p_ref.at[slot(k, c, zb), pl.ds(at, rows)], acc.at[b], lsem.at[b])

    def across(k, zb):
        source = p_ref.at[slot(k, 1 - c, zb), pl.ds(at, rows)]
        return copy(C0 + k, zb, source, crecv.at[k * zn + zb], nc)

    def add(dst, start, count, terms):
        size = step if count % step == 0 else 16

        @pl.loop(0, count // size)
        def _(i):
            here = pl.ds(pl.multiple_of(start + i * size, 16), size)
            total = None
            for ref, base in terms:
                part = ref[pl.ds(pl.multiple_of(start - base + i * size, 16), size), :].astype(jnp.float32)
                total = part if total is None else total + part
            dst[here, :] = total.astype(dst.dtype)

    for k in (3, 1, 2, 0):
        for zb in zorder:
            across(k, zb).start()
            load(k, zb).start()

    def ready(k, zb):
        load(k, zb).wait()
        across(k, zb).wait_recv()

    for zb in zorder:
        yield
        ready(3, zb)
        b = 3 * zn + zb
        add(acc.at[b], 0, rows, [(acc.at[b], 0), (crecv.at[b], 0)])
        copy(DX, zb, acc.at[b, pl.ds(0, h0)], dxr.at[zb], nx).start()
        copy(DY, zb, acc.at[b, pl.ds(h0, h1)], dyr.at[zb], ny).start()
    for zb in zorder:
        yield
        ready(1, zb)
        b = zn + zb
        add(acc.at[b], 0, h0, [(acc.at[b], 0), (crecv.at[b], 0)])
        copy(DY, zb, dyr.at[zb], dyr.at[zb], ny).wait_recv()
        add(acc.at[b], h0, h1, [(acc.at[b], 0), (crecv.at[b], 0), (dyr.at[zb], h0)])
        copy(X, zb, acc.at[b], xr.at[zb], nx).start()
        yield
        ready(2, zb)
        b = 2 * zn + zb
        add(acc.at[b], h0, h1, [(acc.at[b], 0), (crecv.at[b], 0)])
        copy(DX, zb, dxr.at[zb], dxr.at[zb], nx).wait_recv()
        add(acc.at[b], 0, h0, [(acc.at[b], 0), (crecv.at[b], 0), (dxr.at[zb], 0)])
        copy(Y, zb, acc.at[b], yr.at[zb], ny).start()

    def column(zb):
        return [(acc.at[zb], 0), (crecv.at[zb], 0), (xr.at[zb], 0), (yr.at[zb], 0)]

    for zb in zorder:
        yield
        ready(0, zb)
        copy(X, zb, acc.at[zb], xr.at[zb], nx).wait_recv()
        copy(Y, zb, acc.at[zb], yr.at[zb], ny).wait_recv()
        if zn == 1:
            add(out_rows, 0, rows, column(0))
            continue

        def upward(zb=zb):
            return copy(ZU, zb, acc.at[zb], zur.at[zb], {"z": z + 1})

        def downward(zb=zb):
            return copy(ZD, zb, acc.at[zb], zdr.at[zb], {"z": z - 1})

        @pl.when(z == zb)
        def _():
            add(acc.at[zb], 0, rows, column(zb))

        @pl.when((z < zb) & (z == 0))
        def _():
            add(acc.at[zb], 0, rows, column(zb))
            upward().start()

        @pl.when((z < zb) & (z > 0))
        def _():
            upward().wait_recv()
            add(acc.at[zb], 0, rows, column(zb) + [(zur.at[zb], 0)])
            upward().start()

        @pl.when((z > zb) & (z == zn - 1))
        def _():
            add(acc.at[zb], 0, rows, column(zb))
            downward().start()

        @pl.when((z > zb) & (z < zn - 1))
        def _():
            downward().wait_recv()
            add(acc.at[zb], 0, rows, column(zb) + [(zdr.at[zb], 0)])
            downward().start()

    yield
    if zn > 1:

        @pl.when(z == 0)
        def _():
            copy(ZD, me, acc.at[me], zdr.at[me], {"z": z + 1}).wait_recv()
            add(out_rows, 0, rows, [(acc.at[me], 0), (zdr.at[me], 0)])

        @pl.when(z == zn - 1)
        def _():
            copy(ZU, me, acc.at[me], zur.at[me], {"z": z - 1}).wait_recv()
            add(out_rows, 0, rows, [(acc.at[me], 0), (zur.at[me], 0)])

        @pl.when((z > 0) & (z < zn - 1))
        def _():
            copy(ZD, me, acc.at[me], zdr.at[me], {"z": z + 1}).wait_recv()
            copy(ZU, me, acc.at[me], zur.at[me], {"z": z + 1}).wait_recv()
            add(out_rows, 0, rows, [(acc.at[me], 0), (zdr.at[me], 0), (zur.at[me], 0)])

    for zb in range(zn):
        for k in range(4):
            across(k, zb).wait_send()
        copy(DX, zb, dxr.at[zb], dxr.at[zb], nx).wait_send()
        copy(DY, zb, dyr.at[zb], dyr.at[zb], ny).wait_send()
        copy(X, zb, xr.at[zb], xr.at[zb], nx).wait_send()
        copy(Y, zb, yr.at[zb], yr.at[zb], ny).wait_send()
        if zn > 1:

            @pl.when(z < zb)
            def _():
                copy(ZU, zb, zur.at[zb], zur.at[zb], {"z": z + 1}).wait_send()

            @pl.when(z > zb)
            def _():
                copy(ZD, zb, zdr.at[zb], zdr.at[zb], {"z": z - 1}).wait_send()


def segments_of(rows):
    if rows < 192:
        return [(0, rows)]
    first = (rows // 2 + 31) // 32 * 32
    return [(0, first), (first, rows - first)]


def reduce_plan(zn, p_refs, o_ref, scratch):
    parts, base = [], 0
    for p_ref in p_refs:
        for at, rows in segments_of(p_ref.shape[1]):
            mine, scratch = scratch[:11], scratch[11:]
            parts.append((LAG * len(parts), reduce_steps(zn, p_ref, at, o_ref, base + at, *mine)))
        base += p_ref.shape[1]
    return parts


def reduce_kernel(zn, p_ref, o_ref, *scratch):
    greet(zn, *[lax.axis_index(n) for n in ALL])
    run_steps(*reduce_plan(zn, [p_ref], o_ref, scratch))


def reduce_scratch(zn, rows, cols, dtype):
    entries = []
    for _, n in segments_of(rows):
        h0 = half_rows(n, dtype)
        sems = pltpu.SemaphoreType.DMA((10, zn))
        counts = [(4 * zn, n), (4 * zn, n), (zn, h0), (zn, n - h0)] + [(zn, n)] * 4
        entries += [pltpu.VMEM((m, r, cols), dtype) for m, r in counts]
        entries += [sems, sems, pltpu.SemaphoreType.DMA((4 * zn,))]
    return entries


def reduce_scatter(p, zn, ident, name, out_dtype=None):
    count, rows, cols = p.shape
    return pl.pallas_call(
        functools.partial(reduce_kernel, zn),
        out_shape=jax.ShapeDtypeStruct((rows, cols), out_dtype or p.dtype),
        in_specs=[pl.BlockSpec(memory_space=pl.ANY)],
        out_specs=pl.BlockSpec(memory_space=pltpu.VMEM),
        scratch_shapes=reduce_scratch(zn, rows, cols, p.dtype),
        compiler_params=pltpu.CompilerParams(
            collective_id=ident, has_side_effects=True, vmem_limit_bytes=VMEM
        ),
        name=name,
    )(p)


def both_kernel(inputs, zr, zg, *refs):
    p_refs, (x_ref, r_ref, o_ref), scratch = refs[:inputs], refs[inputs : inputs + 3], refs[inputs + 3 :]
    greet(max(zr, zg), *[lax.axis_index(n) for n in ALL])
    gather = (0, gather_steps(zg, x_ref, o_ref, *scratch[-4:]))
    run_steps(gather, *reduce_plan(zr, p_refs, r_ref, scratch[:-4]))


def scatter_and_gather(parts, zr, x, zg, ident, name):
    inputs = len(parts)
    count, each, cols = parts[0].shape
    rows, dtype = inputs * each, parts[0].dtype
    return pl.pallas_call(
        functools.partial(both_kernel, inputs, zr, zg),
        out_shape=(
            jax.ShapeDtypeStruct((rows, cols), dtype),
            jax.ShapeDtypeStruct((8 * zg,) + x.shape, x.dtype),
        ),
        in_specs=[pl.BlockSpec(memory_space=pl.ANY)] * (inputs + 1),
        out_specs=(pl.BlockSpec(memory_space=pltpu.VMEM), pl.BlockSpec(memory_space=pl.ANY)),
        scratch_shapes=reduce_scratch(zr, each, cols, dtype) * inputs
        + gather_scratch(zg, x.shape, x.dtype),
        compiler_params=pltpu.CompilerParams(
            collective_id=ident, has_side_effects=True, vmem_limit_bytes=VMEM
        ),
        name=name,
    )(*parts, x)


def greet_pair(x, c):
    barrier = pltpu.get_barrier_semaphore()
    for to in ({"x": 1 - x}, {"c": 1 - c}):
        pl.semaphore_signal(barrier, inc=1, device_id=to, device_id_type=MESH)
    pl.semaphore_wait(barrier, 2)


def keys_gather_kernel(x_ref, o_ref, hold, ssem, rsem, lsem):
    x, c = lax.axis_index("x"), lax.axis_index("c")
    me, far = x * 2 + c, (1 - x) * 2 + c
    nx, nc = {"x": 1 - x}, {"c": 1 - c}
    load = pltpu.make_async_copy(x_ref, hold, lsem.at[0])
    load.start()
    greet_pair(x, c)
    out = remote(x_ref, o_ref.at[me], ssem.at[0], rsem.at[0], **nx)
    out.start()
    near = remote(x_ref, o_ref.at[me], ssem.at[1], rsem.at[1], **nc)
    near.start()
    load.wait()
    keep = pltpu.make_async_copy(hold, o_ref.at[me], lsem.at[1])
    keep.start()
    out.wait_recv()
    on = remote(o_ref.at[far], o_ref.at[far], ssem.at[2], rsem.at[2], **nc)
    on.start()
    near.wait_recv()
    on.wait_recv()
    keep.wait()
    out.wait_send()
    near.wait_send()
    on.wait_send()


def keys_gather(v, ident):
    sems = pltpu.SemaphoreType.DMA((3,))
    return pl.pallas_call(
        keys_gather_kernel,
        out_shape=jax.ShapeDtypeStruct((4,) + v.shape, v.dtype),
        in_specs=[pl.BlockSpec(memory_space=pl.ANY)],
        out_specs=pl.BlockSpec(memory_space=pl.ANY),
        scratch_shapes=[pltpu.VMEM(v.shape, v.dtype), sems, sems, pltpu.SemaphoreType.DMA((2,))],
        compiler_params=pltpu.CompilerParams(
            collective_id=ident, has_side_effects=True, vmem_limit_bytes=VMEM
        ),
        name="keys_gather",
    )(v)


def keys_reduce_kernel(p_ref, o_ref, acc, crecv, xr, ssem, rsem, lsem):
    x, c = lax.axis_index("x"), lax.axis_index("c")
    nx, nc = {"x": 1 - x}, {"c": 1 - c}
    rows = p_ref.shape[1]
    places = [(1 - x) * 2, x * 2]
    loads = [pltpu.make_async_copy(p_ref.at[places[i] + c], acc.at[i], lsem.at[i]) for i in range(2)]
    for load in loads:
        load.start()
    greet_pair(x, c)
    across = [
        remote(p_ref.at[places[i] + 1 - c], crecv.at[i], ssem.at[i], rsem.at[i], **nc) for i in range(2)
    ]
    for copy in across:
        copy.start()

    def add(dst, terms):
        @pl.loop(0, rows // 16)
        def _(i):
            at = pl.ds(pl.multiple_of(i * 16, 16), 16)
            total = terms[0][at, :].astype(jnp.float32)
            for term in terms[1:]:
                total = total + term[at, :].astype(jnp.float32)
            dst[at, :] = total.astype(dst.dtype)

    loads[0].wait()
    across[0].wait_recv()
    add(acc.at[0], [acc.at[0], crecv.at[0]])
    out = remote(acc.at[0], xr, ssem.at[2], rsem.at[2], **nx)
    out.start()
    loads[1].wait()
    across[1].wait_recv()
    out.wait_recv()
    add(o_ref, [acc.at[1], crecv.at[1], xr])
    for copy in across + [out]:
        copy.wait_send()


def keys_reduce(p, ident):
    block = p.shape[1:]
    sems = pltpu.SemaphoreType.DMA((3,))
    return pl.pallas_call(
        keys_reduce_kernel,
        out_shape=jax.ShapeDtypeStruct(block, p.dtype),
        in_specs=[pl.BlockSpec(memory_space=pl.ANY)],
        out_specs=pl.BlockSpec(memory_space=pltpu.VMEM),
        scratch_shapes=[
            pltpu.VMEM((2,) + block, p.dtype), pltpu.VMEM((2,) + block, p.dtype),
            pltpu.VMEM(block, p.dtype), sems, sems, pltpu.SemaphoreType.DMA((2,)),
        ],
        compiler_params=pltpu.CompilerParams(
            collective_id=ident, has_side_effects=True, vmem_limit_bytes=VMEM
        ),
        name="keys_reduce",
    )(p)


def fits():
    return [lax.axis_size(n) for n in ALL] == [2, 2, 2, 4]


def gather_all(v, ident, name):
    if fits():
        return all_gather(v, 4, ident, name)
    return lax.all_gather(v, ALL, axis=0)


def gather_plane(v, ident, name):
    if fits():
        return all_gather(v, 1, ident, name)
    return lax.all_gather(v, DP, axis=0)


def scatter_all(p, ident, name):
    if fits():
        return reduce_scatter(p, 4, ident, name)
    return lax.psum_scatter(p, ALL, scatter_dimension=0)


def scatter_plane(p, ident, name):
    if fits():
        return reduce_scatter(p, 1, ident, name)
    return lax.psum_scatter(p, DP, scatter_dimension=0)


def keys_all_gather(v):
    if fits():
        return keys_gather(v, 11).reshape(-1, v.shape[1])
    return lax.all_gather(v, PART, axis=0, tiled=True)


def keys_sum_scatter(p):
    if fits():
        return keys_reduce(p.reshape(4, -1, p.shape[1]), 12)
    return lax.psum_scatter(p, PART, scatter_dimension=0, tiled=True)


def tile_spec(dp, deep, tile_rows, index, local=None):
    def place(t):
        j = index(t)
        return (j % dp, 0, j // dp if local is None else local, 0, 0)

    return pl.BlockSpec((None, deep, None, tile_rows, D), place)


def weight_specs(weights, *groups):
    arrays, specs = [], []
    for first, offset in groups:
        array, local = weights[first // weights[0][0].shape[0]]
        dp, deep, _, tile_rows, _ = array.shape
        arrays.append(array)
        specs.append(
            tile_spec(dp, deep, tile_rows, lambda t, f=first, o=offset: f + o(t), local)
        )
    return arrays, specs


def whole(shape):
    return pl.BlockSpec(shape, lambda t: (0,) * len(shape))


def dot_nn(a, b):
    return lax.dot_general(a, b, (((1,), (0,)), ((), ())), preferred_element_type=jnp.float32)


def dot_nt(a, b):
    return lax.dot_general(a, b, (((1,), (1,)), ((), ())), preferred_element_type=jnp.float32)


def dot_tn(a, b):
    return lax.dot_general(a, b, (((0,), (0,)), ((), ())), preferred_element_type=jnp.float32)


def turned(u, cos, sin):
    lane = lax.broadcasted_iota(jnp.int32, (u.shape[0], 128), 1)
    low = (lane % HD) < HD // 2
    parts = []
    for i in range(D // 128):
        v = u[:, i * 128 : (i + 1) * 128]
        other = jnp.where(low, pltpu.roll(v, 128 - HD // 2, 1), pltpu.roll(v, HD // 2, 1))
        parts.append(v * cos + other * sin)
    return jnp.concatenate(parts, axis=1)


def project_kernel(x_ref, g_ref, cos_ref, sin_ref, w_ref, q_ref, kv_ref, a_ref):
    t = pl.program_id(0)

    @pl.when(t == 0)
    def _():
        a_ref[...] = root_norm(x_ref[...], g_ref[...]).astype(jnp.bfloat16)

    m = dot_nn(a_ref[...], w_ref[...].reshape(D, D))

    @pl.when(t == 0)
    def _():
        q_ref[...] = turned(m, cos_ref[...], sin_ref[...]).astype(jnp.bfloat16)

    @pl.when(t == 1)
    def _():
        kv_ref[...] = turned(m, cos_ref[...], sin_ref[...]).astype(jnp.bfloat16)

    @pl.when(t == 2)
    def _():
        kv_ref[...] = m.astype(jnp.bfloat16)


def project(x, gain, cos, sin, weights):
    rows = x.shape[0]
    arrays, specs = weight_specs(weights, (0, lambda t: t))
    return pl.pallas_call(
        project_kernel,
        grid=(3,),
        out_shape=(
            jax.ShapeDtypeStruct((rows, D), jnp.bfloat16),
            jax.ShapeDtypeStruct((2, rows, D), jnp.bfloat16),
        ),
        in_specs=[
            whole((rows, D)), whole((1, D)), whole((rows, 128)), whole((rows, 128)), *specs,
        ],
        out_specs=(
            whole((rows, D)),
            pl.BlockSpec((None, rows, D), lambda t: (jnp.maximum(t - 1, 0), 0, 0)),
        ),
        scratch_shapes=[pltpu.VMEM((rows, D), jnp.bfloat16)],
        compiler_params=pltpu.CompilerParams(vmem_limit_bytes=VMEM),
        name="project",
    )(x, gain, cos, sin, *arrays)


def mask_bias(bias_ref, kseg_ref, qseg_ref, qpos_ref):
    kpos = lax.broadcasted_iota(jnp.int32, bias_ref.shape, 0)
    allowed = (kpos <= qpos_ref[...]) & (kseg_ref[...] == qseg_ref[...])
    bias_ref[...] = jnp.where(allowed, 0.0, MASKED)


def head_lanes(shape, head):
    return (lax.broadcasted_iota(jnp.int32, shape, 1) // HD) == head


def attend_kernel(q_ref, k_ref, v_ref, kseg_ref, qseg_ref, qpos_ref, o_ref, lse_ref, bias_ref):
    @pl.when(pl.program_id(0) == 0)
    def _():
        mask_bias(bias_ref, kseg_ref, qseg_ref, qpos_ref)

    length = bias_ref.shape[0]
    q = q_ref[...] * HD ** (-0.5)
    k, v = k_ref[...].reshape(length, 128), v_ref[...].reshape(length, 128)
    outs = []
    for head in range(2):
        mine = head_lanes(q.shape, head)
        s = dot_nt(k, jnp.where(mine, q, jnp.zeros_like(q))) + bias_ref[...]
        top = jnp.max(s, axis=0, keepdims=True)
        e = jnp.exp(s - top)
        total = jnp.sum(e, axis=0, keepdims=True)
        p = (e * (1.0 / total)).astype(jnp.bfloat16)
        outs.append(dot_tn(p, v))
        lse_ref[head : head + 1, :] = top + jnp.log(total)
    o_ref[...] = jnp.where(head_lanes(outs[0].shape, 0), outs[0], outs[1]).astype(jnp.bfloat16)


def attend_specs(rows, parts):
    length = parts * rows
    pair = pl.BlockSpec((rows, 128), lambda t: (0, t))
    return pair, [
        pair,
        pl.BlockSpec((parts, None, rows, 128), lambda t: (0, 0, 0, t)),
        pl.BlockSpec((parts, None, rows, 128), lambda t: (0, 1, 0, t)),
        whole((length, 1)), whole((1, rows)), whole((1, rows)),
    ]


def attend(q, kv, kseg, qseg, qpos):
    rows, parts = q.shape[0], kv.shape[0]
    pair, specs = attend_specs(rows, parts)
    return pl.pallas_call(
        attend_kernel,
        grid=(HEADS // 2,),
        out_shape=(
            jax.ShapeDtypeStruct((rows, D), jnp.bfloat16),
            jax.ShapeDtypeStruct((HEADS // 2, 8, rows), jnp.float32),
        ),
        in_specs=specs,
        out_specs=(pair, pl.BlockSpec((None, 8, rows), lambda t: (t, 0, 0))),
        scratch_shapes=[pltpu.VMEM((parts * rows, rows), jnp.float32)],
        compiler_params=pltpu.CompilerParams(vmem_limit_bytes=VMEM),
        name="attend",
    )(q, kv, kv, kseg, qseg, qpos)


def feed_kernel(x_ref, o_ref, g_ref, wo_ref, wg_ref, wu_ref, wd_ref, mid_ref, out_ref, b_ref):
    t = pl.program_id(0)

    @pl.when(t == 0)
    def _():
        mid = x_ref[...] + dot_nn(o_ref[...], wo_ref[...].reshape(D, D))
        mid_ref[...] = mid
        out_ref[...] = mid
        b_ref[...] = root_norm(mid, g_ref[...]).astype(jnp.bfloat16)

    @pl.when(t > 0)
    def _():
        gate = dot_nn(b_ref[...], wg_ref[...].reshape(D, D))
        up = dot_nn(b_ref[...], wu_ref[...].reshape(D, D))
        h = (gate * jax.nn.sigmoid(gate) * up).astype(jnp.bfloat16)
        out_ref[...] += dot_nn(h, wd_ref[...].reshape(D, D))


def feed(x, o, gain, weights):
    rows = x.shape[0]
    unit = lambda t: jnp.maximum(t - 1, 0)
    arrays, specs = weight_specs(
        weights, (3, lambda t: 0 * t), (4, unit), (4 + UNITS, unit), (4 + 2 * UNITS, unit)
    )
    state = jax.ShapeDtypeStruct((rows, D), jnp.float32)
    return pl.pallas_call(
        feed_kernel,
        grid=(1 + UNITS,),
        out_shape=(state, state),
        in_specs=[
            whole((rows, D)), whole((rows, D)), whole((1, D)), *specs,
        ],
        out_specs=(whole((rows, D)), whole((rows, D))),
        scratch_shapes=[pltpu.VMEM((rows, D), jnp.bfloat16)],
        compiler_params=pltpu.CompilerParams(vmem_limit_bytes=VMEM),
        name="feed",
    )(x, o, gain, *arrays)


def feed_back_kernel(
    groups, dy_ref, mid_ref, g_ref, o_ref, wo_ref, wg_ref, wu_ref, wd_ref, dx_ref, do_ref, dgain_ref,
    *refs,
):
    grad_refs, (b_ref, bt_ref, e_ref, dg_ref, du_ref, db_ref) = refs[:-6], refs[-6:]
    t = pl.program_id(0)
    last = pl.num_programs(0) - 1

    def emit(kind, g):
        ref = grad_refs[groups[kind]]
        ref[...] = g.astype(jnp.bfloat16).reshape(ref.shape)

    @pl.when(t == 0)
    def _():
        b = root_norm(mid_ref[...], g_ref[...])
        b_ref[...] = b.astype(jnp.bfloat16)
        bt_ref[...] = b.T.astype(jnp.bfloat16)
        e_ref[...] = dy_ref[...].astype(jnp.bfloat16)
        db_ref[...] = jnp.zeros_like(db_ref)

    @pl.when((t % 3 == 0) & (t < last))
    def _():
        gate = dot_nn(b_ref[...], wg_ref[...].reshape(D, D))
        up = dot_nn(b_ref[...], wu_ref[...].reshape(D, D))
        sigma = jax.nn.sigmoid(gate)
        h = (gate * sigma * up).astype(jnp.bfloat16)
        emit(0, dot_tn(h, e_ref[...]))
        dh = dot_nt(e_ref[...], wd_ref[...].reshape(D, D))
        dg_ref[...] = (dh * up * sigma * (1.0 + gate * (1.0 - sigma))).astype(jnp.bfloat16)
        du_ref[...] = (dh * gate * sigma).astype(jnp.bfloat16)

    @pl.when(t % 3 == 1)
    def _():
        emit(1, dot_nn(bt_ref[...], dg_ref[...]))
        db_ref[...] += dot_nt(dg_ref[...], wg_ref[...].reshape(D, D))

    @pl.when(t % 3 == 2)
    def _():
        emit(2, dot_nn(bt_ref[...], du_ref[...]))
        db_ref[...] += dot_nt(du_ref[...], wu_ref[...].reshape(D, D))

    @pl.when(t == last)
    def _():
        back, gain_back = norm_back(mid_ref[...], g_ref[...], db_ref[...])
        dx = dy_ref[...] + back
        dx_ref[...] = dx
        dgain_ref[...] = jnp.broadcast_to(gain_back[None, :], dgain_ref.shape)
        e1 = dx.astype(jnp.bfloat16)
        emit(3, dot_tn(o_ref[...], e1))
        do_ref[...] = dot_nt(e1, wo_ref[...].reshape(D, D)).astype(jnp.bfloat16)


def feed_back(dy, mid, gain, o, weights):
    rows = dy.shape[0]
    dp, deep, _, tile_rows, _ = weights[0][0].shape
    unit = lambda t: jnp.minimum(t // 3, UNITS - 1)
    arrays, specs = weight_specs(
        weights, (3, lambda t: 0 * t), (4, unit), (4 + UNITS, unit), (4 + 2 * UNITS, unit)
    )
    firsts = [4 + 2 * UNITS, 4, 4 + UNITS, 3]
    groups = [first // dp for first in firsts]

    def grad_tile(group, t):
        kinds = [k for k in range(3) if groups[k] == group]
        s, k = unit(t), t % 3
        tile = firsts[kinds[0]] + jnp.where(k < kinds[0], jnp.maximum(s - 1, 0), s)
        for kind in kinds[1:]:
            tile = jnp.where(k >= kind, firsts[kind] + s, tile)
        final = 3 if groups[3] == group else firsts[kinds[-1]] + UNITS - 1
        return jnp.where(t == 3 * UNITS, final, tile)

    return pl.pallas_call(
        functools.partial(feed_back_kernel, groups),
        grid=(3 * UNITS + 1,),
        out_shape=(
            jax.ShapeDtypeStruct((rows, D), jnp.float32),
            jax.ShapeDtypeStruct((rows, D), jnp.bfloat16),
            jax.ShapeDtypeStruct((8, D), jnp.float32),
        )
        + (jax.ShapeDtypeStruct((dp, deep, 1, tile_rows, D), jnp.bfloat16),) * len(weights),
        in_specs=[
            whole((rows, D)), whole((rows, D)), whole((1, D)), whole((rows, D)), *specs,
        ],
        out_specs=(whole((rows, D)), whole((rows, D)), whole((8, D)))
        + tuple(
            tile_spec(dp, deep, tile_rows, functools.partial(grad_tile, group), 0)
            for group in range(len(weights))
        ),
        scratch_shapes=[
            pltpu.VMEM((rows, D), jnp.bfloat16), pltpu.VMEM((D, rows), jnp.bfloat16),
            pltpu.VMEM((rows, D), jnp.bfloat16), pltpu.VMEM((rows, D), jnp.bfloat16),
            pltpu.VMEM((rows, D), jnp.bfloat16), pltpu.VMEM((rows, D), jnp.float32),
        ],
        compiler_params=pltpu.CompilerParams(vmem_limit_bytes=VMEM),
        name="feed_back",
    )(dy, mid, gain, o, *arrays)


def attend_back_kernel(
    q_ref, k_ref, v_ref, kseg_ref, qseg_ref, qpos_ref, do_ref, lse_ref, dq_ref, dkv_ref, bias_ref
):
    @pl.when(pl.program_id(0) == 0)
    def _():
        mask_bias(bias_ref, kseg_ref, qseg_ref, qpos_ref)

    length = bias_ref.shape[0]
    parts, rows = dkv_ref.shape[0], q_ref.shape[0]
    q, do = q_ref[...] * HD ** (-0.5), do_ref[...]
    k, v = k_ref[...].reshape(length, 128), v_ref[...].reshape(length, 128)
    dqs, dk, dv = [], None, None
    for head in range(2):
        mine = head_lanes(q.shape, head)
        qm = jnp.where(mine, q, jnp.zeros_like(q))
        dom = jnp.where(mine, do, jnp.zeros_like(do))
        s = dot_nt(k, qm) + bias_ref[...]
        p = jnp.exp(s - lse_ref[head : head + 1, :])
        dp = dot_nt(v, dom)
        delta = jnp.sum(p * dp, axis=0, keepdims=True)
        ds = (p * (dp - delta)).astype(jnp.bfloat16)
        dv_part = dot_nn(p.astype(jnp.bfloat16), dom)
        dk_part = dot_nn(ds, qm)
        dv = dv_part if dv is None else dv + dv_part
        dk = dk_part if dk is None else dk + dk_part
        dqs.append(dot_tn(ds, k))
    dq_ref[...] = jnp.where(head_lanes(dqs[0].shape, 0), dqs[0], dqs[1]) * HD ** (-0.5)
    dkv_ref[:, 0] = dk.astype(jnp.bfloat16).reshape(parts, rows, 128)
    dkv_ref[:, 1] = dv.astype(jnp.bfloat16).reshape(parts, rows, 128)


def attend_back(q, kv, kseg, qseg, qpos, do, lse):
    rows, parts = q.shape[0], kv.shape[0]
    pair, specs = attend_specs(rows, parts)
    return pl.pallas_call(
        attend_back_kernel,
        grid=(HEADS // 2,),
        out_shape=(
            jax.ShapeDtypeStruct((rows, D), jnp.float32),
            jax.ShapeDtypeStruct((parts, 2, rows, D), jnp.bfloat16),
        ),
        in_specs=specs + [pair, pl.BlockSpec((None, 8, rows), lambda t: (t, 0, 0))],
        out_specs=(pair, pl.BlockSpec((parts, 2, rows, 128), lambda t: (0, 0, 0, t))),
        scratch_shapes=[pltpu.VMEM((parts * rows, rows), jnp.float32)],
        compiler_params=pltpu.CompilerParams(vmem_limit_bytes=VMEM),
        name="attend_back",
    )(q, kv, kv, kseg, qseg, qpos, do, lse)


def project_back_kernel(
    dx_ref, x_ref, g_ref, cos_ref, sin_ref, dq_ref, dkv_ref, w_ref, held_ref,
    grad_ref, out_ref, dgain_ref, a_ref, dm_ref, da_ref,
):
    t = pl.program_id(0)
    deep, tile_rows = grad_ref.shape[0], grad_ref.shape[1]

    @pl.when(t == 0)
    def _():
        a_ref[...] = root_norm(x_ref[...], g_ref[...]).astype(jnp.bfloat16)
        da_ref[...] = jnp.zeros_like(da_ref)
        dm_ref[...] = turned(dq_ref[...], cos_ref[...], -sin_ref[...]).astype(jnp.bfloat16)

    @pl.when(t == 1)
    def _():
        dk = dkv_ref[0].astype(jnp.float32)
        dm_ref[...] = turned(dk, cos_ref[...], -sin_ref[...]).astype(jnp.bfloat16)

    @pl.when(t == 2)
    def _():
        dm_ref[...] = dkv_ref[1]

    grad = dot_tn(a_ref[...], dm_ref[...])
    grad_ref[...] = grad.astype(jnp.bfloat16).reshape(deep, tile_rows, D)
    da_ref[...] += dot_nt(dm_ref[...], w_ref[...].reshape(D, D))

    @pl.when(t == 2)
    def _():
        back, gain_back = norm_back(x_ref[...], g_ref[...], da_ref[...])
        out_ref[...] = dx_ref[...] + back
        dgain_ref[...] = jnp.broadcast_to(gain_back[None, :], dgain_ref.shape)


def project_back(dx, x, gain, cos, sin, dq, dkv, weights, grads):
    rows = x.shape[0]
    dp, deep, _, tile_rows, _ = weights[0][0].shape
    arrays, specs = weight_specs(weights, (0, lambda t: t))
    return pl.pallas_call(
        project_back_kernel,
        grid=(3,),
        out_shape=(
            jax.ShapeDtypeStruct(grads.shape, grads.dtype),
            jax.ShapeDtypeStruct((rows, D), jnp.float32),
            jax.ShapeDtypeStruct((8, D), jnp.float32),
        ),
        in_specs=[
            whole((rows, D)), whole((rows, D)), whole((1, D)), whole((rows, 128)),
            whole((rows, 128)), whole((rows, D)), whole((2, rows, D)),
            *specs,
            pl.BlockSpec(memory_space=pl.ANY),
        ],
        out_specs=(
            tile_spec(dp, deep, tile_rows, lambda t: t, 0), whole((rows, D)), whole((8, D)),
        ),
        scratch_shapes=[
            pltpu.VMEM((rows, D), jnp.bfloat16), pltpu.VMEM((rows, D), jnp.bfloat16),
            pltpu.VMEM((rows, D), jnp.float32),
        ],
        input_output_aliases={8: 0},
        compiler_params=pltpu.CompilerParams(vmem_limit_bytes=VMEM),
        name="project_back",
    )(dx, x, gain, cos, sin, dq, dkv, *arrays, grads)


def layer_forward(state, weights, layer, gains, cos, sin, marks):
    rows = state.shape[0]
    q, kv = project(state, gains[2 * layer : 2 * layer + 1], cos, sin, weights)
    kv = keys_all_gather(kv.reshape(2 * rows, D)).reshape(-1, 2, rows, D)
    o, lse = attend(q, kv, *marks)
    mid, out = feed(state, o, gains[2 * layer + 1 : 2 * layer + 2], weights)
    return out, (state, mid, q, kv, lse, o)


def layer_backward(grad, kept, weights, layer, gains, cos, sin, marks):
    state, mid, q, kv, lse, o = kept
    rows = state.shape[0]
    dx, do, feed_gain, *grads = feed_back(
        grad, mid, gains[2 * layer + 1 : 2 * layer + 2], o, weights
    )
    dq, dkv = attend_back(q, kv, *marks, do, lse)
    dkv = keys_sum_scatter(dkv.reshape(-1, D)).reshape(2, rows, D)
    grads[0], dx, input_gain = project_back(
        dx, state, gains[2 * layer : 2 * layer + 1], cos, sin, dq, dkv, weights, grads[0]
    )
    return dx, grads, [input_gain[0], feed_gain[0]]


def padded(v):
    count = -(-v.shape[0] // 2048) * 2048
    return jnp.pad(v, (0, count - v.shape[0])).reshape(-1, 128)


def place_kernel(slot_ref, mine_ref, w_ref, o_ref):
    g = pl.program_id(0)
    count = o_ref.shape[0]
    for i in range(count):
        t = g * count + i
        o_ref[i] = jnp.where(mine_ref[t] > 0, w_ref[slot_ref[t]], 0.0).astype(jnp.bfloat16)


def place_tiles(tile_weight, slots, mine, dp_size):
    count = slots.shape[0] // dp_size
    cap, rows, cols = tile_weight.shape
    return pl.pallas_call(
        place_kernel,
        grid_spec=pltpu.PrefetchScalarGridSpec(
            num_scalar_prefetch=2,
            grid=(dp_size,),
            in_specs=[pl.BlockSpec((cap, rows, cols), lambda g, *_: (0, 0, 0))],
            out_specs=pl.BlockSpec((count, rows, cols), lambda g, *_: (g, 0, 0)),
        ),
        out_shape=jax.ShapeDtypeStruct((dp_size * count, rows, cols), jnp.bfloat16),
        compiler_params=pltpu.CompilerParams(vmem_limit_bytes=VMEM),
        name="place_tiles",
    )(slots, mine, tile_weight)


def shards(
    tokens,
    segments,
    completion,
    targets,
    owners,
    step_count,
    tile_weight,
    tile_first,
    tile_second,
    table_weight,
    table_first,
    table_second,
    head_weight,
    head_first,
    head_second,
    gain_weight,
    gain_first,
    gain_second,
):
    a_size, b_size, rep_size = lax.axis_size("y"), lax.axis_size(PART), lax.axis_size("z")
    a_index, b_index, rep_index = lax.axis_index("y"), lax.axis_index(PART), lax.axis_index("z")
    dp_size = a_size * b_size
    devices = dp_size * rep_size
    dp_index = a_index * b_size + b_index
    device = dp_index * rep_size + rep_index
    rows = tokens.shape[1]
    length = segments.shape[1]
    comp = completion.shape[1]
    slots_cap, tile_rows = tile_weight.shape[:2]
    tile_count = owners.shape[0]
    home_tiles = tile_count // dp_size
    vocab_rows = table_weight.shape[0]
    vocab_start = device * vocab_rows
    sequence = a_index * rep_size + rep_index

    own_part = jnp.concatenate(
        [
            tokens[0],
            lax.dynamic_slice_in_dim(segments[0], rep_index * rows, rows),
            lax.dynamic_slice_in_dim(completion[0], rep_index * (comp // rep_size), comp // rep_size),
            lax.dynamic_slice_in_dim(targets[0], rep_index * (comp // rep_size), comp // rep_size),
        ]
    )
    slots = tile_slots(owners)
    mine = owners == dp_index
    per = TILES_PER // dp_size
    home_ids = (
        jnp.arange(LAYERS)[None, :, None] * TILES_PER
        + jnp.arange(per)[None, None, :] * dp_size
        + jnp.arange(dp_size)[:, None, None]
    ).reshape(-1)
    home_mine = jnp.take(mine, home_ids)
    home_slots = jnp.where(home_mine, jnp.take(slots, home_ids), 0)
    placed = place_tiles(tile_weight, home_slots, home_mine.astype(jnp.int32), dp_size)
    placed = placed.reshape(dp_size, -1, D)
    if fits():
        home, packed = scatter_and_gather([placed], 1, padded(own_part), 4, 0, "home_and_ids")
    else:
        home = lax.psum_scatter(placed, DP, scatter_dimension=0)
        packed = lax.all_gather(padded(own_part), ALL, axis=0)
    packed = packed.reshape(devices, -1)[:, : own_part.shape[0]]
    packed = packed.reshape(dp_size, rep_size, -1)
    tokens_all = packed[:, :, :rows].reshape(dp_size, length)
    segments_all = packed[:, :, rows : 2 * rows].reshape(dp_size, length)
    edge = 2 * rows + comp // rep_size
    completion_all = packed[:, :, 2 * rows : edge].reshape(dp_size, comp)
    targets_all = packed[:, :, edge:].reshape(dp_size, comp)

    home = home.reshape(LAYERS, per, tile_rows, D)
    spread = lax.all_gather(home[0], ALL, axis=0)
    spread = spread.reshape(dp_size, rep_size, per, tile_rows, D)
    weights = [[(spread, i) for i in range(per)]]
    later = [[lax.all_gather(home[index, i], ALL, axis=0) for i in range(1, per)] for index in range(1, LAYERS)]

    order = tokens_all.reshape(a_size, rep_size, b_size, rows).transpose(0, 2, 1, 3).reshape(-1)
    place = order - vocab_start
    vocab_iota = jnp.arange(vocab_rows)
    token_hot = (place[:, None] == vocab_iota[None, :]).astype(jnp.bfloat16)
    picked = jnp.dot(
        token_hot, table_weight.astype(jnp.bfloat16), preferred_element_type=jnp.float32
    ).astype(jnp.bfloat16)
    state = scatter_all(picked.reshape(devices, rows, D), 8, "rows_scatter").astype(jnp.float32)

    for index in range(1, LAYERS):
        first, state = lax.optimization_barrier((home[index, 0], state))
        first = gather_all(first, 1, "weights_gather")
        weights.append(
            [
                (array.reshape(dp_size, rep_size, 1, tile_rows, D), 0)
                for array in [first] + later[index - 1]
            ]
        )
    first_place = b_index * rows
    places = first_place + jnp.arange(rows)
    cosine, sine = rope_tables(places.astype(jnp.float32))
    own_segments = lax.dynamic_index_in_dim(segments_all, sequence, 0, False)
    query_segments = lax.dynamic_slice_in_dim(own_segments, first_place, rows)
    marks = (own_segments[:, None], query_segments[None, :], places[None, :])
    kept_list = []
    for index in range(LAYERS):
        state, kept = layer_forward(
            state, weights[index], index, gain_weight, cosine, sine, marks
        )
        kept_list.append(kept)
    final_gain = gain_weight[2 * LAYERS]
    final = root_norm(state, final_gain).astype(jnp.bfloat16)

    capacity = 3 * comp // (2 * rep_size)
    block = completion_all // rows
    inside = block[:, None, :] == jnp.arange(b_size)[None, :, None]
    before = jnp.sum((block[:, None, :] < jnp.arange(b_size)[None, :, None]).astype(jnp.int32), axis=2)
    rank = jnp.arange(comp)[None, None, :] - before[:, :, None]
    slot_pick = inside[..., None] & (rank[..., None] == jnp.arange(capacity))
    filled = jnp.any(slot_pick, axis=2)
    wanted = jnp.where(
        filled, jnp.sum(jnp.where(slot_pick, targets_all[:, None, :, None], 0), axis=2), -1
    )
    spots = jnp.where(
        filled, jnp.sum(jnp.where(slot_pick, (completion_all % rows)[:, None, :, None], 0), axis=2), -1
    )
    all_wanted = (
        wanted.reshape(a_size, rep_size, b_size, capacity).transpose(0, 2, 1, 3).reshape(-1)
    )
    own_spots = lax.dynamic_index_in_dim(
        lax.dynamic_index_in_dim(spots, sequence, 0, False), b_index, 0, False
    )
    select = (own_spots[:, None] == jnp.arange(rows)[None, :]).astype(jnp.bfloat16)
    chosen = jnp.dot(select, final, preferred_element_type=jnp.float32).astype(jnp.bfloat16)
    all_rows = gather_all(chosen, 3, "chosen_gather").reshape(-1, D)
    head_low = head_weight.astype(jnp.bfloat16)
    logits = jnp.einsum("rd,vd->rv", all_rows, head_low, preferred_element_type=jnp.float32)
    hot = vocab_iota[None, :] == (all_wanted - vocab_start)[:, None]
    local_top = jnp.max(logits, axis=-1)
    local_total = jnp.sum(jnp.exp(logits - local_top[:, None]), axis=-1)
    local_hit = jnp.sum(jnp.where(hot, logits, 0.0), axis=-1)
    own_stats = jnp.concatenate(
        [v.reshape(-1, 128) for v in (local_top, local_total, local_hit)]
    )
    stats = gather_all(own_stats, 4, "stats_gather")
    tops, totals, hits = jnp.split(stats, 3, axis=1)
    top = jnp.max(tops, axis=0)
    total = jnp.sum(totals * jnp.exp(tops - top[None]), axis=0)
    log_total = (top + jnp.log(total)).reshape(-1)
    target_hit = jnp.sum(hits, axis=0).reshape(-1)
    valid = all_wanted >= 0
    scored = dp_size * comp
    loss = jnp.sum(jnp.where(valid, log_total - target_hit, 0.0)) / scored
    logit_grad = jnp.where(
        valid[:, None],
        (jnp.exp(logits - log_total[:, None]) - jnp.where(hot, 1.0, 0.0)) / scored,
        0.0,
    ).astype(jnp.bfloat16)
    logit_grad = lax.optimization_barrier(logit_grad)
    rows_grad = jnp.dot(logit_grad, head_low, preferred_element_type=jnp.float32)
    own_rows = scatter_all(
        rows_grad.astype(jnp.bfloat16).reshape(devices, -1, D), 9, "back_scatter"
    )
    head_grad = jnp.einsum("rv,rd->vd", logit_grad, all_rows, preferred_element_type=jnp.float32)
    final_grad = jnp.einsum("ct,cd->td", select, own_rows, preferred_element_type=jnp.float32)
    state_grad, final_gain_grad = norm_back(state, final_gain, final_grad)
    tile_parts = [None] * LAYERS
    gain_parts = [None] * LAYERS
    for index in reversed(range(LAYERS)):
        state_grad, tile_parts[index], gain_parts[index] = layer_backward(
            state_grad, kept_list[index], weights[index], index, gain_weight, cosine, sine, marks
        )
    entry = state_grad.astype(jnp.bfloat16)
    flat = [[part.reshape(devices, -1, D) for part in layer] for layer in tile_parts]
    if fits():
        tail = [lax.psum_scatter(flat[-1][-1], ALL, scatter_dimension=0)]
        firsts = [part for layer in flat for part in layer][:-1]
        body, piece_grads = scatter_and_gather(firsts, 4, entry, 4, 2, "grads_and_entry")
        home_grads = [body] + tail
    else:
        home_grads = [
            lax.psum_scatter(part, ALL, scatter_dimension=0) for layer in flat for part in layer
        ]
        piece_grads = lax.all_gather(entry, ALL, axis=0)
    table_grad = jnp.einsum(
        "tv,td->vd", token_hot, piece_grads.reshape(-1, D), preferred_element_type=jnp.float32
    )
    plane_grad = gather_plane(jnp.concatenate(home_grads), 6, "owners_gather")
    plane_grad = plane_grad.reshape(tile_count, tile_rows, D)
    own_count = jnp.sum(mine.astype(jnp.int32))
    slot_ids = jnp.arange(slots_cap)
    picks = mine[home_ids][None, :] & (slots[home_ids][None, :] == slot_ids[:, None])
    tile_of_slot = jnp.sum(jnp.where(picks, jnp.arange(tile_count)[None, :], 0), axis=1)
    slot_valid = (slot_ids < own_count)[:, None, None]
    own_grad = jnp.where(
        slot_valid, jnp.take(plane_grad, tile_of_slot, axis=0).astype(jnp.float32), 0.0
    )
    gain_grads = jnp.stack([g for pair in gain_parts for g in pair] + [final_gain_grad])
    square = (
        jnp.sum(own_grad * own_grad)
        + jnp.sum(table_grad * table_grad)
        + jnp.sum(head_grad * head_grad)
    )
    sums = gather_all(
        padded(jnp.concatenate([square[None], gain_grads.reshape(-1)])), 5, "sums_gather"
    )
    sums = jnp.sum(sums.reshape(devices, -1), axis=0)
    square, gain_grads = sums[0], sums[1 : 1 + gain_grads.size].reshape(gain_grads.shape)
    norm = jnp.sqrt(square + jnp.sum(gain_grads * gain_grads))
    factor = jnp.minimum(1.0, CLIP_NORM / norm)
    steps = step_count[0].astype(jnp.float32)
    tile_new, tile_first_new, tile_second_new = adam(
        tile_weight, tile_first, tile_second, own_grad, factor, RATE_TILE, DECAY, steps
    )
    tile_new = jnp.where(slot_valid, tile_new, 0.0)
    tile_first_new = jnp.where(slot_valid, tile_first_new, 0.0)
    tile_second_new = jnp.where(slot_valid, tile_second_new, 0.0)
    table_new, table_first_new, table_second_new = adam(
        table_weight, table_first, table_second, table_grad, factor, RATE_TABLE, DECAY, steps
    )
    head_new, head_first_new, head_second_new = adam(
        head_weight, head_first, head_second, head_grad, factor, RATE_HEAD, DECAY, steps
    )
    gain_new, gain_first_new, gain_second_new = adam(
        gain_weight, gain_first, gain_second, gain_grads, factor, RATE_GAIN, 0.0, steps
    )
    return (
        loss,
        norm,
        tile_new,
        tile_new.astype(jnp.bfloat16),
        tile_first_new,
        tile_second_new,
        table_new,
        table_new.astype(jnp.bfloat16),
        table_first_new,
        table_second_new,
        head_new,
        head_new.astype(jnp.bfloat16),
        head_first_new,
        head_second_new,
        gain_new,
        gain_first_new,
        gain_second_new,
    )


def solution(mesh):
    dp_size, rep_size = mesh.shape["dp"], mesh.shape["rep"]
    split = Mesh(mesh.devices.reshape(dp_size // rep_size, rep_size // 2, 2, rep_size), ALL)
    return jax.shard_map(
        shards,
        mesh=split,
        in_specs=(
            P(DP, "z"),
            P(DP, None),
            P(DP, None),
            P(DP, None),
            P(),
            P(),
            P(ALL, None, None),
            P(ALL, None, None),
            P(ALL, None, None),
            P(ALL, None),
            P(ALL, None),
            P(ALL, None),
            P(ALL, None),
            P(ALL, None),
            P(ALL, None),
            P(),
            P(),
            P(),
        ),
        out_specs=(
            P(),
            P(),
            P(ALL, None, None),
            P(ALL, None, None),
            P(ALL, None, None),
            P(ALL, None, None),
            P(ALL, None),
            P(ALL, None),
            P(ALL, None),
            P(ALL, None),
            P(ALL, None),
            P(ALL, None),
            P(ALL, None),
            P(ALL, None),
            P(),
            P(),
            P(),
        ),
        check_vma=False,
    )
```

```python
import functools

import jax
import jax.numpy as jnp
from jax import lax
from jax.experimental import pallas as pl
from jax.experimental.pallas import tpu as pltpu
from jax.sharding import Mesh, PartitionSpec as P

D = 768
HEADS = 12
HD = 64
FF = 3072
LAYERS = 2


EPS_NORM = 1e-05
EPS_ADAM = 1e-08
CLIP_NORM = 0.005
BETA_FIRST = 0.5
BETA_SECOND = 0.5
DECAY = 0.1
RATE_TILE = 0.02
RATE_HEAD = 0.05
RATE_TABLE = 0.5
RATE_GAIN = 0.3
MASKED = -1e30


def root_norm(training_state, gain):
    return (
        training_state
        * lax.rsqrt(jnp.mean(training_state * training_state, axis=-1, keepdims=True) + EPS_NORM)
        * gain
    )


def norm_back(training_state, gain, grad):
    scale = lax.rsqrt(jnp.mean(training_state * training_state, axis=-1, keepdims=True) + EPS_NORM)
    scaled = grad * gain
    state_grad = scale * scaled - training_state * scale**3 * jnp.mean(
        scaled * training_state, axis=-1, keepdims=True
    )
    gain_grad = jnp.sum(
        (grad * training_state * scale).reshape(-1, training_state.shape[-1]), axis=0
    )
    return (state_grad, gain_grad)


def rope_tables(places):
    freqs = jnp.power(10000.0, -2.0 * jnp.arange(HD // 2).astype(jnp.float32) / HD)
    angle = places[:, None] * freqs[None, :]
    cosine, sine = jnp.cos(angle), jnp.sin(angle)
    return jnp.concatenate([cosine] * 4, axis=1), jnp.concatenate([-sine, sine] * 2, axis=1)


def tile_slots(owners):
    order = jnp.arange(owners.shape[0], dtype=jnp.int32)
    same = (owners[:, None] == owners[None, :]) & (order[None, :] < order[:, None])
    return jnp.sum(same.astype(jnp.int32), axis=1)


def adam(weight, first, second, grad, factor, rate, decay, steps):
    grad = grad * factor
    first = BETA_FIRST * first + (1.0 - BETA_FIRST) * grad
    second = BETA_SECOND * second + (1.0 - BETA_SECOND) * grad * grad
    first_hat = first / (1.0 - jnp.power(BETA_FIRST, steps))
    second_hat = second / (1.0 - jnp.power(BETA_SECOND, steps))
    weight = weight - rate * (first_hat / (jnp.sqrt(second_hat) + EPS_ADAM) + decay * weight)
    return (weight, first, second)


ALL = ("y", "x", "c", "z")
DP = ("y", "x", "c")
PART = ("x", "c")
UNITS = FF // D
TILES_PER = 4 + 3 * UNITS


MESH = pl.DeviceIdType.MESH
LAG_ONE, LAG_MANY = 8, 6
VMEM = 60 << 20


def half_rows(rows, dtype):
    unit = 16 if jnp.dtype(dtype).itemsize == 2 else 8
    return (rows // 2 + unit - 1) // unit * unit


def remote(src, dst, ssem, rsem, **to):
    return pltpu.make_async_remote_copy(
        src_ref=src, dst_ref=dst, send_sem=ssem, recv_sem=rsem, device_id=to, device_id_type=MESH
    )


def greet(zn, y, x, c, z):
    barrier = pltpu.get_barrier_semaphore()
    for to in ({"x": 1 - x}, {"y": 1 - y}, {"c": 1 - c}):
        pl.semaphore_signal(barrier, inc=1, device_id=to, device_id_type=MESH)
    if zn > 1:

        @pl.when(z < zn - 1)
        def _():
            pl.semaphore_signal(barrier, inc=1, device_id={"z": z + 1}, device_id_type=MESH)

        @pl.when(z > 0)
        def _():
            pl.semaphore_signal(barrier, inc=1, device_id={"z": z - 1}, device_id_type=MESH)

        @pl.when((z > 0) & (z < zn - 1))
        def _():
            pl.semaphore_wait(barrier, 5)

        @pl.when((z == 0) | (z == zn - 1))
        def _():
            pl.semaphore_wait(barrier, 4)
    else:
        pl.semaphore_wait(barrier, 3)


def gather_steps(zn, x_ref, o_ref, hold, ssem, rsem, lsem):
    y, x, c, z = [lax.axis_index(n) for n in ALL]
    me = z if zn > 1 else 0
    rows = x_ref.shape[0]
    h0 = half_rows(rows, x_ref.dtype)
    lo, hi = pl.ds(0, h0), pl.ds(h0, rows - h0)
    X, Y, DX, DY, CO, CX, CY, C0, C1, ZU, ZD = range(11)
    nx, ny, nc = {"x": 1 - x}, {"y": 1 - y}, {"c": 1 - c}

    def slot(yy, xx, zz):
        return ((yy * 2 + xx) * 2 + c) * zn + zz

    def copy(kind, k, src, dst, to):
        return remote(src, dst, ssem.at[kind, k], rsem.at[kind, k], **to)

    def block(s):
        return o_ref.at[s]

    local = pltpu.make_async_copy(x_ref, hold, lsem.at[0])
    local.start()
    keep = pltpu.make_async_copy(hold, o_ref.at[slot(y, x, me)], lsem.at[1])

    def spread(zb, src):
        dst = block(slot(y, x, zb))
        copy(X, zb, src, dst, nx).start()
        copy(Y, zb, src, dst, ny).start()
        copy(CO, zb, src, dst, nc).start()

    def up(s):
        zb = z - (s - 1)
        b = block(slot(y, x, zb))
        return copy(ZU, s, x_ref if s == 1 else b, b, {"z": z + 1})

    def down(s):
        zb = z + (s - 1)
        b = block(slot(y, x, zb))
        return copy(ZD, s, x_ref if s == 1 else b, b, {"z": z - 1})

    for s in range(1, zn):

        @pl.when((z < zn - 1) & (z - (s - 1) >= 0))
        def _():
            up(s).start()

        @pl.when((z > 0) & (z + (s - 1) < zn))
        def _():
            down(s).start()

        if s == 1:
            spread(me, x_ref)
            local.wait()
            keep.start()
        yield

        @pl.when(z - s >= 0)
        def _():
            copy(ZU, s, x_ref, x_ref, nx).wait_recv()
            spread(z - s, block(slot(y, x, z - s)))

        @pl.when(z + s < zn)
        def _():
            copy(ZD, s, x_ref, x_ref, nx).wait_recv()
            spread(z + s, block(slot(y, x, z + s)))

    if zn == 1:
        spread(0, x_ref)
        local.wait()
        keep.start()
    order = [lax.rem(z + j, zn) if zn > 1 else 0 for j in range(zn)]
    for zb in order:
        yield
        sx, sy = slot(y, 1 - x, zb), slot(1 - y, x, zb)
        copy(X, zb, x_ref, x_ref, nx).wait_recv()
        copy(DX, zb, o_ref.at[sx, lo], o_ref.at[sx, lo], ny).start()
        copy(CX, zb, block(sx), block(sx), nc).start()
        copy(Y, zb, x_ref, x_ref, nx).wait_recv()
        copy(DY, zb, o_ref.at[sy, hi], o_ref.at[sy, hi], nx).start()
        copy(CY, zb, block(sy), block(sy), nc).start()
    for zb in order:
        yield
        sd = slot(1 - y, 1 - x, zb)
        copy(DX, zb, x_ref.at[lo], x_ref.at[lo], nx).wait_recv()
        copy(C0, zb, o_ref.at[sd, lo], o_ref.at[sd, lo], nc).start()
        copy(DY, zb, x_ref.at[hi], x_ref.at[hi], nx).wait_recv()
        copy(C1, zb, o_ref.at[sd, hi], o_ref.at[sd, hi], nc).start()
    yield
    for zb in range(zn):
        for kind, part in ((CO, x_ref), (CX, x_ref), (CY, x_ref), (C0, x_ref.at[lo]), (C1, x_ref.at[hi])):
            copy(kind, zb, part, part, nx).wait_recv()
        for kind, part in (
            (X, x_ref), (Y, x_ref), (CO, x_ref), (CX, x_ref), (CY, x_ref),
            (DX, x_ref.at[lo]), (DY, x_ref.at[hi]), (C0, x_ref.at[lo]), (C1, x_ref.at[hi]),
        ):
            copy(kind, zb, part, part, nx).wait_send()
    for s in range(1, zn):

        @pl.when((z < zn - 1) & (z - (s - 1) >= 0))
        def _():
            up(s).wait_send()

        @pl.when((z > 0) & (z + (s - 1) < zn))
        def _():
            down(s).wait_send()

    keep.wait()


def run_steps(*parts):
    parts, turn = list(parts), 0
    while parts:
        for part in list(parts):
            if turn >= part[0] and next(part[1], part) is part:
                parts.remove(part)
        turn += 1


def gather_kernel(zn, *refs):
    greet(zn, *[lax.axis_index(n) for n in ALL])
    run_steps((0, gather_steps(zn, *refs)))


def gather_scratch(zn, shape, dtype):
    sems = pltpu.SemaphoreType.DMA((11, zn))
    return [pltpu.VMEM(shape, dtype), sems, sems, pltpu.SemaphoreType.DMA((2,))]


def all_gather(x, zn, ident, name):
    return pl.pallas_call(
        functools.partial(gather_kernel, zn),
        out_shape=jax.ShapeDtypeStruct((8 * zn,) + x.shape, x.dtype),
        in_specs=[pl.BlockSpec(memory_space=pl.ANY)],
        out_specs=pl.BlockSpec(memory_space=pl.ANY),
        scratch_shapes=gather_scratch(zn, x.shape, x.dtype),
        compiler_params=pltpu.CompilerParams(
            collective_id=ident, has_side_effects=True, vmem_limit_bytes=VMEM
        ),
        name=name,
    )(x)


def reduce_steps(zn, p_ref, at, o_ref, to, acc, crecv, dxr, dyr, xr, yr, zur, zdr, ssem, rsem, lsem):
    y, x, c, z = [lax.axis_index(n) for n in ALL]
    me = z if zn > 1 else 0
    rows = acc.shape[1]
    h0 = half_rows(rows, acc.dtype)
    h1 = rows - h0
    X, Y, DX, DY, ZU, ZD, C0 = range(7)
    nx, ny, nc = {"x": 1 - x}, {"y": 1 - y}, {"c": 1 - c}
    kinds = [(y, x), (y, 1 - x), (1 - y, x), (1 - y, 1 - x)]
    step = 32 if rows % 32 == 0 else 16
    zorder = sorted(range(zn), key=lambda zb: (abs(2 * zb - zn + 1), zb), reverse=True)
    out_rows = o_ref.at[pl.ds(to, rows)]

    def slot(k, cc, zz):
        yy, xx = kinds[k]
        return ((yy * 2 + xx) * 2 + cc) * zn + zz

    def copy(kind, k, src, dst, to):
        return remote(src, dst, ssem.at[kind, k], rsem.at[kind, k], **to)

    def load(k, zb):
        b = k * zn + zb
        return pltpu.make_async_copy(p_ref.at[slot(k, c, zb), pl.ds(at, rows)], acc.at[b], lsem.at[b])

    def across(k, zb):
        source = p_ref.at[slot(k, 1 - c, zb), pl.ds(at, rows)]
        return copy(C0 + k, zb, source, crecv.at[k * zn + zb], nc)

    def add(dst, start, count, terms):
        size = step if count % step == 0 else 16

        @pl.loop(0, count // size)
        def _(i):
            here = pl.ds(pl.multiple_of(start + i * size, 16), size)
            total = None
            for ref, base in terms:
                part = ref[pl.ds(pl.multiple_of(start - base + i * size, 16), size), :].astype(jnp.float32)
                total = part if total is None else total + part
            dst[here, :] = total.astype(dst.dtype)

    for k in (3, 1, 2, 0):
        for zb in zorder:
            across(k, zb).start()
            load(k, zb).start()

    def ready(k, zb):
        load(k, zb).wait()
        across(k, zb).wait_recv()

    for zb in zorder:
        yield
        ready(3, zb)
        b = 3 * zn + zb
        add(acc.at[b], 0, rows, [(acc.at[b], 0), (crecv.at[b], 0)])
        copy(DX, zb, acc.at[b, pl.ds(0, h0)], dxr.at[zb], nx).start()
        copy(DY, zb, acc.at[b, pl.ds(h0, h1)], dyr.at[zb], ny).start()
    for zb in zorder:
        yield
        ready(1, zb)
        b = zn + zb
        add(acc.at[b], 0, h0, [(acc.at[b], 0), (crecv.at[b], 0)])
        copy(DY, zb, dyr.at[zb], dyr.at[zb], ny).wait_recv()
        add(acc.at[b], h0, h1, [(acc.at[b], 0), (crecv.at[b], 0), (dyr.at[zb], h0)])
        copy(X, zb, acc.at[b], xr.at[zb], nx).start()
        yield
        ready(2, zb)
        b = 2 * zn + zb
        add(acc.at[b], h0, h1, [(acc.at[b], 0), (crecv.at[b], 0)])
        copy(DX, zb, dxr.at[zb], dxr.at[zb], nx).wait_recv()
        add(acc.at[b], 0, h0, [(acc.at[b], 0), (crecv.at[b], 0), (dxr.at[zb], 0)])
        copy(Y, zb, acc.at[b], yr.at[zb], ny).start()

    def column(zb):
        return [(acc.at[zb], 0), (crecv.at[zb], 0), (xr.at[zb], 0), (yr.at[zb], 0)]

    for zb in zorder:
        yield
        ready(0, zb)
        copy(X, zb, acc.at[zb], xr.at[zb], nx).wait_recv()
        copy(Y, zb, acc.at[zb], yr.at[zb], ny).wait_recv()
        if zn == 1:
            add(out_rows, 0, rows, column(0))
            continue

        def upward(zb=zb):
            return copy(ZU, zb, acc.at[zb], zur.at[zb], {"z": z + 1})

        def downward(zb=zb):
            return copy(ZD, zb, acc.at[zb], zdr.at[zb], {"z": z - 1})

        @pl.when(z == zb)
        def _():
            add(acc.at[zb], 0, rows, column(zb))

        @pl.when((z < zb) & (z == 0))
        def _():
            add(acc.at[zb], 0, rows, column(zb))
            upward().start()

        @pl.when((z < zb) & (z > 0))
        def _():
            upward().wait_recv()
            add(acc.at[zb], 0, rows, column(zb) + [(zur.at[zb], 0)])
            upward().start()

        @pl.when((z > zb) & (z == zn - 1))
        def _():
            add(acc.at[zb], 0, rows, column(zb))
            downward().start()

        @pl.when((z > zb) & (z < zn - 1))
        def _():
            downward().wait_recv()
            add(acc.at[zb], 0, rows, column(zb) + [(zdr.at[zb], 0)])
            downward().start()

    yield
    if zn > 1:

        @pl.when(z == 0)
        def _():
            copy(ZD, me, acc.at[me], zdr.at[me], {"z": z + 1}).wait_recv()
            add(out_rows, 0, rows, [(acc.at[me], 0), (zdr.at[me], 0)])

        @pl.when(z == zn - 1)
        def _():
            copy(ZU, me, acc.at[me], zur.at[me], {"z": z - 1}).wait_recv()
            add(out_rows, 0, rows, [(acc.at[me], 0), (zur.at[me], 0)])

        @pl.when((z > 0) & (z < zn - 1))
        def _():
            copy(ZD, me, acc.at[me], zdr.at[me], {"z": z + 1}).wait_recv()
            copy(ZU, me, acc.at[me], zur.at[me], {"z": z + 1}).wait_recv()
            add(out_rows, 0, rows, [(acc.at[me], 0), (zdr.at[me], 0), (zur.at[me], 0)])

    for zb in range(zn):
        for k in range(4):
            across(k, zb).wait_send()
        copy(DX, zb, dxr.at[zb], dxr.at[zb], nx).wait_send()
        copy(DY, zb, dyr.at[zb], dyr.at[zb], ny).wait_send()
        copy(X, zb, xr.at[zb], xr.at[zb], nx).wait_send()
        copy(Y, zb, yr.at[zb], yr.at[zb], ny).wait_send()
        if zn > 1:

            @pl.when(z < zb)
            def _():
                copy(ZU, zb, zur.at[zb], zur.at[zb], {"z": z + 1}).wait_send()

            @pl.when(z > zb)
            def _():
                copy(ZD, zb, zdr.at[zb], zdr.at[zb], {"z": z - 1}).wait_send()


def reduce_z_first_steps(
    zn, p_ref, at, o_ref, to, acc, crecv, zur, zdr, dxr, dyr, xr, yr, ssem, rsem, lsem
):
    y, x, c, z = [lax.axis_index(n) for n in ALL]
    rows = acc.shape[1]
    h0 = half_rows(rows, acc.dtype)
    h1 = rows - h0
    X, Y, DX, DY, C, ZU, ZD = range(7)
    nx, ny, nc = {"x": 1 - x}, {"y": 1 - y}, {"c": 1 - c}
    up, down = {"z": z + 1}, {"z": z - 1}
    kinds = [(y, x), (y, 1 - x), (1 - y, x), (1 - y, 1 - x)]
    zorder = sorted(range(zn), key=lambda zb: (abs(2 * zb - zn + 1), zb), reverse=True)
    blocks = [(k, zb) for k in range(4) for zb in range(zn)]

    def slot(k, cc, zz):
        yy, xx = kinds[k]
        return ((yy * 2 + xx) * 2 + cc) * zn + zz

    def copy(kind, k, src, dst, to):
        return remote(src, dst, ssem.at[kind, k], rsem.at[kind, k], **to)

    def load(k, zb):
        b = k * zn + zb
        return pltpu.make_async_copy(p_ref.at[slot(k, c, zb), pl.ds(at, rows)], acc.at[b], lsem.at[b])

    def across(k, zb):
        b = k * zn + zb
        return copy(C, b, p_ref.at[slot(k, 1 - c, zb), pl.ds(at, rows)], crecv.at[b], nc)

    def upward(b):
        return copy(ZU, b, acc.at[b], zur.at[b], up)

    def downward(b):
        return copy(ZD, b, acc.at[b], zdr.at[b], down)

    def add(dst, start, count, terms):
        @pl.loop(0, count // 16)
        def _(i):
            total = None
            for ref, base in terms:
                part = ref[pl.ds(pl.multiple_of(start - base + i * 16, 16), 16), :]
                part = part.astype(jnp.float32)
                total = part if total is None else total + part
            dst[pl.ds(pl.multiple_of(start + i * 16, 16), 16), :] = total.astype(dst.dtype)

    def flow(k, zb):
        b = k * zn + zb
        load(k, zb).wait()
        across(k, zb).wait_recv()
        both = [(acc.at[b], 0), (crecv.at[b], 0)]

        @pl.when((z == zb) | ((z < zb) & (z == 0)) | ((z > zb) & (z == zn - 1)))
        def _():
            add(acc.at[b], 0, rows, both)

        @pl.when((z < zb) & (z > 0))
        def _():
            upward(b).wait_recv()
            add(acc.at[b], 0, rows, both + [(zur.at[b], 0)])

        @pl.when((z > zb) & (z < zn - 1))
        def _():
            downward(b).wait_recv()
            add(acc.at[b], 0, rows, both + [(zdr.at[b], 0)])

        @pl.when(z < zb)
        def _():
            upward(b).start()

        @pl.when(z > zb)
        def _():
            downward(b).start()

    def settle(k):
        b = k * zn + z

        @pl.when(z > 0)
        def _():
            upward(b).wait_recv()
            add(acc.at[b], 0, rows, [(acc.at[b], 0), (zur.at[b], 0)])

        @pl.when(z < zn - 1)
        def _():
            downward(b).wait_recv()
            add(acc.at[b], 0, rows, [(acc.at[b], 0), (zdr.at[b], 0)])

        return acc.at[b]

    for k in (3, 1, 2, 0):
        for zb in zorder:
            across(k, zb).start()
            load(k, zb).start()
    lo, hi = pl.ds(0, h0), pl.ds(h0, h1)
    for k in (3, 1):
        for zb in zorder:
            yield
            flow(k, zb)
    yield
    block = settle(3)
    copy(DX, 0, block.at[lo], dxr, nx).start()
    copy(DY, 0, block.at[hi], dyr, ny).start()
    for k in (2, 0):
        for zb in zorder:
            yield
            flow(k, zb)
    yield
    block = settle(1)
    copy(DY, 0, dyr, dyr, ny).wait_recv()
    add(block, h0, h1, [(block, 0), (dyr, h0)])
    copy(X, 0, block, xr, nx).start()
    yield
    block = settle(2)
    copy(DX, 0, dxr, dxr, nx).wait_recv()
    add(block, 0, h0, [(block, 0), (dxr, 0)])
    copy(Y, 0, block, yr, ny).start()
    yield
    block = settle(0)
    copy(X, 0, xr, xr, nx).wait_recv()
    copy(Y, 0, yr, yr, ny).wait_recv()
    add(o_ref.at[pl.ds(to, rows)], 0, rows, [(block, 0), (xr, 0), (yr, 0)])
    for kind, ref in ((DX, dxr), (DY, dyr), (X, xr), (Y, yr)):
        copy(kind, 0, ref, ref, nx).wait_send()
    for k, zb in blocks:
        b = k * zn + zb
        across(k, zb).wait_send()

        @pl.when(z < zb)
        def _():
            upward(b).wait_send()

        @pl.when(z > zb)
        def _():
            downward(b).wait_send()


def segments_of(rows, inputs=1):
    if rows < 192 or inputs > 1:
        return [(0, rows)]
    first = (rows // 2 + 31) // 32 * 32
    return [(0, first), (first, rows - first)]


def reduce_plan(zn, p_refs, o_ref, scratch, z_first=()):
    parts, base, lag = [], 0, 0
    for i, p_ref in enumerate(p_refs):
        for at, rows in segments_of(p_ref.shape[1], len(p_refs)):
            mine, scratch = scratch[:11], scratch[11:]
            if i in z_first:
                parts.append((0, reduce_z_first_steps(zn, p_ref, at, o_ref, base + at, *mine)))
                continue
            parts.append((lag, reduce_steps(zn, p_ref, at, o_ref, base + at, *mine)))
            lag += LAG_ONE if len(p_refs) == 1 else LAG_MANY
        base += p_ref.shape[1]
    return parts


def reduce_kernel(zn, p_ref, o_ref, *scratch):
    greet(zn, *[lax.axis_index(n) for n in ALL])
    run_steps(*reduce_plan(zn, [p_ref], o_ref, scratch))


def reduce_scratch(zn, rows, cols, dtype, inputs=1, z_first=False):
    entries = []
    for _, n in segments_of(rows, inputs):
        h0 = half_rows(n, dtype)
        if z_first:
            shapes = [(4 * zn, n, cols)] * 4 + [(h0, cols), (n - h0, cols), (n, cols), (n, cols)]
            sems = pltpu.SemaphoreType.DMA((7, 4 * zn))
        else:
            counts = [(4 * zn, n), (4 * zn, n), (zn, h0), (zn, n - h0)] + [(zn, n)] * 4
            shapes = [(m, r, cols) for m, r in counts]
            sems = pltpu.SemaphoreType.DMA((10, zn))
        entries += [pltpu.VMEM(shape, dtype) for shape in shapes]
        entries += [sems, sems, pltpu.SemaphoreType.DMA((4 * zn,))]
    return entries


def reduce_scatter(p, zn, ident, name, out_dtype=None):
    count, rows, cols = p.shape
    return pl.pallas_call(
        functools.partial(reduce_kernel, zn),
        out_shape=jax.ShapeDtypeStruct((rows, cols), out_dtype or p.dtype),
        in_specs=[pl.BlockSpec(memory_space=pl.ANY)],
        out_specs=pl.BlockSpec(memory_space=pltpu.VMEM),
        scratch_shapes=reduce_scratch(zn, rows, cols, p.dtype),
        compiler_params=pltpu.CompilerParams(
            collective_id=ident, has_side_effects=True, vmem_limit_bytes=VMEM
        ),
        name=name,
    )(p)


def both_kernel(inputs, z_first, zr, zg, *refs):
    p_refs, (x_ref, r_ref, o_ref), scratch = refs[:inputs], refs[inputs : inputs + 3], refs[inputs + 3 :]
    greet(max(zr, zg), *[lax.axis_index(n) for n in ALL])
    gather = (0, gather_steps(zg, x_ref, o_ref, *scratch[-4:]))
    run_steps(gather, *reduce_plan(zr, p_refs, r_ref, scratch[:-4], z_first))


def scatter_and_gather(parts, zr, x, zg, ident, name, z_first=()):
    inputs = len(parts)
    count, each, cols = parts[0].shape
    rows, dtype = inputs * each, parts[0].dtype
    return pl.pallas_call(
        functools.partial(both_kernel, inputs, z_first, zr, zg),
        out_shape=(
            jax.ShapeDtypeStruct((rows, cols), dtype),
            jax.ShapeDtypeStruct((8 * zg,) + x.shape, x.dtype),
        ),
        in_specs=[pl.BlockSpec(memory_space=pl.ANY)] * (inputs + 1),
        out_specs=(pl.BlockSpec(memory_space=pltpu.VMEM), pl.BlockSpec(memory_space=pl.ANY)),
        scratch_shapes=[
            entry for i in range(inputs) for entry in reduce_scratch(zr, each, cols, dtype, inputs, i in z_first)
        ]
        + gather_scratch(zg, x.shape, x.dtype),
        compiler_params=pltpu.CompilerParams(
            collective_id=ident, has_side_effects=True, vmem_limit_bytes=VMEM
        ),
        name=name,
    )(*parts, x)


def greet_pair(x, c):
    barrier = pltpu.get_barrier_semaphore()
    for to in ({"x": 1 - x}, {"c": 1 - c}):
        pl.semaphore_signal(barrier, inc=1, device_id=to, device_id_type=MESH)
    pl.semaphore_wait(barrier, 2)


def keys_gather_kernel(x_ref, o_ref, hold, ssem, rsem, lsem):
    x, c = lax.axis_index("x"), lax.axis_index("c")
    me, far = x * 2 + c, (1 - x) * 2 + c
    nx, nc = {"x": 1 - x}, {"c": 1 - c}
    load = pltpu.make_async_copy(x_ref, hold, lsem.at[0])
    load.start()
    greet_pair(x, c)
    out = remote(x_ref, o_ref.at[me], ssem.at[0], rsem.at[0], **nx)
    out.start()
    near = remote(x_ref, o_ref.at[me], ssem.at[1], rsem.at[1], **nc)
    near.start()
    load.wait()
    keep = pltpu.make_async_copy(hold, o_ref.at[me], lsem.at[1])
    keep.start()
    out.wait_recv()
    on = remote(o_ref.at[far], o_ref.at[far], ssem.at[2], rsem.at[2], **nc)
    on.start()
    near.wait_recv()
    on.wait_recv()
    keep.wait()
    out.wait_send()
    near.wait_send()
    on.wait_send()


def keys_gather(v, ident):
    sems = pltpu.SemaphoreType.DMA((3,))
    return pl.pallas_call(
        keys_gather_kernel,
        out_shape=jax.ShapeDtypeStruct((4,) + v.shape, v.dtype),
        in_specs=[pl.BlockSpec(memory_space=pl.ANY)],
        out_specs=pl.BlockSpec(memory_space=pl.ANY),
        scratch_shapes=[pltpu.VMEM(v.shape, v.dtype), sems, sems, pltpu.SemaphoreType.DMA((2,))],
        compiler_params=pltpu.CompilerParams(
            collective_id=ident, has_side_effects=True, vmem_limit_bytes=VMEM
        ),
        name="keys_gather",
    )(v)


def keys_reduce_kernel(p_ref, o_ref, acc, crecv, xr, ssem, rsem, lsem):
    x, c = lax.axis_index("x"), lax.axis_index("c")
    nx, nc = {"x": 1 - x}, {"c": 1 - c}
    rows = p_ref.shape[1]
    places = [(1 - x) * 2, x * 2]
    loads = [pltpu.make_async_copy(p_ref.at[places[i] + c], acc.at[i], lsem.at[i]) for i in range(2)]
    for load in loads:
        load.start()
    greet_pair(x, c)
    across = [
        remote(p_ref.at[places[i] + 1 - c], crecv.at[i], ssem.at[i], rsem.at[i], **nc) for i in range(2)
    ]
    for copy in across:
        copy.start()

    def add(dst, terms):
        @pl.loop(0, rows // 16)
        def _(i):
            at = pl.ds(pl.multiple_of(i * 16, 16), 16)
            total = terms[0][at, :].astype(jnp.float32)
            for term in terms[1:]:
                total = total + term[at, :].astype(jnp.float32)
            dst[at, :] = total.astype(dst.dtype)

    loads[0].wait()
    across[0].wait_recv()
    add(acc.at[0], [acc.at[0], crecv.at[0]])
    out = remote(acc.at[0], xr, ssem.at[2], rsem.at[2], **nx)
    out.start()
    loads[1].wait()
    across[1].wait_recv()
    out.wait_recv()
    add(o_ref, [acc.at[1], crecv.at[1], xr])
    for copy in across + [out]:
        copy.wait_send()


def keys_reduce(p, ident):
    block = p.shape[1:]
    sems = pltpu.SemaphoreType.DMA((3,))
    return pl.pallas_call(
        keys_reduce_kernel,
        out_shape=jax.ShapeDtypeStruct(block, p.dtype),
        in_specs=[pl.BlockSpec(memory_space=pl.ANY)],
        out_specs=pl.BlockSpec(memory_space=pltpu.VMEM),
        scratch_shapes=[
            pltpu.VMEM((2,) + block, p.dtype), pltpu.VMEM((2,) + block, p.dtype),
            pltpu.VMEM(block, p.dtype), sems, sems, pltpu.SemaphoreType.DMA((2,)),
        ],
        compiler_params=pltpu.CompilerParams(
            collective_id=ident, has_side_effects=True, vmem_limit_bytes=VMEM
        ),
        name="keys_reduce",
    )(p)


def fits():
    return [lax.axis_size(n) for n in ALL] == [2, 2, 2, 4]


def gather_all(v, ident, name):
    if fits():
        return all_gather(v, 4, ident, name)
    return lax.all_gather(v, ALL, axis=0)


def gather_plane(v, ident, name):
    if fits():
        return all_gather(v, 1, ident, name)
    return lax.all_gather(v, DP, axis=0)


def scatter_all(p, ident, name):
    if fits():
        return reduce_scatter(p, 4, ident, name)
    return lax.psum_scatter(p, ALL, scatter_dimension=0)


def scatter_plane(p, ident, name):
    if fits():
        return reduce_scatter(p, 1, ident, name)
    return lax.psum_scatter(p, DP, scatter_dimension=0)


def keys_all_gather(v):
    if fits():
        return keys_gather(v, 11).reshape(-1, v.shape[1])
    return lax.all_gather(v, PART, axis=0, tiled=True)


def keys_sum_scatter(p):
    if fits():
        return keys_reduce(p.reshape(4, -1, p.shape[1]), 12)
    return lax.psum_scatter(p, PART, scatter_dimension=0, tiled=True)


def tile_spec(dp, deep, tile_rows, index, local=None):
    def place(t):
        j = index(t)
        return (j % dp, 0, j // dp if local is None else local, 0, 0)

    return pl.BlockSpec((None, deep, None, tile_rows, D), place)


def weight_specs(weights, *groups):
    arrays, specs = [], []
    for first, offset in groups:
        array, local = weights[first // weights[0][0].shape[0]]
        dp, deep, _, tile_rows, _ = array.shape
        arrays.append(array)
        specs.append(
            tile_spec(dp, deep, tile_rows, lambda t, f=first, o=offset: f + o(t), local)
        )
    return arrays, specs


def whole(shape):
    return pl.BlockSpec(shape, lambda t: (0,) * len(shape))


def dot_nn(a, b):
    return lax.dot_general(a, b, (((1,), (0,)), ((), ())), preferred_element_type=jnp.float32)


def dot_nt(a, b):
    return lax.dot_general(a, b, (((1,), (1,)), ((), ())), preferred_element_type=jnp.float32)


def dot_tn(a, b):
    return lax.dot_general(a, b, (((0,), (0,)), ((), ())), preferred_element_type=jnp.float32)


def turned(u, cos, sin):
    lane = lax.broadcasted_iota(jnp.int32, (u.shape[0], 128), 1)
    low = (lane % HD) < HD // 2
    parts = []
    for i in range(D // 128):
        v = u[:, i * 128 : (i + 1) * 128]
        other = jnp.where(low, pltpu.roll(v, 128 - HD // 2, 1), pltpu.roll(v, HD // 2, 1))
        parts.append(v * cos + other * sin)
    return jnp.concatenate(parts, axis=1)


def project_kernel(x_ref, g_ref, cos_ref, sin_ref, w_ref, q_ref, kv_ref, a_ref):
    t = pl.program_id(0)

    @pl.when(t == 0)
    def _():
        a_ref[...] = root_norm(x_ref[...], g_ref[...]).astype(jnp.bfloat16)

    m = dot_nn(a_ref[...], w_ref[...].reshape(D, D))

    @pl.when(t == 0)
    def _():
        q_ref[...] = turned(m, cos_ref[...], sin_ref[...]).astype(jnp.bfloat16)

    @pl.when(t == 1)
    def _():
        kv_ref[...] = turned(m, cos_ref[...], sin_ref[...]).astype(jnp.bfloat16)

    @pl.when(t == 2)
    def _():
        kv_ref[...] = m.astype(jnp.bfloat16)


def project(x, gain, cos, sin, weights):
    rows = x.shape[0]
    arrays, specs = weight_specs(weights, (0, lambda t: t))
    return pl.pallas_call(
        project_kernel,
        grid=(3,),
        out_shape=(
            jax.ShapeDtypeStruct((rows, D), jnp.bfloat16),
            jax.ShapeDtypeStruct((2, rows, D), jnp.bfloat16),
        ),
        in_specs=[
            whole((rows, D)), whole((1, D)), whole((rows, 128)), whole((rows, 128)), *specs,
        ],
        out_specs=(
            whole((rows, D)),
            pl.BlockSpec((None, rows, D), lambda t: (jnp.maximum(t - 1, 0), 0, 0)),
        ),
        scratch_shapes=[pltpu.VMEM((rows, D), jnp.bfloat16)],
        compiler_params=pltpu.CompilerParams(vmem_limit_bytes=VMEM),
        name="project",
    )(x, gain, cos, sin, *arrays)


def mask_bias(bias_ref, kseg_ref, qseg_ref, qpos_ref):
    kpos = lax.broadcasted_iota(jnp.int32, bias_ref.shape, 0)
    allowed = (kpos <= qpos_ref[...]) & (kseg_ref[...] == qseg_ref[...])
    bias_ref[...] = jnp.where(allowed, 0.0, MASKED)


def head_lanes(shape, head):
    return (lax.broadcasted_iota(jnp.int32, shape, 1) // HD) == head


def attend_kernel(q_ref, k_ref, v_ref, kseg_ref, qseg_ref, qpos_ref, o_ref, lse_ref, bias_ref):
    @pl.when(pl.program_id(0) == 0)
    def _():
        mask_bias(bias_ref, kseg_ref, qseg_ref, qpos_ref)

    length = bias_ref.shape[0]
    q = q_ref[...] * HD ** (-0.5)
    k, v = k_ref[...].reshape(length, 128), v_ref[...].reshape(length, 128)
    outs = []
    for head in range(2):
        mine = head_lanes(q.shape, head)
        s = dot_nt(k, jnp.where(mine, q, jnp.zeros_like(q))) + bias_ref[...]
        top = jnp.max(s, axis=0, keepdims=True)
        e = jnp.exp(s - top)
        total = jnp.sum(e, axis=0, keepdims=True)
        p = (e * (1.0 / total)).astype(jnp.bfloat16)
        outs.append(dot_tn(p, v))
        lse_ref[head : head + 1, :] = top + jnp.log(total)
    o_ref[...] = jnp.where(head_lanes(outs[0].shape, 0), outs[0], outs[1]).astype(jnp.bfloat16)


def attend_specs(rows, parts):
    length = parts * rows
    pair = pl.BlockSpec((rows, 128), lambda t: (0, t))
    return pair, [
        pair,
        pl.BlockSpec((parts, None, rows, 128), lambda t: (0, 0, 0, t)),
        pl.BlockSpec((parts, None, rows, 128), lambda t: (0, 1, 0, t)),
        whole((length, 1)), whole((1, rows)), whole((1, rows)),
    ]


def attend(q, kv, kseg, qseg, qpos):
    rows, parts = q.shape[0], kv.shape[0]
    pair, specs = attend_specs(rows, parts)
    return pl.pallas_call(
        attend_kernel,
        grid=(HEADS // 2,),
        out_shape=(
            jax.ShapeDtypeStruct((rows, D), jnp.bfloat16),
            jax.ShapeDtypeStruct((HEADS // 2, 8, rows), jnp.float32),
        ),
        in_specs=specs,
        out_specs=(pair, pl.BlockSpec((None, 8, rows), lambda t: (t, 0, 0))),
        scratch_shapes=[pltpu.VMEM((parts * rows, rows), jnp.float32)],
        compiler_params=pltpu.CompilerParams(vmem_limit_bytes=VMEM),
        name="attend",
    )(q, kv, kv, kseg, qseg, qpos)


def feed_kernel(x_ref, o_ref, g_ref, wo_ref, wg_ref, wu_ref, wd_ref, mid_ref, out_ref, b_ref):
    t = pl.program_id(0)

    @pl.when(t == 0)
    def _():
        mid = x_ref[...] + dot_nn(o_ref[...], wo_ref[...].reshape(D, D))
        mid_ref[...] = mid
        out_ref[...] = mid
        b_ref[...] = root_norm(mid, g_ref[...]).astype(jnp.bfloat16)

    @pl.when(t > 0)
    def _():
        gate = dot_nn(b_ref[...], wg_ref[...].reshape(D, D))
        up = dot_nn(b_ref[...], wu_ref[...].reshape(D, D))
        h = (gate * jax.nn.sigmoid(gate) * up).astype(jnp.bfloat16)
        out_ref[...] += dot_nn(h, wd_ref[...].reshape(D, D))


def feed(x, o, gain, weights):
    rows = x.shape[0]
    unit = lambda t: jnp.maximum(t - 1, 0)
    arrays, specs = weight_specs(
        weights, (3, lambda t: 0 * t), (4, unit), (4 + UNITS, unit), (4 + 2 * UNITS, unit)
    )
    state = jax.ShapeDtypeStruct((rows, D), jnp.float32)
    return pl.pallas_call(
        feed_kernel,
        grid=(1 + UNITS,),
        out_shape=(state, state),
        in_specs=[
            whole((rows, D)), whole((rows, D)), whole((1, D)), *specs,
        ],
        out_specs=(whole((rows, D)), whole((rows, D))),
        scratch_shapes=[pltpu.VMEM((rows, D), jnp.bfloat16)],
        compiler_params=pltpu.CompilerParams(vmem_limit_bytes=VMEM),
        name="feed",
    )(x, o, gain, *arrays)


def feed_back_kernel(
    groups, dy_ref, mid_ref, g_ref, o_ref, wo_ref, wg_ref, wu_ref, wd_ref, dx_ref, do_ref, dgain_ref,
    *refs,
):
    grad_refs, (b_ref, bt_ref, e_ref, dg_ref, du_ref, db_ref) = refs[:-6], refs[-6:]
    t = pl.program_id(0)
    last = pl.num_programs(0) - 1

    def emit(kind, g):
        ref = grad_refs[groups[kind]]
        ref[...] = g.astype(jnp.bfloat16).reshape(ref.shape)

    @pl.when(t == 0)
    def _():
        b = root_norm(mid_ref[...], g_ref[...])
        b_ref[...] = b.astype(jnp.bfloat16)
        bt_ref[...] = b.T.astype(jnp.bfloat16)
        e_ref[...] = dy_ref[...].astype(jnp.bfloat16)
        db_ref[...] = jnp.zeros_like(db_ref)

    @pl.when((t % 3 == 0) & (t < last))
    def _():
        gate = dot_nn(b_ref[...], wg_ref[...].reshape(D, D))
        up = dot_nn(b_ref[...], wu_ref[...].reshape(D, D))
        sigma = jax.nn.sigmoid(gate)
        h = (gate * sigma * up).astype(jnp.bfloat16)
        emit(0, dot_tn(h, e_ref[...]))
        dh = dot_nt(e_ref[...], wd_ref[...].reshape(D, D))
        dg_ref[...] = (dh * up * sigma * (1.0 + gate * (1.0 - sigma))).astype(jnp.bfloat16)
        du_ref[...] = (dh * gate * sigma).astype(jnp.bfloat16)

    @pl.when(t % 3 == 1)
    def _():
        emit(1, dot_nn(bt_ref[...], dg_ref[...]))
        db_ref[...] += dot_nt(dg_ref[...], wg_ref[...].reshape(D, D))

    @pl.when(t % 3 == 2)
    def _():
        emit(2, dot_nn(bt_ref[...], du_ref[...]))
        db_ref[...] += dot_nt(du_ref[...], wu_ref[...].reshape(D, D))

    @pl.when(t == last)
    def _():
        back, gain_back = norm_back(mid_ref[...], g_ref[...], db_ref[...])
        dx = dy_ref[...] + back
        dx_ref[...] = dx
        dgain_ref[...] = jnp.broadcast_to(gain_back[None, :], dgain_ref.shape)
        e1 = dx.astype(jnp.bfloat16)
        emit(3, dot_tn(o_ref[...], e1))
        do_ref[...] = dot_nt(e1, wo_ref[...].reshape(D, D)).astype(jnp.bfloat16)


def feed_back(dy, mid, gain, o, weights):
    rows = dy.shape[0]
    dp, deep, _, tile_rows, _ = weights[0][0].shape
    unit = lambda t: jnp.minimum(t // 3, UNITS - 1)
    arrays, specs = weight_specs(
        weights, (3, lambda t: 0 * t), (4, unit), (4 + UNITS, unit), (4 + 2 * UNITS, unit)
    )
    firsts = [4 + 2 * UNITS, 4, 4 + UNITS, 3]
    groups = [first // dp for first in firsts]

    def grad_tile(group, t):
        kinds = [k for k in range(3) if groups[k] == group]
        s, k = unit(t), t % 3
        tile = firsts[kinds[0]] + jnp.where(k < kinds[0], jnp.maximum(s - 1, 0), s)
        for kind in kinds[1:]:
            tile = jnp.where(k >= kind, firsts[kind] + s, tile)
        final = 3 if groups[3] == group else firsts[kinds[-1]] + UNITS - 1
        return jnp.where(t == 3 * UNITS, final, tile)

    return pl.pallas_call(
        functools.partial(feed_back_kernel, groups),
        grid=(3 * UNITS + 1,),
        out_shape=(
            jax.ShapeDtypeStruct((rows, D), jnp.float32),
            jax.ShapeDtypeStruct((rows, D), jnp.bfloat16),
            jax.ShapeDtypeStruct((8, D), jnp.float32),
        )
        + (jax.ShapeDtypeStruct((dp, deep, 1, tile_rows, D), jnp.bfloat16),) * len(weights),
        in_specs=[
            whole((rows, D)), whole((rows, D)), whole((1, D)), whole((rows, D)), *specs,
        ],
        out_specs=(whole((rows, D)), whole((rows, D)), whole((8, D)))
        + tuple(
            tile_spec(dp, deep, tile_rows, functools.partial(grad_tile, group), 0)
            for group in range(len(weights))
        ),
        scratch_shapes=[
            pltpu.VMEM((rows, D), jnp.bfloat16), pltpu.VMEM((D, rows), jnp.bfloat16),
            pltpu.VMEM((rows, D), jnp.bfloat16), pltpu.VMEM((rows, D), jnp.bfloat16),
            pltpu.VMEM((rows, D), jnp.bfloat16), pltpu.VMEM((rows, D), jnp.float32),
        ],
        compiler_params=pltpu.CompilerParams(vmem_limit_bytes=VMEM),
        name="feed_back",
    )(dy, mid, gain, o, *arrays)


def attend_back_kernel(
    q_ref, k_ref, v_ref, kseg_ref, qseg_ref, qpos_ref, do_ref, lse_ref, dq_ref, dkv_ref, bias_ref
):
    @pl.when(pl.program_id(0) == 0)
    def _():
        mask_bias(bias_ref, kseg_ref, qseg_ref, qpos_ref)

    length = bias_ref.shape[0]
    parts, rows = dkv_ref.shape[0], q_ref.shape[0]
    q, do = q_ref[...] * HD ** (-0.5), do_ref[...]
    k, v = k_ref[...].reshape(length, 128), v_ref[...].reshape(length, 128)
    dqs, dk, dv = [], None, None
    for head in range(2):
        mine = head_lanes(q.shape, head)
        qm = jnp.where(mine, q, jnp.zeros_like(q))
        dom = jnp.where(mine, do, jnp.zeros_like(do))
        s = dot_nt(k, qm) + bias_ref[...]
        p = jnp.exp(s - lse_ref[head : head + 1, :])
        dp = dot_nt(v, dom)
        delta = jnp.sum(p * dp, axis=0, keepdims=True)
        ds = (p * (dp - delta)).astype(jnp.bfloat16)
        dv_part = dot_nn(p.astype(jnp.bfloat16), dom)
        dk_part = dot_nn(ds, qm)
        dv = dv_part if dv is None else dv + dv_part
        dk = dk_part if dk is None else dk + dk_part
        dqs.append(dot_tn(ds, k))
    dq_ref[...] = jnp.where(head_lanes(dqs[0].shape, 0), dqs[0], dqs[1]) * HD ** (-0.5)
    dkv_ref[:, 0] = dk.astype(jnp.bfloat16).reshape(parts, rows, 128)
    dkv_ref[:, 1] = dv.astype(jnp.bfloat16).reshape(parts, rows, 128)


def attend_back(q, kv, kseg, qseg, qpos, do, lse):
    rows, parts = q.shape[0], kv.shape[0]
    pair, specs = attend_specs(rows, parts)
    return pl.pallas_call(
        attend_back_kernel,
        grid=(HEADS // 2,),
        out_shape=(
            jax.ShapeDtypeStruct((rows, D), jnp.float32),
            jax.ShapeDtypeStruct((parts, 2, rows, D), jnp.bfloat16),
        ),
        in_specs=specs + [pair, pl.BlockSpec((None, 8, rows), lambda t: (t, 0, 0))],
        out_specs=(pair, pl.BlockSpec((parts, 2, rows, 128), lambda t: (0, 0, 0, t))),
        scratch_shapes=[pltpu.VMEM((parts * rows, rows), jnp.float32)],
        compiler_params=pltpu.CompilerParams(vmem_limit_bytes=VMEM),
        name="attend_back",
    )(q, kv, kv, kseg, qseg, qpos, do, lse)


def project_back_kernel(
    dx_ref, x_ref, g_ref, cos_ref, sin_ref, dq_ref, dkv_ref, w_ref, held_ref,
    grad_ref, out_ref, dgain_ref, a_ref, dm_ref, da_ref,
):
    t = pl.program_id(0)
    deep, tile_rows = grad_ref.shape[0], grad_ref.shape[1]

    @pl.when(t == 0)
    def _():
        a_ref[...] = root_norm(x_ref[...], g_ref[...]).astype(jnp.bfloat16)
        da_ref[...] = jnp.zeros_like(da_ref)
        dm_ref[...] = turned(dq_ref[...], cos_ref[...], -sin_ref[...]).astype(jnp.bfloat16)

    @pl.when(t == 1)
    def _():
        dk = dkv_ref[0].astype(jnp.float32)
        dm_ref[...] = turned(dk, cos_ref[...], -sin_ref[...]).astype(jnp.bfloat16)

    @pl.when(t == 2)
    def _():
        dm_ref[...] = dkv_ref[1]

    grad = dot_tn(a_ref[...], dm_ref[...])
    grad_ref[...] = grad.astype(jnp.bfloat16).reshape(deep, tile_rows, D)
    da_ref[...] += dot_nt(dm_ref[...], w_ref[...].reshape(D, D))

    @pl.when(t == 2)
    def _():
        back, gain_back = norm_back(x_ref[...], g_ref[...], da_ref[...])
        out_ref[...] = dx_ref[...] + back
        dgain_ref[...] = jnp.broadcast_to(gain_back[None, :], dgain_ref.shape)


def project_back(dx, x, gain, cos, sin, dq, dkv, weights, grads):
    rows = x.shape[0]
    dp, deep, _, tile_rows, _ = weights[0][0].shape
    arrays, specs = weight_specs(weights, (0, lambda t: t))
    return pl.pallas_call(
        project_back_kernel,
        grid=(3,),
        out_shape=(
            jax.ShapeDtypeStruct(grads.shape, grads.dtype),
            jax.ShapeDtypeStruct((rows, D), jnp.float32),
            jax.ShapeDtypeStruct((8, D), jnp.float32),
        ),
        in_specs=[
            whole((rows, D)), whole((rows, D)), whole((1, D)), whole((rows, 128)),
            whole((rows, 128)), whole((rows, D)), whole((2, rows, D)),
            *specs,
            pl.BlockSpec(memory_space=pl.ANY),
        ],
        out_specs=(
            tile_spec(dp, deep, tile_rows, lambda t: t, 0), whole((rows, D)), whole((8, D)),
        ),
        scratch_shapes=[
            pltpu.VMEM((rows, D), jnp.bfloat16), pltpu.VMEM((rows, D), jnp.bfloat16),
            pltpu.VMEM((rows, D), jnp.float32),
        ],
        input_output_aliases={8: 0},
        compiler_params=pltpu.CompilerParams(vmem_limit_bytes=VMEM),
        name="project_back",
    )(dx, x, gain, cos, sin, dq, dkv, *arrays, grads)


def layer_forward(state, weights, layer, gains, cos, sin, marks):
    rows = state.shape[0]
    q, kv = project(state, gains[2 * layer : 2 * layer + 1], cos, sin, weights)
    kv = keys_all_gather(kv.reshape(2 * rows, D)).reshape(-1, 2, rows, D)
    o, lse = attend(q, kv, *marks)
    mid, out = feed(state, o, gains[2 * layer + 1 : 2 * layer + 2], weights)
    return out, (state, mid, q, kv, lse, o)


def layer_backward(grad, kept, weights, layer, gains, cos, sin, marks):
    state, mid, q, kv, lse, o = kept
    rows = state.shape[0]
    dx, do, feed_gain, *grads = feed_back(
        grad, mid, gains[2 * layer + 1 : 2 * layer + 2], o, weights
    )
    dq, dkv = attend_back(q, kv, *marks, do, lse)
    dkv = keys_sum_scatter(dkv.reshape(-1, D)).reshape(2, rows, D)
    grads[0], dx, input_gain = project_back(
        dx, state, gains[2 * layer : 2 * layer + 1], cos, sin, dq, dkv, weights, grads[0]
    )
    return dx, grads, [input_gain[0], feed_gain[0]]


def padded(v):
    count = -(-v.shape[0] // 2048) * 2048
    return jnp.pad(v, (0, count - v.shape[0])).reshape(-1, 128)


def place_kernel(slot_ref, mine_ref, w_ref, o_ref):
    g = pl.program_id(0)
    count = o_ref.shape[0]
    for i in range(count):
        t = g * count + i
        o_ref[i] = jnp.where(mine_ref[t] > 0, w_ref[slot_ref[t]], 0.0).astype(jnp.bfloat16)


def place_tiles(tile_weight, slots, mine, dp_size):
    count = slots.shape[0] // dp_size
    cap, rows, cols = tile_weight.shape
    return pl.pallas_call(
        place_kernel,
        grid_spec=pltpu.PrefetchScalarGridSpec(
            num_scalar_prefetch=2,
            grid=(dp_size,),
            in_specs=[pl.BlockSpec((cap, rows, cols), lambda g, *_: (0, 0, 0))],
            out_specs=pl.BlockSpec((count, rows, cols), lambda g, *_: (g, 0, 0)),
        ),
        out_shape=jax.ShapeDtypeStruct((dp_size * count, rows, cols), jnp.bfloat16),
        compiler_params=pltpu.CompilerParams(vmem_limit_bytes=VMEM),
        name="place_tiles",
    )(slots, mine, tile_weight)


def shards(
    tokens,
    segments,
    completion,
    targets,
    owners,
    step_count,
    tile_weight,
    tile_first,
    tile_second,
    table_weight,
    table_first,
    table_second,
    head_weight,
    head_first,
    head_second,
    gain_weight,
    gain_first,
    gain_second,
):
    a_size, b_size, rep_size = lax.axis_size("y"), lax.axis_size(PART), lax.axis_size("z")
    a_index, b_index, rep_index = lax.axis_index("y"), lax.axis_index(PART), lax.axis_index("z")
    dp_size = a_size * b_size
    devices = dp_size * rep_size
    dp_index = a_index * b_size + b_index
    device = dp_index * rep_size + rep_index
    rows = tokens.shape[1]
    length = segments.shape[1]
    comp = completion.shape[1]
    slots_cap, tile_rows = tile_weight.shape[:2]
    tile_count = owners.shape[0]
    home_tiles = tile_count // dp_size
    vocab_rows = table_weight.shape[0]
    vocab_start = device * vocab_rows
    sequence = a_index * rep_size + rep_index

    own_part = jnp.concatenate(
        [
            tokens[0],
            lax.dynamic_slice_in_dim(segments[0], rep_index * rows, rows),
            lax.dynamic_slice_in_dim(completion[0], rep_index * (comp // rep_size), comp // rep_size),
            lax.dynamic_slice_in_dim(targets[0], rep_index * (comp // rep_size), comp // rep_size),
        ]
    )
    slots = tile_slots(owners)
    mine = owners == dp_index
    per = TILES_PER // dp_size
    home_ids = (
        jnp.arange(LAYERS)[None, :, None] * TILES_PER
        + jnp.arange(per)[None, None, :] * dp_size
        + jnp.arange(dp_size)[:, None, None]
    ).reshape(-1)
    home_mine = jnp.take(mine, home_ids)
    home_slots = jnp.where(home_mine, jnp.take(slots, home_ids), 0)
    placed = place_tiles(tile_weight, home_slots, home_mine.astype(jnp.int32), dp_size)
    placed = placed.reshape(dp_size, -1, D)
    if fits():
        home, packed = scatter_and_gather([placed], 1, padded(own_part), 4, 0, "home_and_ids")
    else:
        home = lax.psum_scatter(placed, DP, scatter_dimension=0)
        packed = lax.all_gather(padded(own_part), ALL, axis=0)
    packed = packed.reshape(devices, -1)[:, : own_part.shape[0]]
    packed = packed.reshape(dp_size, rep_size, -1)
    tokens_all = packed[:, :, :rows].reshape(dp_size, length)
    segments_all = packed[:, :, rows : 2 * rows].reshape(dp_size, length)
    edge = 2 * rows + comp // rep_size
    completion_all = packed[:, :, 2 * rows : edge].reshape(dp_size, comp)
    targets_all = packed[:, :, edge:].reshape(dp_size, comp)

    home = home.reshape(LAYERS, per, tile_rows, D)
    spread = lax.all_gather(home[0], ALL, axis=0)
    spread = spread.reshape(dp_size, rep_size, per, tile_rows, D)
    weights = [[(spread, i) for i in range(per)]]
    later = [[lax.all_gather(home[index, i], ALL, axis=0) for i in range(1, per)] for index in range(1, LAYERS)]

    order = tokens_all.reshape(a_size, rep_size, b_size, rows).transpose(0, 2, 1, 3).reshape(-1)
    place = order - vocab_start
    vocab_iota = jnp.arange(vocab_rows)
    token_hot = (place[:, None] == vocab_iota[None, :]).astype(jnp.bfloat16)
    picked = jnp.dot(
        token_hot, table_weight.astype(jnp.bfloat16), preferred_element_type=jnp.float32
    ).astype(jnp.bfloat16)
    picked = picked.reshape(devices, rows, D)
    early = {}
    if fits():
        state, early[1] = scatter_and_gather([picked], 4, home[1, 0], 4, 8, "rows_and_weights")
    else:
        state = lax.psum_scatter(picked, ALL, scatter_dimension=0)
    state = state.astype(jnp.float32)

    for index in range(1, LAYERS):
        first = early[index] if index in early else gather_all(home[index, 0], 1, "weights_gather")
        weights.append(
            [
                (array.reshape(dp_size, rep_size, 1, tile_rows, D), 0)
                for array in [first] + later[index - 1]
            ]
        )
    first_place = b_index * rows
    places = first_place + jnp.arange(rows)
    cosine, sine = rope_tables(places.astype(jnp.float32))
    own_segments = lax.dynamic_index_in_dim(segments_all, sequence, 0, False)
    query_segments = lax.dynamic_slice_in_dim(own_segments, first_place, rows)
    marks = (own_segments[:, None], query_segments[None, :], places[None, :])
    kept_list = []
    for index in range(LAYERS):
        state, kept = layer_forward(
            state, weights[index], index, gain_weight, cosine, sine, marks
        )
        kept_list.append(kept)
    final_gain = gain_weight[2 * LAYERS]
    final = root_norm(state, final_gain).astype(jnp.bfloat16)

    capacity = 3 * comp // (2 * rep_size)
    block = completion_all // rows
    inside = block[:, None, :] == jnp.arange(b_size)[None, :, None]
    before = jnp.sum((block[:, None, :] < jnp.arange(b_size)[None, :, None]).astype(jnp.int32), axis=2)
    rank = jnp.arange(comp)[None, None, :] - before[:, :, None]
    slot_pick = inside[..., None] & (rank[..., None] == jnp.arange(capacity))
    filled = jnp.any(slot_pick, axis=2)
    wanted = jnp.where(
        filled, jnp.sum(jnp.where(slot_pick, targets_all[:, None, :, None], 0), axis=2), -1
    )
    spots = jnp.where(
        filled, jnp.sum(jnp.where(slot_pick, (completion_all % rows)[:, None, :, None], 0), axis=2), -1
    )
    all_wanted = (
        wanted.reshape(a_size, rep_size, b_size, capacity).transpose(0, 2, 1, 3).reshape(-1)
    )
    own_spots = lax.dynamic_index_in_dim(
        lax.dynamic_index_in_dim(spots, sequence, 0, False), b_index, 0, False
    )
    select = (own_spots[:, None] == jnp.arange(rows)[None, :]).astype(jnp.bfloat16)
    chosen = jnp.dot(select, final, preferred_element_type=jnp.float32).astype(jnp.bfloat16)
    all_rows = gather_all(chosen, 3, "chosen_gather").reshape(-1, D)
    head_low = head_weight.astype(jnp.bfloat16)
    logits = jnp.einsum("rd,vd->rv", all_rows, head_low, preferred_element_type=jnp.float32)
    hot = vocab_iota[None, :] == (all_wanted - vocab_start)[:, None]
    local_top = jnp.max(logits, axis=-1)
    local_total = jnp.sum(jnp.exp(logits - local_top[:, None]), axis=-1)
    local_hit = jnp.sum(jnp.where(hot, logits, 0.0), axis=-1)
    own_stats = jnp.concatenate(
        [v.reshape(-1, 128) for v in (local_top, local_total, local_hit)]
    )
    stats = gather_all(own_stats, 4, "stats_gather")
    tops, totals, hits = jnp.split(stats, 3, axis=1)
    top = jnp.max(tops, axis=0)
    total = jnp.sum(totals * jnp.exp(tops - top[None]), axis=0)
    log_total = (top + jnp.log(total)).reshape(-1)
    target_hit = jnp.sum(hits, axis=0).reshape(-1)
    valid = all_wanted >= 0
    scored = dp_size * comp
    loss = jnp.sum(jnp.where(valid, log_total - target_hit, 0.0)) / scored
    logit_grad = jnp.where(
        valid[:, None],
        (jnp.exp(logits - log_total[:, None]) - jnp.where(hot, 1.0, 0.0)) / scored,
        0.0,
    ).astype(jnp.bfloat16)
    logit_grad = lax.optimization_barrier(logit_grad)
    rows_grad = jnp.dot(logit_grad, head_low, preferred_element_type=jnp.float32)
    own_rows = scatter_all(
        rows_grad.astype(jnp.bfloat16).reshape(devices, -1, D), 9, "back_scatter"
    )
    head_grad = jnp.einsum("rv,rd->vd", logit_grad, all_rows, preferred_element_type=jnp.float32)
    final_grad = jnp.einsum("ct,cd->td", select, own_rows, preferred_element_type=jnp.float32)
    state_grad, final_gain_grad = norm_back(state, final_gain, final_grad)
    tile_parts = [None] * LAYERS
    gain_parts = [None] * LAYERS
    for index in reversed(range(LAYERS)):
        state_grad, tile_parts[index], gain_parts[index] = layer_backward(
            state_grad, kept_list[index], weights[index], index, gain_weight, cosine, sine, marks
        )
    entry = state_grad.astype(jnp.bfloat16)
    flat = [[part.reshape(devices, -1, D) for part in layer] for layer in tile_parts]
    if fits():
        tail = [lax.psum_scatter(flat[-1][-1], ALL, scatter_dimension=0)]
        firsts = [part for layer in flat for part in layer][:-1]
        body, piece_grads = scatter_and_gather(firsts, 4, entry, 4, 2, "grads_and_entry", (2,))
        home_grads = [body] + tail
    else:
        home_grads = [
            lax.psum_scatter(part, ALL, scatter_dimension=0) for layer in flat for part in layer
        ]
        piece_grads = lax.all_gather(entry, ALL, axis=0)
    table_grad = jnp.einsum(
        "tv,td->vd", token_hot, piece_grads.reshape(-1, D), preferred_element_type=jnp.float32
    )
    plane_grad = lax.all_gather(jnp.concatenate(home_grads), DP, axis=0)
    plane_grad = plane_grad.reshape(tile_count, tile_rows, D)
    own_count = jnp.sum(mine.astype(jnp.int32))
    slot_ids = jnp.arange(slots_cap)
    picks = mine[home_ids][None, :] & (slots[home_ids][None, :] == slot_ids[:, None])
    tile_of_slot = jnp.sum(jnp.where(picks, jnp.arange(tile_count)[None, :], 0), axis=1)
    slot_valid = (slot_ids < own_count)[:, None, None]
    own_grad = jnp.where(
        slot_valid, jnp.take(plane_grad, tile_of_slot, axis=0).astype(jnp.float32), 0.0
    )
    gain_grads = jnp.stack([g for pair in gain_parts for g in pair] + [final_gain_grad])
    square = (
        jnp.sum(own_grad * own_grad)
        + jnp.sum(table_grad * table_grad)
        + jnp.sum(head_grad * head_grad)
    )
    sums = gather_all(
        padded(jnp.concatenate([square[None], gain_grads.reshape(-1)])), 5, "sums_gather"
    )
    sums = jnp.sum(sums.reshape(devices, -1), axis=0)
    square, gain_grads = sums[0], sums[1 : 1 + gain_grads.size].reshape(gain_grads.shape)
    norm = jnp.sqrt(square + jnp.sum(gain_grads * gain_grads))
    factor = jnp.minimum(1.0, CLIP_NORM / norm)
    steps = step_count[0].astype(jnp.float32)
    tile_new, tile_first_new, tile_second_new = adam(
        tile_weight, tile_first, tile_second, own_grad, factor, RATE_TILE, DECAY, steps
    )
    tile_new = jnp.where(slot_valid, tile_new, 0.0)
    tile_first_new = jnp.where(slot_valid, tile_first_new, 0.0)
    tile_second_new = jnp.where(slot_valid, tile_second_new, 0.0)
    table_new, table_first_new, table_second_new = adam(
        table_weight, table_first, table_second, table_grad, factor, RATE_TABLE, DECAY, steps
    )
    head_new, head_first_new, head_second_new = adam(
        head_weight, head_first, head_second, head_grad, factor, RATE_HEAD, DECAY, steps
    )
    gain_new, gain_first_new, gain_second_new = adam(
        gain_weight, gain_first, gain_second, gain_grads, factor, RATE_GAIN, 0.0, steps
    )
    return (
        loss,
        norm,
        tile_new,
        tile_new.astype(jnp.bfloat16),
        tile_first_new,
        tile_second_new,
        table_new,
        table_new.astype(jnp.bfloat16),
        table_first_new,
        table_second_new,
        head_new,
        head_new.astype(jnp.bfloat16),
        head_first_new,
        head_second_new,
        gain_new,
        gain_first_new,
        gain_second_new,
    )


def solution(mesh):
    dp_size, rep_size = mesh.shape["dp"], mesh.shape["rep"]
    split = Mesh(mesh.devices.reshape(dp_size // rep_size, rep_size // 2, 2, rep_size), ALL)
    return jax.shard_map(
        shards,
        mesh=split,
        in_specs=(
            P(DP, "z"),
            P(DP, None),
            P(DP, None),
            P(DP, None),
            P(),
            P(),
            P(ALL, None, None),
            P(ALL, None, None),
            P(ALL, None, None),
            P(ALL, None),
            P(ALL, None),
            P(ALL, None),
            P(ALL, None),
            P(ALL, None),
            P(ALL, None),
            P(),
            P(),
            P(),
        ),
        out_specs=(
            P(),
            P(),
            P(ALL, None, None),
            P(ALL, None, None),
            P(ALL, None, None),
            P(ALL, None, None),
            P(ALL, None),
            P(ALL, None),
            P(ALL, None),
            P(ALL, None),
            P(ALL, None),
            P(ALL, None),
            P(ALL, None),
            P(ALL, None),
            P(),
            P(),
            P(),
        ),
        check_vma=False,
    )
```

```python
import functools

import jax
import jax.numpy as jnp
from jax import lax
from jax.experimental import pallas as pl
from jax.experimental.pallas import tpu as pltpu
from jax.sharding import Mesh, PartitionSpec as P

D = 768
HEADS = 12
HD = 64
FF = 3072
LAYERS = 2


EPS_NORM = 1e-05
EPS_ADAM = 1e-08
CLIP_NORM = 0.005
BETA_FIRST = 0.5
BETA_SECOND = 0.5
DECAY = 0.1
RATE_TILE = 0.02
RATE_HEAD = 0.05
RATE_TABLE = 0.5
RATE_GAIN = 0.3
MASKED = -1e30


def root_norm(training_state, gain):
    return (
        training_state
        * lax.rsqrt(jnp.mean(training_state * training_state, axis=-1, keepdims=True) + EPS_NORM)
        * gain
    )


def norm_back(training_state, gain, grad):
    scale = lax.rsqrt(jnp.mean(training_state * training_state, axis=-1, keepdims=True) + EPS_NORM)
    scaled = grad * gain
    state_grad = scale * scaled - training_state * scale**3 * jnp.mean(
        scaled * training_state, axis=-1, keepdims=True
    )
    gain_grad = jnp.sum(
        (grad * training_state * scale).reshape(-1, training_state.shape[-1]), axis=0
    )
    return (state_grad, gain_grad)


def rope_tables(places):
    freqs = jnp.power(10000.0, -2.0 * jnp.arange(HD // 2).astype(jnp.float32) / HD)
    angle = places[:, None] * freqs[None, :]
    cosine, sine = jnp.cos(angle), jnp.sin(angle)
    return jnp.concatenate([cosine] * 4, axis=1), jnp.concatenate([-sine, sine] * 2, axis=1)


def tile_slots(owners):
    order = jnp.arange(owners.shape[0], dtype=jnp.int32)
    same = (owners[:, None] == owners[None, :]) & (order[None, :] < order[:, None])
    return jnp.sum(same.astype(jnp.int32), axis=1)


def adam(weight, first, second, grad, factor, rate, decay, steps):
    grad = grad * factor
    first = BETA_FIRST * first + (1.0 - BETA_FIRST) * grad
    second = BETA_SECOND * second + (1.0 - BETA_SECOND) * grad * grad
    first_hat = first / (1.0 - jnp.power(BETA_FIRST, steps))
    second_hat = second / (1.0 - jnp.power(BETA_SECOND, steps))
    weight = weight - rate * (first_hat / (jnp.sqrt(second_hat) + EPS_ADAM) + decay * weight)
    return (weight, first, second)


ALL = ("y", "x", "c", "z")
DP = ("y", "x", "c")
PART = ("x", "c")
UNITS = FF // D
TILES_PER = 4 + 3 * UNITS


MESH = pl.DeviceIdType.MESH
LAG_ONE, LAG_MANY = 8, 6
VMEM, VMEM_LAYER = 60 << 20, 44 << 20


def half_rows(rows, dtype):
    unit = 16 if jnp.dtype(dtype).itemsize == 2 else 8
    return (rows // 2 + unit - 1) // unit * unit


def remote(src, dst, ssem, rsem, **to):
    return pltpu.make_async_remote_copy(
        src_ref=src, dst_ref=dst, send_sem=ssem, recv_sem=rsem, device_id=to, device_id_type=MESH
    )


def greet(zn, y, x, c, z):
    barrier = pltpu.get_barrier_semaphore()
    for to in ({"x": 1 - x}, {"y": 1 - y}, {"c": 1 - c}):
        pl.semaphore_signal(barrier, inc=1, device_id=to, device_id_type=MESH)
    if zn > 1:

        @pl.when(z < zn - 1)
        def _():
            pl.semaphore_signal(barrier, inc=1, device_id={"z": z + 1}, device_id_type=MESH)

        @pl.when(z > 0)
        def _():
            pl.semaphore_signal(barrier, inc=1, device_id={"z": z - 1}, device_id_type=MESH)

        @pl.when((z > 0) & (z < zn - 1))
        def _():
            pl.semaphore_wait(barrier, 5)

        @pl.when((z == 0) | (z == zn - 1))
        def _():
            pl.semaphore_wait(barrier, 4)
    else:
        pl.semaphore_wait(barrier, 3)


def gather_steps(zn, x_ref, o_ref, hold, ssem, rsem, lsem):
    y, x, c, z = [lax.axis_index(n) for n in ALL]
    me = z if zn > 1 else 0
    rows = x_ref.shape[0]
    h0 = half_rows(rows, x_ref.dtype)
    lo, hi = pl.ds(0, h0), pl.ds(h0, rows - h0)
    X, Y, DX, DY, CO, CX, CY, C0, C1, ZU, ZD = range(11)
    nx, ny, nc = {"x": 1 - x}, {"y": 1 - y}, {"c": 1 - c}

    def slot(yy, xx, zz):
        return ((yy * 2 + xx) * 2 + c) * zn + zz

    def copy(kind, k, src, dst, to):
        return remote(src, dst, ssem.at[kind, k], rsem.at[kind, k], **to)

    def block(s):
        return o_ref.at[s]

    local = pltpu.make_async_copy(x_ref, hold, lsem.at[0])
    local.start()
    keep = pltpu.make_async_copy(hold, o_ref.at[slot(y, x, me)], lsem.at[1])

    def spread(zb, src):
        dst = block(slot(y, x, zb))
        copy(X, zb, src, dst, nx).start()
        copy(Y, zb, src, dst, ny).start()
        copy(CO, zb, src, dst, nc).start()

    def up(s):
        zb = z - (s - 1)
        b = block(slot(y, x, zb))
        return copy(ZU, s, x_ref if s == 1 else b, b, {"z": z + 1})

    def down(s):
        zb = z + (s - 1)
        b = block(slot(y, x, zb))
        return copy(ZD, s, x_ref if s == 1 else b, b, {"z": z - 1})

    for s in range(1, zn):

        @pl.when((z < zn - 1) & (z - (s - 1) >= 0))
        def _():
            up(s).start()

        @pl.when((z > 0) & (z + (s - 1) < zn))
        def _():
            down(s).start()

        if s == 1:
            spread(me, x_ref)
            local.wait()
            keep.start()
        yield

        @pl.when(z - s >= 0)
        def _():
            copy(ZU, s, x_ref, x_ref, nx).wait_recv()
            spread(z - s, block(slot(y, x, z - s)))

        @pl.when(z + s < zn)
        def _():
            copy(ZD, s, x_ref, x_ref, nx).wait_recv()
            spread(z + s, block(slot(y, x, z + s)))

    if zn == 1:
        spread(0, x_ref)
        local.wait()
        keep.start()
    order = [lax.rem(z + j, zn) if zn > 1 else 0 for j in range(zn)]
    for zb in order:
        yield
        sx, sy = slot(y, 1 - x, zb), slot(1 - y, x, zb)
        copy(X, zb, x_ref, x_ref, nx).wait_recv()
        copy(DX, zb, o_ref.at[sx, lo], o_ref.at[sx, lo], ny).start()
        copy(CX, zb, block(sx), block(sx), nc).start()
        copy(Y, zb, x_ref, x_ref, nx).wait_recv()
        copy(DY, zb, o_ref.at[sy, hi], o_ref.at[sy, hi], nx).start()
        copy(CY, zb, block(sy), block(sy), nc).start()
    for zb in order:
        yield
        sd = slot(1 - y, 1 - x, zb)
        copy(DX, zb, x_ref.at[lo], x_ref.at[lo], nx).wait_recv()
        copy(C0, zb, o_ref.at[sd, lo], o_ref.at[sd, lo], nc).start()
        copy(DY, zb, x_ref.at[hi], x_ref.at[hi], nx).wait_recv()
        copy(C1, zb, o_ref.at[sd, hi], o_ref.at[sd, hi], nc).start()
    yield
    for zb in range(zn):
        for kind, part in ((CO, x_ref), (CX, x_ref), (CY, x_ref), (C0, x_ref.at[lo]), (C1, x_ref.at[hi])):
            copy(kind, zb, part, part, nx).wait_recv()
        for kind, part in (
            (X, x_ref), (Y, x_ref), (CO, x_ref), (CX, x_ref), (CY, x_ref),
            (DX, x_ref.at[lo]), (DY, x_ref.at[hi]), (C0, x_ref.at[lo]), (C1, x_ref.at[hi]),
        ):
            copy(kind, zb, part, part, nx).wait_send()
    for s in range(1, zn):

        @pl.when((z < zn - 1) & (z - (s - 1) >= 0))
        def _():
            up(s).wait_send()

        @pl.when((z > 0) & (z + (s - 1) < zn))
        def _():
            down(s).wait_send()

    keep.wait()


def run_steps(*parts):
    parts, turn = list(parts), 0
    while parts:
        for part in list(parts):
            if turn >= part[0] and next(part[1], part) is part:
                parts.remove(part)
        turn += 1


def gather_kernel(zn, *refs):
    greet(zn, *[lax.axis_index(n) for n in ALL])
    run_steps((0, gather_steps(zn, *refs)))


def gather_scratch(zn, shape, dtype):
    sems = pltpu.SemaphoreType.DMA((11, zn))
    return [pltpu.VMEM(shape, dtype), sems, sems, pltpu.SemaphoreType.DMA((2,))]


def all_gather(x, zn, ident, name):
    return pl.pallas_call(
        functools.partial(gather_kernel, zn),
        out_shape=jax.ShapeDtypeStruct((8 * zn,) + x.shape, x.dtype),
        in_specs=[pl.BlockSpec(memory_space=pl.ANY)],
        out_specs=pl.BlockSpec(memory_space=pl.ANY),
        scratch_shapes=gather_scratch(zn, x.shape, x.dtype),
        compiler_params=pltpu.CompilerParams(
            collective_id=ident, has_side_effects=True, vmem_limit_bytes=VMEM
        ),
        name=name,
    )(x)


def reduce_steps(zn, p_ref, at, o_ref, to, acc, crecv, dxr, dyr, xr, yr, zur, zdr, ssem, rsem, lsem):
    y, x, c, z = [lax.axis_index(n) for n in ALL]
    me = z if zn > 1 else 0
    rows = acc.shape[1]
    h0 = half_rows(rows, acc.dtype)
    h1 = rows - h0
    X, Y, DX, DY, ZU, ZD, C0 = range(7)
    nx, ny, nc = {"x": 1 - x}, {"y": 1 - y}, {"c": 1 - c}
    kinds = [(y, x), (y, 1 - x), (1 - y, x), (1 - y, 1 - x)]
    step = 32 if rows % 32 == 0 else 16
    zorder = sorted(range(zn), key=lambda zb: (abs(2 * zb - zn + 1), zb), reverse=True)
    out_rows = o_ref.at[pl.ds(to, rows)]

    def slot(k, cc, zz):
        yy, xx = kinds[k]
        return ((yy * 2 + xx) * 2 + cc) * zn + zz

    def copy(kind, k, src, dst, to):
        return remote(src, dst, ssem.at[kind, k], rsem.at[kind, k], **to)

    def load(k, zb):
        b = k * zn + zb
        return pltpu.make_async_copy(p_ref.at[slot(k, c, zb), pl.ds(at, rows)], acc.at[b], lsem.at[b])

    def across(k, zb):
        source = p_ref.at[slot(k, 1 - c, zb), pl.ds(at, rows)]
        return copy(C0 + k, zb, source, crecv.at[k * zn + zb], nc)

    def add(dst, start, count, terms):
        size = step if count % step == 0 else 16

        @pl.loop(0, count // size)
        def _(i):
            here = pl.ds(pl.multiple_of(start + i * size, 16), size)
            total = None
            for ref, base in terms:
                part = ref[pl.ds(pl.multiple_of(start - base + i * size, 16), size), :].astype(jnp.float32)
                total = part if total is None else total + part
            dst[here, :] = total.astype(dst.dtype)

    for k in (3, 1, 2, 0):
        for zb in zorder:
            across(k, zb).start()
            load(k, zb).start()

    def ready(k, zb):
        load(k, zb).wait()
        across(k, zb).wait_recv()

    for zb in zorder:
        yield
        ready(3, zb)
        b = 3 * zn + zb
        add(acc.at[b], 0, rows, [(acc.at[b], 0), (crecv.at[b], 0)])
        copy(DX, zb, acc.at[b, pl.ds(0, h0)], dxr.at[zb], nx).start()
        copy(DY, zb, acc.at[b, pl.ds(h0, h1)], dyr.at[zb], ny).start()
    for zb in zorder:
        yield
        ready(1, zb)
        b = zn + zb
        add(acc.at[b], 0, h0, [(acc.at[b], 0), (crecv.at[b], 0)])
        copy(DY, zb, dyr.at[zb], dyr.at[zb], ny).wait_recv()
        add(acc.at[b], h0, h1, [(acc.at[b], 0), (crecv.at[b], 0), (dyr.at[zb], h0)])
        copy(X, zb, acc.at[b], xr.at[zb], nx).start()
        yield
        ready(2, zb)
        b = 2 * zn + zb
        add(acc.at[b], h0, h1, [(acc.at[b], 0), (crecv.at[b], 0)])
        copy(DX, zb, dxr.at[zb], dxr.at[zb], nx).wait_recv()
        add(acc.at[b], 0, h0, [(acc.at[b], 0), (crecv.at[b], 0), (dxr.at[zb], 0)])
        copy(Y, zb, acc.at[b], yr.at[zb], ny).start()

    def column(zb):
        return [(acc.at[zb], 0), (crecv.at[zb], 0), (xr.at[zb], 0), (yr.at[zb], 0)]

    for zb in zorder:
        yield
        ready(0, zb)
        copy(X, zb, acc.at[zb], xr.at[zb], nx).wait_recv()
        copy(Y, zb, acc.at[zb], yr.at[zb], ny).wait_recv()
        if zn == 1:
            add(out_rows, 0, rows, column(0))
            continue

        def upward(zb=zb):
            return copy(ZU, zb, acc.at[zb], zur.at[zb], {"z": z + 1})

        def downward(zb=zb):
            return copy(ZD, zb, acc.at[zb], zdr.at[zb], {"z": z - 1})

        @pl.when(z == zb)
        def _():
            add(acc.at[zb], 0, rows, column(zb))

        @pl.when((z < zb) & (z == 0))
        def _():
            add(acc.at[zb], 0, rows, column(zb))
            upward().start()

        @pl.when((z < zb) & (z > 0))
        def _():
            upward().wait_recv()
            add(acc.at[zb], 0, rows, column(zb) + [(zur.at[zb], 0)])
            upward().start()

        @pl.when((z > zb) & (z == zn - 1))
        def _():
            add(acc.at[zb], 0, rows, column(zb))
            downward().start()

        @pl.when((z > zb) & (z < zn - 1))
        def _():
            downward().wait_recv()
            add(acc.at[zb], 0, rows, column(zb) + [(zdr.at[zb], 0)])
            downward().start()

    yield
    if zn > 1:

        @pl.when(z == 0)
        def _():
            copy(ZD, me, acc.at[me], zdr.at[me], {"z": z + 1}).wait_recv()
            add(out_rows, 0, rows, [(acc.at[me], 0), (zdr.at[me], 0)])

        @pl.when(z == zn - 1)
        def _():
            copy(ZU, me, acc.at[me], zur.at[me], {"z": z - 1}).wait_recv()
            add(out_rows, 0, rows, [(acc.at[me], 0), (zur.at[me], 0)])

        @pl.when((z > 0) & (z < zn - 1))
        def _():
            copy(ZD, me, acc.at[me], zdr.at[me], {"z": z + 1}).wait_recv()
            copy(ZU, me, acc.at[me], zur.at[me], {"z": z + 1}).wait_recv()
            add(out_rows, 0, rows, [(acc.at[me], 0), (zdr.at[me], 0), (zur.at[me], 0)])

    for zb in range(zn):
        for k in range(4):
            across(k, zb).wait_send()
        copy(DX, zb, dxr.at[zb], dxr.at[zb], nx).wait_send()
        copy(DY, zb, dyr.at[zb], dyr.at[zb], ny).wait_send()
        copy(X, zb, xr.at[zb], xr.at[zb], nx).wait_send()
        copy(Y, zb, yr.at[zb], yr.at[zb], ny).wait_send()
        if zn > 1:

            @pl.when(z < zb)
            def _():
                copy(ZU, zb, zur.at[zb], zur.at[zb], {"z": z + 1}).wait_send()

            @pl.when(z > zb)
            def _():
                copy(ZD, zb, zdr.at[zb], zdr.at[zb], {"z": z - 1}).wait_send()


def reduce_z_first_steps(
    zn, p_ref, at, o_ref, to, acc, crecv, zur, zdr, dxr, dyr, xr, yr, ssem, rsem, lsem
):
    y, x, c, z = [lax.axis_index(n) for n in ALL]
    rows = acc.shape[1]
    h0 = half_rows(rows, acc.dtype)
    h1 = rows - h0
    X, Y, DX, DY, C, ZU, ZD = range(7)
    nx, ny, nc = {"x": 1 - x}, {"y": 1 - y}, {"c": 1 - c}
    up, down = {"z": z + 1}, {"z": z - 1}
    kinds = [(y, x), (y, 1 - x), (1 - y, x), (1 - y, 1 - x)]
    zorder = sorted(range(zn), key=lambda zb: (abs(2 * zb - zn + 1), zb), reverse=True)
    blocks = [(k, zb) for k in range(4) for zb in range(zn)]

    def slot(k, cc, zz):
        yy, xx = kinds[k]
        return ((yy * 2 + xx) * 2 + cc) * zn + zz

    def copy(kind, k, src, dst, to):
        return remote(src, dst, ssem.at[kind, k], rsem.at[kind, k], **to)

    def load(k, zb):
        b = k * zn + zb
        return pltpu.make_async_copy(p_ref.at[slot(k, c, zb), pl.ds(at, rows)], acc.at[b], lsem.at[b])

    def across(k, zb):
        b = k * zn + zb
        return copy(C, b, p_ref.at[slot(k, 1 - c, zb), pl.ds(at, rows)], crecv.at[b], nc)

    def upward(b):
        return copy(ZU, b, acc.at[b], zur.at[b], up)

    def downward(b):
        return copy(ZD, b, acc.at[b], zdr.at[b], down)

    def add(dst, start, count, terms):
        @pl.loop(0, count // 16)
        def _(i):
            total = None
            for ref, base in terms:
                part = ref[pl.ds(pl.multiple_of(start - base + i * 16, 16), 16), :]
                part = part.astype(jnp.float32)
                total = part if total is None else total + part
            dst[pl.ds(pl.multiple_of(start + i * 16, 16), 16), :] = total.astype(dst.dtype)

    def flow(k, zb):
        b = k * zn + zb
        load(k, zb).wait()
        across(k, zb).wait_recv()
        both = [(acc.at[b], 0), (crecv.at[b], 0)]

        @pl.when((z == zb) | ((z < zb) & (z == 0)) | ((z > zb) & (z == zn - 1)))
        def _():
            add(acc.at[b], 0, rows, both)

        @pl.when((z < zb) & (z > 0))
        def _():
            upward(b).wait_recv()
            add(acc.at[b], 0, rows, both + [(zur.at[b], 0)])

        @pl.when((z > zb) & (z < zn - 1))
        def _():
            downward(b).wait_recv()
            add(acc.at[b], 0, rows, both + [(zdr.at[b], 0)])

        @pl.when(z < zb)
        def _():
            upward(b).start()

        @pl.when(z > zb)
        def _():
            downward(b).start()

    def settle(k):
        b = k * zn + z

        @pl.when(z > 0)
        def _():
            upward(b).wait_recv()
            add(acc.at[b], 0, rows, [(acc.at[b], 0), (zur.at[b], 0)])

        @pl.when(z < zn - 1)
        def _():
            downward(b).wait_recv()
            add(acc.at[b], 0, rows, [(acc.at[b], 0), (zdr.at[b], 0)])

        return acc.at[b]

    for k in (3, 1, 2, 0):
        for zb in zorder:
            across(k, zb).start()
            load(k, zb).start()
    lo, hi = pl.ds(0, h0), pl.ds(h0, h1)
    for k in (3, 1):
        for zb in zorder:
            yield
            flow(k, zb)
    yield
    block = settle(3)
    copy(DX, 0, block.at[lo], dxr, nx).start()
    copy(DY, 0, block.at[hi], dyr, ny).start()
    for k in (2, 0):
        for zb in zorder:
            yield
            flow(k, zb)
    yield
    block = settle(1)
    copy(DY, 0, dyr, dyr, ny).wait_recv()
    add(block, h0, h1, [(block, 0), (dyr, h0)])
    copy(X, 0, block, xr, nx).start()
    yield
    block = settle(2)
    copy(DX, 0, dxr, dxr, nx).wait_recv()
    add(block, 0, h0, [(block, 0), (dxr, 0)])
    copy(Y, 0, block, yr, ny).start()
    yield
    block = settle(0)
    copy(X, 0, xr, xr, nx).wait_recv()
    copy(Y, 0, yr, yr, ny).wait_recv()
    add(o_ref.at[pl.ds(to, rows)], 0, rows, [(block, 0), (xr, 0), (yr, 0)])
    for kind, ref in ((DX, dxr), (DY, dyr), (X, xr), (Y, yr)):
        copy(kind, 0, ref, ref, nx).wait_send()
    for k, zb in blocks:
        b = k * zn + zb
        across(k, zb).wait_send()

        @pl.when(z < zb)
        def _():
            upward(b).wait_send()

        @pl.when(z > zb)
        def _():
            downward(b).wait_send()


def segments_of(rows, inputs=1):
    if rows < 192 or inputs > 1:
        return [(0, rows)]
    first = (rows // 2 + 31) // 32 * 32
    return [(0, first), (first, rows - first)]


def reduce_plan(zn, p_refs, o_ref, scratch, z_first=()):
    parts, base, lag = [], 0, 0
    for i, p_ref in enumerate(p_refs):
        for at, rows in segments_of(p_ref.shape[1], len(p_refs)):
            mine, scratch = scratch[:11], scratch[11:]
            if i in z_first:
                parts.append((0, reduce_z_first_steps(zn, p_ref, at, o_ref, base + at, *mine)))
                continue
            parts.append((lag, reduce_steps(zn, p_ref, at, o_ref, base + at, *mine)))
            lag += LAG_ONE if len(p_refs) == 1 else LAG_MANY
        base += p_ref.shape[1]
    return parts


def reduce_kernel(zn, p_ref, o_ref, *scratch):
    greet(zn, *[lax.axis_index(n) for n in ALL])
    run_steps(*reduce_plan(zn, [p_ref], o_ref, scratch))


def reduce_scratch(zn, rows, cols, dtype, inputs=1, z_first=False):
    entries = []
    for _, n in segments_of(rows, inputs):
        h0 = half_rows(n, dtype)
        if z_first:
            shapes = [(4 * zn, n, cols)] * 4 + [(h0, cols), (n - h0, cols), (n, cols), (n, cols)]
            sems = pltpu.SemaphoreType.DMA((7, 4 * zn))
        else:
            counts = [(4 * zn, n), (4 * zn, n), (zn, h0), (zn, n - h0)] + [(zn, n)] * 4
            shapes = [(m, r, cols) for m, r in counts]
            sems = pltpu.SemaphoreType.DMA((10, zn))
        entries += [pltpu.VMEM(shape, dtype) for shape in shapes]
        entries += [sems, sems, pltpu.SemaphoreType.DMA((4 * zn,))]
    return entries


def reduce_scatter(p, zn, ident, name, out_dtype=None):
    count, rows, cols = p.shape
    return pl.pallas_call(
        functools.partial(reduce_kernel, zn),
        out_shape=jax.ShapeDtypeStruct((rows, cols), out_dtype or p.dtype),
        in_specs=[pl.BlockSpec(memory_space=pl.ANY)],
        out_specs=pl.BlockSpec(memory_space=pltpu.VMEM),
        scratch_shapes=reduce_scratch(zn, rows, cols, p.dtype),
        compiler_params=pltpu.CompilerParams(
            collective_id=ident, has_side_effects=True, vmem_limit_bytes=VMEM
        ),
        name=name,
    )(p)


def both_kernel(inputs, z_first, zr, zg, *refs):
    p_refs, (x_ref, r_ref, o_ref), scratch = refs[:inputs], refs[inputs : inputs + 3], refs[inputs + 3 :]
    greet(max(zr, zg), *[lax.axis_index(n) for n in ALL])
    gather = (0, gather_steps(zg, x_ref, o_ref, *scratch[-4:]))
    run_steps(gather, *reduce_plan(zr, p_refs, r_ref, scratch[:-4], z_first))


def scatter_and_gather(parts, zr, x, zg, ident, name, z_first=()):
    inputs = len(parts)
    count, each, cols = parts[0].shape
    rows, dtype = inputs * each, parts[0].dtype
    return pl.pallas_call(
        functools.partial(both_kernel, inputs, z_first, zr, zg),
        out_shape=(
            jax.ShapeDtypeStruct((rows, cols), dtype),
            jax.ShapeDtypeStruct((8 * zg,) + x.shape, x.dtype),
        ),
        in_specs=[pl.BlockSpec(memory_space=pl.ANY)] * (inputs + 1),
        out_specs=(pl.BlockSpec(memory_space=pltpu.VMEM), pl.BlockSpec(memory_space=pl.ANY)),
        scratch_shapes=[
            entry for i in range(inputs) for entry in reduce_scratch(zr, each, cols, dtype, inputs, i in z_first)
        ]
        + gather_scratch(zg, x.shape, x.dtype),
        compiler_params=pltpu.CompilerParams(
            collective_id=ident, has_side_effects=True, vmem_limit_bytes=VMEM
        ),
        name=name,
    )(*parts, x)


def greet_pair(x, c):
    barrier = pltpu.get_barrier_semaphore()
    for to in ({"x": 1 - x}, {"c": 1 - c}):
        pl.semaphore_signal(barrier, inc=1, device_id=to, device_id_type=MESH)
    pl.semaphore_wait(barrier, 2)


def keys_gather_kernel(x_ref, o_ref, hold, ssem, rsem, lsem):
    x, c = lax.axis_index("x"), lax.axis_index("c")
    me, far = x * 2 + c, (1 - x) * 2 + c
    nx, nc = {"x": 1 - x}, {"c": 1 - c}
    load = pltpu.make_async_copy(x_ref, hold, lsem.at[0])
    load.start()
    greet_pair(x, c)
    out = remote(x_ref, o_ref.at[me], ssem.at[0], rsem.at[0], **nx)
    out.start()
    near = remote(x_ref, o_ref.at[me], ssem.at[1], rsem.at[1], **nc)
    near.start()
    load.wait()
    keep = pltpu.make_async_copy(hold, o_ref.at[me], lsem.at[1])
    keep.start()
    out.wait_recv()
    on = remote(o_ref.at[far], o_ref.at[far], ssem.at[2], rsem.at[2], **nc)
    on.start()
    near.wait_recv()
    on.wait_recv()
    keep.wait()
    out.wait_send()
    near.wait_send()
    on.wait_send()


def keys_gather(v, ident):
    sems = pltpu.SemaphoreType.DMA((3,))
    return pl.pallas_call(
        keys_gather_kernel,
        out_shape=jax.ShapeDtypeStruct((4,) + v.shape, v.dtype),
        in_specs=[pl.BlockSpec(memory_space=pl.ANY)],
        out_specs=pl.BlockSpec(memory_space=pl.ANY),
        scratch_shapes=[pltpu.VMEM(v.shape, v.dtype), sems, sems, pltpu.SemaphoreType.DMA((2,))],
        compiler_params=pltpu.CompilerParams(
            collective_id=ident, has_side_effects=True, vmem_limit_bytes=VMEM
        ),
        name="keys_gather",
    )(v)


def keys_reduce_kernel(p_ref, o_ref, acc, crecv, xr, ssem, rsem, lsem):
    x, c = lax.axis_index("x"), lax.axis_index("c")
    nx, nc = {"x": 1 - x}, {"c": 1 - c}
    rows = p_ref.shape[1]
    places = [(1 - x) * 2, x * 2]
    loads = [pltpu.make_async_copy(p_ref.at[places[i] + c], acc.at[i], lsem.at[i]) for i in range(2)]
    for load in loads:
        load.start()
    greet_pair(x, c)
    across = [
        remote(p_ref.at[places[i] + 1 - c], crecv.at[i], ssem.at[i], rsem.at[i], **nc) for i in range(2)
    ]
    for copy in across:
        copy.start()

    def add(dst, terms):
        @pl.loop(0, rows // 16)
        def _(i):
            at = pl.ds(pl.multiple_of(i * 16, 16), 16)
            total = terms[0][at, :].astype(jnp.float32)
            for term in terms[1:]:
                total = total + term[at, :].astype(jnp.float32)
            dst[at, :] = total.astype(dst.dtype)

    loads[0].wait()
    across[0].wait_recv()
    add(acc.at[0], [acc.at[0], crecv.at[0]])
    out = remote(acc.at[0], xr, ssem.at[2], rsem.at[2], **nx)
    out.start()
    loads[1].wait()
    across[1].wait_recv()
    out.wait_recv()
    add(o_ref, [acc.at[1], crecv.at[1], xr])
    for copy in across + [out]:
        copy.wait_send()


def keys_reduce(p, ident):
    block = p.shape[1:]
    sems = pltpu.SemaphoreType.DMA((3,))
    return pl.pallas_call(
        keys_reduce_kernel,
        out_shape=jax.ShapeDtypeStruct(block, p.dtype),
        in_specs=[pl.BlockSpec(memory_space=pl.ANY)],
        out_specs=pl.BlockSpec(memory_space=pltpu.VMEM),
        scratch_shapes=[
            pltpu.VMEM((2,) + block, p.dtype), pltpu.VMEM((2,) + block, p.dtype),
            pltpu.VMEM(block, p.dtype), sems, sems, pltpu.SemaphoreType.DMA((2,)),
        ],
        compiler_params=pltpu.CompilerParams(
            collective_id=ident, has_side_effects=True, vmem_limit_bytes=VMEM
        ),
        name="keys_reduce",
    )(p)


def fits():
    return [lax.axis_size(n) for n in ALL] == [2, 2, 2, 4]


def gather_all(v, ident, name):
    if fits():
        return all_gather(v, 4, ident, name)
    return lax.all_gather(v, ALL, axis=0)


def gather_plane(v, ident, name):
    if fits():
        return all_gather(v, 1, ident, name)
    return lax.all_gather(v, DP, axis=0)


def scatter_all(p, ident, name):
    if fits():
        return reduce_scatter(p, 4, ident, name)
    return lax.psum_scatter(p, ALL, scatter_dimension=0)


def scatter_plane(p, ident, name):
    if fits():
        return reduce_scatter(p, 1, ident, name)
    return lax.psum_scatter(p, DP, scatter_dimension=0)


def keys_all_gather(v):
    if fits():
        return keys_gather(v, 11).reshape(-1, v.shape[1])
    return lax.all_gather(v, PART, axis=0, tiled=True)


def keys_sum_scatter(p):
    if fits():
        return keys_reduce(p.reshape(4, -1, p.shape[1]), 12)
    return lax.psum_scatter(p, PART, scatter_dimension=0, tiled=True)


def tile_spec(dp, deep, tile_rows, index, local=None):
    def place(t):
        j = index(t)
        return (j % dp, 0, j // dp if local is None else local, 0, 0)

    return pl.BlockSpec((None, deep, None, tile_rows, D), place)


def weight_specs(weights, *groups):
    arrays, specs = [], []
    for first, offset in groups:
        array, local = weights[first // weights[0][0].shape[0]]
        dp, deep, _, tile_rows, _ = array.shape
        arrays.append(array)
        specs.append(
            tile_spec(dp, deep, tile_rows, lambda t, f=first, o=offset: f + o(t), local)
        )
    return arrays, specs


def whole(shape):
    return pl.BlockSpec(shape, lambda t: (0,) * len(shape))


def dot_nn(a, b):
    return lax.dot_general(a, b, (((1,), (0,)), ((), ())), preferred_element_type=jnp.float32)


def dot_nt(a, b):
    return lax.dot_general(a, b, (((1,), (1,)), ((), ())), preferred_element_type=jnp.float32)


def dot_tn(a, b):
    return lax.dot_general(a, b, (((0,), (0,)), ((), ())), preferred_element_type=jnp.float32)


def turned(u, cos, sin):
    lane = lax.broadcasted_iota(jnp.int32, (u.shape[0], 128), 1)
    low = (lane % HD) < HD // 2
    parts = []
    for i in range(D // 128):
        v = u[:, i * 128 : (i + 1) * 128]
        other = jnp.where(low, pltpu.roll(v, 128 - HD // 2, 1), pltpu.roll(v, HD // 2, 1))
        parts.append(v * cos + other * sin)
    return jnp.concatenate(parts, axis=1)


def project_kernel(x_ref, g_ref, cos_ref, sin_ref, w_ref, q_ref, kv_ref, a_ref):
    t = pl.program_id(0)

    @pl.when(t == 0)
    def _():
        a_ref[...] = root_norm(x_ref[...], g_ref[...]).astype(jnp.bfloat16)

    m = dot_nn(a_ref[...], w_ref[...].reshape(D, D))

    @pl.when(t == 0)
    def _():
        q_ref[...] = turned(m, cos_ref[...], sin_ref[...]).astype(jnp.bfloat16)

    @pl.when(t == 1)
    def _():
        kv_ref[...] = turned(m, cos_ref[...], sin_ref[...]).astype(jnp.bfloat16)

    @pl.when(t == 2)
    def _():
        kv_ref[...] = m.astype(jnp.bfloat16)


def project(x, gain, cos, sin, weights):
    rows = x.shape[0]
    arrays, specs = weight_specs(weights, (0, lambda t: t))
    return pl.pallas_call(
        project_kernel,
        grid=(3,),
        out_shape=(
            jax.ShapeDtypeStruct((rows, D), jnp.bfloat16),
            jax.ShapeDtypeStruct((2, rows, D), jnp.bfloat16),
        ),
        in_specs=[
            whole((rows, D)), whole((1, D)), whole((rows, 128)), whole((rows, 128)), *specs,
        ],
        out_specs=(
            whole((rows, D)),
            pl.BlockSpec((None, rows, D), lambda t: (jnp.maximum(t - 1, 0), 0, 0)),
        ),
        scratch_shapes=[pltpu.VMEM((rows, D), jnp.bfloat16)],
        compiler_params=pltpu.CompilerParams(vmem_limit_bytes=VMEM_LAYER),
        name="project",
    )(x, gain, cos, sin, *arrays)


def mask_bias(bias_ref, kseg_ref, qseg_ref, qpos_ref):
    kpos = lax.broadcasted_iota(jnp.int32, bias_ref.shape, 0)
    allowed = (kpos <= qpos_ref[...]) & (kseg_ref[...] == qseg_ref[...])
    bias_ref[...] = jnp.where(allowed, 0.0, MASKED)


def head_lanes(shape, head):
    return (lax.broadcasted_iota(jnp.int32, shape, 1) // HD) == head


def attend_kernel(q_ref, k_ref, v_ref, kseg_ref, qseg_ref, qpos_ref, o_ref, lse_ref, bias_ref):
    @pl.when(pl.program_id(0) == 0)
    def _():
        mask_bias(bias_ref, kseg_ref, qseg_ref, qpos_ref)

    length = bias_ref.shape[0]
    q = q_ref[...] * HD ** (-0.5)
    k, v = k_ref[...].reshape(length, 128), v_ref[...].reshape(length, 128)
    vt = v.T
    outs = []
    for head in range(2):
        mine = head_lanes(q.shape, head)
        s = dot_nt(k, jnp.where(mine, q, jnp.zeros_like(q))) + bias_ref[...]
        top = jnp.max(s, axis=0, keepdims=True)
        e = jnp.exp(s - top)
        total = jnp.sum(e, axis=0, keepdims=True)
        p = (e * (1.0 / total)).astype(jnp.bfloat16)
        outs.append(dot_nn(vt[head * HD : (head + 1) * HD], p))
        lse_ref[head : head + 1, :] = top + jnp.log(total)
    o_ref[...] = jnp.concatenate(outs, axis=0).T.astype(jnp.bfloat16)


def attend_specs(rows, parts):
    length = parts * rows
    pair = pl.BlockSpec((rows, 128), lambda t: (0, t))
    return pair, [
        pair,
        pl.BlockSpec((parts, None, rows, 128), lambda t: (0, 0, 0, t)),
        pl.BlockSpec((parts, None, rows, 128), lambda t: (0, 1, 0, t)),
        whole((length, 1)), whole((1, rows)), whole((1, rows)),
    ]


def attend(q, kv, kseg, qseg, qpos):
    rows, parts = q.shape[0], kv.shape[0]
    pair, specs = attend_specs(rows, parts)
    return pl.pallas_call(
        attend_kernel,
        grid=(HEADS // 2,),
        out_shape=(
            jax.ShapeDtypeStruct((rows, D), jnp.bfloat16),
            jax.ShapeDtypeStruct((HEADS // 2, 8, rows), jnp.float32),
        ),
        in_specs=specs,
        out_specs=(pair, pl.BlockSpec((None, 8, rows), lambda t: (t, 0, 0))),
        scratch_shapes=[pltpu.VMEM((parts * rows, rows), jnp.float32)],
        compiler_params=pltpu.CompilerParams(vmem_limit_bytes=VMEM_LAYER),
        name="attend",
    )(q, kv, kv, kseg, qseg, qpos)


def feed_kernel(x_ref, o_ref, g_ref, wo_ref, wg_ref, wu_ref, wd_ref, mid_ref, out_ref, b_ref):
    t = pl.program_id(0)

    @pl.when(t == 0)
    def _():
        mid = x_ref[...] + dot_nn(o_ref[...], wo_ref[...].reshape(D, D))
        mid_ref[...] = mid
        out_ref[...] = mid
        b_ref[...] = root_norm(mid, g_ref[...]).astype(jnp.bfloat16)

    @pl.when(t > 0)
    def _():
        gate = dot_nn(b_ref[...], wg_ref[...].reshape(D, D))
        up = dot_nn(b_ref[...], wu_ref[...].reshape(D, D))
        h = (gate * jax.nn.sigmoid(gate) * up).astype(jnp.bfloat16)
        out_ref[...] += dot_nn(h, wd_ref[...].reshape(D, D))


def feed(x, o, gain, weights):
    rows = x.shape[0]
    unit = lambda t: jnp.maximum(t - 1, 0)
    arrays, specs = weight_specs(
        weights, (3, lambda t: 0 * t), (4, unit), (4 + UNITS, unit), (4 + 2 * UNITS, unit)
    )
    state = jax.ShapeDtypeStruct((rows, D), jnp.float32)
    return pl.pallas_call(
        feed_kernel,
        grid=(1 + UNITS,),
        out_shape=(state, state),
        in_specs=[
            whole((rows, D)), whole((rows, D)), whole((1, D)), *specs,
        ],
        out_specs=(whole((rows, D)), whole((rows, D))),
        scratch_shapes=[pltpu.VMEM((rows, D), jnp.bfloat16)],
        compiler_params=pltpu.CompilerParams(vmem_limit_bytes=VMEM_LAYER),
        name="feed",
    )(x, o, gain, *arrays)


def feed_back_kernel(
    groups, dy_ref, mid_ref, g_ref, o_ref, wo_ref, wg_ref, wu_ref, wd_ref, dx_ref, do_ref, dgain_ref,
    *refs,
):
    grad_refs, (b_ref, bt_ref, e_ref, dg_ref, du_ref, db_ref) = refs[:-6], refs[-6:]
    t = pl.program_id(0)
    last = pl.num_programs(0) - 1

    def emit(kind, g):
        ref = grad_refs[groups[kind]]
        ref[...] = g.astype(jnp.bfloat16).reshape(ref.shape)

    @pl.when(t == 0)
    def _():
        b = root_norm(mid_ref[...], g_ref[...])
        b_ref[...] = b.astype(jnp.bfloat16)
        bt_ref[...] = b.T.astype(jnp.bfloat16)
        e_ref[...] = dy_ref[...].astype(jnp.bfloat16)
        db_ref[...] = jnp.zeros_like(db_ref)

    @pl.when((t % 3 == 0) & (t < last))
    def _():
        gate = dot_nn(b_ref[...], wg_ref[...].reshape(D, D))
        up = dot_nn(b_ref[...], wu_ref[...].reshape(D, D))
        sigma = jax.nn.sigmoid(gate)
        h = (gate * sigma * up).astype(jnp.bfloat16)
        emit(0, dot_tn(h, e_ref[...]))
        dh = dot_nt(e_ref[...], wd_ref[...].reshape(D, D))
        dg_ref[...] = (dh * up * sigma * (1.0 + gate * (1.0 - sigma))).astype(jnp.bfloat16)
        du_ref[...] = (dh * gate * sigma).astype(jnp.bfloat16)

    @pl.when(t % 3 == 1)
    def _():
        emit(1, dot_nn(bt_ref[...], dg_ref[...]))
        db_ref[...] += dot_nt(dg_ref[...], wg_ref[...].reshape(D, D))

    @pl.when(t % 3 == 2)
    def _():
        emit(2, dot_nn(bt_ref[...], du_ref[...]))
        db_ref[...] += dot_nt(du_ref[...], wu_ref[...].reshape(D, D))

    @pl.when(t == last)
    def _():
        back, gain_back = norm_back(mid_ref[...], g_ref[...], db_ref[...])
        dx = dy_ref[...] + back
        dx_ref[...] = dx
        dgain_ref[...] = jnp.broadcast_to(gain_back[None, :], dgain_ref.shape)
        e1 = dx.astype(jnp.bfloat16)
        emit(3, dot_tn(o_ref[...], e1))
        do_ref[...] = dot_nt(e1, wo_ref[...].reshape(D, D)).astype(jnp.bfloat16)


def feed_back(dy, mid, gain, o, weights):
    rows = dy.shape[0]
    dp, deep, _, tile_rows, _ = weights[0][0].shape
    unit = lambda t: jnp.minimum(t // 3, UNITS - 1)
    arrays, specs = weight_specs(
        weights, (3, lambda t: 0 * t), (4, unit), (4 + UNITS, unit), (4 + 2 * UNITS, unit)
    )
    firsts = [4 + 2 * UNITS, 4, 4 + UNITS, 3]
    groups = [first // dp for first in firsts]

    def grad_tile(group, t):
        kinds = [k for k in range(3) if groups[k] == group]
        s, k = unit(t), t % 3
        tile = firsts[kinds[0]] + jnp.where(k < kinds[0], jnp.maximum(s - 1, 0), s)
        for kind in kinds[1:]:
            tile = jnp.where(k >= kind, firsts[kind] + s, tile)
        final = 3 if groups[3] == group else firsts[kinds[-1]] + UNITS - 1
        return jnp.where(t == 3 * UNITS, final, tile)

    return pl.pallas_call(
        functools.partial(feed_back_kernel, groups),
        grid=(3 * UNITS + 1,),
        out_shape=(
            jax.ShapeDtypeStruct((rows, D), jnp.float32),
            jax.ShapeDtypeStruct((rows, D), jnp.bfloat16),
            jax.ShapeDtypeStruct((8, D), jnp.float32),
        )
        + (jax.ShapeDtypeStruct((dp, deep, 1, tile_rows, D), jnp.bfloat16),) * len(weights),
        in_specs=[
            whole((rows, D)), whole((rows, D)), whole((1, D)), whole((rows, D)), *specs,
        ],
        out_specs=(whole((rows, D)), whole((rows, D)), whole((8, D)))
        + tuple(
            tile_spec(dp, deep, tile_rows, functools.partial(grad_tile, group), 0)
            for group in range(len(weights))
        ),
        scratch_shapes=[
            pltpu.VMEM((rows, D), jnp.bfloat16), pltpu.VMEM((D, rows), jnp.bfloat16),
            pltpu.VMEM((rows, D), jnp.bfloat16), pltpu.VMEM((rows, D), jnp.bfloat16),
            pltpu.VMEM((rows, D), jnp.bfloat16), pltpu.VMEM((rows, D), jnp.float32),
        ],
        compiler_params=pltpu.CompilerParams(vmem_limit_bytes=VMEM_LAYER),
        name="feed_back",
    )(dy, mid, gain, o, *arrays)


def attend_back_kernel(
    q_ref, k_ref, v_ref, kseg_ref, qseg_ref, qpos_ref, do_ref, lse_ref, dq_ref, dkv_ref, bias_ref
):
    @pl.when(pl.program_id(0) == 0)
    def _():
        mask_bias(bias_ref, kseg_ref, qseg_ref, qpos_ref)

    length = bias_ref.shape[0]
    parts, rows = dkv_ref.shape[0], q_ref.shape[0]
    q, do = q_ref[...] * HD ** (-0.5), do_ref[...]
    k, v = k_ref[...].reshape(length, 128), v_ref[...].reshape(length, 128)
    kt = k.T
    dqs, dk, dv = [], None, None
    for head in range(2):
        mine = head_lanes(q.shape, head)
        qm = jnp.where(mine, q, jnp.zeros_like(q))
        dom = jnp.where(mine, do, jnp.zeros_like(do))
        s = dot_nt(k, qm) + bias_ref[...]
        p = jnp.exp(s - lse_ref[head : head + 1, :])
        dp = dot_nt(v, dom)
        delta = jnp.sum(p * dp, axis=0, keepdims=True)
        ds = (p * (dp - delta)).astype(jnp.bfloat16)
        dv_part = dot_nn(p.astype(jnp.bfloat16), dom)
        dk_part = dot_nn(ds, qm)
        dv = dv_part if dv is None else dv + dv_part
        dk = dk_part if dk is None else dk + dk_part
        dqs.append(dot_nn(kt[head * HD : (head + 1) * HD], ds))
    dq_ref[...] = jnp.concatenate(dqs, axis=0).T * HD ** (-0.5)
    dkv_ref[:, 0] = dk.astype(jnp.bfloat16).reshape(parts, rows, 128)
    dkv_ref[:, 1] = dv.astype(jnp.bfloat16).reshape(parts, rows, 128)


def attend_back(q, kv, kseg, qseg, qpos, do, lse):
    rows, parts = q.shape[0], kv.shape[0]
    pair, specs = attend_specs(rows, parts)
    return pl.pallas_call(
        attend_back_kernel,
        grid=(HEADS // 2,),
        out_shape=(
            jax.ShapeDtypeStruct((rows, D), jnp.float32),
            jax.ShapeDtypeStruct((parts, 2, rows, D), jnp.bfloat16),
        ),
        in_specs=specs + [pair, pl.BlockSpec((None, 8, rows), lambda t: (t, 0, 0))],
        out_specs=(pair, pl.BlockSpec((parts, 2, rows, 128), lambda t: (0, 0, 0, t))),
        scratch_shapes=[pltpu.VMEM((parts * rows, rows), jnp.float32)],
        compiler_params=pltpu.CompilerParams(vmem_limit_bytes=VMEM_LAYER),
        name="attend_back",
    )(q, kv, kv, kseg, qseg, qpos, do, lse)


def project_back_kernel(
    dx_ref, x_ref, g_ref, cos_ref, sin_ref, dq_ref, dkv_ref, w_ref, held_ref,
    grad_ref, out_ref, dgain_ref, a_ref, dm_ref, da_ref,
):
    t = pl.program_id(0)
    deep, tile_rows = grad_ref.shape[0], grad_ref.shape[1]

    @pl.when(t == 0)
    def _():
        a_ref[...] = root_norm(x_ref[...], g_ref[...]).astype(jnp.bfloat16)
        da_ref[...] = jnp.zeros_like(da_ref)
        dm_ref[...] = turned(dq_ref[...], cos_ref[...], -sin_ref[...]).astype(jnp.bfloat16)

    @pl.when(t == 1)
    def _():
        dk = dkv_ref[0].astype(jnp.float32)
        dm_ref[...] = turned(dk, cos_ref[...], -sin_ref[...]).astype(jnp.bfloat16)

    @pl.when(t == 2)
    def _():
        dm_ref[...] = dkv_ref[1]

    grad = dot_tn(a_ref[...], dm_ref[...])
    grad_ref[...] = grad.astype(jnp.bfloat16).reshape(deep, tile_rows, D)
    da_ref[...] += dot_nt(dm_ref[...], w_ref[...].reshape(D, D))

    @pl.when(t == 2)
    def _():
        back, gain_back = norm_back(x_ref[...], g_ref[...], da_ref[...])
        out_ref[...] = dx_ref[...] + back
        dgain_ref[...] = jnp.broadcast_to(gain_back[None, :], dgain_ref.shape)


def project_back(dx, x, gain, cos, sin, dq, dkv, weights, grads):
    rows = x.shape[0]
    dp, deep, _, tile_rows, _ = weights[0][0].shape
    arrays, specs = weight_specs(weights, (0, lambda t: t))
    return pl.pallas_call(
        project_back_kernel,
        grid=(3,),
        out_shape=(
            jax.ShapeDtypeStruct(grads.shape, grads.dtype),
            jax.ShapeDtypeStruct((rows, D), jnp.float32),
            jax.ShapeDtypeStruct((8, D), jnp.float32),
        ),
        in_specs=[
            whole((rows, D)), whole((rows, D)), whole((1, D)), whole((rows, 128)),
            whole((rows, 128)), whole((rows, D)), whole((2, rows, D)),
            *specs,
            pl.BlockSpec(memory_space=pl.ANY),
        ],
        out_specs=(
            tile_spec(dp, deep, tile_rows, lambda t: t, 0), whole((rows, D)), whole((8, D)),
        ),
        scratch_shapes=[
            pltpu.VMEM((rows, D), jnp.bfloat16), pltpu.VMEM((rows, D), jnp.bfloat16),
            pltpu.VMEM((rows, D), jnp.float32),
        ],
        input_output_aliases={8: 0},
        compiler_params=pltpu.CompilerParams(vmem_limit_bytes=VMEM_LAYER),
        name="project_back",
    )(dx, x, gain, cos, sin, dq, dkv, *arrays, grads)


def layer_forward(state, weights, layer, gains, cos, sin, marks):
    rows = state.shape[0]
    q, kv = project(state, gains[2 * layer : 2 * layer + 1], cos, sin, weights)
    kv = keys_all_gather(kv.reshape(2 * rows, D)).reshape(-1, 2, rows, D)
    o, lse = attend(q, kv, *marks)
    mid, out = feed(state, o, gains[2 * layer + 1 : 2 * layer + 2], weights)
    return out, (state, mid, q, kv, lse, o)


def layer_backward(grad, kept, weights, layer, gains, cos, sin, marks):
    state, mid, q, kv, lse, o = kept
    rows = state.shape[0]
    dx, do, feed_gain, *grads = feed_back(
        grad, mid, gains[2 * layer + 1 : 2 * layer + 2], o, weights
    )
    dq, dkv = attend_back(q, kv, *marks, do, lse)
    dkv = keys_sum_scatter(dkv.reshape(-1, D)).reshape(2, rows, D)
    grads[0], dx, input_gain = project_back(
        dx, state, gains[2 * layer : 2 * layer + 1], cos, sin, dq, dkv, weights, grads[0]
    )
    return dx, grads, [input_gain[0], feed_gain[0]]


def padded(v):
    count = -(-v.shape[0] // 2048) * 2048
    return jnp.pad(v, (0, count - v.shape[0])).reshape(-1, 128)


def place_kernel(slot_ref, mine_ref, w_ref, o_ref):
    g = pl.program_id(0)
    count = o_ref.shape[0]
    for i in range(count):
        t = g * count + i
        o_ref[i] = jnp.where(mine_ref[t] > 0, w_ref[slot_ref[t]], 0.0).astype(jnp.bfloat16)


def place_tiles(tile_weight, slots, mine, dp_size):
    count = slots.shape[0] // dp_size
    cap, rows, cols = tile_weight.shape
    return pl.pallas_call(
        place_kernel,
        grid_spec=pltpu.PrefetchScalarGridSpec(
            num_scalar_prefetch=2,
            grid=(dp_size,),
            in_specs=[pl.BlockSpec((cap, rows, cols), lambda g, *_: (0, 0, 0))],
            out_specs=pl.BlockSpec((count, rows, cols), lambda g, *_: (g, 0, 0)),
        ),
        out_shape=jax.ShapeDtypeStruct((dp_size * count, rows, cols), jnp.bfloat16),
        compiler_params=pltpu.CompilerParams(vmem_limit_bytes=VMEM),
        name="place_tiles",
    )(slots, mine, tile_weight)


def shards(
    tokens,
    segments,
    completion,
    targets,
    owners,
    step_count,
    tile_weight,
    tile_first,
    tile_second,
    table_weight,
    table_first,
    table_second,
    head_weight,
    head_first,
    head_second,
    gain_weight,
    gain_first,
    gain_second,
):
    a_size, b_size, rep_size = lax.axis_size("y"), lax.axis_size(PART), lax.axis_size("z")
    a_index, b_index, rep_index = lax.axis_index("y"), lax.axis_index(PART), lax.axis_index("z")
    dp_size = a_size * b_size
    devices = dp_size * rep_size
    dp_index = a_index * b_size + b_index
    device = dp_index * rep_size + rep_index
    rows = tokens.shape[1]
    length = segments.shape[1]
    comp = completion.shape[1]
    slots_cap, tile_rows = tile_weight.shape[:2]
    tile_count = owners.shape[0]
    home_tiles = tile_count // dp_size
    vocab_rows = table_weight.shape[0]
    vocab_start = device * vocab_rows
    sequence = a_index * rep_size + rep_index

    own_part = jnp.concatenate(
        [
            tokens[0],
            lax.dynamic_slice_in_dim(segments[0], rep_index * rows, rows),
            lax.dynamic_slice_in_dim(completion[0], rep_index * (comp // rep_size), comp // rep_size),
            lax.dynamic_slice_in_dim(targets[0], rep_index * (comp // rep_size), comp // rep_size),
        ]
    )
    slots = tile_slots(owners)
    mine = owners == dp_index
    per = TILES_PER // dp_size
    home_ids = (
        jnp.arange(LAYERS)[None, :, None] * TILES_PER
        + jnp.arange(per)[None, None, :] * dp_size
        + jnp.arange(dp_size)[:, None, None]
    ).reshape(-1)
    home_mine = jnp.take(mine, home_ids)
    home_slots = jnp.where(home_mine, jnp.take(slots, home_ids), 0)
    placed = place_tiles(tile_weight, home_slots, home_mine.astype(jnp.int32), dp_size)
    placed = placed.reshape(dp_size, -1, D)
    if fits():
        home, packed = scatter_and_gather([placed], 1, padded(own_part), 4, 0, "home_and_ids")
    else:
        home = lax.psum_scatter(placed, DP, scatter_dimension=0)
        packed = lax.all_gather(padded(own_part), ALL, axis=0)
    packed = packed.reshape(devices, -1)[:, : own_part.shape[0]]
    packed = packed.reshape(dp_size, rep_size, -1)
    tokens_all = packed[:, :, :rows].reshape(dp_size, length)
    segments_all = packed[:, :, rows : 2 * rows].reshape(dp_size, length)
    edge = 2 * rows + comp // rep_size
    completion_all = packed[:, :, 2 * rows : edge].reshape(dp_size, comp)
    targets_all = packed[:, :, edge:].reshape(dp_size, comp)

    home = home.reshape(LAYERS, per, tile_rows, D)
    spread = lax.all_gather(home[0], ALL, axis=0)
    spread = spread.reshape(dp_size, rep_size, per, tile_rows, D)
    weights = [[(spread, i) for i in range(per)]]
    later = [[lax.all_gather(home[index, i], ALL, axis=0) for i in range(1, per)] for index in range(1, LAYERS)]

    order = tokens_all.reshape(a_size, rep_size, b_size, rows).transpose(0, 2, 1, 3).reshape(-1)
    place = order - vocab_start
    vocab_iota = jnp.arange(vocab_rows)
    token_hot = (place[:, None] == vocab_iota[None, :]).astype(jnp.bfloat16)
    picked = jnp.dot(
        token_hot, table_weight.astype(jnp.bfloat16), preferred_element_type=jnp.float32
    ).astype(jnp.bfloat16)
    picked = picked.reshape(devices, rows, D)
    early = {}
    if fits():
        state, early[1] = scatter_and_gather([picked], 4, home[1, 0], 4, 8, "rows_and_weights")
    else:
        state = lax.psum_scatter(picked, ALL, scatter_dimension=0)
    state = state.astype(jnp.float32)

    for index in range(1, LAYERS):
        first = early[index] if index in early else gather_all(home[index, 0], 1, "weights_gather")
        weights.append(
            [
                (array.reshape(dp_size, rep_size, 1, tile_rows, D), 0)
                for array in [first] + later[index - 1]
            ]
        )
    first_place = b_index * rows
    places = first_place + jnp.arange(rows)
    cosine, sine = rope_tables(places.astype(jnp.float32))
    own_segments = lax.dynamic_index_in_dim(segments_all, sequence, 0, False)
    query_segments = lax.dynamic_slice_in_dim(own_segments, first_place, rows)
    marks = (own_segments[:, None], query_segments[None, :], places[None, :])
    kept_list = []
    for index in range(LAYERS):
        state, kept = layer_forward(
            state, weights[index], index, gain_weight, cosine, sine, marks
        )
        kept_list.append(kept)
    final_gain = gain_weight[2 * LAYERS]
    final = root_norm(state, final_gain).astype(jnp.bfloat16)

    capacity = 3 * comp // (2 * rep_size)
    block = completion_all // rows
    inside = block[:, None, :] == jnp.arange(b_size)[None, :, None]
    before = jnp.sum((block[:, None, :] < jnp.arange(b_size)[None, :, None]).astype(jnp.int32), axis=2)
    rank = jnp.arange(comp)[None, None, :] - before[:, :, None]
    slot_pick = inside[..., None] & (rank[..., None] == jnp.arange(capacity))
    filled = jnp.any(slot_pick, axis=2)
    wanted = jnp.where(
        filled, jnp.sum(jnp.where(slot_pick, targets_all[:, None, :, None], 0), axis=2), -1
    )
    spots = jnp.where(
        filled, jnp.sum(jnp.where(slot_pick, (completion_all % rows)[:, None, :, None], 0), axis=2), -1
    )
    all_wanted = (
        wanted.reshape(a_size, rep_size, b_size, capacity).transpose(0, 2, 1, 3).reshape(-1)
    )
    own_spots = lax.dynamic_index_in_dim(
        lax.dynamic_index_in_dim(spots, sequence, 0, False), b_index, 0, False
    )
    select = (own_spots[:, None] == jnp.arange(rows)[None, :]).astype(jnp.bfloat16)
    chosen = jnp.dot(select, final, preferred_element_type=jnp.float32).astype(jnp.bfloat16)
    all_rows = gather_all(chosen, 3, "chosen_gather").reshape(-1, D)
    head_low = head_weight.astype(jnp.bfloat16)
    logits = jnp.einsum("rd,vd->rv", all_rows, head_low, preferred_element_type=jnp.float32)
    hot = vocab_iota[None, :] == (all_wanted - vocab_start)[:, None]
    local_top = jnp.max(logits, axis=-1)
    local_total = jnp.sum(jnp.exp(logits - local_top[:, None]), axis=-1)
    local_hit = jnp.sum(jnp.where(hot, logits, 0.0), axis=-1)
    own_stats = jnp.concatenate(
        [v.reshape(-1, 128) for v in (local_top, local_total, local_hit)]
    )
    stats = gather_all(own_stats, 4, "stats_gather")
    tops, totals, hits = jnp.split(stats, 3, axis=1)
    top = jnp.max(tops, axis=0)
    total = jnp.sum(totals * jnp.exp(tops - top[None]), axis=0)
    log_total = (top + jnp.log(total)).reshape(-1)
    target_hit = jnp.sum(hits, axis=0).reshape(-1)
    valid = all_wanted >= 0
    scored = dp_size * comp
    loss = jnp.sum(jnp.where(valid, log_total - target_hit, 0.0)) / scored
    logit_grad = jnp.where(
        valid[:, None],
        (jnp.exp(logits - log_total[:, None]) - jnp.where(hot, 1.0, 0.0)) / scored,
        0.0,
    ).astype(jnp.bfloat16)
    logit_grad = lax.optimization_barrier(logit_grad)
    rows_grad = jnp.dot(logit_grad, head_low, preferred_element_type=jnp.float32)
    own_rows = scatter_all(
        rows_grad.astype(jnp.bfloat16).reshape(devices, -1, D), 9, "back_scatter"
    )
    head_grad = jnp.einsum("rv,rd->vd", logit_grad, all_rows, preferred_element_type=jnp.float32)
    final_grad = jnp.einsum("ct,cd->td", select, own_rows, preferred_element_type=jnp.float32)
    state_grad, final_gain_grad = norm_back(state, final_gain, final_grad)
    tile_parts = [None] * LAYERS
    gain_parts = [None] * LAYERS
    for index in reversed(range(LAYERS)):
        state_grad, tile_parts[index], gain_parts[index] = layer_backward(
            state_grad, kept_list[index], weights[index], index, gain_weight, cosine, sine, marks
        )
    entry = state_grad.astype(jnp.bfloat16)
    flat = [[part.reshape(devices, -1, D) for part in layer] for layer in tile_parts]
    if fits():
        tail = [lax.psum_scatter(flat[-1][-1], ALL, scatter_dimension=0)]
        firsts = [part for layer in flat for part in layer][:-1]
        body, piece_grads = scatter_and_gather(firsts, 4, entry, 4, 2, "grads_and_entry", (2,))
        home_grads = [body] + tail
    else:
        home_grads = [
            lax.psum_scatter(part, ALL, scatter_dimension=0) for layer in flat for part in layer
        ]
        piece_grads = lax.all_gather(entry, ALL, axis=0)
    table_grad = jnp.einsum(
        "tv,td->vd", token_hot, piece_grads.reshape(-1, D), preferred_element_type=jnp.float32
    )
    plane_grad = lax.all_gather(jnp.concatenate(home_grads), DP, axis=0)
    plane_grad = plane_grad.reshape(tile_count, tile_rows, D)
    own_count = jnp.sum(mine.astype(jnp.int32))
    slot_ids = jnp.arange(slots_cap)
    picks = mine[home_ids][None, :] & (slots[home_ids][None, :] == slot_ids[:, None])
    tile_of_slot = jnp.sum(jnp.where(picks, jnp.arange(tile_count)[None, :], 0), axis=1)
    slot_valid = (slot_ids < own_count)[:, None, None]
    own_grad = jnp.where(
        slot_valid, jnp.take(plane_grad, tile_of_slot, axis=0).astype(jnp.float32), 0.0
    )
    gain_grads = jnp.stack([g for pair in gain_parts for g in pair] + [final_gain_grad])
    square = (
        jnp.sum(own_grad * own_grad)
        + jnp.sum(table_grad * table_grad)
        + jnp.sum(head_grad * head_grad)
    )
    sums = gather_all(
        padded(jnp.concatenate([square[None], gain_grads.reshape(-1)])), 5, "sums_gather"
    )
    sums = jnp.sum(sums.reshape(devices, -1), axis=0)
    square, gain_grads = sums[0], sums[1 : 1 + gain_grads.size].reshape(gain_grads.shape)
    norm = jnp.sqrt(square + jnp.sum(gain_grads * gain_grads))
    factor = jnp.minimum(1.0, CLIP_NORM / norm)
    steps = step_count[0].astype(jnp.float32)
    tile_new, tile_first_new, tile_second_new = adam(
        tile_weight, tile_first, tile_second, own_grad, factor, RATE_TILE, DECAY, steps
    )
    tile_new = jnp.where(slot_valid, tile_new, 0.0)
    tile_first_new = jnp.where(slot_valid, tile_first_new, 0.0)
    tile_second_new = jnp.where(slot_valid, tile_second_new, 0.0)
    table_new, table_first_new, table_second_new = adam(
        table_weight, table_first, table_second, table_grad, factor, RATE_TABLE, DECAY, steps
    )
    head_new, head_first_new, head_second_new = adam(
        head_weight, head_first, head_second, head_grad, factor, RATE_HEAD, DECAY, steps
    )
    gain_new, gain_first_new, gain_second_new = adam(
        gain_weight, gain_first, gain_second, gain_grads, factor, RATE_GAIN, 0.0, steps
    )
    return (
        loss,
        norm,
        tile_new,
        tile_new.astype(jnp.bfloat16),
        tile_first_new,
        tile_second_new,
        table_new,
        table_new.astype(jnp.bfloat16),
        table_first_new,
        table_second_new,
        head_new,
        head_new.astype(jnp.bfloat16),
        head_first_new,
        head_second_new,
        gain_new,
        gain_first_new,
        gain_second_new,
    )


def solution(mesh):
    dp_size, rep_size = mesh.shape["dp"], mesh.shape["rep"]
    split = Mesh(mesh.devices.reshape(dp_size // rep_size, rep_size // 2, 2, rep_size), ALL)
    return jax.shard_map(
        shards,
        mesh=split,
        in_specs=(
            P(DP, "z"),
            P(DP, None),
            P(DP, None),
            P(DP, None),
            P(),
            P(),
            P(ALL, None, None),
            P(ALL, None, None),
            P(ALL, None, None),
            P(ALL, None),
            P(ALL, None),
            P(ALL, None),
            P(ALL, None),
            P(ALL, None),
            P(ALL, None),
            P(),
            P(),
            P(),
        ),
        out_specs=(
            P(),
            P(),
            P(ALL, None, None),
            P(ALL, None, None),
            P(ALL, None, None),
            P(ALL, None, None),
            P(ALL, None),
            P(ALL, None),
            P(ALL, None),
            P(ALL, None),
            P(ALL, None),
            P(ALL, None),
            P(ALL, None),
            P(ALL, None),
            P(),
            P(),
            P(),
        ),
        check_vma=False,
    )
```
